32 devices in a mesh: grp: 2 (over x), ctx: 8 (over z, y), wsh: 2 (over core).
Axes of the slice: x: 2, y: 2, z: 4, core: 2. Of those that a mesh axis runs over, the one named last changes fastest.
Arguments:
- layer_in: bfloat16 [2, 2048, 768], P('grp', ('ctx', 'wsh')), may hold values from -6 to 6
- encoded: bfloat16 [2, 64, 768], P('grp', ('ctx', 'wsh')), may hold values from -6 to 6
- cotangent: bfloat16 [2, 2048, 768], P('grp', ('ctx', 'wsh')), may hold values from -6 to 6
- deal_table: int32 [16, 2], replicated, may hold values from 0 to 31, as said below
- self_query: bfloat16 [768, 768], P(('ctx', 'wsh')), may hold values from -0.0546875 to 0.0546875
- self_key: bfloat16 [768, 768], P(('ctx', 'wsh')), may hold values from -0.21875 to 0.21875
- self_value: bfloat16 [768, 768], P(('ctx', 'wsh')), may hold values from -0.21875 to 0.21875
- self_output: bfloat16 [768, 768], P(('ctx', 'wsh')), may hold values from -1.75 to 1.75
- cross_query: bfloat16 [768, 768], P(('ctx', 'wsh')), may hold values from -0.0546875 to 0.0546875
- cross_key: bfloat16 [768, 768], P(('ctx', 'wsh')), may hold values from -0.21875 to 0.21875
- cross_value: bfloat16 [768, 768], P(('ctx', 'wsh')), may hold values from -0.21875 to 0.21875
- cross_output: bfloat16 [768, 768], P(('ctx', 'wsh')), may hold values from -0.75 to 0.75
- feed_gate: bfloat16 [768, 2048], P(('ctx', 'wsh')), may hold values from -0.21875 to 0.21875
- feed_up: bfloat16 [768, 2048], P(('ctx', 'wsh')), may hold values from -0.21875 to 0.21875
- feed_down: bfloat16 [2048, 768], P(('ctx', 'wsh')), may hold values from -0.125 to 0.125
- gain_self: bfloat16 [768], P(('ctx', 'wsh')), may hold values from 0.5 to 1.5
- gain_cross: bfloat16 [768], P(('ctx', 'wsh')), may hold values from 0.5 to 1.5
- gain_feed: bfloat16 [768], P(('ctx', 'wsh')), may hold values from 0.5 to 1.5
- relative_bias: bfloat16 [32, 12], replicated, may hold values from -3 to 3
Outputs:
- layer_out: bfloat16 [2, 2048, 768], P('grp', ('ctx', 'wsh'))
- grad_input: float32 [2, 2048, 768], P('grp', ('ctx', 'wsh'))
- grad_encoded: float32 [2, 64, 768], P('grp', ('ctx', 'wsh'))
- grad_self_query: float32 [768, 768], P(('ctx', 'wsh'))
- grad_self_key: float32 [768, 768], P(('ctx', 'wsh'))
- grad_self_value: float32 [768, 768], P(('ctx', 'wsh'))
- grad_self_output: float32 [768, 768], P(('ctx', 'wsh'))
- grad_cross_query: float32 [768, 768], P(('ctx', 'wsh'))
- grad_cross_key: float32 [768, 768], P(('ctx', 'wsh'))
- grad_cross_value: float32 [768, 768], P(('ctx', 'wsh'))
- grad_cross_output: float32 [768, 768], P(('ctx', 'wsh'))
- grad_feed_gate: float32 [768, 2048], P(('ctx', 'wsh'))
- grad_feed_up: float32 [768, 2048], P(('ctx', 'wsh'))
- grad_feed_down: float32 [2048, 768], P(('ctx', 'wsh'))
- grad_gain_self: float32 [768], P(('ctx', 'wsh'))
- grad_gain_cross: float32 [768], P(('ctx', 'wsh'))
- grad_gain_feed: float32 [768], P(('ctx', 'wsh'))
- grad_relative_bias: float32 [32, 12], replicated
The draws below stay inside these ranges and needn't reach their ends.
Inputs may be any that keep to these rules, and one draw needn't show every extreme that they name: `deal_table`: each of the 32 blocks of 64 tokens appears once. Ranking the blocks by how many earlier tokens of their own attention they follow (a prompt block by its index, a block of a continuation by 16 plus its index inside the continuation; ties by block number), every row holds the k-th and the k-th from last for one k, in either order.
All inputs are finite; a program needn't handle non-finite values.
Results may differ from the reference program's by a relative error of at most 0.028.
Values may be sent and summed in bfloat16 or wider, within the bound.
A program may use at most 384 MiB of HBM per device.

```python
import math
import jax
import jax.numpy as jnp
from jax import lax

D = 768
HEADS = 12
HD = 64
FF = 2048
BUCKETS = 32
MAXDIST = 128
INNER = 768
GROUPS = 2
SHARDS = 16
GT = 2048
ENC = 64
BLK = 64
NBLK = 32
CLEN = 1024
PROMPT = 1024
PBLK = 16
CBLK = 16
QROWS = 256


def draw_deal_table(key, part):
    numbers = jnp.arange(NBLK, dtype=jnp.int32)
    weight = jnp.where(numbers < PBLK, numbers, PBLK + (numbers - PBLK) % CBLK)
    ranking = jnp.argsort(weight * NBLK + numbers).astype(jnp.int32)
    lighter = ranking[:SHARDS]
    heavier = ranking[::-1][:SHARDS]
    first_key, second_key = jax.random.split(key)
    shuffle = jax.random.permutation(first_key, SHARDS)
    swapped = jax.random.randint(second_key, (SHARDS,), 0, 2)
    lighter = lighter[shuffle]
    heavier = heavier[shuffle]
    leading = jnp.where(swapped == 1, heavier, lighter)
    trailing = jnp.where(swapped == 1, lighter, heavier)
    return jnp.stack([leading, trailing], axis=1).astype(jnp.int32)


def block_scale(key, extent, cuts, least, top_value):
    def one(dim, blocks):
        draws = jax.random.uniform(jax.random.fold_in(jax.random.fold_in(key, 6), dim), (blocks,), jnp.float32, least / len(cuts), top_value / len(cuts))
        return jnp.repeat(jnp.exp(draws), extent[dim] // blocks).reshape((-1,) + (1,) * (len(extent) - dim - 1))

    level = one(*cuts[0])
    for cut in cuts[1:]:
        level = level * one(*cut)
    return level


def noise(key, extent, width, most, pieces=(), held_as=jnp.bfloat16):
    values = width * jax.random.normal(key, extent, jnp.float32)
    if pieces:
        values = values * block_scale(key, extent, pieces, -0.22, 0.18)
    return jnp.clip(values, -most, most).astype(held_as)


def setup_inputs(seed: int = 0) -> dict:
    splits = jax.random.split(jax.random.key(seed), 20)
    layer_in = noise(splits[0], (GROUPS, GT, D), 1.0, 6.0, ((0, 2), (1, 16)))
    encoded = noise(splits[1], (GROUPS, ENC, D), 1.0, 6.0, ((0, 2), (1, 16)))
    cotangent = noise(splits[2], (GROUPS, GT, D), 1.0, 6.0, ((0, 2), (1, 16)))
    deal_table = draw_deal_table(jax.random.fold_in(splits[19], 71), 0)
    self_query = noise(splits[4], (D, INNER), (16 * D) ** -0.5, 0.0546875, ((0, 16),))
    self_key = noise(splits[5], (D, INNER), D ** -0.5, 0.21875, ((0, 16),))
    self_value = noise(splits[6], (D, INNER), D ** -0.5, 0.21875, ((0, 16),))
    self_output = noise(splits[7], (INNER, D), HEADS ** -0.5, 1.75, ((0, 16),))
    cross_query = noise(splits[8], (D, INNER), (16 * D) ** -0.5, 0.0546875, ((0, 16),))
    cross_key = noise(splits[9], (D, INNER), D ** -0.5, 0.21875, ((0, 16),))
    cross_value = noise(splits[10], (D, INNER), D ** -0.5, 0.21875, ((0, 16),))
    cross_output = noise(splits[11], (INNER, D), HD ** -0.5, 0.75, ((0, 16),))
    feed_gate = noise(splits[12], (D, FF), D ** -0.5, 0.21875, ((0, 16),))
    feed_up = noise(splits[13], (D, FF), D ** -0.5, 0.21875, ((0, 16),))
    feed_down = noise(splits[14], (FF, D), FF ** -0.5, 0.125, ((0, 16),))
    gain_self = jnp.clip(1.0 + 0.1 * jax.random.normal(splits[15], (D,), jnp.float32), 0.5, 1.5).astype(jnp.bfloat16)
    gain_cross = jnp.clip(1.0 + 0.1 * jax.random.normal(splits[16], (D,), jnp.float32), 0.5, 1.5).astype(jnp.bfloat16)
    gain_feed = jnp.clip(1.0 + 0.1 * jax.random.normal(splits[17], (D,), jnp.float32), 0.5, 1.5).astype(jnp.bfloat16)
    relative_bias = noise(splits[18], (BUCKETS, HEADS), 0.5, 3.0)
    return dict(layer_in=layer_in, encoded=encoded, cotangent=cotangent, deal_table=deal_table, self_query=self_query, self_key=self_key, self_value=self_value, self_output=self_output, cross_query=cross_query, cross_key=cross_key, cross_value=cross_value, cross_output=cross_output, feed_gate=feed_gate, feed_up=feed_up, feed_down=feed_down, gain_self=gain_self, gain_cross=gain_cross, gain_feed=gain_feed, relative_bias=relative_bias)


MASKED = -1e+30
EPSILON = 1e-06
PRECISE = lax.Precision.HIGHEST

@jax.custom_vjp
def low(v):
    return lax.optimization_barrier(v.astype(jnp.bfloat16)).astype(jnp.float32)

@jax.custom_vjp
def low_back(v):
    return v

def low_keep(v):
    return (low(v), None)

def low_pass(kept, grad):
    return (grad,)

def back_keep(v):
    return (v, None)

def back_low(kept, grad):
    return (low(grad),)
low.defvjp(low_keep, low_pass)
low_back.defvjp(back_keep, back_low)

def rounded_both(value):
    return low_back(low(value))

def matmul(left, right):
    return jnp.dot(left, right, precision=PRECISE)

def rms_norm(hidden, gain_vector):
    return hidden * lax.rsqrt(lax.optimization_barrier(jnp.mean(hidden * hidden, axis=-1, keepdims=True)) + EPSILON) * gain_vector

def bucket_ids(distance):
    exact_half = BUCKETS // 2
    counted = jnp.minimum(distance, exact_half)
    for number in range(1, exact_half):
        boundary = int(math.ceil(exact_half * math.pow(MAXDIST / exact_half, number / exact_half)))
        counted = counted + (distance >= boundary).astype(jnp.int32)
    return counted

def token_place(tokens):
    beyond = tokens - PROMPT
    in_prompt = tokens < PROMPT
    sequence = jnp.where(in_prompt, 0, 1 + beyond // CLEN).astype(jnp.int32)
    position = jnp.where(in_prompt, tokens, PROMPT + beyond % CLEN).astype(jnp.int32)
    return (sequence, position)

def self_attention(queries, key_rows, value_rows, sequence, position, rel_table):
    blocks = GT // QROWS
    key_heads = key_rows.reshape(GT, HEADS, HD)
    value_heads = value_rows.reshape(GT, HEADS, HD)

    def one_block(operands):
        query_block, seq_block, pos_block = operands
        scores = jnp.einsum('qhd,khd->hqk', query_block, key_heads, precision=PRECISE)
        distance = jnp.maximum(pos_block[:, None] - position[None, :], 0)
        scores = scores + jnp.transpose(rel_table[bucket_ids(distance)], (2, 0, 1))
        scores = low_back(scores)
        earlier = position[None, :] <= pos_block[:, None]
        visible = (sequence[None, :] == seq_block[:, None]) | (sequence[None, :] == 0)
        scores = jnp.where((earlier & visible)[None], scores, MASKED)
        peak = lax.optimization_barrier(jnp.max(scores, axis=-1, keepdims=True))
        log_total = peak + jnp.log(lax.optimization_barrier(jnp.sum(jnp.exp(scores - peak), axis=-1, keepdims=True)))
        probs_full = jnp.exp(scores - log_total)
        return jnp.einsum('hqk,khd->qhd', low(probs_full), value_heads, precision=PRECISE)
    outputs = lax.map(jax.checkpoint(one_block), (queries.reshape(blocks, QROWS, HEADS, HD), sequence.reshape(blocks, QROWS), position.reshape(blocks, QROWS)))
    return outputs.reshape(GT, INNER)

def cross_attention(queries, key_rows, value_rows):
    blocks = GT // QROWS
    key_heads = key_rows.reshape(ENC, HEADS, HD)
    value_heads = value_rows.reshape(ENC, HEADS, HD)

    def one_block(query_block):
        scores = low_back(jnp.einsum('qhd,khd->hqk', query_block, key_heads, precision=PRECISE))
        peak = lax.optimization_barrier(jnp.max(scores, axis=-1, keepdims=True))
        log_total = peak + jnp.log(lax.optimization_barrier(jnp.sum(jnp.exp(scores - peak), axis=-1, keepdims=True)))
        probs_full = jnp.exp(scores - log_total)
        return jnp.einsum('hqk,khd->qhd', low(probs_full), value_heads, precision=PRECISE)
    outputs = lax.map(jax.checkpoint(one_block), queries.reshape(blocks, QROWS, HEADS, HD))
    return outputs.reshape(GT, INNER)

def group_layer(inputs, encoder_rows, tokens, weights):
    w_query, w_key, w_value, w_output, c_query, c_key, c_value, c_output, f_gate, f_up, f_down, g_self, g_cross, g_feed, rel_table = weights
    sequence, position = token_place(tokens)
    normed_one = low(rms_norm(inputs, g_self))
    queries = rounded_both(matmul(normed_one, w_query))
    key_rows = rounded_both(matmul(normed_one, w_key))
    value_rows = rounded_both(matmul(normed_one, w_value))
    attended = rounded_both(self_attention(queries, key_rows, value_rows, sequence, position, rel_table))
    hidden_one = inputs + low_back(matmul(attended, w_output))
    normed_two = low(rms_norm(hidden_one, g_cross))
    cross_queries = rounded_both(matmul(normed_two, c_query))
    cross_keys = rounded_both(matmul(encoder_rows, c_key))
    cross_values = rounded_both(matmul(encoder_rows, c_value))
    attended_cross = rounded_both(cross_attention(cross_queries, cross_keys, cross_values))
    hidden_two = hidden_one + low_back(matmul(attended_cross, c_output))
    normed_three = low(rms_norm(hidden_two, g_feed))
    gate_pre = low_back(matmul(normed_three, f_gate))
    up_pre = low_back(matmul(normed_three, f_up))
    mixed_hidden = rounded_both(jax.nn.gelu(gate_pre, approximate=True) * up_pre)
    return hidden_two + low_back(matmul(mixed_hidden, f_down))

def reference(layer_in, encoded, cotangent, deal_table, self_query, self_key, self_value, self_output, cross_query, cross_key, cross_value, cross_output, feed_gate, feed_up, feed_down, gain_self, gain_cross, gain_feed, relative_bias):
    tokens = (deal_table.reshape(-1).astype(jnp.int32)[:, None] * BLK + jnp.arange(BLK, dtype=jnp.int32)[None, :]).reshape(GT)
    floats = [value.astype(jnp.float32) for value in (layer_in, encoded, self_query, self_key, self_value, self_output, cross_query, cross_key, cross_value, cross_output, feed_gate, feed_up, feed_down, gain_self, gain_cross, gain_feed, relative_bias)]

    def forward(inputs, encoder_all, *weights):
        results = [group_layer(inputs[group_index], encoder_all[group_index], tokens, weights) for group_index in range(GROUPS)]
        return jnp.stack(results)
    output_sum, pull = jax.vjp(forward, *floats)
    grads = pull(cotangent.astype(jnp.float32))
    grad_input, grad_encoded, grad_self_query, grad_self_key, grad_self_value, grad_self_output, grad_cross_query, grad_cross_key, grad_cross_value, grad_cross_output, grad_feed_gate, grad_feed_up, grad_feed_down, grad_gain_self, grad_gain_cross, grad_gain_feed, grad_relative_bias = grads
    return (output_sum.astype(jnp.bfloat16), grad_input, grad_encoded, grad_self_query, grad_self_key, grad_self_value, grad_self_output, grad_cross_query, grad_cross_key, grad_cross_value, grad_cross_output, grad_feed_gate, grad_feed_up, grad_feed_down, grad_gain_self, grad_gain_cross, grad_gain_feed, grad_relative_bias)
```

```python
import functools
import math

import jax
import jax.numpy as jnp
from jax import lax
from jax.experimental import pallas as pl
from jax.experimental.pallas import tpu as pltpu
from jax.sharding import PartitionSpec as P

GRP, CTX, WSH = "grp", "ctx", "wsh"
AXES = (CTX, WSH)
EVERY = (GRP, CTX, WSH)
QK = "qhd,khd->hqk"
PV = "hqk,khd->qhd"
PTQ = "hqk,qhd->khd"
TF_TD = "tf,td->fd"
TD_FD = "td,fd->tf"
TD_TF = "td,tf->df"
TF_DF = "tf,df->td"
TC_TD = "tc,td->cd"
TD_CD = "td,cd->tc"
TD_TC = "td,tc->dc"
TC_DC = "tc,dc->td"

BUCKETS = 32
MAXDIST = 128
CONT_TOK = 2048


MASKED = -1e30
EPSILON = 1e-06


def rms_norm(hidden, gain_vector):
    return (
        hidden
        * lax.rsqrt(jnp.mean(hidden * hidden, axis=-1, keepdims=True) + EPSILON)
        * gain_vector
    )


def gated(gate_pre, up_pre):
    return jax.nn.gelu(gate_pre, approximate=True) * up_pre


def bounce(values):
    return lax.optimization_barrier(values.astype(jnp.bfloat16)).astype(jnp.float32)


def split_probs(probs_full):
    probs_high = probs_full.astype(jnp.bfloat16)
    probs_rest = (probs_full - probs_high.astype(jnp.float32)).astype(jnp.bfloat16)
    return (probs_high, probs_rest)


def bucket_ids(distance):
    exact_half = BUCKETS // 2
    counted = jnp.minimum(distance, exact_half)
    for number in range(1, exact_half):
        boundary = int(math.ceil(exact_half * math.pow(MAXDIST / exact_half, number / exact_half)))
        counted = counted + (distance >= boundary).astype(jnp.int32)
    return counted


def token_place(tokens, prompt_len, cont_len):
    beyond = tokens - prompt_len
    in_prompt = tokens < prompt_len
    sequence = jnp.where(in_prompt, 0, 1 + beyond // cont_len)
    position = jnp.where(in_prompt, tokens, prompt_len + beyond % cont_len)
    return (sequence, position)


def pair_mask(seq_query, pos_query, seq_key, pos_key):
    earlier = pos_key[None, :] <= pos_query[:, None]
    visible = (seq_key[None, :] == seq_query[:, None]) | (seq_key[None, :] == 0)
    return earlier & visible


def bucket_bias(pos_query, pos_key, table_hb):
    buckets = bucket_ids(jnp.maximum(pos_query[:, None] - pos_key[None, :], 0))
    picks = (
        buckets[None, :, :, None]
        == jnp.arange(table_hb.shape[1], dtype=jnp.int32)[None, None, None, :]
    )
    return (buckets, jnp.sum(jnp.where(picks, table_hb[:, None, None, :], 0.0), axis=-1))


def bucket_grad(buckets, grad_scores, bucket_count):
    picks = (
        buckets[None, :, :, None] == jnp.arange(bucket_count, dtype=jnp.int32)[None, None, None, :]
    )
    return jnp.sum(
        jnp.where(picks, grad_scores.astype(jnp.float32)[:, :, :, None], 0.0), axis=(1, 2)
    )


def masked_scores(query_heads, key_heads, bias, allowed):
    direct = jnp.einsum(QK, query_heads, key_heads, preferred_element_type=jnp.float32)
    return jnp.where(allowed[None], direct + bias, MASKED)


def score_grads(scores, log_total, delta_row, grad_heads, value_heads):
    probs_full = jnp.exp(scores - log_total[:, :, None])
    grad_probs = jnp.einsum(
        QK, grad_heads, value_heads, preferred_element_type=jnp.float32
    )
    grad_scores = (probs_full * (grad_probs - delta_row[:, :, None])).astype(jnp.bfloat16)
    return (probs_full.astype(jnp.bfloat16), grad_scores)


def key_view(seq_all, pos_all, step_index, key_rows, seq_query, pos_query):
    seq_key = lax.dynamic_slice_in_dim(seq_all, step_index * key_rows, key_rows)
    pos_key = lax.dynamic_slice_in_dim(pos_all, step_index * key_rows, key_rows)
    return (pos_key, pair_mask(seq_query, pos_query, seq_key, pos_key))


def self_forward(
    query_heads, key_heads, value_heads, seq_all, pos_all, seq_query, pos_query, table_hb, key_rows
):
    total_rows = key_heads.shape[0]
    head_count = query_heads.shape[1]
    rows_here = query_heads.shape[0]
    step_list = jnp.arange(total_rows // key_rows, dtype=jnp.int32)

    def total_step(carried, step_index):
        pos_key, allowed = key_view(seq_all, pos_all, step_index, key_rows, seq_query, pos_query)

        def total_accumulate(current):
            running_max, running_sum = current
            key_block = lax.dynamic_slice_in_dim(key_heads, step_index * key_rows, key_rows)
            bias = bucket_bias(pos_query, pos_key, table_hb)[1]
            scores = masked_scores(query_heads, key_block, bias, allowed)
            new_max = jnp.maximum(running_max, jnp.max(scores, axis=-1))
            weights = jnp.where(allowed[None], jnp.exp(scores - new_max[:, :, None]), 0.0)
            return (
                new_max,
                running_sum * jnp.exp(running_max - new_max) + jnp.sum(weights, axis=-1),
            )

        return (
            lax.cond(jnp.any(allowed), total_accumulate, lambda current: current, carried),
            None,
        )

    start_state = (
        jnp.full((head_count, rows_here), MASKED, jnp.float32),
        jnp.zeros((head_count, rows_here), jnp.float32),
    )
    (running_max, running_sum), _ = lax.scan(total_step, start_state, step_list)
    log_total = running_max + jnp.log(running_sum)

    def output_step(carried, step_index):
        pos_key, allowed = key_view(seq_all, pos_all, step_index, key_rows, seq_query, pos_query)

        def output_accumulate(current):
            rounded_sum, rest_sum = current
            key_block = lax.dynamic_slice_in_dim(key_heads, step_index * key_rows, key_rows)
            value_block = lax.dynamic_slice_in_dim(value_heads, step_index * key_rows, key_rows)
            bias = bucket_bias(pos_query, pos_key, table_hb)[1]
            scores = masked_scores(query_heads, key_block, bias, allowed)
            probs_high, probs_rest = split_probs(jnp.exp(scores - log_total[:, :, None]))
            rounded_sum = rounded_sum + jnp.einsum(
                PV, probs_high, value_block, preferred_element_type=jnp.float32
            )
            rest_sum = rest_sum + jnp.einsum(
                PV, probs_rest, value_block, preferred_element_type=jnp.float32
            )
            return (rounded_sum, rest_sum)

        return (
            lax.cond(jnp.any(allowed), output_accumulate, lambda current: current, carried),
            None,
        )

    zero_heads = jnp.zeros(query_heads.shape, jnp.float32)
    (rounded_sum, rest_sum), _ = lax.scan(output_step, (zero_heads, zero_heads), step_list)
    return (log_total, rounded_sum, rounded_sum + rest_sum)


def query_backward(
    query_heads,
    key_heads,
    value_heads,
    grad_heads,
    log_total,
    delta_row,
    seq_all,
    pos_all,
    seq_query,
    pos_query,
    table_hb,
    key_rows,
):
    total_rows = key_heads.shape[0]
    inner_width = key_heads.shape[1] * key_heads.shape[2]
    bucket_count = table_hb.shape[1]
    step_list = jnp.arange(total_rows // key_rows, dtype=jnp.int32)

    def step_body(carried, step_index):
        pos_key, allowed = key_view(seq_all, pos_all, step_index, key_rows, seq_query, pos_query)

        def step_accumulate(current):
            grad_query, grad_bias = current
            key_block = lax.dynamic_slice_in_dim(key_heads, step_index * key_rows, key_rows)
            value_block = lax.dynamic_slice_in_dim(value_heads, step_index * key_rows, key_rows)
            buckets, bias = bucket_bias(pos_query, pos_key, table_hb)
            scores = masked_scores(query_heads, key_block, bias, allowed)
            probs_low, grad_scores = score_grads(
                scores, log_total, delta_row, grad_heads, value_block
            )
            grad_query = grad_query + jnp.einsum(
                PV, grad_scores, key_block, preferred_element_type=jnp.float32
            )
            grad_bias = grad_bias + bucket_grad(buckets, grad_scores, bucket_count)
            grad_key = jnp.einsum(
                PTQ, grad_scores, query_heads, preferred_element_type=jnp.float32
            ).reshape(key_rows, inner_width)
            grad_value = jnp.einsum(
                PTQ, probs_low, grad_heads, preferred_element_type=jnp.float32
            ).reshape(key_rows, inner_width)
            return ((grad_query, grad_bias), jnp.concatenate([grad_key, grad_value], axis=1))

        blank_block = jnp.zeros((key_rows, 2 * inner_width), jnp.float32)
        return lax.cond(
            jnp.any(allowed), step_accumulate, lambda current: (current, blank_block), carried
        )

    start_state = (
        jnp.zeros(query_heads.shape, jnp.float32),
        jnp.zeros(table_hb.shape, jnp.float32),
    )
    final_state, key_blocks = lax.scan(step_body, start_state, step_list)
    return (final_state[0], final_state[1], key_blocks.reshape(total_rows, 2 * inner_width))


def local(
    layer_in,
    encoded,
    cotangent,
    deal_table,
    self_query,
    self_key,
    self_value,
    self_output,
    cross_query,
    cross_key,
    cross_value,
    cross_output,
    feed_gate,
    feed_up,
    feed_down,
    gain_self,
    gain_cross,
    gain_feed,
    relative_bias,
):
    shards = lax.axis_size(AXES)
    device = lax.axis_index(AXES)
    ctx_count = lax.axis_size(CTX)
    core_count = lax.axis_size(WSH)
    local_rows = layer_in.shape[1]
    total_rows = local_rows * shards
    block_len = local_rows // 2
    cont_len = min(CONT_TOK, total_rows // 2)
    prompt_len = total_rows - total_rows // 2 // cont_len * cont_len
    key_rows = min(1024, total_rows)
    head_count = relative_bias.shape[1]
    inner_width = self_query.shape[1]
    head_size = inner_width // head_count
    enc_rows = encoded.shape[1] * shards
    table_hb = relative_bias.astype(jnp.float32).T
    flat_table = deal_table.reshape(-1)
    all_tokens = (
        flat_table[:, None] * block_len + jnp.arange(block_len, dtype=jnp.int32)[None, :]
    ).reshape(-1)
    seq_all, pos_all = token_place(all_tokens, prompt_len, cont_len)
    seq_mine = lax.dynamic_slice_in_dim(seq_all, device * local_rows, local_rows)
    pos_mine = lax.dynamic_slice_in_dim(pos_all, device * local_rows, local_rows)
    forward_weights = (
        lax.all_gather(self_query, AXES, axis=0, tiled=True),
        lax.all_gather(self_key, AXES, axis=0, tiled=True),
        lax.all_gather(self_value, AXES, axis=0, tiled=True),
        lax.all_gather(self_output, AXES, axis=0, tiled=True),
        lax.all_gather(cross_query, AXES, axis=0, tiled=True),
        lax.all_gather(cross_key, AXES, axis=0, tiled=True),
        lax.all_gather(cross_value, AXES, axis=0, tiled=True),
        lax.all_gather(cross_output, AXES, axis=0, tiled=True),
        lax.all_gather(feed_gate, AXES, axis=0, tiled=True),
        lax.all_gather(feed_up, AXES, axis=0, tiled=True),
        lax.all_gather(feed_down, AXES, axis=0, tiled=True),
        lax.all_gather(gain_self, AXES, axis=0, tiled=True),
        lax.all_gather(gain_cross, AXES, axis=0, tiled=True),
        lax.all_gather(gain_feed, AXES, axis=0, tiled=True),
    )
    (
        query_weight,
        key_weight,
        value_weight,
        output_weight,
        cq_weight,
        ck_weight,
        cv_weight,
        co_weight,
        gate_weight,
        up_weight,
        down_weight,
        gain_one,
        gain_two,
        gain_three,
    ) = forward_weights
    inputs32 = layer_in[0].astype(jnp.float32)
    normed_one = rms_norm(inputs32, gain_one.astype(jnp.float32)).astype(jnp.bfloat16)
    queries = jnp.dot(normed_one, query_weight, preferred_element_type=jnp.float32).astype(
        jnp.bfloat16
    )
    keys_local = jnp.dot(normed_one, key_weight, preferred_element_type=jnp.float32).astype(
        jnp.bfloat16
    )
    values_local = jnp.dot(normed_one, value_weight, preferred_element_type=jnp.float32).astype(
        jnp.bfloat16
    )
    keys_all, values_all = (
        lax.all_gather(keys_local, AXES, axis=0, tiled=True),
        lax.all_gather(values_local, AXES, axis=0, tiled=True),
    )
    query_heads = queries.reshape(local_rows, head_count, head_size)
    key_heads = keys_all.reshape(total_rows, head_count, head_size)
    value_heads = values_all.reshape(total_rows, head_count, head_size)
    log_self, attn_sum, attn_exact = self_forward(
        query_heads,
        key_heads,
        value_heads,
        seq_all,
        pos_all,
        seq_mine,
        pos_mine,
        table_hb,
        key_rows,
    )
    attended = attn_sum.reshape(local_rows, inner_width).astype(jnp.bfloat16)
    hidden_one = inputs32 + jnp.dot(attended, output_weight, preferred_element_type=jnp.float32)
    normed_two = rms_norm(hidden_one, gain_two.astype(jnp.float32)).astype(jnp.bfloat16)
    cross_queries = jnp.dot(normed_two, cq_weight, preferred_element_type=jnp.float32).astype(
        jnp.bfloat16
    )
    enc_keys = jnp.dot(encoded[0], ck_weight, preferred_element_type=jnp.float32).astype(
        jnp.bfloat16
    )
    enc_values = jnp.dot(encoded[0], cv_weight, preferred_element_type=jnp.float32).astype(
        jnp.bfloat16
    )
    cross_keys, cross_values = (
        lax.all_gather(enc_keys, AXES, axis=0, tiled=True),
        lax.all_gather(enc_values, AXES, axis=0, tiled=True),
    )
    cq_heads = cross_queries.reshape(local_rows, head_count, head_size)
    ck_heads = cross_keys.reshape(enc_rows, head_count, head_size)
    cv_heads = cross_values.reshape(enc_rows, head_count, head_size)
    cross_scores = jnp.einsum(
        QK, cq_heads, ck_heads, preferred_element_type=jnp.float32
    )
    cross_peak = jnp.max(cross_scores, axis=-1)
    log_cross = cross_peak + jnp.log(
        jnp.sum(jnp.exp(cross_scores - cross_peak[:, :, None]), axis=-1)
    )
    cross_probs = jnp.exp(cross_scores - log_cross[:, :, None])
    cross_high, cross_rest = split_probs(cross_probs)
    cross_sum = jnp.einsum(PV, cross_high, cv_heads, preferred_element_type=jnp.float32)
    cross_exact = cross_sum + jnp.einsum(
        PV, cross_rest, cv_heads, preferred_element_type=jnp.float32
    )
    attended_cross = cross_sum.reshape(local_rows, inner_width).astype(jnp.bfloat16)
    hidden_two = hidden_one + jnp.dot(attended_cross, co_weight, preferred_element_type=jnp.float32)
    normed_three = rms_norm(hidden_two, gain_three.astype(jnp.float32)).astype(jnp.bfloat16)
    gate_pre = jnp.dot(normed_three, gate_weight, preferred_element_type=jnp.float32)
    up_pre = jnp.dot(normed_three, up_weight, preferred_element_type=jnp.float32)
    mixed_hidden = gated(gate_pre, up_pre).astype(jnp.bfloat16)
    output_sum = hidden_two + jnp.dot(mixed_hidden, down_weight, preferred_element_type=jnp.float32)
    layer_out = output_sum.astype(jnp.bfloat16)[None]
    back_weights = (
        lax.all_gather(self_query, AXES, axis=0, tiled=True),
        lax.all_gather(self_key, AXES, axis=0, tiled=True),
        lax.all_gather(self_value, AXES, axis=0, tiled=True),
        lax.all_gather(self_output, AXES, axis=0, tiled=True),
        lax.all_gather(cross_query, AXES, axis=0, tiled=True),
        lax.all_gather(cross_key, AXES, axis=0, tiled=True),
        lax.all_gather(cross_value, AXES, axis=0, tiled=True),
        lax.all_gather(cross_output, AXES, axis=0, tiled=True),
        lax.all_gather(feed_gate, AXES, axis=0, tiled=True),
        lax.all_gather(feed_up, AXES, axis=0, tiled=True),
        lax.all_gather(feed_down, AXES, axis=0, tiled=True),
        lax.all_gather(gain_self, AXES, axis=0, tiled=True),
        lax.all_gather(gain_cross, AXES, axis=0, tiled=True),
        lax.all_gather(gain_feed, AXES, axis=0, tiled=True),
    )
    (
        query_back,
        key_back,
        value_back,
        output_back,
        cq_back,
        ck_back,
        cv_back,
        co_back,
        gate_back,
        up_back,
        down_back,
        gain_one_back,
        gain_two_back,
        gain_three_back,
    ) = back_weights
    grad_out = cotangent[0]
    grad_down_w = jnp.einsum(
        TF_TD, mixed_hidden, grad_out, preferred_element_type=jnp.float32
    )
    grad_mixed = jnp.einsum(TD_FD, grad_out, down_back, preferred_element_type=jnp.float32)
    _, gate_pull = jax.vjp(gated, gate_pre, up_pre)
    grad_gate32, grad_up32 = gate_pull(bounce(grad_mixed))
    grad_gate = grad_gate32.astype(jnp.bfloat16)
    grad_up = grad_up32.astype(jnp.bfloat16)
    grad_gate_w = jnp.einsum(
        TD_TF, normed_three, grad_gate, preferred_element_type=jnp.float32
    )
    grad_up_w = jnp.einsum(TD_TF, normed_three, grad_up, preferred_element_type=jnp.float32)
    grad_normed_three = jnp.einsum(
        TF_DF, grad_gate, gate_back, preferred_element_type=jnp.float32
    ) + jnp.einsum(TF_DF, grad_up, up_back, preferred_element_type=jnp.float32)
    _, norm_pull_three = jax.vjp(rms_norm, hidden_two, gain_three_back.astype(jnp.float32))
    back_two, grad_gain_feed = norm_pull_three(grad_normed_three)
    grad_hidden_two = grad_out.astype(jnp.float32) + back_two
    grad_two_low = grad_hidden_two.astype(jnp.bfloat16)
    grad_co_w = jnp.einsum(
        TC_TD, attended_cross, grad_two_low, preferred_element_type=jnp.float32
    )
    grad_attended_cross = jnp.einsum(
        TD_CD, grad_two_low, co_back, preferred_element_type=jnp.float32
    ).astype(jnp.bfloat16)
    grad_ac_heads = grad_attended_cross.reshape(local_rows, head_count, head_size)
    delta_cross = jnp.sum(grad_ac_heads.astype(jnp.float32) * cross_exact, axis=-1).T
    cross_low, grad_cross_scores = score_grads(
        cross_scores, log_cross, delta_cross, grad_ac_heads, cv_heads
    )
    grad_cq = jnp.einsum(
        PV, grad_cross_scores, ck_heads, preferred_element_type=jnp.float32
    )
    grad_ck_part = jnp.einsum(
        PTQ, grad_cross_scores, cq_heads, preferred_element_type=jnp.float32
    ).reshape(enc_rows, inner_width)
    grad_cv_part = jnp.einsum(
        PTQ, cross_low, grad_ac_heads, preferred_element_type=jnp.float32
    ).reshape(enc_rows, inner_width)
    cross_own = lax.psum_scatter(
        jnp.concatenate([grad_ck_part, grad_cv_part], axis=1),
        AXES,
        scatter_dimension=0,
        tiled=True,
    )
    grad_cross_keys = cross_own[:, :inner_width].astype(jnp.bfloat16)
    grad_cross_values = cross_own[:, inner_width:].astype(jnp.bfloat16)
    grad_ck_w = jnp.einsum(
        TD_TC, encoded[0], grad_cross_keys, preferred_element_type=jnp.float32
    )
    grad_cv_w = jnp.einsum(
        TD_TC, encoded[0], grad_cross_values, preferred_element_type=jnp.float32
    )
    grad_encoded = (
        jnp.einsum(TC_DC, grad_cross_keys, ck_back, preferred_element_type=jnp.float32)
        + jnp.einsum(TC_DC, grad_cross_values, cv_back, preferred_element_type=jnp.float32)
    )[None]
    grad_cq_low = grad_cq.reshape(local_rows, inner_width).astype(jnp.bfloat16)
    grad_cq_w = jnp.einsum(TD_TC, normed_two, grad_cq_low, preferred_element_type=jnp.float32)
    grad_normed_two = jnp.einsum(
        TC_DC, grad_cq_low, cq_back, preferred_element_type=jnp.float32
    )
    _, norm_pull_two = jax.vjp(rms_norm, hidden_one, gain_two_back.astype(jnp.float32))
    back_one, grad_gain_cross = norm_pull_two(grad_normed_two)
    grad_hidden_one = grad_hidden_two + back_one
    grad_one_low = grad_hidden_one.astype(jnp.bfloat16)
    grad_o_w = jnp.einsum(TC_TD, attended, grad_one_low, preferred_element_type=jnp.float32)
    grad_attended = jnp.einsum(
        TD_CD, grad_one_low, output_back, preferred_element_type=jnp.float32
    ).astype(jnp.bfloat16)
    grad_att_heads = grad_attended.reshape(local_rows, head_count, head_size)
    delta_self = jnp.sum(grad_att_heads.astype(jnp.float32) * attn_exact, axis=-1).T
    grad_query32, grad_bias_part, kv_blocks = query_backward(
        query_heads,
        key_heads,
        value_heads,
        grad_att_heads,
        log_self,
        delta_self,
        seq_all,
        pos_all,
        seq_mine,
        pos_mine,
        table_hb,
        key_rows,
    )
    kv_own = lax.psum_scatter(kv_blocks, AXES, scatter_dimension=0, tiled=True)
    grad_keys = kv_own[:, :inner_width].astype(jnp.bfloat16)
    grad_values = kv_own[:, inner_width:].astype(jnp.bfloat16)
    grad_queries = grad_query32.reshape(local_rows, inner_width).astype(jnp.bfloat16)
    grad_q_w = jnp.einsum(TD_TC, normed_one, grad_queries, preferred_element_type=jnp.float32)
    grad_k_w = jnp.einsum(TD_TC, normed_one, grad_keys, preferred_element_type=jnp.float32)
    grad_v_w = jnp.einsum(TD_TC, normed_one, grad_values, preferred_element_type=jnp.float32)
    grad_normed_one = (
        jnp.einsum(TC_DC, grad_queries, query_back, preferred_element_type=jnp.float32)
        + jnp.einsum(TC_DC, grad_keys, key_back, preferred_element_type=jnp.float32)
        + jnp.einsum(TC_DC, grad_values, value_back, preferred_element_type=jnp.float32)
    )
    _, norm_pull_one = jax.vjp(rms_norm, inputs32, gain_one_back.astype(jnp.float32))
    back_input, grad_gain_self = norm_pull_one(grad_normed_one)
    grad_input = (grad_hidden_one + back_input)[None]

    def sectioned(grad_full):
        return grad_full.reshape(
            (ctx_count, core_count, grad_full.shape[0] // (ctx_count * core_count))
            + grad_full.shape[1:]
        )

    core_parts = (
        lax.psum_scatter(
            sectioned(grad_q_w).astype(jnp.bfloat16), WSH, scatter_dimension=1, tiled=True
        ).astype(jnp.float32),
        lax.psum_scatter(
            sectioned(grad_k_w).astype(jnp.bfloat16), WSH, scatter_dimension=1, tiled=True
        ).astype(jnp.float32),
        lax.psum_scatter(
            sectioned(grad_v_w).astype(jnp.bfloat16), WSH, scatter_dimension=1, tiled=True
        ).astype(jnp.float32),
        lax.psum_scatter(
            sectioned(grad_o_w).astype(jnp.bfloat16), WSH, scatter_dimension=1, tiled=True
        ).astype(jnp.float32),
        lax.psum_scatter(
            sectioned(grad_cq_w).astype(jnp.bfloat16), WSH, scatter_dimension=1, tiled=True
        ).astype(jnp.float32),
        lax.psum_scatter(
            sectioned(grad_ck_w).astype(jnp.bfloat16), WSH, scatter_dimension=1, tiled=True
        ).astype(jnp.float32),
        lax.psum_scatter(
            sectioned(grad_cv_w).astype(jnp.bfloat16), WSH, scatter_dimension=1, tiled=True
        ).astype(jnp.float32),
        lax.psum_scatter(
            sectioned(grad_co_w).astype(jnp.bfloat16), WSH, scatter_dimension=1, tiled=True
        ).astype(jnp.float32),
        lax.psum_scatter(
            sectioned(grad_gate_w).astype(jnp.bfloat16), WSH, scatter_dimension=1, tiled=True
        ).astype(jnp.float32),
        lax.psum_scatter(
            sectioned(grad_up_w).astype(jnp.bfloat16), WSH, scatter_dimension=1, tiled=True
        ).astype(jnp.float32),
        lax.psum_scatter(
            sectioned(grad_down_w).astype(jnp.bfloat16), WSH, scatter_dimension=1, tiled=True
        ).astype(jnp.float32),
        lax.psum_scatter(
            sectioned(grad_gain_self).astype(jnp.bfloat16), WSH, scatter_dimension=1, tiled=True
        ).astype(jnp.float32),
        lax.psum_scatter(
            sectioned(grad_gain_cross).astype(jnp.bfloat16), WSH, scatter_dimension=1, tiled=True
        ).astype(jnp.float32),
        lax.psum_scatter(
            sectioned(grad_gain_feed).astype(jnp.bfloat16), WSH, scatter_dimension=1, tiled=True
        ).astype(jnp.float32),
    )
    (
        core_q,
        core_k,
        core_v,
        core_o,
        core_cq,
        core_ck,
        core_cv,
        core_co,
        core_gate,
        core_up,
        core_down,
        core_gs,
        core_gc,
        core_gf,
    ) = core_parts
    owned = (
        lax.psum_scatter(core_q, CTX, scatter_dimension=0, tiled=True),
        lax.psum_scatter(core_k, CTX, scatter_dimension=0, tiled=True),
        lax.psum_scatter(core_v, CTX, scatter_dimension=0, tiled=True),
        lax.psum_scatter(core_o, CTX, scatter_dimension=0, tiled=True),
        lax.psum_scatter(core_cq, CTX, scatter_dimension=0, tiled=True),
        lax.psum_scatter(core_ck, CTX, scatter_dimension=0, tiled=True),
        lax.psum_scatter(core_cv, CTX, scatter_dimension=0, tiled=True),
        lax.psum_scatter(core_co, CTX, scatter_dimension=0, tiled=True),
        lax.psum_scatter(core_gate, CTX, scatter_dimension=0, tiled=True),
        lax.psum_scatter(core_up, CTX, scatter_dimension=0, tiled=True),
        lax.psum_scatter(core_down, CTX, scatter_dimension=0, tiled=True),
        lax.psum_scatter(core_gs, CTX, scatter_dimension=0, tiled=True),
        lax.psum_scatter(core_gc, CTX, scatter_dimension=0, tiled=True),
        lax.psum_scatter(core_gf, CTX, scatter_dimension=0, tiled=True),
    )
    (
        own_q,
        own_k,
        own_v,
        own_o,
        own_cq,
        own_ck,
        own_cv,
        own_co,
        own_gate,
        own_up,
        own_down,
        own_gain_self,
        own_gain_cross,
        own_gain_feed,
    ) = [piece.reshape(piece.shape[2:]) for piece in owned]
    summed = (
        lax.psum(own_q.astype(jnp.bfloat16), GRP).astype(jnp.float32),
        lax.psum(own_k.astype(jnp.bfloat16), GRP).astype(jnp.float32),
        lax.psum(own_v.astype(jnp.bfloat16), GRP).astype(jnp.float32),
        lax.psum(own_o.astype(jnp.bfloat16), GRP).astype(jnp.float32),
        lax.psum(own_cq.astype(jnp.bfloat16), GRP).astype(jnp.float32),
        lax.psum(own_ck.astype(jnp.bfloat16), GRP).astype(jnp.float32),
        lax.psum(own_cv.astype(jnp.bfloat16), GRP).astype(jnp.float32),
        lax.psum(own_co.astype(jnp.bfloat16), GRP).astype(jnp.float32),
        lax.psum(own_gate.astype(jnp.bfloat16), GRP).astype(jnp.float32),
        lax.psum(own_up.astype(jnp.bfloat16), GRP).astype(jnp.float32),
        lax.psum(own_down.astype(jnp.bfloat16), GRP).astype(jnp.float32),
        lax.psum(own_gain_self.astype(jnp.bfloat16), GRP).astype(jnp.float32),
        lax.psum(own_gain_cross.astype(jnp.bfloat16), GRP).astype(jnp.float32),
        lax.psum(own_gain_feed.astype(jnp.bfloat16), GRP).astype(jnp.float32),
    )
    grad_relative_bias = lax.psum(grad_bias_part.T, EVERY)
    return (
        layer_out,
        grad_input,
        grad_encoded,
        summed[0],
        summed[1],
        summed[2],
        summed[3],
        summed[4],
        summed[5],
        summed[6],
        summed[7],
        summed[8],
        summed[9],
        summed[10],
        summed[11],
        summed[12],
        summed[13],
        grad_relative_bias,
    )


BIG = 63 << 20
NT = (((1,), (1,)), ((), ()))
TN = (((0,), (0,)), ((), ()))
NN = (((1,), (0,)), ((), ()))
F32 = jnp.float32
BF16 = jnp.bfloat16


def mm(left, right, dims):
    return lax.dot_general(left, right, dims, preferred_element_type=F32)


CH = 256
BLK = 64


def load_in_order(deal, kv_hbm, kvs, sem):
    blocks = kv_hbm.shape[0] // BLK

    def one(index, carry):
        token = deal[index // 2, index % 2] * BLK
        pltpu.make_async_copy(
            kv_hbm.at[pl.ds(index * BLK, BLK)], kvs.at[pl.ds(pl.multiple_of(token, BLK), BLK)], sem
        ).start()
        return carry

    lax.fori_loop(0, blocks, one, 0)


def stack_pair(block, low_lanes):
    zero = jnp.zeros_like(block)
    return jnp.concatenate([jnp.where(low_lanes, block, zero), jnp.where(low_lanes, zero, block)], axis=0)


def fwd_kernel(mine, deal, q_ref, kv_hbm, tb_ref, att_ref, lse_ref, kvs, sco, mx, ls, acc, bias, sem):
    heads2 = q_ref.shape[1] // 128
    load_in_order(deal, kv_hbm, kvs, sem)
    lane = lax.broadcasted_iota(jnp.int32, (BLK, 128), 1)
    low = lane < BLK
    row_i = lax.broadcasted_iota(jnp.int32, (BLK, CH), 0)
    col_j = lax.broadcasted_iota(jnp.int32, (BLK, CH), 1)
    for qb in range(2):
        rank = mine[0, qb]
        for kind in range(2):
            gap = rank % 4 + 4 * kind
            dist = gap * BLK + row_i - col_j
            bucket = bucket_ids(jnp.maximum(dist, 0))
            for pair in range(heads2):
                for head in range(2):
                    row = jnp.broadcast_to(tb_ref[pl.ds(2 * pair + head, 1), :], (BLK, 128))
                    parts = [
                        jnp.take_along_axis(row, bucket[:, 128 * half : 128 * half + 128], axis=1)
                        for half in range(2)
                    ]
                    tile = jnp.concatenate(parts, axis=1)
                    if kind == 0:
                        tile = jnp.where(dist >= 0, tile, MASKED)
                    bias[qb, kind, pair, pl.ds(head * BLK, BLK), :] = tile
        for pair in range(heads2):
            for head in range(2):
                bias[qb, 2, pair, pl.ds(head * BLK, BLK), :] = jnp.broadcast_to(
                    tb_ref[pl.ds(2 * pair + head, 1), pl.ds(BUCKETS - 1, 1)], (BLK, CH)
                )
    pltpu.make_async_copy(kv_hbm, kvs, sem).wait()
    for qb in range(2):
        rank = mine[0, qb]
        last = rank // 4
        for pair in range(heads2):
            mx[pair] = jnp.full((2 * BLK, 128), -3e38, F32)
            ls[pair] = jnp.zeros((2 * BLK, 128), F32)
            acc[pair] = jnp.zeros((2 * BLK, 128), F32)

        def first(chunk, carry):
            kind = jnp.minimum(last - chunk, 2)
            keys = pl.ds(pl.multiple_of(chunk * CH, CH), CH)
            for pair in range(heads2):
                lanes = pl.ds(128 * pair, 128)
                qm = stack_pair(q_ref[pl.ds(qb * BLK, BLK), lanes], low)
                s = mm(qm, kvs[keys, lanes], NT) + bias[qb, kind, pair]
                sco[pair, :, keys] = s
                mx[pair] = jnp.maximum(mx[pair], jnp.maximum(s[:, :128], s[:, 128:]))
            return carry

        lax.fori_loop(0, last + 1, first, 0)
        for pair in range(heads2):
            mx[pair] = jnp.broadcast_to(jnp.max(mx[pair], axis=1, keepdims=True), (2 * BLK, 128))

        def second(chunk, carry):
            keys = pl.ds(pl.multiple_of(chunk * CH, CH), CH)
            for pair in range(heads2):
                top = mx[pair]
                s = sco[pair, :, keys]
                p = jnp.exp(s - jnp.concatenate([top, top], axis=1))
                ls[pair] += p[:, :128] + p[:, 128:]
                acc[pair] += mm(p.astype(BF16), kvs[keys, pl.ds(128 * heads2 + 128 * pair, 128)], NN)
            return carry

        lax.fori_loop(0, last + 1, second, 0)
        for pair in range(heads2):
            total = jnp.sum(ls[pair], axis=1, keepdims=True)
            out = acc[pair] / total
            att_ref[pl.ds(qb * BLK, BLK), pl.ds(128 * pair, 128)] = jnp.where(low, out[:BLK], out[BLK:])
            lse = mx[pair] + jnp.broadcast_to(jnp.log(total), (2 * BLK, 128))
            lse_ref[pl.ds(qb * heads2 + pair, 1), :] = lse.T[:1]


def attn_fwd(mine, deal, q, kv, tb):
    rows, inner = q.shape
    h2 = inner // 128
    total = kv.shape[0]
    sm = pl.BlockSpec(memory_space=pltpu.SMEM)
    vm = pl.BlockSpec(memory_space=pltpu.VMEM)
    return pl.pallas_call(
        fwd_kernel,
        name="attn_fwd",
        out_shape=(
            jax.ShapeDtypeStruct((rows, inner), F32),
            jax.ShapeDtypeStruct((2 * h2, 128), F32),
        ),
        in_specs=[sm, sm, vm, pl.BlockSpec(memory_space=pl.ANY), vm],
        out_specs=(vm, vm),
        scratch_shapes=[
            pltpu.VMEM((total, 2 * inner), BF16),
            pltpu.VMEM((h2, 2 * BLK, total), F32),
            pltpu.VMEM((h2, 2 * BLK, 128), F32),
            pltpu.VMEM((h2, 2 * BLK, 128), F32),
            pltpu.VMEM((h2, 2 * BLK, 128), F32),
            pltpu.VMEM((2, 3, h2, 2 * BLK, CH), F32),
            pltpu.SemaphoreType.DMA,
        ],
        compiler_params=pltpu.CompilerParams(vmem_limit_bytes=BIG),
    )(mine, deal, q, kv, tb)


def bwd_kernel(
    mine, deal, q_ref, kv_hbm, tb_ref, go_ref, att_ref, lse_ref,
    dq_ref, dkv_hbm, gb_ref,
    kvs, dkv, stage, bias, qm, dom, rows, dqa, near, nacc, tot, sem, osem,
):
    heads2 = q_ref.shape[1] // 128
    load_in_order(deal, kv_hbm, kvs, sem)
    lane = lax.broadcasted_iota(jnp.int32, (BLK, 128), 1)
    low = lane < BLK
    key_j = lax.broadcasted_iota(jnp.int32, (CH, 128), 0)
    lane_i = lax.broadcasted_iota(jnp.int32, (CH, 128), 1)
    high = lane_i >= BLK
    row_i = jnp.where(high, lane_i - BLK, lane_i)
    shift = jnp.where(high, BLK, 0)
    tot[...] = jnp.zeros_like(tot)
    nacc[...] = jnp.zeros_like(nacc)
    for qb in range(2):
        rank = mine[0, qb]
        for kind in range(2):
            gap = rank % 4 + 4 * kind
            dist = gap * BLK + row_i - key_j
            bucket = bucket_ids(jnp.maximum(dist, 0)) + shift
            for pair in range(heads2):
                tile = jnp.take_along_axis(jnp.broadcast_to(tb_ref[pl.ds(pair, 1), :], (CH, 128)), bucket, axis=1)
                if kind == 0:
                    tile = jnp.where(dist >= 0, tile, MASKED)
                bias[qb, kind, pair] = tile
        for pair in range(heads2):
            lanes = pl.ds(128 * pair, 128)
            far = jnp.where(
                high,
                tb_ref[pl.ds(pair, 1), pl.ds(BLK + BUCKETS - 1, 1)],
                tb_ref[pl.ds(pair, 1), pl.ds(BUCKETS - 1, 1)],
            )
            bias[qb, 2, pair] = far
            mine_rows = pl.ds(qb * BLK, BLK)
            qm[qb, pair] = stack_pair(q_ref[mine_rows, lanes], low)
            grad = go_ref[mine_rows, lanes]
            dom[qb, pair] = stack_pair(grad, low)
            prod = (grad.astype(F32) * att_ref[mine_rows, lanes]).T
            rows[qb, pair, pl.ds(0, 1), :] = lse_ref[pl.ds(qb * heads2 + pair, 1), :]
            rows[qb, pair, pl.ds(1, 1), :] = jnp.concatenate(
                [jnp.sum(prod[:BLK], axis=0, keepdims=True), jnp.sum(prod[BLK:], axis=0, keepdims=True)], axis=1
            )
    pltpu.make_async_copy(kv_hbm, kvs, sem).wait()
    dkv[...] = jnp.zeros_like(dkv)
    for qb in range(2):
        rank = mine[0, qb]
        last = rank // 4
        dqa[...] = jnp.zeros_like(dqa)

        @pl.when(last == 0)
        def _():
            for pair in range(heads2):
                near[pair, pl.ds(0, CH), :] = jnp.zeros((CH, 128), F32)

        def step(chunk, carry):
            kind = jnp.minimum(last - chunk, 2)
            keys = pl.ds(pl.multiple_of(chunk * CH, CH), CH)
            keep = jnp.maximum(chunk - last + 1, 0)
            for pair in range(heads2):
                klanes = pl.ds(128 * pair, 128)
                vlanes = pl.ds(128 * heads2 + 128 * pair, 128)
                kp = kvs[keys, klanes]
                qp = qm[qb, pair]
                gp = dom[qb, pair]
                st = mm(kp, qp, NT) + bias[qb, kind, pair]
                pt = jnp.exp(st - rows[qb, pair, pl.ds(0, 1), :])
                dp = mm(kvs[keys, vlanes], gp, NT)
                ds = pt * (dp - rows[qb, pair, pl.ds(1, 1), :])
                dsb = ds.astype(BF16)
                dkv[keys, vlanes] += mm(pt.astype(BF16), gp, NN)
                dkv[keys, klanes] += mm(dsb, qp, NN)
                dqa[pair] += mm(dsb, kp, TN)
                tot[pair] += jnp.sum(ds.reshape(CH // 8, 8, 128), axis=0)
                near[pair, pl.ds(pl.multiple_of(keep * CH, CH), CH), :] = ds
            return carry

        lax.fori_loop(0, last + 1, step, 0)
        for pair in range(heads2):
            out = dqa[pair]
            dq_ref[pl.ds(qb * BLK, BLK), pl.ds(128 * pair, 128)] = jnp.where(low, out[:BLK], out[BLK:]).astype(BF16)
            for gap in range(3):
                offset = pl.multiple_of((rank - gap - 4 * (last - 1)) * BLK, BLK)
                nacc[gap, pair] += near[pair, pl.ds(offset, BLK), :]
    blocks = kv_hbm.shape[0] // BLK

    def out_one(index, carry):
        token = pl.multiple_of(deal[index // 2, index % 2] * BLK, BLK)
        here = pl.ds(token, BLK)
        stage[here, :] = dkv[here, :].astype(BF16)
        pltpu.make_async_copy(stage.at[here], dkv_hbm.at[pl.ds(index * BLK, BLK)], osem).start()
        return carry

    lax.fori_loop(0, blocks, out_one, 0)
    key_s = lax.broadcasted_iota(jnp.int32, (BLK, 128), 0)
    row_s = jnp.where(low, lane, lane - BLK)
    buckets = [bucket_ids(jnp.maximum(gap * BLK + row_s - key_s, 0)) for gap in range(3)]
    out_lane = lax.broadcasted_iota(jnp.int32, (8, 128), 1)
    for pair in range(heads2):
        whole = jnp.sum(tot[pair], axis=0, keepdims=True)
        for gap in range(3):
            whole = whole - jnp.sum(nacc[gap, pair], axis=0, keepdims=True)
        lines = []
        for number in range(BUCKETS):
            line = jnp.zeros((1, 128), F32)
            for gap in range(3):
                line = line + jnp.sum(jnp.where(buckets[gap] == number, nacc[gap, pair], 0.0), axis=0, keepdims=True)
            if number == BUCKETS - 1:
                line = line + whole
            lines.append(line)
        grid = jnp.concatenate(lines, axis=0)
        lo = jnp.sum(jnp.where(lax.broadcasted_iota(jnp.int32, (BUCKETS, 128), 1) < BLK, grid, 0.0), axis=1, keepdims=True)
        hi = jnp.sum(jnp.where(lax.broadcasted_iota(jnp.int32, (BUCKETS, 128), 1) < BLK, 0.0, grid), axis=1, keepdims=True)
        gb_ref[:, pl.ds(2 * pair, 1)] = lo
        gb_ref[:, pl.ds(2 * pair + 1, 1)] = hi
    pltpu.make_async_copy(stage, dkv_hbm, osem).wait()


def attn_bwd(mine, deal, q, kv, tb, go, att, lse):
    rows, inner = q.shape
    h2 = inner // 128
    total = kv.shape[0]
    sm = pl.BlockSpec(memory_space=pltpu.SMEM)
    vm = pl.BlockSpec(memory_space=pltpu.VMEM)
    hb = pl.BlockSpec(memory_space=pl.ANY)
    return pl.pallas_call(
        bwd_kernel,
        name="attn_bwd",
        out_shape=(
            jax.ShapeDtypeStruct((rows, inner), BF16),
            jax.ShapeDtypeStruct((total, 2 * inner), BF16),
            jax.ShapeDtypeStruct((BUCKETS, 2 * h2), F32),
        ),
        in_specs=[sm, sm, vm, hb, vm, vm, vm, vm],
        out_specs=(vm, hb, vm),
        scratch_shapes=[
            pltpu.VMEM((total, 2 * inner), BF16),
            pltpu.VMEM((total, 2 * inner), F32),
            pltpu.VMEM((total, 2 * inner), BF16),
            pltpu.VMEM((2, 3, h2, CH, 128), F32),
            pltpu.VMEM((2, h2, 2 * BLK, 128), BF16),
            pltpu.VMEM((2, h2, 2 * BLK, 128), BF16),
            pltpu.VMEM((2, h2, 8, 128), F32),
            pltpu.VMEM((h2, 2 * BLK, 128), F32),
            pltpu.VMEM((h2, 2 * CH, 128), F32),
            pltpu.VMEM((3, h2, BLK, 128), F32),
            pltpu.VMEM((h2, 8, 128), F32),
            pltpu.SemaphoreType.DMA,
            pltpu.SemaphoreType.DMA,
        ],
        compiler_params=pltpu.CompilerParams(vmem_limit_bytes=BIG),
    )(mine, deal, q, kv, tb, go, att, lse)


def pair_table(table_hb):
    heads = table_hb.shape[0]
    padded = jnp.pad(table_hb, ((0, 0), (0, BLK - BUCKETS)))
    return padded.reshape(heads // 2, 2 * BLK)

MESH = pl.DeviceIdType.MESH


class Place:
    def __init__(self, nz):
        self.nz = nz
        self.g = lax.axis_index(GRP)
        self.c = lax.axis_index(CTX)
        self.w = lax.axis_index(WSH)
        self.z = self.c // 2
        self.y = lax.rem(self.c, 2)
        self.me = self.c * 2 + self.w

    def at(self, g=None, z=None, y=None, w=None):
        z = self.z if z is None else z
        y = self.y if y is None else y
        return (self.g if g is None else g, z * 2 + y, self.w if w is None else w)

    def twin(self):
        return self.at(g=1 - self.g)

    def over(self):
        return self.at(y=1 - self.y)

    def mate(self):
        return self.at(w=1 - self.w)

    def up(self, dz):
        return lax.rem(self.z + dz, self.nz)

    def down(self, dz):
        return lax.rem(self.z + self.nz - dz, self.nz)

    def meet(self):
        barrier = pltpu.get_barrier_semaphore()
        partners = [self.twin(), self.over(), self.mate()]
        partners += [self.at(z=self.up(dz)) for dz in range(1, self.nz)]
        for partner in partners:
            pl.semaphore_signal(barrier, inc=1, device_id=partner, device_id_type=MESH)
        pl.semaphore_wait(barrier, len(partners))


def push(src, dst, ssem, rsem, to):
    return pltpu.make_async_remote_copy(src, dst, ssem, rsem, device_id=to, device_id_type=MESH)


def half(wide, index):
    return pl.ds(pl.multiple_of(index * (wide // 2), 128), wide // 2)


class Gather:
    COUNT = 9

    def __init__(self, at, parts, whole, sems, split):
        self.at, self.nz, self.parts, self.whole, self.split = at, at.nz, parts, whole, split
        (self.zs, self.zr, self.ys, self.yr, self.xs, self.xr, self.ws, self.wr, self.lc) = sems
        self.sent = []

    @staticmethod
    def scratch(nz, n):
        dma = pltpu.SemaphoreType.DMA
        return [dma((nz,))] * 4 + [dma((2 * nz,))] * 2 + [dma((4 * nz,))] * 2 + [dma((n,))]

    def spot(self, z, y, w, side=None):
        view = self.whole.at[:, (z * 2 + y) * 2 + w]
        if self.split and side is not None:
            return view.at[:, :, half(self.whole.shape[-1], side)]
        return view

    def post(self, view, ssem, rsem, to):
        copy = push(view, view, ssem, rsem, to)
        copy.start()
        self.sent.append(copy)

    def to_y(self, z):
        at = self.at
        self.post(self.spot(z, at.y, at.w, at.g), self.ys.at[z], self.yr.at[z], at.over())

    def to_x(self, z, y):
        at = self.at
        if self.split:
            k = z * 2 + y
            self.post(self.spot(z, y, at.w, at.g), self.xs.at[k], self.xr.at[k], at.twin())

    def to_w(self, z, y, side):
        at = self.at
        k = (z * 2 + y) * 2 + (side if self.split and side is not None else 0)
        self.post(self.spot(z, y, at.w, side), self.ws.at[k], self.wr.at[k], at.mate())

    def place(self):
        self.local = [
            pltpu.make_async_copy(part, self.whole.at[i, self.at.me], self.lc.at[i]) for i, part in enumerate(self.parts)
        ]
        for copy in self.local:
            copy.start()

    def placed(self):
        for copy in self.local:
            copy.wait()

    def send(self):
        at = self.at
        for dz in range(1, self.nz):
            to = at.up(dz)
            self.post(self.spot(at.z, at.y, at.w, at.g), self.zs.at[to], self.zr.at[at.z], at.at(z=to))
        self.to_y(at.z)
        self.to_w(at.z, at.y, None)

    def after_z(self):
        at = self.at
        for dz in range(1, self.nz):
            z = at.down(dz)
            view = self.spot(z, at.y, at.w, at.g)
            push(view, view, self.zs.at[z], self.zr.at[z], at.at(z=z)).wait_recv()
            self.to_y(z)
            self.to_x(z, at.y)
            self.to_w(z, at.y, at.g)

    def after_y(self):
        at = self.at
        for dz in range(self.nz):
            z = at.down(dz)
            view = self.spot(z, 1 - at.y, at.w, at.g)
            push(view, view, self.ys.at[z], self.yr.at[z], at.over()).wait_recv()
            self.to_x(z, 1 - at.y)
            self.to_w(z, 1 - at.y, at.g)

    def others(self):
        for dy in range(2):
            for dz in range(self.nz):
                yield self.at.down(dz), lax.rem(self.at.y + dy, 2), dy == 0 and dz == 0

    def after_x(self):
        at = self.at
        if not self.split:
            return
        for z, y, own in self.others():
            if not own:
                k = z * 2 + y
                view = self.spot(z, y, at.w, 1 - at.g)
                push(view, view, self.xs.at[k], self.xr.at[k], at.twin()).wait_recv()
                self.to_w(z, y, 1 - at.g)

    def end(self):
        at = self.at
        for z, y, own in self.others():
            for side in range(2 if self.split and not own else 1):
                k = (z * 2 + y) * 2 + side
                view = self.spot(z, y, 1 - at.w, None if own else side)
                push(view, view, self.ws.at[k], self.wr.at[k], at.mate()).wait_recv()

    def close(self):
        for copy in self.sent:
            copy.wait_send()


class Reduce:
    COUNT = 16

    @staticmethod
    def scratch(nz, r, wide, kind, dtype, part=True):
        cols = wide // 2 if kind == "x" else wide
        dma = pltpu.SemaphoreType.DMA
        vmem = pltpu.VMEM
        none = vmem((1, 16, 128), dtype)
        return [
            vmem((2 * nz, 2, r, wide), dtype) if part else none,
            vmem((2 * nz, r, wide), dtype),
            vmem((2 * nz, r, cols), dtype) if kind == "x" else none,
            vmem((nz, r, cols), dtype),
            vmem((nz, r, cols), dtype),
            vmem((2, r, cols), dtype) if kind != "none" else none,
        ] + [dma((2 * nz,))] * 4 + [dma((nz,))] * 4 + [dma((2,))] * 2

    def __init__(self, at, out, refs, kind):
        self.at, self.nz, self.out, self.kind = at, at.nz, out, kind
        (self.part, self.wb, self.xb, self.yb, self.zb, self.fb) = refs[:6]
        (self.ws, self.wr, self.xs, self.xr, self.ys, self.yr, self.zs, self.zr, self.fs, self.fr) = refs[6:]
        self.wide = self.wb.shape[-1]
        self.local_part = None

    def c_w(self, k):
        at = self.at
        return push(self.part.at[k, 1 - at.w], self.wb.at[k], self.ws.at[k], self.wr.at[k], at.mate())

    def c_x(self, k):
        at = self.at
        src = self.wb.at[k].at[:, half(self.wide, 1 - at.g)]
        return push(src, self.xb.at[k], self.xs.at[k], self.xr.at[k], at.twin())

    def mid(self):
        return self.xb if self.kind == "x" else self.wb

    def c_y(self, z):
        at = self.at
        return push(self.mid().at[z * 2 + 1 - at.y], self.yb.at[z], self.ys.at[z], self.yr.at[z], at.over())

    def c_z(self, to):
        at = self.at
        return push(self.yb.at[to], self.zb.at[at.z], self.zs.at[to], self.zr.at[at.z], at.at(z=to))

    def c_zin(self, z):
        return push(self.yb.at[z], self.zb.at[z], self.zs.at[z], self.zr.at[z], self.at.at(z=z))

    def c_f(self):
        return push(self.fb.at[0], self.fb.at[1], self.fs.at[0], self.fr.at[0], self.at.twin())

    def piece(self, t):
        z = lax.rem(self.at.z + 1 + t // 2, self.nz)
        y = lax.rem(self.at.y + 1 + t, 2)
        return z * 2 + y

    def send(self):
        def one(t, carry):
            self.c_w(self.piece(t)).start()
            return carry

        lax.fori_loop(0, 2 * self.nz, one, 0)

    def after_w(self):
        at = self.at

        def one(t):
            k = self.piece(t)
            self.c_w(k).wait_recv()
            here = self.part[k, at.w] if self.local_part is None else self.local_part[k]
            total = self.wb[k].astype(F32) + here.astype(F32)
            self.wb[k] = total.astype(self.wb.dtype)
            if self.kind == "x":
                self.c_x(k).start()

        def both(t, carry):
            one(2 * t)
            if self.kind != "x":
                self.c_y(self.piece(2 * t) // 2).start()
            one(2 * t + 1)
            return carry

        lax.fori_loop(0, self.nz, both, 0)

    def after_x(self):
        if self.kind != "x":
            return

        def one(t):
            k = self.piece(t)
            self.c_x(k).wait_recv()
            total = self.xb[k].astype(F32) + self.wb[k, :, half(self.wide, self.at.g)].astype(F32)
            self.xb[k] = total.astype(self.xb.dtype)

        def both(t, carry):
            one(2 * t)
            self.c_y(self.piece(2 * t) // 2).start()
            one(2 * t + 1)
            return carry

        lax.fori_loop(0, self.nz, both, 0)

    def after_y(self):
        at, nz = self.at, self.nz

        def one(t, carry):
            z = lax.rem(at.z + 1 + t, nz)
            self.c_y(z).wait_recv()
            total = self.yb[z].astype(F32) + self.mid()[z * 2 + at.y].astype(F32)
            self.yb[z] = total.astype(self.yb.dtype)

            @pl.when(t < nz - 1)
            def _():
                self.c_z(z).start()

            return carry

        lax.fori_loop(0, nz, one, 0)

    def after_z(self):
        at, nz = self.at, self.nz
        for dz in range(1, nz):
            self.c_zin(at.up(dz)).wait_recv()
        total = self.yb[at.z].astype(F32)
        for dz in range(1, nz):
            total = total + self.zb[at.up(dz)].astype(F32)
        if self.kind == "x":
            self.out[:, half(self.wide, at.g)] = total
        else:
            self.out[...] = total
        if self.kind != "none":
            self.fb[0] = total.astype(self.fb.dtype)
            self.c_f().start()

    def end(self):
        at, nz = self.at, self.nz
        if self.kind != "none":
            self.c_f().wait_recv()
            other = self.fb[1].astype(F32)
            if self.kind == "x":
                self.out[:, half(self.wide, 1 - at.g)] = other
            else:
                self.out[...] = self.out[...] + other
            self.c_f().wait_send()

    def close(self):
        at, nz = self.at, self.nz

        def sends(t, carry):
            self.c_w(t).wait_send()
            if self.kind == "x":
                self.c_x(t).wait_send()
            return carry

        lax.fori_loop(0, 2 * nz, sends, 0)

        def sends_y(t, carry):
            self.c_y(t).wait_send()
            return carry

        lax.fori_loop(0, nz, sends_y, 0)
        for dz in range(1, nz):
            self.c_z(at.up(dz)).wait_send()


class Total:
    COUNT = 3

    @staticmethod
    def scratch(nz, r, wide):
        dma = pltpu.SemaphoreType.DMA
        return [pltpu.VMEM((4 + nz, r, wide), F32), dma((4 + nz,)), dma((4 + nz,))]

    def __init__(self, at, refs):
        self.at, self.nz = at, at.nz
        self.buf, self.ss, self.rs = refs

    def hop(self, i):
        at = self.at
        to = (at.mate(), at.twin(), at.over())[i]
        return push(self.buf.at[0], self.buf.at[1 + i], self.ss.at[i], self.rs.at[i], to)

    def send(self):
        self.hop(0).start()

    def after(self, i):
        hop = self.hop(i)
        hop.wait_send()
        hop.wait_recv()
        self.buf[0] = self.buf[0] + self.buf[1 + i]
        if i < 2:
            self.hop(i + 1).start()
        else:
            for dz in range(1, self.nz):
                self.along(self.at.z, self.at.up(dz)).start()

    def along(self, source, to):
        base = 4
        return push(self.buf.at[0], self.buf.at[base + source], self.ss.at[base + to], self.rs.at[base + source], self.at.at(z=to))

    def end(self):
        total = None
        for dz in range(1, self.nz):
            z = self.at.up(dz)
            self.along(z, z).wait_recv()
            self.along(self.at.z, z).wait_send()
        self.buf[4 + self.at.z] = self.buf[0]
        total = self.buf[4]
        for z in range(1, self.nz):
            total = total + self.buf[4 + z]
        return total


def dot(left, right):
    return jnp.dot(left, right, preferred_element_type=F32)


def einsum(form, left, right):
    return jnp.einsum(form, left, right, preferred_element_type=F32)


def back(grad, weight):
    return einsum(TC_DC, grad, weight)


def normed(hidden, gain):
    return hidden * lax.rsqrt(jnp.mean(hidden * hidden, axis=-1, keepdims=True) + EPSILON) * gain


def norm_back(hidden, gain, grad):
    scale = lax.rsqrt(jnp.mean(hidden * hidden, axis=-1, keepdims=True) + EPSILON)
    inner = jnp.mean(hidden * gain * grad, axis=-1, keepdims=True)
    rows = scale * gain * grad - hidden * (scale * scale * scale) * inner
    return rows, jnp.sum(grad * hidden * scale, axis=0, keepdims=True)


FRONT_SIZES = (1, 3, 5, 2, 1, 1)


def front_kernel(nz, splits, order, *refs):
    n_in = 2 + sum(FRONT_SIZES[1:5])
    ins, refs = refs[:n_in], refs[n_in:]
    wholes, (q_ref, normed_ref, gains_ref), refs = refs[:6], refs[6:9], refs[9:]
    (wbuf, kvown, wsem), sems = refs[:3], refs[3:]
    at = Place(nz)
    parts, taken = [], 1
    for size in FRONT_SIZES[:5]:
        parts.append(ins[taken : taken + size])
        taken += size
    parts.append((kvown,))
    jobs = {}
    for i, name in enumerate(("small", "qkv", "mid", "ffn", "down", "kv")):
        jobs[name] = Gather(at, parts[i], wholes[i], sems[Gather.COUNT * i : Gather.COUNT * (i + 1)], splits[i])
    for name in ("small", "qkv", "mid", "ffn", "down"):
        jobs[name].place()
    at.meet()

    def project():
        load = pltpu.make_async_copy(wholes[1], wbuf, wsem)
        load.start()
        total = wholes[0][0, 0].astype(F32)
        for device in range(1, wholes[0].shape[1]):
            total = total + wholes[0][0, device].astype(F32)
        gains_ref[...] = total
        x = ins[0][...].astype(F32)
        norm = normed(x, total[4:5]).astype(BF16)
        normed_ref[...] = norm
        load.wait()
        width = x.shape[1]
        out = [mm(norm, wbuf[i].reshape(width, -1), NN).astype(BF16) for i in range(3)]
        q_ref[...] = out[0]
        kvown[:, :width] = out[1]
        kvown[:, width:] = out[2]
        jobs["kv"].place()

    for line in order:
        name, step = line
        if name == "project":
            project()
        else:
            getattr(jobs[name], step)()
    for job in jobs.values():
        job.close()


FRONT_ORDER = [
    ("small", "placed"), ("small", "send"), ("qkv", "placed"), ("qkv", "send"),
    ("mid", "placed"), ("ffn", "placed"), ("down", "placed"),
    ("small", "after_z"), ("qkv", "after_z"), ("mid", "send"), ("small", "after_y"), ("qkv", "after_y"),
    ("qkv", "after_x"), ("small", "end"), ("qkv", "end"), ("project", ""), ("kv", "placed"), ("kv", "send"),
    ("mid", "after_z"), ("ffn", "send"), ("mid", "after_y"), ("kv", "after_z"), ("mid", "after_x"),
    ("ffn", "after_z"), ("down", "send"), ("kv", "after_y"), ("ffn", "after_y"),
    ("down", "after_z"), ("ffn", "after_x"), ("down", "after_y"), ("down", "after_x"),
    ("mid", "end"), ("kv", "end"), ("ffn", "end"), ("down", "end"),
]
FRONT_SPLITS = (False, False, True, True, True, False)


def front(x, small, weights, nz, shards, collective_id=1, splits=FRONT_SPLITS, order=FRONT_ORDER):
    hb = pl.BlockSpec(memory_space=pl.ANY)
    vm = pl.BlockSpec(memory_space=pltpu.VMEM)
    rows, width = x.shape
    shapes, taken = [(1, shards) + small.shape], 0
    for size in FRONT_SIZES[1:5]:
        shapes.append((size, shards) + weights[taken].shape)
        taken += size
    inner = weights[0].shape[1]
    shapes.append((1, shards, rows, 2 * inner))
    scratch = [pltpu.VMEM(shapes[1], BF16), pltpu.VMEM((rows, 2 * inner), BF16), pltpu.SemaphoreType.DMA]
    for size in FRONT_SIZES:
        scratch += Gather.scratch(nz, size)
    return pl.pallas_call(
        functools.partial(front_kernel, nz, splits, order),
        name="front",
        out_shape=tuple([jax.ShapeDtypeStruct(s, BF16) for s in shapes])
        + (
            jax.ShapeDtypeStruct((rows, inner), BF16),
            jax.ShapeDtypeStruct((rows, width), BF16),
            jax.ShapeDtypeStruct(small.shape, F32),
        ),
        in_specs=[vm] + [hb] * (1 + len(weights)),
        out_specs=tuple([vm] + [hb] * 5 + [vm] * 3),
        scratch_shapes=scratch,
        compiler_params=pltpu.CompilerParams(
            collective_id=collective_id, has_side_effects=True, vmem_limit_bytes=BIG
        ),
    )(x, small, *weights)


BACK_JOBS = (
    ("kv", "none"), ("cross", "none"), ("gate", "x"), ("up", "x"), ("down", "x"), ("co", "x"), ("cq", "late"),
    ("ck", "late"), ("cv", "late"), ("q", "late"), ("o", "late"), ("k", "late"), ("v", "late"),
)
BACK_ORDER = ("cross", "kv", "gate", "up", "down", "co", "o", "cq", "ck", "cv", "k", "v", "q")


def back_kernel(nz, order, *refs):
    (
        kvp, crossp, wqkv, wmid, x_ref, gains_ref, gh_ref, gpart_ref, enc_ref,
        n3, mixed, att, n2, attc, n1, gg, gu, go, g1, gcq, g2, dq,
    ) = refs[:22]
    refs = refs[22:]
    names = [name for name, _ in BACK_JOBS]
    outs = dict(zip(names[2:], refs[:11]))
    gx_ref, genc_ref, total_ref = refs[11:14]
    refs = refs[14:]
    kvown, crown, low, wbuf, kvl, kls, wsem = refs[:7]
    refs = refs[7:]
    outs["kv"], outs["cross"] = kvown, crown
    at = Place(nz)
    jobs = {}
    for i, (name, kind) in enumerate(BACK_JOBS):
        mine = list(refs[Reduce.COUNT * i : Reduce.COUNT * (i + 1)])
        if name == "cross":
            mine[0] = crossp
        jobs[name] = Reduce(at, outs[name], mine, kind)
    everyone = Total(at, refs[Reduce.COUNT * len(BACK_JOBS) :])
    jobs["kv"].part = kvp
    load_w = pltpu.make_async_copy(wqkv, wbuf, wsem.at[0])
    load_c = pltpu.make_async_copy(wmid.at[pl.ds(2, 2)], wbuf.at[pl.ds(0, 2)], wsem.at[1])
    load_c.start()
    kv_local = [pltpu.make_async_copy(kvp.at[k, at.w], kvl.at[k], kls.at[k]) for k in range(2 * nz)]
    for copy in kv_local:
        copy.start()
    at.meet()
    width = x_ref.shape[1]
    inner = dq.shape[1]

    def grad_of(name, left, right):
        part = jobs[name].part
        chips, _, r, wide = part.shape
        take = 4 if r % 128 else 1
        tile = wide // 2 if wide <= 768 else 512
        for first in range(0, chips, take):
            lanes = slice(first * 2 * r, (first + take) * 2 * r)
            piece = left[:, lanes]
            for c in range(0, wide, tile):
                out = mm(piece, right[:, c : c + tile], TN).astype(BF16)
                part[first : first + take, :, :, c : c + tile] = out.reshape(take, 2, r, tile)

    def make(name):
        if name == "kv":
            return
        if name == "cross":
            return
        if name in ("ck", "cv"):
            grad = low[:, 128 * 0 : inner] if name == "ck" else low[:, inner:]
            grad_of(name, enc_ref[...], grad)
            return
        if name == "k":
            grad_of(name, n1[...], kvl[0][:, :inner])
            return
        if name == "v":
            grad_of(name, n1[...], kvl[0][:, inner:])
            return
        left, right = {
            "gate": (n3, gg), "up": (n3, gu), "down": (mixed, go), "o": (att, g1), "cq": (n2, gcq), "co": (attc, g2),
            "q": (n1, dq),
        }[name]
        grad_of(name, left[...], right[...])

    def after_cross():
        both = crown[...]
        low[...] = jnp.concatenate([both, jnp.zeros_like(both)], axis=0).astype(BF16)
        load_c.wait()
        genc = mm(low[:, :inner], wbuf[0].reshape(width, inner), NT) + mm(low[:, inner:], wbuf[1].reshape(width, inner), NT)
        genc_ref[...] = genc[:8]
        load_w.start()

    def after_kv():
        kvl[0] = kvown[...].astype(BF16)
        load_w.wait()
        grad = mm(dq[...], wbuf[0].reshape(width, inner), NT)
        grad = grad + mm(kvl[0][:, :inner], wbuf[1].reshape(width, inner), NT)
        grad = grad + mm(kvl[0][:, inner:], wbuf[2].reshape(width, inner), NT)
        rows, gain = norm_back(x_ref[...].astype(F32), gains_ref[4:5], grad)
        gx_ref[...] = gh_ref[...] + rows
        everyone.buf[0] = gpart_ref[...]
        everyone.buf[0, 0:1, :] = gain
        everyone.send()

    stages = ("send", "after_w", "after_x", "after_y", "after_z", "end")
    count = len(order)
    kv_turn = order.index("kv") + len(stages) - 1
    for turn in range(count + len(stages) - 1):
        for i, name in enumerate(order):
            stage = turn - i
            if not 0 <= stage < len(stages):
                continue
            job = jobs[name]
            if stage == 0:
                make(name)
            if name == "kv" and stage == 1:
                for copy in kv_local:
                    copy.wait()
                job.local_part = kvl
            getattr(job, stages[stage])()
            if stage == len(stages) - 1:
                if name == "cross":
                    after_cross()
                if name == "kv":
                    after_kv()
        if 0 < turn - kv_turn <= 3:
            everyone.after(turn - kv_turn - 1)
    total_ref[...] = everyone.end()
    for job in jobs.values():
        job.close()


def back_step(kv_part, cross_part, whole_qkv, whole_mid, x, gains, grad_hidden, gpart, enc, acts, shapes, nz, collective_id=2, order=BACK_ORDER):
    hb = pl.BlockSpec(memory_space=pl.ANY)
    vm = pl.BlockSpec(memory_space=pltpu.VMEM)
    rows, width = x.shape
    inner = acts[-1].shape[1]
    dma = pltpu.SemaphoreType.DMA
    own = [jax.ShapeDtypeStruct(shapes[name], F32) for name, _ in BACK_JOBS[2:]]
    scratch = [
        pltpu.VMEM((rows, 2 * inner), F32),
        pltpu.VMEM((8, 2 * inner), F32),
        pltpu.VMEM((16, 2 * inner), BF16),
        pltpu.VMEM(whole_qkv.shape, BF16),
        pltpu.VMEM((2 * nz, rows, 2 * inner), BF16),
        dma((2 * nz,)),
        dma((2,)),
    ]
    for name, kind in BACK_JOBS:
        if name == "kv":
            scratch += Reduce.scratch(nz, rows, 2 * inner, kind, BF16, part=False)
        elif name == "cross":
            scratch += Reduce.scratch(nz, 8, 2 * inner, kind, F32, part=False)
        else:
            scratch += Reduce.scratch(nz, *shapes[name], kind, BF16)
    scratch += Total.scratch(nz, 8, width)
    return pl.pallas_call(
        functools.partial(back_kernel, nz, order),
        name="back",
        out_shape=tuple(own)
        + (
            jax.ShapeDtypeStruct((rows, width), F32),
            jax.ShapeDtypeStruct((8, width), F32),
            jax.ShapeDtypeStruct((8, width), F32),
        ),
        in_specs=[hb, vm, hb, hb] + [vm] * (5 + len(acts)),
        out_specs=tuple([vm] * (len(own) + 3)),
        scratch_shapes=scratch,
        compiler_params=pltpu.CompilerParams(
            collective_id=collective_id, has_side_effects=True, vmem_limit_bytes=BIG
        ),
    )(kv_part, cross_part, whole_qkv, whole_mid, x, gains, grad_hidden, gpart, enc, *acts)


def fits(*operands):
    layer_in, encoded, self_query, relative_bias = operands[0], operands[1], operands[4], operands[18]
    total = layer_in.shape[1] * lax.axis_size(AXES)
    return (
        lax.axis_size(GRP) == 2
        and lax.axis_size(WSH) == 2
        and lax.axis_size(CTX) == 8
        and layer_in.shape[1] == 2 * BLK
        and encoded.shape[1] == 4
        and total // 2 <= CONT_TOK
        and self_query.shape[0] % 16 == 0
        and self_query.shape[1] == relative_bias.shape[1] * BLK
        and self_query.shape[1] % 256 == 0
    )


def fast(
    layer_in, encoded, cotangent, deal_table, self_query, self_key, self_value, self_output, cross_query, cross_key,
    cross_value, cross_output, feed_gate, feed_up, feed_down, gain_self, gain_cross, gain_feed, relative_bias,
):
    nz = lax.axis_size(CTX) // 2
    shards = lax.axis_size(AXES)
    device = lax.axis_index(AXES)
    rows = layer_in.shape[1]
    width = layer_in.shape[2]
    heads = relative_bias.shape[1]
    inner = self_query.shape[1]
    head_size = inner // heads
    owned = gain_self.shape[0]
    enc_own = encoded.shape[1]
    table_hb = relative_bias.astype(F32).T
    mine = lax.dynamic_slice_in_dim(deal_table, device, 1)

    gains_here = lax.dynamic_update_slice(
        jnp.zeros((3, width), BF16), jnp.stack([gain_self, gain_cross, gain_feed]), (0, device * owned)
    )
    small = jnp.concatenate([encoded[0], gains_here, jnp.zeros((9, width), BF16)], axis=0)
    whole_small, whole_qkv, whole_mid, whole_ffn, whole_down, kv_all, queries, normed_one, gains = front(
        layer_in[0],
        small,
        (
            self_query, self_key, self_value, self_output, cross_query, cross_key, cross_value, cross_output,
            feed_gate, feed_up, feed_down,
        ),
        nz,
        shards,
    )
    output_weight, cq_weight, ck_weight, cv_weight, co_weight = [whole_mid[i].reshape(width, inner) for i in range(5)]
    gate_weight, up_weight = [whole_ffn[i].reshape(width, -1) for i in range(2)]
    down_weight = whole_down[0].reshape(-1, width)
    enc_all = whole_small[0, :, :enc_own].reshape(shards * enc_own, width)
    kv_all = kv_all.reshape(shards * rows, 2 * inner)

    inputs32 = layer_in[0].astype(F32)
    attn_sum, log_self = attn_fwd(mine, deal_table, queries, kv_all, jnp.pad(table_hb, ((0, 0), (0, 128 - BUCKETS))))
    attended = attn_sum.astype(BF16)
    hidden_one = inputs32 + dot(attended, output_weight)
    normed_two = rms_norm(hidden_one, gains[5]).astype(BF16)
    cross_queries = dot(normed_two, cq_weight).astype(BF16)
    cross_keys = dot(enc_all, ck_weight).astype(BF16)
    cross_values = dot(enc_all, cv_weight).astype(BF16)
    enc_rows = enc_all.shape[0]
    cq_heads = cross_queries.reshape(rows, heads, head_size)
    ck_heads = cross_keys.reshape(enc_rows, heads, head_size)
    cv_heads = cross_values.reshape(enc_rows, heads, head_size)
    cross_scores = einsum(QK, cq_heads, ck_heads)
    cross_peak = jnp.max(cross_scores, axis=-1)
    log_cross = cross_peak + jnp.log(jnp.sum(jnp.exp(cross_scores - cross_peak[:, :, None]), axis=-1))
    cross_probs = jnp.exp(cross_scores - log_cross[:, :, None])
    cross_high, cross_rest = split_probs(cross_probs)
    cross_sum = einsum(PV, cross_high, cv_heads)
    cross_exact = cross_sum + einsum(PV, cross_rest, cv_heads)
    attended_cross = cross_sum.reshape(rows, inner).astype(BF16)
    hidden_two = hidden_one + dot(attended_cross, co_weight)
    normed_three = rms_norm(hidden_two, gains[6]).astype(BF16)
    gate_pre = dot(normed_three, gate_weight)
    up_pre = dot(normed_three, up_weight)
    mixed_hidden = gated(gate_pre, up_pre).astype(BF16)
    output_sum = hidden_two + dot(mixed_hidden, down_weight)
    layer_out = output_sum.astype(BF16)[None]

    grad_out = cotangent[0]
    grad_mixed = back(grad_out, down_weight)
    _, gate_pull = jax.vjp(gated, gate_pre, up_pre)
    grad_gate32, grad_up32 = gate_pull(bounce(grad_mixed))
    grad_gate = grad_gate32.astype(BF16)
    grad_up = grad_up32.astype(BF16)
    grad_normed_three = back(grad_gate, gate_weight) + back(grad_up, up_weight)
    _, norm_pull_three = jax.vjp(rms_norm, hidden_two, gains[6])
    back_two, grad_gain_feed = norm_pull_three(grad_normed_three)
    grad_hidden_two = grad_out.astype(F32) + back_two
    grad_two_low = grad_hidden_two.astype(BF16)
    grad_attended_cross = back(grad_two_low, co_weight).astype(BF16)
    grad_ac_heads = grad_attended_cross.reshape(rows, heads, head_size)
    delta_cross = jnp.sum(grad_ac_heads.astype(F32) * cross_exact, axis=-1).T
    cross_low, grad_cross_scores = score_grads(cross_scores, log_cross, delta_cross, grad_ac_heads, cv_heads)
    grad_cq_low = einsum(PV, grad_cross_scores, ck_heads).reshape(rows, inner).astype(BF16)
    grad_ck_part = einsum(PTQ, grad_cross_scores, cq_heads).reshape(enc_rows, inner)
    grad_cv_part = einsum(PTQ, cross_low, grad_ac_heads).reshape(enc_rows, inner)
    cross_part = jnp.concatenate([grad_ck_part, grad_cv_part], axis=1).reshape(2 * nz, 2, enc_own, 2 * inner)
    cross_part = jnp.pad(cross_part, ((0, 0), (0, 0), (0, 8 - enc_own), (0, 0)))
    grad_normed_two = back(grad_cq_low, cq_weight)
    _, norm_pull_two = jax.vjp(rms_norm, hidden_one, gains[5])
    back_one, grad_gain_cross = norm_pull_two(grad_normed_two)
    grad_hidden_one = grad_hidden_two + back_one
    grad_one_low = grad_hidden_one.astype(BF16)
    grad_attended = back(grad_one_low, output_weight).astype(BF16)
    grad_queries, kv_part, grad_bias_part = attn_bwd(
        mine, deal_table, queries, kv_all, pair_table(table_hb), grad_attended, attn_sum, log_self
    )
    bias_line = jnp.pad(grad_bias_part.reshape(1, -1), ((0, 0), (0, width - BUCKETS * heads)))
    gpart = jnp.concatenate(
        [jnp.zeros((1, width), F32), grad_gain_cross[None], grad_gain_feed[None], bias_line, jnp.zeros((4, width), F32)]
    )
    ff = gate_weight.shape[1]
    square = (owned, inner)
    shapes = dict(
        gate=(owned, ff), up=(owned, ff), down=(feed_down.shape[0], width), co=(inner // shards, width), cq=square,
        ck=square, cv=square, q=square, o=(inner // shards, width), k=square, v=square,
    )
    enc_padded = jnp.pad(encoded[0], ((0, 16 - enc_own), (0, 0)))
    result = back_step(
        kv_part.reshape(2 * nz, 2, rows, 2 * inner), cross_part, whole_qkv, whole_mid, layer_in[0], gains,
        grad_hidden_one, gpart, enc_padded,
        (
            normed_three, mixed_hidden, attended, normed_two, attended_cross, normed_one, grad_gate, grad_up, grad_out,
            grad_one_low, grad_cq_low, grad_two_low, grad_queries,
        ),
        shapes,
        nz,
    )
    got = dict(zip([name for name, _ in BACK_JOBS[2:]], result))
    grad_input, grad_enc, total = result[11:]
    gain_grads = [lax.dynamic_slice_in_dim(total[i], device * owned, owned) for i in range(3)]
    grad_relative_bias = total[3, : BUCKETS * heads].reshape(BUCKETS, heads)
    return (
        layer_out, grad_input[None], grad_enc[None, :enc_own],
        got["q"], got["k"], got["v"], got["o"], got["cq"], got["ck"], got["cv"], got["co"], got["gate"], got["up"], got["down"],
        gain_grads[0], gain_grads[1], gain_grads[2], grad_relative_bias,
    )


def solution(mesh):
    return jax.shard_map(
        lambda *operands: (fast if fits(*operands) else local)(*operands),
        mesh=mesh,
        in_specs=(
            P(GRP, AXES, None),
            P(GRP, AXES, None),
            P(GRP, AXES, None),
            P(),
            P(AXES, None),
            P(AXES, None),
            P(AXES, None),
            P(AXES, None),
            P(AXES, None),
            P(AXES, None),
            P(AXES, None),
            P(AXES, None),
            P(AXES, None),
            P(AXES, None),
            P(AXES, None),
            P(AXES),
            P(AXES),
            P(AXES),
            P(),
        ),
        out_specs=(
            P(GRP, AXES, None),
            P(GRP, AXES, None),
            P(GRP, AXES, None),
            P(AXES, None),
            P(AXES, None),
            P(AXES, None),
            P(AXES, None),
            P(AXES, None),
            P(AXES, None),
            P(AXES, None),
            P(AXES, None),
            P(AXES, None),
            P(AXES, None),
            P(AXES, None),
            P(AXES),
            P(AXES),
            P(AXES),
            P(),
        ),
        check_vma=False,
    )
```

```python
import functools
import math

import jax
import jax.numpy as jnp
from jax import lax
from jax.experimental import pallas as pl
from jax.experimental.pallas import tpu as pltpu
from jax.sharding import PartitionSpec as P

GRP, CTX, WSH = "grp", "ctx", "wsh"
AXES = (CTX, WSH)
EVERY = (GRP, CTX, WSH)
QK = "qhd,khd->hqk"
PV = "hqk,khd->qhd"
PTQ = "hqk,qhd->khd"
TF_TD = "tf,td->fd"
TD_FD = "td,fd->tf"
TD_TF = "td,tf->df"
TF_DF = "tf,df->td"
TC_TD = "tc,td->cd"
TD_CD = "td,cd->tc"
TD_TC = "td,tc->dc"
TC_DC = "tc,dc->td"

BUCKETS = 32
MAXDIST = 128
CONT_TOK = 2048


MASKED = -1e30
EPSILON = 1e-06


def rms_norm(hidden, gain_vector):
    return (
        hidden
        * lax.rsqrt(jnp.mean(hidden * hidden, axis=-1, keepdims=True) + EPSILON)
        * gain_vector
    )


def gated(gate_pre, up_pre):
    return jax.nn.gelu(gate_pre, approximate=True) * up_pre


def bounce(values):
    return lax.optimization_barrier(values.astype(jnp.bfloat16)).astype(jnp.float32)


def split_probs(probs_full):
    probs_high = probs_full.astype(jnp.bfloat16)
    probs_rest = (probs_full - probs_high.astype(jnp.float32)).astype(jnp.bfloat16)
    return (probs_high, probs_rest)


def bucket_ids(distance):
    exact_half = BUCKETS // 2
    counted = jnp.minimum(distance, exact_half)
    for number in range(1, exact_half):
        boundary = int(math.ceil(exact_half * math.pow(MAXDIST / exact_half, number / exact_half)))
        counted = counted + (distance >= boundary).astype(jnp.int32)
    return counted


def token_place(tokens, prompt_len, cont_len):
    beyond = tokens - prompt_len
    in_prompt = tokens < prompt_len
    sequence = jnp.where(in_prompt, 0, 1 + beyond // cont_len)
    position = jnp.where(in_prompt, tokens, prompt_len + beyond % cont_len)
    return (sequence, position)


def pair_mask(seq_query, pos_query, seq_key, pos_key):
    earlier = pos_key[None, :] <= pos_query[:, None]
    visible = (seq_key[None, :] == seq_query[:, None]) | (seq_key[None, :] == 0)
    return earlier & visible


def bucket_bias(pos_query, pos_key, table_hb):
    buckets = bucket_ids(jnp.maximum(pos_query[:, None] - pos_key[None, :], 0))
    picks = (
        buckets[None, :, :, None]
        == jnp.arange(table_hb.shape[1], dtype=jnp.int32)[None, None, None, :]
    )
    return (buckets, jnp.sum(jnp.where(picks, table_hb[:, None, None, :], 0.0), axis=-1))


def bucket_grad(buckets, grad_scores, bucket_count):
    picks = (
        buckets[None, :, :, None] == jnp.arange(bucket_count, dtype=jnp.int32)[None, None, None, :]
    )
    return jnp.sum(
        jnp.where(picks, grad_scores.astype(jnp.float32)[:, :, :, None], 0.0), axis=(1, 2)
    )


def masked_scores(query_heads, key_heads, bias, allowed):
    direct = jnp.einsum(QK, query_heads, key_heads, preferred_element_type=jnp.float32)
    return jnp.where(allowed[None], direct + bias, MASKED)


def score_grads(scores, log_total, delta_row, grad_heads, value_heads):
    probs_full = jnp.exp(scores - log_total[:, :, None])
    grad_probs = jnp.einsum(
        QK, grad_heads, value_heads, preferred_element_type=jnp.float32
    )
    grad_scores = (probs_full * (grad_probs - delta_row[:, :, None])).astype(jnp.bfloat16)
    return (probs_full.astype(jnp.bfloat16), grad_scores)


def key_view(seq_all, pos_all, step_index, key_rows, seq_query, pos_query):
    seq_key = lax.dynamic_slice_in_dim(seq_all, step_index * key_rows, key_rows)
    pos_key = lax.dynamic_slice_in_dim(pos_all, step_index * key_rows, key_rows)
    return (pos_key, pair_mask(seq_query, pos_query, seq_key, pos_key))


def self_forward(
    query_heads, key_heads, value_heads, seq_all, pos_all, seq_query, pos_query, table_hb, key_rows
):
    total_rows = key_heads.shape[0]
    head_count = query_heads.shape[1]
    rows_here = query_heads.shape[0]
    step_list = jnp.arange(total_rows // key_rows, dtype=jnp.int32)

    def total_step(carried, step_index):
        pos_key, allowed = key_view(seq_all, pos_all, step_index, key_rows, seq_query, pos_query)

        def total_accumulate(current):
            running_max, running_sum = current
            key_block = lax.dynamic_slice_in_dim(key_heads, step_index * key_rows, key_rows)
            bias = bucket_bias(pos_query, pos_key, table_hb)[1]
            scores = masked_scores(query_heads, key_block, bias, allowed)
            new_max = jnp.maximum(running_max, jnp.max(scores, axis=-1))
            weights = jnp.where(allowed[None], jnp.exp(scores - new_max[:, :, None]), 0.0)
            return (
                new_max,
                running_sum * jnp.exp(running_max - new_max) + jnp.sum(weights, axis=-1),
            )

        return (
            lax.cond(jnp.any(allowed), total_accumulate, lambda current: current, carried),
            None,
        )

    start_state = (
        jnp.full((head_count, rows_here), MASKED, jnp.float32),
        jnp.zeros((head_count, rows_here), jnp.float32),
    )
    (running_max, running_sum), _ = lax.scan(total_step, start_state, step_list)
    log_total = running_max + jnp.log(running_sum)

    def output_step(carried, step_index):
        pos_key, allowed = key_view(seq_all, pos_all, step_index, key_rows, seq_query, pos_query)

        def output_accumulate(current):
            rounded_sum, rest_sum = current
            key_block = lax.dynamic_slice_in_dim(key_heads, step_index * key_rows, key_rows)
            value_block = lax.dynamic_slice_in_dim(value_heads, step_index * key_rows, key_rows)
            bias = bucket_bias(pos_query, pos_key, table_hb)[1]
            scores = masked_scores(query_heads, key_block, bias, allowed)
            probs_high, probs_rest = split_probs(jnp.exp(scores - log_total[:, :, None]))
            rounded_sum = rounded_sum + jnp.einsum(
                PV, probs_high, value_block, preferred_element_type=jnp.float32
            )
            rest_sum = rest_sum + jnp.einsum(
                PV, probs_rest, value_block, preferred_element_type=jnp.float32
            )
            return (rounded_sum, rest_sum)

        return (
            lax.cond(jnp.any(allowed), output_accumulate, lambda current: current, carried),
            None,
        )

    zero_heads = jnp.zeros(query_heads.shape, jnp.float32)
    (rounded_sum, rest_sum), _ = lax.scan(output_step, (zero_heads, zero_heads), step_list)
    return (log_total, rounded_sum, rounded_sum + rest_sum)


def query_backward(
    query_heads,
    key_heads,
    value_heads,
    grad_heads,
    log_total,
    delta_row,
    seq_all,
    pos_all,
    seq_query,
    pos_query,
    table_hb,
    key_rows,
):
    total_rows = key_heads.shape[0]
    inner_width = key_heads.shape[1] * key_heads.shape[2]
    bucket_count = table_hb.shape[1]
    step_list = jnp.arange(total_rows // key_rows, dtype=jnp.int32)

    def step_body(carried, step_index):
        pos_key, allowed = key_view(seq_all, pos_all, step_index, key_rows, seq_query, pos_query)

        def step_accumulate(current):
            grad_query, grad_bias = current
            key_block = lax.dynamic_slice_in_dim(key_heads, step_index * key_rows, key_rows)
            value_block = lax.dynamic_slice_in_dim(value_heads, step_index * key_rows, key_rows)
            buckets, bias = bucket_bias(pos_query, pos_key, table_hb)
            scores = masked_scores(query_heads, key_block, bias, allowed)
            probs_low, grad_scores = score_grads(
                scores, log_total, delta_row, grad_heads, value_block
            )
            grad_query = grad_query + jnp.einsum(
                PV, grad_scores, key_block, preferred_element_type=jnp.float32
            )
            grad_bias = grad_bias + bucket_grad(buckets, grad_scores, bucket_count)
            grad_key = jnp.einsum(
                PTQ, grad_scores, query_heads, preferred_element_type=jnp.float32
            ).reshape(key_rows, inner_width)
            grad_value = jnp.einsum(
                PTQ, probs_low, grad_heads, preferred_element_type=jnp.float32
            ).reshape(key_rows, inner_width)
            return ((grad_query, grad_bias), jnp.concatenate([grad_key, grad_value], axis=1))

        blank_block = jnp.zeros((key_rows, 2 * inner_width), jnp.float32)
        return lax.cond(
            jnp.any(allowed), step_accumulate, lambda current: (current, blank_block), carried
        )

    start_state = (
        jnp.zeros(query_heads.shape, jnp.float32),
        jnp.zeros(table_hb.shape, jnp.float32),
    )
    final_state, key_blocks = lax.scan(step_body, start_state, step_list)
    return (final_state[0], final_state[1], key_blocks.reshape(total_rows, 2 * inner_width))


def local(
    layer_in,
    encoded,
    cotangent,
    deal_table,
    self_query,
    self_key,
    self_value,
    self_output,
    cross_query,
    cross_key,
    cross_value,
    cross_output,
    feed_gate,
    feed_up,
    feed_down,
    gain_self,
    gain_cross,
    gain_feed,
    relative_bias,
):
    shards = lax.axis_size(AXES)
    device = lax.axis_index(AXES)
    ctx_count = lax.axis_size(CTX)
    core_count = lax.axis_size(WSH)
    local_rows = layer_in.shape[1]
    total_rows = local_rows * shards
    block_len = local_rows // 2
    cont_len = min(CONT_TOK, total_rows // 2)
    prompt_len = total_rows - total_rows // 2 // cont_len * cont_len
    key_rows = min(1024, total_rows)
    head_count = relative_bias.shape[1]
    inner_width = self_query.shape[1]
    head_size = inner_width // head_count
    enc_rows = encoded.shape[1] * shards
    table_hb = relative_bias.astype(jnp.float32).T
    flat_table = deal_table.reshape(-1)
    all_tokens = (
        flat_table[:, None] * block_len + jnp.arange(block_len, dtype=jnp.int32)[None, :]
    ).reshape(-1)
    seq_all, pos_all = token_place(all_tokens, prompt_len, cont_len)
    seq_mine = lax.dynamic_slice_in_dim(seq_all, device * local_rows, local_rows)
    pos_mine = lax.dynamic_slice_in_dim(pos_all, device * local_rows, local_rows)
    forward_weights = (
        lax.all_gather(self_query, AXES, axis=0, tiled=True),
        lax.all_gather(self_key, AXES, axis=0, tiled=True),
        lax.all_gather(self_value, AXES, axis=0, tiled=True),
        lax.all_gather(self_output, AXES, axis=0, tiled=True),
        lax.all_gather(cross_query, AXES, axis=0, tiled=True),
        lax.all_gather(cross_key, AXES, axis=0, tiled=True),
        lax.all_gather(cross_value, AXES, axis=0, tiled=True),
        lax.all_gather(cross_output, AXES, axis=0, tiled=True),
        lax.all_gather(feed_gate, AXES, axis=0, tiled=True),
        lax.all_gather(feed_up, AXES, axis=0, tiled=True),
        lax.all_gather(feed_down, AXES, axis=0, tiled=True),
        lax.all_gather(gain_self, AXES, axis=0, tiled=True),
        lax.all_gather(gain_cross, AXES, axis=0, tiled=True),
        lax.all_gather(gain_feed, AXES, axis=0, tiled=True),
    )
    (
        query_weight,
        key_weight,
        value_weight,
        output_weight,
        cq_weight,
        ck_weight,
        cv_weight,
        co_weight,
        gate_weight,
        up_weight,
        down_weight,
        gain_one,
        gain_two,
        gain_three,
    ) = forward_weights
    inputs32 = layer_in[0].astype(jnp.float32)
    normed_one = rms_norm(inputs32, gain_one.astype(jnp.float32)).astype(jnp.bfloat16)
    queries = jnp.dot(normed_one, query_weight, preferred_element_type=jnp.float32).astype(
        jnp.bfloat16
    )
    keys_local = jnp.dot(normed_one, key_weight, preferred_element_type=jnp.float32).astype(
        jnp.bfloat16
    )
    values_local = jnp.dot(normed_one, value_weight, preferred_element_type=jnp.float32).astype(
        jnp.bfloat16
    )
    keys_all, values_all = (
        lax.all_gather(keys_local, AXES, axis=0, tiled=True),
        lax.all_gather(values_local, AXES, axis=0, tiled=True),
    )
    query_heads = queries.reshape(local_rows, head_count, head_size)
    key_heads = keys_all.reshape(total_rows, head_count, head_size)
    value_heads = values_all.reshape(total_rows, head_count, head_size)
    log_self, attn_sum, attn_exact = self_forward(
        query_heads,
        key_heads,
        value_heads,
        seq_all,
        pos_all,
        seq_mine,
        pos_mine,
        table_hb,
        key_rows,
    )
    attended = attn_sum.reshape(local_rows, inner_width).astype(jnp.bfloat16)
    hidden_one = inputs32 + jnp.dot(attended, output_weight, preferred_element_type=jnp.float32)
    normed_two = rms_norm(hidden_one, gain_two.astype(jnp.float32)).astype(jnp.bfloat16)
    cross_queries = jnp.dot(normed_two, cq_weight, preferred_element_type=jnp.float32).astype(
        jnp.bfloat16
    )
    enc_keys = jnp.dot(encoded[0], ck_weight, preferred_element_type=jnp.float32).astype(
        jnp.bfloat16
    )
    enc_values = jnp.dot(encoded[0], cv_weight, preferred_element_type=jnp.float32).astype(
        jnp.bfloat16
    )
    cross_keys, cross_values = (
        lax.all_gather(enc_keys, AXES, axis=0, tiled=True),
        lax.all_gather(enc_values, AXES, axis=0, tiled=True),
    )
    cq_heads = cross_queries.reshape(local_rows, head_count, head_size)
    ck_heads = cross_keys.reshape(enc_rows, head_count, head_size)
    cv_heads = cross_values.reshape(enc_rows, head_count, head_size)
    cross_scores = jnp.einsum(
        QK, cq_heads, ck_heads, preferred_element_type=jnp.float32
    )
    cross_peak = jnp.max(cross_scores, axis=-1)
    log_cross = cross_peak + jnp.log(
        jnp.sum(jnp.exp(cross_scores - cross_peak[:, :, None]), axis=-1)
    )
    cross_probs = jnp.exp(cross_scores - log_cross[:, :, None])
    cross_high, cross_rest = split_probs(cross_probs)
    cross_sum = jnp.einsum(PV, cross_high, cv_heads, preferred_element_type=jnp.float32)
    cross_exact = cross_sum + jnp.einsum(
        PV, cross_rest, cv_heads, preferred_element_type=jnp.float32
    )
    attended_cross = cross_sum.reshape(local_rows, inner_width).astype(jnp.bfloat16)
    hidden_two = hidden_one + jnp.dot(attended_cross, co_weight, preferred_element_type=jnp.float32)
    normed_three = rms_norm(hidden_two, gain_three.astype(jnp.float32)).astype(jnp.bfloat16)
    gate_pre = jnp.dot(normed_three, gate_weight, preferred_element_type=jnp.float32)
    up_pre = jnp.dot(normed_three, up_weight, preferred_element_type=jnp.float32)
    mixed_hidden = gated(gate_pre, up_pre).astype(jnp.bfloat16)
    output_sum = hidden_two + jnp.dot(mixed_hidden, down_weight, preferred_element_type=jnp.float32)
    layer_out = output_sum.astype(jnp.bfloat16)[None]
    back_weights = (
        lax.all_gather(self_query, AXES, axis=0, tiled=True),
        lax.all_gather(self_key, AXES, axis=0, tiled=True),
        lax.all_gather(self_value, AXES, axis=0, tiled=True),
        lax.all_gather(self_output, AXES, axis=0, tiled=True),
        lax.all_gather(cross_query, AXES, axis=0, tiled=True),
        lax.all_gather(cross_key, AXES, axis=0, tiled=True),
        lax.all_gather(cross_value, AXES, axis=0, tiled=True),
        lax.all_gather(cross_output, AXES, axis=0, tiled=True),
        lax.all_gather(feed_gate, AXES, axis=0, tiled=True),
        lax.all_gather(feed_up, AXES, axis=0, tiled=True),
        lax.all_gather(feed_down, AXES, axis=0, tiled=True),
        lax.all_gather(gain_self, AXES, axis=0, tiled=True),
        lax.all_gather(gain_cross, AXES, axis=0, tiled=True),
        lax.all_gather(gain_feed, AXES, axis=0, tiled=True),
    )
    (
        query_back,
        key_back,
        value_back,
        output_back,
        cq_back,
        ck_back,
        cv_back,
        co_back,
        gate_back,
        up_back,
        down_back,
        gain_one_back,
        gain_two_back,
        gain_three_back,
    ) = back_weights
    grad_out = cotangent[0]
    grad_down_w = jnp.einsum(
        TF_TD, mixed_hidden, grad_out, preferred_element_type=jnp.float32
    )
    grad_mixed = jnp.einsum(TD_FD, grad_out, down_back, preferred_element_type=jnp.float32)
    _, gate_pull = jax.vjp(gated, gate_pre, up_pre)
    grad_gate32, grad_up32 = gate_pull(bounce(grad_mixed))
    grad_gate = grad_gate32.astype(jnp.bfloat16)
    grad_up = grad_up32.astype(jnp.bfloat16)
    grad_gate_w = jnp.einsum(
        TD_TF, normed_three, grad_gate, preferred_element_type=jnp.float32
    )
    grad_up_w = jnp.einsum(TD_TF, normed_three, grad_up, preferred_element_type=jnp.float32)
    grad_normed_three = jnp.einsum(
        TF_DF, grad_gate, gate_back, preferred_element_type=jnp.float32
    ) + jnp.einsum(TF_DF, grad_up, up_back, preferred_element_type=jnp.float32)
    _, norm_pull_three = jax.vjp(rms_norm, hidden_two, gain_three_back.astype(jnp.float32))
    back_two, grad_gain_feed = norm_pull_three(grad_normed_three)
    grad_hidden_two = grad_out.astype(jnp.float32) + back_two
    grad_two_low = grad_hidden_two.astype(jnp.bfloat16)
    grad_co_w = jnp.einsum(
        TC_TD, attended_cross, grad_two_low, preferred_element_type=jnp.float32
    )
    grad_attended_cross = jnp.einsum(
        TD_CD, grad_two_low, co_back, preferred_element_type=jnp.float32
    ).astype(jnp.bfloat16)
    grad_ac_heads = grad_attended_cross.reshape(local_rows, head_count, head_size)
    delta_cross = jnp.sum(grad_ac_heads.astype(jnp.float32) * cross_exact, axis=-1).T
    cross_low, grad_cross_scores = score_grads(
        cross_scores, log_cross, delta_cross, grad_ac_heads, cv_heads
    )
    grad_cq = jnp.einsum(
        PV, grad_cross_scores, ck_heads, preferred_element_type=jnp.float32
    )
    grad_ck_part = jnp.einsum(
        PTQ, grad_cross_scores, cq_heads, preferred_element_type=jnp.float32
    ).reshape(enc_rows, inner_width)
    grad_cv_part = jnp.einsum(
        PTQ, cross_low, grad_ac_heads, preferred_element_type=jnp.float32
    ).reshape(enc_rows, inner_width)
    cross_own = lax.psum_scatter(
        jnp.concatenate([grad_ck_part, grad_cv_part], axis=1),
        AXES,
        scatter_dimension=0,
        tiled=True,
    )
    grad_cross_keys = cross_own[:, :inner_width].astype(jnp.bfloat16)
    grad_cross_values = cross_own[:, inner_width:].astype(jnp.bfloat16)
    grad_ck_w = jnp.einsum(
        TD_TC, encoded[0], grad_cross_keys, preferred_element_type=jnp.float32
    )
    grad_cv_w = jnp.einsum(
        TD_TC, encoded[0], grad_cross_values, preferred_element_type=jnp.float32
    )
    grad_encoded = (
        jnp.einsum(TC_DC, grad_cross_keys, ck_back, preferred_element_type=jnp.float32)
        + jnp.einsum(TC_DC, grad_cross_values, cv_back, preferred_element_type=jnp.float32)
    )[None]
    grad_cq_low = grad_cq.reshape(local_rows, inner_width).astype(jnp.bfloat16)
    grad_cq_w = jnp.einsum(TD_TC, normed_two, grad_cq_low, preferred_element_type=jnp.float32)
    grad_normed_two = jnp.einsum(
        TC_DC, grad_cq_low, cq_back, preferred_element_type=jnp.float32
    )
    _, norm_pull_two = jax.vjp(rms_norm, hidden_one, gain_two_back.astype(jnp.float32))
    back_one, grad_gain_cross = norm_pull_two(grad_normed_two)
    grad_hidden_one = grad_hidden_two + back_one
    grad_one_low = grad_hidden_one.astype(jnp.bfloat16)
    grad_o_w = jnp.einsum(TC_TD, attended, grad_one_low, preferred_element_type=jnp.float32)
    grad_attended = jnp.einsum(
        TD_CD, grad_one_low, output_back, preferred_element_type=jnp.float32
    ).astype(jnp.bfloat16)
    grad_att_heads = grad_attended.reshape(local_rows, head_count, head_size)
    delta_self = jnp.sum(grad_att_heads.astype(jnp.float32) * attn_exact, axis=-1).T
    grad_query32, grad_bias_part, kv_blocks = query_backward(
        query_heads,
        key_heads,
        value_heads,
        grad_att_heads,
        log_self,
        delta_self,
        seq_all,
        pos_all,
        seq_mine,
        pos_mine,
        table_hb,
        key_rows,
    )
    kv_own = lax.psum_scatter(kv_blocks, AXES, scatter_dimension=0, tiled=True)
    grad_keys = kv_own[:, :inner_width].astype(jnp.bfloat16)
    grad_values = kv_own[:, inner_width:].astype(jnp.bfloat16)
    grad_queries = grad_query32.reshape(local_rows, inner_width).astype(jnp.bfloat16)
    grad_q_w = jnp.einsum(TD_TC, normed_one, grad_queries, preferred_element_type=jnp.float32)
    grad_k_w = jnp.einsum(TD_TC, normed_one, grad_keys, preferred_element_type=jnp.float32)
    grad_v_w = jnp.einsum(TD_TC, normed_one, grad_values, preferred_element_type=jnp.float32)
    grad_normed_one = (
        jnp.einsum(TC_DC, grad_queries, query_back, preferred_element_type=jnp.float32)
        + jnp.einsum(TC_DC, grad_keys, key_back, preferred_element_type=jnp.float32)
        + jnp.einsum(TC_DC, grad_values, value_back, preferred_element_type=jnp.float32)
    )
    _, norm_pull_one = jax.vjp(rms_norm, inputs32, gain_one_back.astype(jnp.float32))
    back_input, grad_gain_self = norm_pull_one(grad_normed_one)
    grad_input = (grad_hidden_one + back_input)[None]

    def sectioned(grad_full):
        return grad_full.reshape(
            (ctx_count, core_count, grad_full.shape[0] // (ctx_count * core_count))
            + grad_full.shape[1:]
        )

    core_parts = (
        lax.psum_scatter(
            sectioned(grad_q_w).astype(jnp.bfloat16), WSH, scatter_dimension=1, tiled=True
        ).astype(jnp.float32),
        lax.psum_scatter(
            sectioned(grad_k_w).astype(jnp.bfloat16), WSH, scatter_dimension=1, tiled=True
        ).astype(jnp.float32),
        lax.psum_scatter(
            sectioned(grad_v_w).astype(jnp.bfloat16), WSH, scatter_dimension=1, tiled=True
        ).astype(jnp.float32),
        lax.psum_scatter(
            sectioned(grad_o_w).astype(jnp.bfloat16), WSH, scatter_dimension=1, tiled=True
        ).astype(jnp.float32),
        lax.psum_scatter(
            sectioned(grad_cq_w).astype(jnp.bfloat16), WSH, scatter_dimension=1, tiled=True
        ).astype(jnp.float32),
        lax.psum_scatter(
            sectioned(grad_ck_w).astype(jnp.bfloat16), WSH, scatter_dimension=1, tiled=True
        ).astype(jnp.float32),
        lax.psum_scatter(
            sectioned(grad_cv_w).astype(jnp.bfloat16), WSH, scatter_dimension=1, tiled=True
        ).astype(jnp.float32),
        lax.psum_scatter(
            sectioned(grad_co_w).astype(jnp.bfloat16), WSH, scatter_dimension=1, tiled=True
        ).astype(jnp.float32),
        lax.psum_scatter(
            sectioned(grad_gate_w).astype(jnp.bfloat16), WSH, scatter_dimension=1, tiled=True
        ).astype(jnp.float32),
        lax.psum_scatter(
            sectioned(grad_up_w).astype(jnp.bfloat16), WSH, scatter_dimension=1, tiled=True
        ).astype(jnp.float32),
        lax.psum_scatter(
            sectioned(grad_down_w).astype(jnp.bfloat16), WSH, scatter_dimension=1, tiled=True
        ).astype(jnp.float32),
        lax.psum_scatter(
            sectioned(grad_gain_self).astype(jnp.bfloat16), WSH, scatter_dimension=1, tiled=True
        ).astype(jnp.float32),
        lax.psum_scatter(
            sectioned(grad_gain_cross).astype(jnp.bfloat16), WSH, scatter_dimension=1, tiled=True
        ).astype(jnp.float32),
        lax.psum_scatter(
            sectioned(grad_gain_feed).astype(jnp.bfloat16), WSH, scatter_dimension=1, tiled=True
        ).astype(jnp.float32),
    )
    (
        core_q,
        core_k,
        core_v,
        core_o,
        core_cq,
        core_ck,
        core_cv,
        core_co,
        core_gate,
        core_up,
        core_down,
        core_gs,
        core_gc,
        core_gf,
    ) = core_parts
    owned = (
        lax.psum_scatter(core_q, CTX, scatter_dimension=0, tiled=True),
        lax.psum_scatter(core_k, CTX, scatter_dimension=0, tiled=True),
        lax.psum_scatter(core_v, CTX, scatter_dimension=0, tiled=True),
        lax.psum_scatter(core_o, CTX, scatter_dimension=0, tiled=True),
        lax.psum_scatter(core_cq, CTX, scatter_dimension=0, tiled=True),
        lax.psum_scatter(core_ck, CTX, scatter_dimension=0, tiled=True),
        lax.psum_scatter(core_cv, CTX, scatter_dimension=0, tiled=True),
        lax.psum_scatter(core_co, CTX, scatter_dimension=0, tiled=True),
        lax.psum_scatter(core_gate, CTX, scatter_dimension=0, tiled=True),
        lax.psum_scatter(core_up, CTX, scatter_dimension=0, tiled=True),
        lax.psum_scatter(core_down, CTX, scatter_dimension=0, tiled=True),
        lax.psum_scatter(core_gs, CTX, scatter_dimension=0, tiled=True),
        lax.psum_scatter(core_gc, CTX, scatter_dimension=0, tiled=True),
        lax.psum_scatter(core_gf, CTX, scatter_dimension=0, tiled=True),
    )
    (
        own_q,
        own_k,
        own_v,
        own_o,
        own_cq,
        own_ck,
        own_cv,
        own_co,
        own_gate,
        own_up,
        own_down,
        own_gain_self,
        own_gain_cross,
        own_gain_feed,
    ) = [piece.reshape(piece.shape[2:]) for piece in owned]
    summed = (
        lax.psum(own_q.astype(jnp.bfloat16), GRP).astype(jnp.float32),
        lax.psum(own_k.astype(jnp.bfloat16), GRP).astype(jnp.float32),
        lax.psum(own_v.astype(jnp.bfloat16), GRP).astype(jnp.float32),
        lax.psum(own_o.astype(jnp.bfloat16), GRP).astype(jnp.float32),
        lax.psum(own_cq.astype(jnp.bfloat16), GRP).astype(jnp.float32),
        lax.psum(own_ck.astype(jnp.bfloat16), GRP).astype(jnp.float32),
        lax.psum(own_cv.astype(jnp.bfloat16), GRP).astype(jnp.float32),
        lax.psum(own_co.astype(jnp.bfloat16), GRP).astype(jnp.float32),
        lax.psum(own_gate.astype(jnp.bfloat16), GRP).astype(jnp.float32),
        lax.psum(own_up.astype(jnp.bfloat16), GRP).astype(jnp.float32),
        lax.psum(own_down.astype(jnp.bfloat16), GRP).astype(jnp.float32),
        lax.psum(own_gain_self.astype(jnp.bfloat16), GRP).astype(jnp.float32),
        lax.psum(own_gain_cross.astype(jnp.bfloat16), GRP).astype(jnp.float32),
        lax.psum(own_gain_feed.astype(jnp.bfloat16), GRP).astype(jnp.float32),
    )
    grad_relative_bias = lax.psum(grad_bias_part.T, EVERY)
    return (
        layer_out,
        grad_input,
        grad_encoded,
        summed[0],
        summed[1],
        summed[2],
        summed[3],
        summed[4],
        summed[5],
        summed[6],
        summed[7],
        summed[8],
        summed[9],
        summed[10],
        summed[11],
        summed[12],
        summed[13],
        grad_relative_bias,
    )


BIG = 63 << 20
NT = (((1,), (1,)), ((), ()))
TN = (((0,), (0,)), ((), ()))
NN = (((1,), (0,)), ((), ()))
F32 = jnp.float32
BF16 = jnp.bfloat16
CH = 256
BLK = 64


def mm(left, right, dims):
    return lax.dot_general(left, right, dims, preferred_element_type=F32)


def load_in_order(deal, k_hbm, v_hbm, kvs, sem):
    blocks, inner = k_hbm.shape[0] // BLK, k_hbm.shape[1]

    def one(index, carry):
        here = pl.ds(index * BLK, BLK)
        rows = kvs.at[pl.ds(pl.multiple_of(deal[index // 2, index % 2] * BLK, BLK), BLK)]
        pltpu.make_async_copy(k_hbm.at[here], rows.at[:, pl.ds(0, inner)], sem.at[0]).start()
        pltpu.make_async_copy(v_hbm.at[here], rows.at[:, pl.ds(inner, inner)], sem.at[1]).start()
        return carry

    lax.fori_loop(0, blocks, one, 0)


def loaded(k_hbm, v_hbm, kvs, sem):
    inner = k_hbm.shape[1]
    pltpu.make_async_copy(k_hbm, kvs.at[:, pl.ds(0, inner)], sem.at[0]).wait()
    pltpu.make_async_copy(v_hbm, kvs.at[:, pl.ds(inner, inner)], sem.at[1]).wait()


def stack_pair(block, low_lanes):
    zero = jnp.zeros_like(block)
    return jnp.concatenate([jnp.where(low_lanes, block, zero), jnp.where(low_lanes, zero, block)], axis=0)


def pair_table(table_hb):
    heads = table_hb.shape[0]
    padded = jnp.pad(table_hb, ((0, 0), (0, BLK - BUCKETS)))
    return padded.reshape(heads // 2, 2 * BLK)

MESH = pl.DeviceIdType.MESH


class Place:
    def __init__(self, nz):
        self.nz = nz
        self.g = lax.axis_index(GRP)
        self.c = lax.axis_index(CTX)
        self.w = lax.axis_index(WSH)
        self.z = self.c // 2
        self.y = lax.rem(self.c, 2)
        self.me = self.c * 2 + self.w

    def at(self, g=None, z=None, y=None, w=None):
        z = self.z if z is None else z
        y = self.y if y is None else y
        return (self.g if g is None else g, z * 2 + y, self.w if w is None else w)

    def twin(self):
        return self.at(g=1 - self.g)

    def over(self):
        return self.at(y=1 - self.y)

    def mate(self):
        return self.at(w=1 - self.w)

    def up(self, dz):
        return lax.rem(self.z + dz, self.nz)

    def down(self, dz):
        return lax.rem(self.z + self.nz - dz, self.nz)

    def meet(self):
        barrier = pltpu.get_barrier_semaphore()
        partners = [self.twin(), self.over(), self.mate()]
        partners += [self.at(z=self.up(dz)) for dz in range(1, self.nz)]
        for partner in partners:
            pl.semaphore_signal(barrier, inc=1, device_id=partner, device_id_type=MESH)
        pl.semaphore_wait(barrier, len(partners))


def push(src, dst, ssem, rsem, to):
    return pltpu.make_async_remote_copy(src, dst, ssem, rsem, device_id=to, device_id_type=MESH)


def half(wide, index):
    return pl.ds(pl.multiple_of(index * (wide // 2), 128), wide // 2)


class Gather:
    COUNT = 9

    def __init__(self, at, part, whole, sems, split, chunk=0, chunks=1):
        self.at, self.nz, self.part, self.whole, self.split = at, at.nz, part, whole, split
        (self.zs, self.zr, self.ys, self.yr, self.xs, self.xr, self.ws, self.wr, self.lc) = sems
        self.wide = whole.shape[-1] // chunks
        self.first = chunk * self.wide
        self.sent = []

    @staticmethod
    def scratch(nz, split):
        dma = pltpu.SemaphoreType.DMA
        x = 2 * nz if split else 1
        w = 4 * nz if split else 2 * nz
        return [dma((nz,))] * 4 + [dma((x,))] * 2 + [dma((w,))] * 2 + [dma((1,))]

    def cols(self, side=None):
        if self.split and side is not None:
            return pl.ds(pl.multiple_of(self.first + side * (self.wide // 2), 128), self.wide // 2)
        return pl.ds(self.first, self.wide)

    def spot(self, z, y, w, side=None):
        return self.whole.at[(z * 2 + y) * 2 + w].at[:, self.cols(side)]

    def post(self, view, ssem, rsem, to):
        copy = push(view, view, ssem, rsem, to)
        copy.start()
        self.sent.append(copy)

    def to_y(self, z):
        at = self.at
        self.post(self.spot(z, at.y, at.w, at.g), self.ys.at[z], self.yr.at[z], at.over())

    def to_x(self, z, y):
        at = self.at
        if self.split:
            k = z * 2 + y
            self.post(self.spot(z, y, at.w, at.g), self.xs.at[k], self.xr.at[k], at.twin())

    def w_sem(self, z, y, side):
        k = z * 2 + y
        return k * 2 + (0 if side is None else side) if self.split else k

    def to_w(self, z, y, side):
        at = self.at
        k = self.w_sem(z, y, side)
        self.post(self.spot(z, y, at.w, side), self.ws.at[k], self.wr.at[k], at.mate())

    def place(self):
        here = self.whole.at[self.at.me].at[:, self.cols()]
        self.local = pltpu.make_async_copy(self.part.at[:, self.cols()], here, self.lc.at[0])
        self.local.start()

    def send(self):
        at = self.at
        self.local.wait()
        for dz in range(1, self.nz):
            to = at.up(dz)
            self.post(self.spot(at.z, at.y, at.w, at.g), self.zs.at[to], self.zr.at[at.z], at.at(z=to))
        self.to_y(at.z)
        self.to_w(at.z, at.y, None)

    def after_z(self):
        at = self.at
        for dz in range(1, self.nz):
            z = at.down(dz)
            view = self.spot(z, at.y, at.w, at.g)
            push(view, view, self.zs.at[z], self.zr.at[z], at.at(z=z)).wait_recv()
            self.to_y(z)
            self.to_x(z, at.y)
            self.to_w(z, at.y, at.g)

    def after_y(self):
        at = self.at
        for dz in range(self.nz):
            z = at.down(dz)
            view = self.spot(z, 1 - at.y, at.w, at.g)
            push(view, view, self.ys.at[z], self.yr.at[z], at.over()).wait_recv()
            self.to_x(z, 1 - at.y)
            self.to_w(z, 1 - at.y, at.g)

    def others(self):
        for dy in range(2):
            for dz in range(self.nz):
                yield self.at.down(dz), lax.rem(self.at.y + dy, 2), dy == 0 and dz == 0

    def after_x(self):
        at = self.at
        if not self.split:
            return
        for z, y, own in self.others():
            if not own:
                k = z * 2 + y
                view = self.spot(z, y, at.w, 1 - at.g)
                push(view, view, self.xs.at[k], self.xr.at[k], at.twin()).wait_recv()
                self.to_w(z, y, 1 - at.g)

    def end(self):
        at = self.at
        for z, y, own in self.others():
            for side in range(2 if self.split and not own else 1):
                k = self.w_sem(z, y, side)
                view = self.spot(z, y, 1 - at.w, None if own else side)
                push(view, view, self.ws.at[k], self.wr.at[k], at.mate()).wait_recv()

    def close(self):
        for copy in self.sent:
            copy.wait_send()


class Reduce:
    COUNT = 16

    @staticmethod
    def scratch(nz, r, wide, kind, dtype, part=True):
        cols = wide // 2 if kind == "x" else wide
        dma = pltpu.SemaphoreType.DMA
        vmem = pltpu.VMEM
        none = vmem((1, 16, 128), dtype)
        return [
            vmem((2 * nz, 2, r, wide), dtype) if part else none,
            vmem((2 * nz, r, wide), dtype),
            vmem((2 * nz, r, cols), dtype) if kind == "x" else none,
            vmem((nz, r, cols), dtype),
            vmem((nz, r, cols), dtype),
            vmem((2, r, cols), dtype) if kind != "none" else none,
        ] + [dma((2 * nz,))] * 4 + [dma((nz,))] * 4 + [dma((2,))] * 2

    def __init__(self, at, out, refs, kind):
        self.at, self.nz, self.out, self.kind = at, at.nz, out, kind
        self.part_cols = None
        (self.part, self.wb, self.xb, self.yb, self.zb, self.fb) = refs[:6]
        (self.ws, self.wr, self.xs, self.xr, self.ys, self.yr, self.zs, self.zr, self.fs, self.fr) = refs[6:]
        self.wide = self.wb.shape[-1]
        self.local_part = None

    def piece_of(self, k, w):
        view = self.part.at[k, w]
        return view if self.part_cols is None else view.at[:, self.part_cols]

    def c_w(self, k):
        at = self.at
        return push(self.piece_of(k, 1 - at.w), self.wb.at[k], self.ws.at[k], self.wr.at[k], at.mate())

    def c_x(self, k):
        at = self.at
        src = self.wb.at[k].at[:, half(self.wide, 1 - at.g)]
        return push(src, self.xb.at[k], self.xs.at[k], self.xr.at[k], at.twin())

    def mid(self):
        return self.xb if self.kind == "x" else self.wb

    def c_y(self, z):
        at = self.at
        return push(self.mid().at[z * 2 + 1 - at.y], self.yb.at[z], self.ys.at[z], self.yr.at[z], at.over())

    def c_z(self, to):
        at = self.at
        return push(self.yb.at[to], self.zb.at[at.z], self.zs.at[to], self.zr.at[at.z], at.at(z=to))

    def c_zin(self, z):
        return push(self.yb.at[z], self.zb.at[z], self.zs.at[z], self.zr.at[z], self.at.at(z=z))

    def c_f(self):
        return push(self.fb.at[0], self.fb.at[1], self.fs.at[0], self.fr.at[0], self.at.twin())

    def piece(self, t):
        z = lax.rem(self.at.z + 1 + t // 2, self.nz)
        y = lax.rem(self.at.y + 1 + t, 2)
        return z * 2 + y

    def send(self):
        def one(t, carry):
            self.c_w(self.piece(t)).start()
            return carry

        lax.fori_loop(0, 2 * self.nz, one, 0)

    def after_w(self):
        at = self.at

        def one(t):
            k = self.piece(t)
            self.c_w(k).wait_recv()
            here = self.part[k, at.w] if self.local_part is None else self.local_part[k, :, self.local_cols]
            total = self.wb[k].astype(F32) + here.astype(F32)
            self.wb[k] = total.astype(self.wb.dtype)
            if self.kind == "x":
                self.c_x(k).start()

        def both(t, carry):
            one(2 * t)
            if self.kind != "x":
                self.c_y(self.piece(2 * t) // 2).start()
            one(2 * t + 1)
            return carry

        lax.fori_loop(0, self.nz, both, 0)

    def after_x(self):
        if self.kind != "x":
            return

        def one(t):
            k = self.piece(t)
            self.c_x(k).wait_recv()
            total = self.xb[k].astype(F32) + self.wb[k, :, half(self.wide, self.at.g)].astype(F32)
            self.xb[k] = total.astype(self.xb.dtype)

        def both(t, carry):
            one(2 * t)
            self.c_y(self.piece(2 * t) // 2).start()
            one(2 * t + 1)
            return carry

        lax.fori_loop(0, self.nz, both, 0)

    def after_y(self):
        at, nz = self.at, self.nz

        def one(t, carry):
            z = lax.rem(at.z + 1 + t, nz)
            self.c_y(z).wait_recv()
            total = self.yb[z].astype(F32) + self.mid()[z * 2 + at.y].astype(F32)
            self.yb[z] = total.astype(self.yb.dtype)

            @pl.when(t < nz - 1)
            def _():
                self.c_z(z).start()

            return carry

        lax.fori_loop(0, nz, one, 0)

    def after_z(self):
        at, nz = self.at, self.nz
        for dz in range(1, nz):
            self.c_zin(at.up(dz)).wait_recv()
        total = self.yb[at.z].astype(F32)
        for dz in range(1, nz):
            total = total + self.zb[at.up(dz)].astype(F32)
        if self.kind == "x":
            self.out[:, half(self.wide, at.g)] = total
        else:
            self.out[...] = total
        if self.kind != "none":
            self.fb[0] = total.astype(self.fb.dtype)
            self.c_f().start()

    def end(self):
        at, nz = self.at, self.nz
        if self.kind != "none":
            self.c_f().wait_recv()
            other = self.fb[1].astype(F32)
            if self.kind == "x":
                self.out[:, half(self.wide, 1 - at.g)] = other
            else:
                self.out[...] = self.out[...] + other
            self.c_f().wait_send()

    def close(self):
        at, nz = self.at, self.nz

        def sends(t, carry):
            self.c_w(t).wait_send()
            if self.kind == "x":
                self.c_x(t).wait_send()
            return carry

        lax.fori_loop(0, 2 * nz, sends, 0)

        def sends_y(t, carry):
            self.c_y(t).wait_send()
            return carry

        lax.fori_loop(0, nz, sends_y, 0)
        for dz in range(1, nz):
            self.c_z(at.up(dz)).wait_send()


class Total:
    COUNT = 3

    @staticmethod
    def scratch(nz, r, wide):
        dma = pltpu.SemaphoreType.DMA
        return [pltpu.VMEM((4 + nz, r, wide), F32), dma((4 + nz,)), dma((4 + nz,))]

    def __init__(self, at, refs):
        self.at, self.nz = at, at.nz
        self.buf, self.ss, self.rs = refs

    def hop(self, i):
        at = self.at
        to = (at.mate(), at.twin(), at.over())[i]
        return push(self.buf.at[0], self.buf.at[1 + i], self.ss.at[i], self.rs.at[i], to)

    def send(self):
        self.hop(0).start()

    def after(self, i):
        hop = self.hop(i)
        hop.wait_send()
        hop.wait_recv()
        self.buf[0] = self.buf[0] + self.buf[1 + i]
        if i < 2:
            self.hop(i + 1).start()
        else:
            for dz in range(1, self.nz):
                self.along(self.at.z, self.at.up(dz)).start()

    def along(self, source, to):
        base = 4
        return push(self.buf.at[0], self.buf.at[base + source], self.ss.at[base + to], self.rs.at[base + source], self.at.at(z=to))

    def end(self):
        total = None
        for dz in range(1, self.nz):
            z = self.at.up(dz)
            self.along(z, z).wait_recv()
            self.along(self.at.z, z).wait_send()
        self.buf[4 + self.at.z] = self.buf[0]
        total = self.buf[4]
        for z in range(1, self.nz):
            total = total + self.buf[4 + z]
        return total


def normed(hidden, gain):
    return hidden * lax.rsqrt(jnp.mean(hidden * hidden, axis=-1, keepdims=True) + EPSILON) * gain


def norm_back(hidden, gain, grad):
    scale = lax.rsqrt(jnp.mean(hidden * hidden, axis=-1, keepdims=True) + EPSILON)
    inner = jnp.mean(hidden * gain * grad, axis=-1, keepdims=True)
    rows = scale * gain * grad - hidden * (scale * scale * scale) * inner
    return rows, jnp.sum(grad * hidden * scale, axis=0, keepdims=True)


FRONT_PARTS = ("small", "k", "v", "q", "o", "cq", "ck", "cv", "co", "gate", "up", "down", "keys", "values")
FRONT_CHUNKS = dict(gate=2, up=2, down=3)
FRONT_WHOLE = ("small", "keys", "values", "ck", "cv", "co")
FRONT_ORDER = (
    ("small", 0), ("gate", 0), ("k", 0), ("v", 0), ("gate", 1), ("q", 0), ("up", 0), ("up", 1), ("down", 0), ("keys", 0),
    ("values", 0), ("down", 1), ("down", 2), ("o", 0), ("cq", 0), ("ck", 0), ("cv", 0), ("co", 0),
)
FRONT_AHEAD = 4


def front_kernel(nz, unshared, order, ahead, *refs):
    count = len(FRONT_PARTS)
    x_ref, ins, wholes, refs = refs[0], refs[1 : count - 1], refs[count - 1 : 2 * count - 1], refs[2 * count - 1 :]
    (q_ref, normed_ref, gains_ref), (wbuf, k_own, v_own, wsem), sems = refs[:3], refs[3:7], refs[7:]
    parts = dict(zip(FRONT_PARTS, tuple(ins) + (k_own, v_own)))
    wholes = dict(zip(FRONT_PARTS, wholes))
    at = Place(nz)
    jobs = []
    for i, (name, chunk) in enumerate(order):
        mine = sems[Gather.COUNT * i : Gather.COUNT * (i + 1)]
        chunks = FRONT_CHUNKS.get(name, 1)
        job = Gather(at, parts[name], wholes[name], mine, name not in unshared, chunk, chunks)
        jobs.append(job)
        if name not in ("keys", "values"):
            job.place()
    at.meet()
    width = x_ref.shape[1]

    def norm():
        every = wholes["small"]
        total = every[0].astype(F32)
        for device in range(1, every.shape[0]):
            total = total + every[device].astype(F32)
        gains_ref[...] = total
        normed_ref[...] = normed(x_ref[...].astype(F32), total[4:5]).astype(BF16)

    def project(name, index, into):
        load = pltpu.make_async_copy(wholes[name], wbuf.at[index], wsem.at[index])
        load.start()
        load.wait()
        into[...] = mm(normed_ref[...], wbuf[index].reshape(width, -1), NN).astype(BF16)

    def follow(name):
        if name == "small":
            norm()
        elif name == "k":
            project(name, 0, k_own)
            jobs[order.index(("keys", 0))].place()
        elif name == "v":
            project(name, 1, v_own)
            jobs[order.index(("values", 0))].place()
        elif name == "q":
            project(name, 2, q_ref)

    for turn in range(-ahead, len(order) + 3):
        for i in range(len(order) - 1, -1, -1):
            name, job = order[i][0], jobs[i]
            stage = turn - i
            if stage == 0:
                job.after_z()
            if stage == 1:
                job.after_y()
            if stage == 2:
                job.after_x()
                if name in ("small", "k", "v", "q"):
                    job.end()
                    follow(name)
        if 0 <= turn + ahead < len(order):
            jobs[turn + ahead].send()
    for (name, _), job in zip(order, jobs):
        if name not in ("small", "k", "v", "q"):
            job.end()
    for job in jobs:
        job.close()


def front(x, parts, nz, shards, collective_id=1, unshared=FRONT_WHOLE, order=FRONT_ORDER, ahead=FRONT_AHEAD):
    hb = pl.BlockSpec(memory_space=pl.ANY)
    vm = pl.BlockSpec(memory_space=pltpu.VMEM)
    rows, width = x.shape
    inner = parts[1].shape[1]
    shapes = [(shards,) + part.shape for part in parts] + [(shards, rows, inner)] * 2
    scratch = [
        pltpu.VMEM((3,) + shapes[1], BF16), pltpu.VMEM((rows, inner), BF16), pltpu.VMEM((rows, inner), BF16),
        pltpu.SemaphoreType.DMA((3,)),
    ]
    for name, _ in order:
        scratch += Gather.scratch(nz, name not in unshared)
    return pl.pallas_call(
        functools.partial(front_kernel, nz, unshared, order, ahead),
        name="front",
        out_shape=tuple([jax.ShapeDtypeStruct(s, BF16) for s in shapes])
        + (
            jax.ShapeDtypeStruct((rows, inner), BF16),
            jax.ShapeDtypeStruct((rows, width), BF16),
            jax.ShapeDtypeStruct(parts[0].shape, F32),
        ),
        in_specs=[vm] + [hb] * len(parts),
        out_specs=tuple([vm] + [hb] * (len(FRONT_PARTS) - 1) + [vm] * 3),
        scratch_shapes=scratch,
        compiler_params=pltpu.CompilerParams(
            collective_id=collective_id, has_side_effects=True, vmem_limit_bytes=BIG
        ),
    )(x, *parts)


BACK_OUT = ("gate", "up", "down", "co", "cq", "ck", "cv", "q", "o", "k", "v")
BACK_CHUNKS = dict(kv=2, gate=2, up=2, down=3)
BACK_NONE = ("kv", "cross")
BACK_LATE = ("q", "k", "v")
BACK_ORDER = (
    ("cross", 0), ("kv", 0), ("kv", 1), ("gate", 0), ("gate", 1), ("up", 0), ("up", 1), ("down", 0), ("down", 1), ("down", 2),
    ("co", 0), ("o", 0), ("cq", 0), ("k", 0), ("v", 0), ("ck", 0), ("cv", 0), ("q", 0),
)
BACK_GAP = 2


def back_kind(name, late):
    return "none" if name in BACK_NONE else "late" if name in late else "x"


def back_kernel(nz, late, order, gap, *refs):
    (
        kvp, crossp, wq, wk, wv, wck, wcv, x_ref, gains_ref, gh_ref, gpart_ref, enc_ref,
        n3, mixed, att, n2, attc, n1, gg, gu, go, g1, gcq, g2, dq,
    ) = refs[:25]
    refs = refs[25:]
    outs = dict(zip(BACK_OUT, refs[: len(BACK_OUT)]))
    gx_ref, genc_ref, total_ref = refs[len(BACK_OUT) : len(BACK_OUT) + 3]
    refs = refs[len(BACK_OUT) + 3 :]
    kvown, crown, low, wbuf, kvl, kls, wsem = refs[:7]
    refs = refs[7:]
    outs["kv"], outs["cross"] = kvown, crown
    at = Place(nz)
    jobs = []
    for i, (name, chunk) in enumerate(order):
        mine = list(refs[Reduce.COUNT * i : Reduce.COUNT * (i + 1)])
        chunks = BACK_CHUNKS.get(name, 1)
        out = outs[name]
        if chunks > 1:
            wide = out.shape[-1] // chunks
            out = out.at[:, pl.ds(chunk * wide, wide)]
        job = Reduce(at, out, mine, back_kind(name, late))
        if name == "cross":
            job.part = crossp
        if name == "kv":
            job.part = kvp
            job.part_cols = pl.ds(chunk * wide, wide)
            job.local_part, job.local_cols = kvl, job.part_cols
        jobs.append(job)
    everyone = Total(at, refs[Reduce.COUNT * len(order) :])
    load_w = [pltpu.make_async_copy(src, wbuf.at[i], wsem.at[i]) for i, src in enumerate((wq, wk, wv))]
    load_c = [pltpu.make_async_copy(src, wbuf.at[i], wsem.at[3 + i]) for i, src in enumerate((wck, wcv))]
    for copy in load_c:
        copy.start()
    kv_local = [pltpu.make_async_copy(kvp.at[k, at.w], kvl.at[k], kls.at[k]) for k in range(2 * nz)]
    for copy in kv_local:
        copy.start()
    at.meet()
    width = x_ref.shape[1]
    inner = dq.shape[1]

    def make(name, chunk, part):
        if name in BACK_NONE:
            return
        chips, _, r, wide = part.shape
        if name in ("ck", "cv"):
            left, right = enc_ref, low.at[:, pl.ds(0 if name == "ck" else inner, inner)]
        elif name in ("k", "v"):
            left, right = n1, kvl.at[0].at[:, pl.ds(0 if name == "k" else inner, inner)]
        else:
            left, right = {
                "gate": (n3, gg), "up": (n3, gu), "down": (mixed, go), "o": (att, g1), "cq": (n2, gcq), "co": (attc, g2),
                "q": (n1, dq),
            }[name]
        take = 4 if r % 128 else 1
        tile = 512 if wide % 512 == 0 else wide // 2 if wide % 256 == 0 and wide > 256 else wide
        for first in range(0, chips, take):
            piece = left[:, first * 2 * r : (first + take) * 2 * r]
            for c in range(0, wide, tile):
                out = mm(piece, right[:, chunk * wide + c : chunk * wide + c + tile], TN).astype(BF16)
                part[first : first + take, :, :, c : c + tile] = out.reshape(take, 2, r, tile)

    def after_cross():
        both = crown[...]
        low[...] = jnp.concatenate([both, jnp.zeros_like(both)], axis=0).astype(BF16)
        for copy in load_c:
            copy.wait()
        genc = mm(low[:, :inner], wbuf[0].reshape(width, inner), NT) + mm(low[:, inner:], wbuf[1].reshape(width, inner), NT)
        genc_ref[...] = genc[:8]
        for copy in load_w:
            copy.start()

    def after_kv():
        kvl[0] = kvown[...].astype(BF16)
        for copy in load_w:
            copy.wait()
        grad = mm(dq[...], wbuf[0].reshape(width, inner), NT)
        grad = grad + mm(kvl[0][:, :inner], wbuf[1].reshape(width, inner), NT)
        grad = grad + mm(kvl[0][:, inner:], wbuf[2].reshape(width, inner), NT)
        rows, gain = norm_back(x_ref[...].astype(F32), gains_ref[4:5], grad)
        gx_ref[...] = gh_ref[...] + rows
        everyone.buf[0] = gpart_ref[...]
        everyone.buf[0, 0:1, :] = gain
        everyone.send()

    count = len(order)
    kv_turn = order.index(("kv", 1)) + 5 * gap
    for turn in range(count + 5 * gap):
        for i in range(count - 1, -1, -1):
            (name, chunk), job = order[i], jobs[i]
            stage = turn - i
            if stage == 0:
                make(name, chunk, job.part)
                job.send()
            if stage == gap:
                if (name, chunk) == ("kv", 0):
                    for copy in kv_local:
                        copy.wait()
                job.after_w()
            if stage == 2 * gap:
                job.after_x()
            if stage == 3 * gap:
                job.after_y()
            if stage == 4 * gap:
                job.after_z()
            if stage == 5 * gap:
                job.end()
                if name == "cross":
                    after_cross()
                if (name, chunk) == ("kv", 1):
                    after_kv()
        if 0 < turn - kv_turn <= 3:
            everyone.after(turn - kv_turn - 1)
    total_ref[...] = everyone.end()
    for job in jobs:
        job.close()


def back_step(
    kv_part, cross_part, weights, x, gains, grad_hidden, gpart, enc, acts, shapes, nz, collective_id=2, late=BACK_LATE,
    order=BACK_ORDER, gap=BACK_GAP,
):
    hb = pl.BlockSpec(memory_space=pl.ANY)
    vm = pl.BlockSpec(memory_space=pltpu.VMEM)
    rows, width = x.shape
    inner = acts[-1].shape[1]
    dma = pltpu.SemaphoreType.DMA
    own = [jax.ShapeDtypeStruct(shapes[name], F32) for name in BACK_OUT]
    scratch = [
        pltpu.VMEM((rows, 2 * inner), F32),
        pltpu.VMEM((8, 2 * inner), F32),
        pltpu.VMEM((16, 2 * inner), BF16),
        pltpu.VMEM((3,) + weights[0].shape, BF16),
        pltpu.VMEM((2 * nz, rows, 2 * inner), BF16),
        dma((2 * nz,)),
        dma((5,)),
    ]
    shapes = dict(shapes, kv=(rows, 2 * inner), cross=(8, 2 * inner))
    for name, _ in order:
        r, wide = shapes[name]
        wide = wide // BACK_CHUNKS.get(name, 1)
        held = name not in BACK_NONE
        scratch += Reduce.scratch(nz, r, wide, back_kind(name, late), F32 if name == "cross" else BF16, part=held)
    scratch += Total.scratch(nz, gpart.shape[0], width)
    return pl.pallas_call(
        functools.partial(back_kernel, nz, late, order, gap),
        name="back",
        out_shape=tuple(own)
        + (
            jax.ShapeDtypeStruct((rows, width), F32),
            jax.ShapeDtypeStruct((8, width), F32),
            jax.ShapeDtypeStruct(gpart.shape, F32),
        ),
        in_specs=[hb, vm] + [hb] * 5 + [vm] * (5 + len(acts)),
        out_specs=tuple([vm] * (len(own) + 3)),
        scratch_shapes=scratch,
        compiler_params=pltpu.CompilerParams(
            collective_id=collective_id, has_side_effects=True, vmem_limit_bytes=BIG
        ),
    )(kv_part, cross_part, *weights, x, gains, grad_hidden, gpart, enc, *acts)


class Bag:
    def __init__(self, names, refs):
        for name, ref in zip(names, refs):
            setattr(self, name, ref)


def flat(ref):
    value = ref[...]
    return value.reshape(-1, value.shape[-1])


def unstack(pair_rows, low):
    rows = pair_rows.shape[0] // 2
    return jnp.where(low, pair_rows[:rows], pair_rows[rows:])


def every_encoded(small_ref, take):
    devices, block, width = small_ref.shape
    rows = devices * take
    row = lax.broadcasted_iota(jnp.int32, (rows, devices * block), 0)
    col = lax.broadcasted_iota(jnp.int32, (rows, devices * block), 1)
    pick = (col == (row // take) * block + lax.rem(row, take)).astype(BF16)
    return mm(pick, small_ref[...].reshape(devices * block, width), NN).astype(BF16)


def cross_forward(b, low):
    pairs = b.cq.shape[1] // 128
    for pair in range(pairs):
        lanes = slice(128 * pair, 128 * pair + 128)
        qm = stack_pair(b.cq[:, lanes], low)
        s = mm(qm, b.ckeys[:, lanes], NT)
        peak = jnp.max(s, axis=1, keepdims=True)
        log_total = peak + jnp.log(jnp.sum(jnp.exp(s - peak), axis=1, keepdims=True))
        p = jnp.exp(s - log_total)
        b.cprob[pair] = p
        b.attc[:, lanes] = unstack(mm(p.astype(BF16), b.cvals[:, lanes], NN), low).astype(BF16)


def cross_backward(b, gac, low, keys_each):
    pairs = b.cq.shape[1] // 128
    inner = b.cq.shape[1]
    owners = b.crossp.shape[0] * b.crossp.shape[1]
    b.crossp[...] = jnp.zeros_like(b.crossp)
    for pair in range(pairs):
        lanes = slice(128 * pair, 128 * pair + 128)
        qm = stack_pair(b.cq[:, lanes], low)
        dom = stack_pair(gac[:, lanes], low)
        p = b.cprob[pair]
        dp = mm(dom, b.cvals[:, lanes], NT)
        ds = (p * (dp - jnp.sum(p * dp, axis=1, keepdims=True))).astype(BF16)
        b.gcq[:, lanes] = unstack(mm(ds, b.ckeys[:, lanes], NN), low).astype(BF16)
        gk = mm(ds, qm, TN)
        gv = mm(p.astype(BF16), dom, TN)
        for owner in range(owners):
            rows = slice(keys_each * owner, keys_each * owner + keys_each)
            b.crossp[owner // 2, owner % 2, 0:keys_each, lanes] = gk[rows]
            b.crossp[owner // 2, owner % 2, 0:keys_each, 128 * pair + inner : 128 * pair + inner + 128] = gv[rows]


GELU_A = 0.7978845608028654
GELU_B = 0.044715


def gelu_parts(v):
    t = jnp.tanh(GELU_A * (v + GELU_B * v * v * v))
    value = 0.5 * v * (1.0 + t)
    slope = 0.5 * (1.0 + t) + 0.5 * v * (1.0 - t * t) * (GELU_A * (1.0 + 3.0 * GELU_B * v * v))
    return value, slope


FF_TILE = 512


def after_attention(b, low):
    b.h1[...] = b.x[...].astype(F32) + mm(b.att[...], flat(b.w_o), NN)
    b.n2[...] = normed(b.h1[...], b.gains[5:6]).astype(BF16)
    b.cq[...] = mm(b.n2[...], flat(b.w_cq), NN).astype(BF16)


def after_cross_attention(b):
    b.h2[...] = b.h1[...] + mm(b.attc[...], flat(b.w_co), NN)
    b.n3[...] = normed(b.h2[...], b.gains[6:7]).astype(BF16)


def feed_forward(b):
    ff = b.mixed.shape[1]
    width = b.x.shape[1]
    for c in range(0, ff, FF_TILE):
        cols = slice(c, c + FF_TILE)
        gate = mm(b.n3[...], b.w_gate[:, :, cols].reshape(width, FF_TILE), NN)
        up = mm(b.n3[...], b.w_up[:, :, cols].reshape(width, FF_TILE), NN)
        value, slope = gelu_parts(gate)
        b.mixed[:, cols] = (value * up).astype(BF16)
        b.hg[:, cols] = value
        b.hs[:, cols] = slope * up
    b.layer_out[...] = (b.h2[...] + mm(b.mixed[...], flat(b.w_down), NN)).astype(BF16)


def feed_backward(b):
    ff = b.mixed.shape[1]
    width = b.x.shape[1]
    down = flat(b.w_down)
    total = jnp.zeros(b.h2.shape, F32)
    for c in range(0, ff, FF_TILE):
        cols = slice(c, c + FF_TILE)
        gm = mm(b.go[...], down[cols], NT).astype(BF16).astype(F32)
        gg = (gm * b.hs[:, cols]).astype(BF16)
        gu = (gm * b.hg[:, cols]).astype(BF16)
        b.gg[:, cols] = gg
        b.gu[:, cols] = gu
        total = total + mm(gg, b.w_gate[:, :, cols].reshape(width, FF_TILE), NT)
        total = total + mm(gu, b.w_up[:, :, cols].reshape(width, FF_TILE), NT)
    rows, gain = norm_back(b.h2[...], b.gains[6:7], total)
    b.gpart[2:3, :] = gain
    b.gh[...] = b.go[...].astype(F32) + rows
    b.g2[...] = b.gh[...].astype(BF16)


def before_attention(b):
    rows, gain = norm_back(b.h1[...], b.gains[5:6], mm(b.gcq[...], flat(b.w_cq), NT))
    b.gpart[1:2, :] = gain
    b.gh[...] = b.gh[...] + rows
    b.g1[...] = b.gh[...].astype(BF16)
    b.gatt[...] = mm(b.g1[...], flat(b.w_o), NT).astype(BF16)


def fill_bias(b, qb, rank):
    pairs = b.q.shape[1] // 128
    key_j = lax.broadcasted_iota(jnp.int32, (CH, 128), 0)
    lane_i = lax.broadcasted_iota(jnp.int32, (CH, 128), 1)
    high = lane_i >= BLK
    row_i = jnp.where(high, lane_i - BLK, lane_i)
    shift = jnp.where(high, BLK, 0)
    for kind in range(2):
        dist = (lax.rem(rank, 4) + 4 * kind) * BLK + row_i - key_j
        bucket = bucket_ids(jnp.maximum(dist, 0)) + shift
        for pair in range(pairs):
            tile = jnp.take_along_axis(jnp.broadcast_to(b.tb[pl.ds(pair, 1), :], (CH, 128)), bucket, axis=1)
            if kind == 0:
                tile = jnp.where(dist >= 0, tile, MASKED)
            b.bias[qb, kind, pair] = tile
    for pair in range(pairs):
        b.bias[qb, 2, pair] = jnp.where(
            high,
            b.tb[pl.ds(pair, 1), pl.ds(BLK + BUCKETS - 1, 1)],
            b.tb[pl.ds(pair, 1), pl.ds(BUCKETS - 1, 1)],
        )


def self_forward_block(b, qb, rank, low):
    pairs = b.q.shape[1] // 128
    inner = b.q.shape[1]
    last = rank // 4
    mine = pl.ds(qb * BLK, BLK)
    for pair in range(pairs):
        b.qm[qb, pair] = stack_pair(b.q[mine, 128 * pair : 128 * pair + 128], low)
        b.top[pair] = jnp.full((8, 128), -3e38, F32)
        b.sums[pair] = jnp.zeros((8, 128), F32)
        b.acc[pair] = jnp.zeros((2 * BLK, 128), F32)

    def first(chunk, carry):
        kind = jnp.minimum(last - chunk, 2)
        keys = pl.ds(pl.multiple_of(chunk * CH, CH), CH)
        for pair in range(pairs):
            s = mm(b.kvs[keys, 128 * pair : 128 * pair + 128], b.qm[qb, pair], NT) + b.bias[qb, kind, pair]
            b.sco[pair, keys, :] = s
            b.top[pair] = jnp.maximum(b.top[pair], jnp.max(s.reshape(CH // 8, 8, 128), axis=0))
        return carry

    lax.fori_loop(0, last + 1, first, 0)
    for pair in range(pairs):
        b.top[pair] = jnp.broadcast_to(jnp.max(b.top[pair], axis=0, keepdims=True), (8, 128))

    def second(chunk, carry):
        keys = pl.ds(pl.multiple_of(chunk * CH, CH), CH)
        for pair in range(pairs):
            p = jnp.exp(b.sco[pair, keys, :] - b.top[pair, 0:1, :])
            b.sums[pair] += jnp.sum(p.reshape(CH // 8, 8, 128), axis=0)
            values = b.kvs[keys, inner + 128 * pair : inner + 128 * pair + 128]
            b.acc[pair] += mm(p.astype(BF16), values, TN)
        return carry

    lax.fori_loop(0, last + 1, second, 0)
    for pair in range(pairs):
        total = jnp.sum(b.sums[pair], axis=0, keepdims=True)
        b.rows[qb, pair, 0:1, :] = b.top[pair, 0:1, :] + jnp.log(total)
        scale = jnp.broadcast_to(total, (128, 128)).T
        out = unstack(b.acc[pair] / scale, low)
        b.att32[mine, 128 * pair : 128 * pair + 128] = out
        b.att[mine, 128 * pair : 128 * pair + 128] = out.astype(BF16)


def self_backward_rows(b, qb, low):
    pairs = b.q.shape[1] // 128
    mine = pl.ds(qb * BLK, BLK)
    for pair in range(pairs):
        lanes = slice(128 * pair, 128 * pair + 128)
        grad = b.gatt[mine, lanes]
        b.dom[qb, pair] = stack_pair(grad, low)
        prod = (grad.astype(F32) * b.att32[mine, lanes]).T
        b.rows[qb, pair, 1:2, :] = jnp.concatenate(
            [jnp.sum(prod[:BLK], axis=0, keepdims=True), jnp.sum(prod[BLK:], axis=0, keepdims=True)], axis=1
        )


def self_backward_block(b, qb, rank, low):
    pairs = b.q.shape[1] // 128
    inner = b.q.shape[1]
    last = rank // 4
    b.acc[...] = jnp.zeros_like(b.acc)

    @pl.when(last == 0)
    def _():
        for pair in range(pairs):
            b.near[pair, pl.ds(0, CH), :] = jnp.zeros((CH, 128), F32)

    def step(chunk, carry):
        kind = jnp.minimum(last - chunk, 2)
        keys = pl.ds(pl.multiple_of(chunk * CH, CH), CH)
        keep = jnp.maximum(chunk - last + 1, 0)
        for pair in range(pairs):
            klanes = slice(128 * pair, 128 * pair + 128)
            vlanes = slice(inner + 128 * pair, inner + 128 * pair + 128)
            kp = b.kvs[keys, klanes]
            qp = b.qm[qb, pair]
            gp = b.dom[qb, pair]
            st = mm(kp, qp, NT) + b.bias[qb, kind, pair]
            pt = jnp.exp(st - b.rows[qb, pair, 0:1, :])
            dp = mm(b.kvs[keys, vlanes], gp, NT)
            ds = pt * (dp - b.rows[qb, pair, 1:2, :])
            dsb = ds.astype(BF16)
            b.dkv[keys, vlanes] += mm(pt.astype(BF16), gp, NN)
            b.dkv[keys, klanes] += mm(dsb, qp, NN)
            b.acc[pair] += mm(dsb, kp, TN)
            b.tot[pair] += jnp.sum(ds.reshape(CH // 8, 8, 128), axis=0)
            b.near[pair, pl.ds(pl.multiple_of(keep * CH, CH), CH), :] = ds
        return carry

    lax.fori_loop(0, last + 1, step, 0)
    for pair in range(pairs):
        b.dq[pl.ds(qb * BLK, BLK), 128 * pair : 128 * pair + 128] = unstack(b.acc[pair], low).astype(BF16)
        for gap in range(3):
            offset = pl.multiple_of((rank - gap - 4 * (last - 1)) * BLK, BLK)
            b.nacc[gap, pair] += b.near[pair, pl.ds(offset, BLK), :]


def bias_gradient(b, low):
    pairs = b.q.shape[1] // 128
    key_s = lax.broadcasted_iota(jnp.int32, (BLK, 128), 0)
    lane = lax.broadcasted_iota(jnp.int32, (BLK, 128), 1)
    row_s = jnp.where(low, lane, lane - BLK)
    buckets = [bucket_ids(jnp.maximum(gap * BLK + row_s - key_s, 0)) for gap in range(3)]
    for pair in range(pairs):
        far = jnp.sum(b.tot[pair], axis=0, keepdims=True)
        for gap in range(3):
            far = far - jnp.sum(b.nacc[gap, pair], axis=0, keepdims=True)
        lines = []
        for number in range(BUCKETS):
            part = jnp.where(buckets[0] == number, b.nacc[0, pair], 0.0)
            for gap in range(1, 3):
                part = part + jnp.where(buckets[gap] == number, b.nacc[gap, pair], 0.0)
            line = jnp.sum(part, axis=0, keepdims=True)
            lines.append(line + far if number == BUCKETS - 1 else line)
        grid = jnp.concatenate(lines + [jnp.zeros((128 - BUCKETS, 128), F32)], axis=0).T
        b.gpart[8 + 2 * pair : 9 + 2 * pair, 0:128] = jnp.sum(grid[:BLK], axis=0, keepdims=True)
        b.gpart[9 + 2 * pair : 10 + 2 * pair, 0:128] = jnp.sum(grid[BLK:], axis=0, keepdims=True)


MID_IN = (
    "mine", "deal", "k_hbm", "v_hbm", "o", "cq_w", "ck", "cv", "co", "gate", "up", "down", "x", "gains", "small", "q", "go", "tb",
)
MID_OUT = (
    "layer_out", "n3", "mixed", "att", "n2", "attc", "gg", "gu", "g1", "gcq", "g2", "dq", "gh", "gpart", "crossp", "dkv_hbm",
)
MID_SCRATCH = (
    "kvs", "dkv", "w_o", "w_cq", "w_ck", "w_cv", "w_co", "w_gate", "w_up", "w_down", "h1", "h2", "cq", "ckeys", "cvals", "cprob",
    "hg", "hs", "gatt", "bias", "qm", "dom", "top", "sums", "acc", "sco", "rows", "att32", "near", "nacc", "tot", "sem", "osem", "wsem",
)


def mid_kernel(enc_own, *refs):
    b = Bag(MID_IN + MID_OUT + MID_SCRATCH, refs)
    load_in_order(b.deal, b.k_hbm, b.v_hbm, b.kvs, b.sem)
    loads = []
    for i, name in enumerate(("o", "cq", "ck", "cv", "co", "gate", "up", "down")):
        source = b.cq_w if name == "cq" else getattr(b, name)
        loads.append(pltpu.make_async_copy(source, getattr(b, "w_" + name), b.wsem.at[i]))
        loads[-1].start()
    low = lax.broadcasted_iota(jnp.int32, (BLK, 128), 1) < BLK
    low2 = lax.broadcasted_iota(jnp.int32, (2 * BLK, 128), 1) < BLK
    ranks = [b.mine[0, qb] for qb in range(2)]
    for qb in range(2):
        fill_bias(b, qb, ranks[qb])
    loaded(b.k_hbm, b.v_hbm, b.kvs, b.sem)
    for qb in range(2):
        self_forward_block(b, qb, ranks[qb], low)
    for load in loads[:5]:
        load.wait()
    after_attention(b, low)
    enc = every_encoded(b.small, enc_own)
    b.ckeys[...] = mm(enc, flat(b.w_ck), NN).astype(BF16)
    b.cvals[...] = mm(enc, flat(b.w_cv), NN).astype(BF16)
    cross_forward(b, low2)
    after_cross_attention(b)
    for load in loads[5:]:
        load.wait()
    feed_forward(b)
    b.gpart[...] = jnp.zeros_like(b.gpart)
    feed_backward(b)
    gac = mm(b.g2[...], flat(b.w_co), NT).astype(BF16)
    cross_backward(b, gac, low2, enc_own)
    before_attention(b)
    b.dkv[...] = jnp.zeros_like(b.dkv)
    b.tot[...] = jnp.zeros_like(b.tot)
    b.nacc[...] = jnp.zeros_like(b.nacc)
    for qb in range(2):
        self_backward_rows(b, qb, low)
        self_backward_block(b, qb, ranks[qb], low)
    blocks = b.k_hbm.shape[0] // BLK

    def out_one(index, carry):
        here = pl.ds(pl.multiple_of(b.deal[index // 2, index % 2] * BLK, BLK), BLK)
        b.kvs[here, :] = b.dkv[here, :].astype(BF16)
        pltpu.make_async_copy(b.kvs.at[here], b.dkv_hbm.at[pl.ds(index * BLK, BLK)], b.osem).start()
        return carry

    lax.fori_loop(0, blocks, out_one, 0)
    bias_gradient(b, low)
    pltpu.make_async_copy(b.kvs, b.dkv_hbm, b.osem).wait()


def mid(mine, deal, keys, values, weights, x, gains, small, q, go, tb, enc_own):
    rows, width = x.shape
    inner = q.shape[1]
    total = keys.shape[0]
    ff = weights[5].shape[2]
    h2 = inner // 128
    shards = weights[0].shape[0]
    enc = shards * enc_own
    sm = pl.BlockSpec(memory_space=pltpu.SMEM)
    vm = pl.BlockSpec(memory_space=pltpu.VMEM)
    hb = pl.BlockSpec(memory_space=pl.ANY)
    out = jax.ShapeDtypeStruct
    return pl.pallas_call(
        functools.partial(mid_kernel, enc_own),
        name="mid",
        out_shape=(
            out((rows, width), BF16), out((rows, width), BF16), out((rows, ff), BF16), out((rows, inner), BF16),
            out((rows, width), BF16), out((rows, inner), BF16), out((rows, ff), BF16), out((rows, ff), BF16),
            out((rows, width), BF16), out((rows, inner), BF16), out((rows, width), BF16), out((rows, inner), BF16),
            out((rows, width), F32), out((24, width), F32), out((shards // 2, 2, 8, 2 * inner), F32),
            out((total, 2 * inner), BF16),
        ),
        in_specs=[sm, sm] + [hb] * (2 + len(weights)) + [vm] * 6,
        out_specs=tuple([vm] * 15 + [hb]),
        scratch_shapes=[
            pltpu.VMEM((total, 2 * inner), BF16),
            pltpu.VMEM((total, 2 * inner), F32),
        ]
        + [pltpu.VMEM(weight.shape, BF16) for weight in weights]
        + [
            pltpu.VMEM((rows, width), F32),
            pltpu.VMEM((rows, width), F32),
            pltpu.VMEM((rows, inner), BF16),
            pltpu.VMEM((enc, inner), BF16),
            pltpu.VMEM((enc, inner), BF16),
            pltpu.VMEM((h2, 2 * rows, enc), F32),
            pltpu.VMEM((rows, ff), F32),
            pltpu.VMEM((rows, ff), F32),
            pltpu.VMEM((rows, inner), BF16),
            pltpu.VMEM((2, 3, h2, CH, 128), F32),
            pltpu.VMEM((2, h2, 2 * BLK, 128), BF16),
            pltpu.VMEM((2, h2, 2 * BLK, 128), BF16),
            pltpu.VMEM((h2, 8, 128), F32),
            pltpu.VMEM((h2, 8, 128), F32),
            pltpu.VMEM((h2, 2 * BLK, 128), F32),
            pltpu.VMEM((h2, total, 128), F32),
            pltpu.VMEM((2, h2, 8, 128), F32),
            pltpu.VMEM((rows, inner), F32),
            pltpu.VMEM((h2, 2 * CH, 128), F32),
            pltpu.VMEM((3, h2, BLK, 128), F32),
            pltpu.VMEM((h2, 8, 128), F32),
            pltpu.SemaphoreType.DMA((2,)),
            pltpu.SemaphoreType.DMA,
            pltpu.SemaphoreType.DMA((8,)),
        ],
        compiler_params=pltpu.CompilerParams(vmem_limit_bytes=BIG),
    )(mine, deal, keys, values, *weights, x, gains, small, q, go, tb)


def fits(*operands):
    layer_in, encoded, self_query, relative_bias = operands[0], operands[1], operands[4], operands[18]
    total = layer_in.shape[1] * lax.axis_size(AXES)
    return (
        lax.axis_size(GRP) == 2
        and lax.axis_size(WSH) == 2
        and lax.axis_size(CTX) == 8
        and layer_in.shape[1] == 2 * BLK
        and encoded.shape[1] == 4
        and total // 2 <= CONT_TOK
        and self_query.shape[0] % 16 == 0
        and self_query.shape[1] == relative_bias.shape[1] * BLK
        and self_query.shape[1] % 256 == 0
    )


def fast(
    layer_in, encoded, cotangent, deal_table, self_query, self_key, self_value, self_output, cross_query, cross_key,
    cross_value, cross_output, feed_gate, feed_up, feed_down, gain_self, gain_cross, gain_feed, relative_bias,
):
    nz = lax.axis_size(CTX) // 2
    shards = lax.axis_size(AXES)
    device = lax.axis_index(AXES)
    rows = layer_in.shape[1]
    width = layer_in.shape[2]
    heads = relative_bias.shape[1]
    inner = self_query.shape[1]
    owned = gain_self.shape[0]
    enc_own = encoded.shape[1]
    table_hb = relative_bias.astype(F32).T
    mine = lax.dynamic_slice_in_dim(deal_table, device, 1)

    gains_here = lax.dynamic_update_slice(
        jnp.zeros((3, width), BF16), jnp.stack([gain_self, gain_cross, gain_feed]), (0, device * owned)
    )
    small = jnp.concatenate([encoded[0], gains_here, jnp.zeros((9, width), BF16)], axis=0)
    *wholes, queries, normed_one, gains = front(
        layer_in[0],
        (
            small, self_key, self_value, self_query, self_output, cross_query, cross_key, cross_value, cross_output,
            feed_gate, feed_up, feed_down,
        ),
        nz,
        shards,
    )
    whole = dict(zip(FRONT_PARTS, wholes))
    in_rows = {name: value.reshape(-1, value.shape[-1]) for name, value in whole.items()}
    (
        layer_out, normed_three, mixed_hidden, attended, normed_two, attended_cross, grad_gate, grad_up, grad_one_low,
        grad_cq_low, grad_two_low, grad_queries, grad_hidden_one, gpart, cross_part, kv_part,
    ) = mid(
        mine, deal_table, in_rows["keys"], in_rows["values"],
        [whole[name] for name in ("o", "cq", "ck", "cv", "co", "gate", "up", "down")],
        layer_in[0], gains, whole["small"], queries, cotangent[0], pair_table(table_hb), enc_own,
    )
    ff = feed_gate.shape[1]
    square = (owned, inner)
    shapes = dict(
        gate=(owned, ff), up=(owned, ff), down=(feed_down.shape[0], width), co=(inner // shards, width), cq=square,
        ck=square, cv=square, q=square, o=(inner // shards, width), k=square, v=square,
    )
    enc_padded = jnp.pad(encoded[0], ((0, 16 - enc_own), (0, 0)))
    result = back_step(
        kv_part.reshape(2 * nz, 2, rows, 2 * inner), cross_part,
        [whole[name] for name in ("q", "k", "v", "ck", "cv")], layer_in[0], gains,
        grad_hidden_one, gpart, enc_padded,
        (
            normed_three, mixed_hidden, attended, normed_two, attended_cross, normed_one, grad_gate, grad_up, cotangent[0],
            grad_one_low, grad_cq_low, grad_two_low, grad_queries,
        ),
        shapes,
        nz,
    )
    got = dict(zip(BACK_OUT, result))
    grad_input, grad_enc, total = result[len(BACK_OUT) :]
    gain_grads = [lax.dynamic_slice_in_dim(total[i], device * owned, owned) for i in range(3)]
    grad_relative_bias = total[8 : 8 + heads, :BUCKETS].T
    return (
        layer_out[None], grad_input[None], grad_enc[None, :enc_own],
        got["q"], got["k"], got["v"], got["o"], got["cq"], got["ck"], got["cv"], got["co"], got["gate"], got["up"], got["down"],
        gain_grads[0], gain_grads[1], gain_grads[2], grad_relative_bias,
    )


def solution(mesh):
    return jax.shard_map(
        lambda *operands: (fast if fits(*operands) else local)(*operands),
        mesh=mesh,
        in_specs=(
            P(GRP, AXES, None),
            P(GRP, AXES, None),
            P(GRP, AXES, None),
            P(),
            P(AXES, None),
            P(AXES, None),
            P(AXES, None),
            P(AXES, None),
            P(AXES, None),
            P(AXES, None),
            P(AXES, None),
            P(AXES, None),
            P(AXES, None),
            P(AXES, None),
            P(AXES, None),
            P(AXES),
            P(AXES),
            P(AXES),
            P(),
        ),
        out_specs=(
            P(GRP, AXES, None),
            P(GRP, AXES, None),
            P(GRP, AXES, None),
            P(AXES, None),
            P(AXES, None),
            P(AXES, None),
            P(AXES, None),
            P(AXES, None),
            P(AXES, None),
            P(AXES, None),
            P(AXES, None),
            P(AXES, None),
            P(AXES, None),
            P(AXES, None),
            P(AXES),
            P(AXES),
            P(AXES),
            P(),
        ),
        check_vma=False,
    )
```

```python
import functools
import math

import jax
import jax.numpy as jnp
from jax import lax
from jax.experimental import pallas as pl
from jax.experimental.pallas import tpu as pltpu
from jax.sharding import PartitionSpec as P

GRP, CTX, WSH = "grp", "ctx", "wsh"
AXES = (CTX, WSH)
EVERY = (GRP, CTX, WSH)
QK = "qhd,khd->hqk"
PV = "hqk,khd->qhd"
PTQ = "hqk,qhd->khd"
TF_TD = "tf,td->fd"
TD_FD = "td,fd->tf"
TD_TF = "td,tf->df"
TF_DF = "tf,df->td"
TC_TD = "tc,td->cd"
TD_CD = "td,cd->tc"
TD_TC = "td,tc->dc"
TC_DC = "tc,dc->td"

BUCKETS = 32
MAXDIST = 128
CONT_TOK = 2048


MASKED = -1e30
EPSILON = 1e-06


def rms_norm(hidden, gain_vector):
    return (
        hidden
        * lax.rsqrt(jnp.mean(hidden * hidden, axis=-1, keepdims=True) + EPSILON)
        * gain_vector
    )


def gated(gate_pre, up_pre):
    return jax.nn.gelu(gate_pre, approximate=True) * up_pre


def bounce(values):
    return lax.optimization_barrier(values.astype(jnp.bfloat16)).astype(jnp.float32)


def split_probs(probs_full):
    probs_high = probs_full.astype(jnp.bfloat16)
    probs_rest = (probs_full - probs_high.astype(jnp.float32)).astype(jnp.bfloat16)
    return (probs_high, probs_rest)


def bucket_ids(distance):
    exact_half = BUCKETS // 2
    counted = jnp.minimum(distance, exact_half)
    for number in range(1, exact_half):
        boundary = int(math.ceil(exact_half * math.pow(MAXDIST / exact_half, number / exact_half)))
        counted = counted + (distance >= boundary).astype(jnp.int32)
    return counted


def token_place(tokens, prompt_len, cont_len):
    beyond = tokens - prompt_len
    in_prompt = tokens < prompt_len
    sequence = jnp.where(in_prompt, 0, 1 + beyond // cont_len)
    position = jnp.where(in_prompt, tokens, prompt_len + beyond % cont_len)
    return (sequence, position)


def pair_mask(seq_query, pos_query, seq_key, pos_key):
    earlier = pos_key[None, :] <= pos_query[:, None]
    visible = (seq_key[None, :] == seq_query[:, None]) | (seq_key[None, :] == 0)
    return earlier & visible


def bucket_bias(pos_query, pos_key, table_hb):
    buckets = bucket_ids(jnp.maximum(pos_query[:, None] - pos_key[None, :], 0))
    picks = (
        buckets[None, :, :, None]
        == jnp.arange(table_hb.shape[1], dtype=jnp.int32)[None, None, None, :]
    )
    return (buckets, jnp.sum(jnp.where(picks, table_hb[:, None, None, :], 0.0), axis=-1))


def bucket_grad(buckets, grad_scores, bucket_count):
    picks = (
        buckets[None, :, :, None] == jnp.arange(bucket_count, dtype=jnp.int32)[None, None, None, :]
    )
    return jnp.sum(
        jnp.where(picks, grad_scores.astype(jnp.float32)[:, :, :, None], 0.0), axis=(1, 2)
    )


def masked_scores(query_heads, key_heads, bias, allowed):
    direct = jnp.einsum(QK, query_heads, key_heads, preferred_element_type=jnp.float32)
    return jnp.where(allowed[None], direct + bias, MASKED)


def score_grads(scores, log_total, delta_row, grad_heads, value_heads):
    probs_full = jnp.exp(scores - log_total[:, :, None])
    grad_probs = jnp.einsum(
        QK, grad_heads, value_heads, preferred_element_type=jnp.float32
    )
    grad_scores = (probs_full * (grad_probs - delta_row[:, :, None])).astype(jnp.bfloat16)
    return (probs_full.astype(jnp.bfloat16), grad_scores)


def key_view(seq_all, pos_all, step_index, key_rows, seq_query, pos_query):
    seq_key = lax.dynamic_slice_in_dim(seq_all, step_index * key_rows, key_rows)
    pos_key = lax.dynamic_slice_in_dim(pos_all, step_index * key_rows, key_rows)
    return (pos_key, pair_mask(seq_query, pos_query, seq_key, pos_key))


def self_forward(
    query_heads, key_heads, value_heads, seq_all, pos_all, seq_query, pos_query, table_hb, key_rows
):
    total_rows = key_heads.shape[0]
    head_count = query_heads.shape[1]
    rows_here = query_heads.shape[0]
    step_list = jnp.arange(total_rows // key_rows, dtype=jnp.int32)

    def total_step(carried, step_index):
        pos_key, allowed = key_view(seq_all, pos_all, step_index, key_rows, seq_query, pos_query)

        def total_accumulate(current):
            running_max, running_sum = current
            key_block = lax.dynamic_slice_in_dim(key_heads, step_index * key_rows, key_rows)
            bias = bucket_bias(pos_query, pos_key, table_hb)[1]
            scores = masked_scores(query_heads, key_block, bias, allowed)
            new_max = jnp.maximum(running_max, jnp.max(scores, axis=-1))
            weights = jnp.where(allowed[None], jnp.exp(scores - new_max[:, :, None]), 0.0)
            return (
                new_max,
                running_sum * jnp.exp(running_max - new_max) + jnp.sum(weights, axis=-1),
            )

        return (
            lax.cond(jnp.any(allowed), total_accumulate, lambda current: current, carried),
            None,
        )

    start_state = (
        jnp.full((head_count, rows_here), MASKED, jnp.float32),
        jnp.zeros((head_count, rows_here), jnp.float32),
    )
    (running_max, running_sum), _ = lax.scan(total_step, start_state, step_list)
    log_total = running_max + jnp.log(running_sum)

    def output_step(carried, step_index):
        pos_key, allowed = key_view(seq_all, pos_all, step_index, key_rows, seq_query, pos_query)

        def output_accumulate(current):
            rounded_sum, rest_sum = current
            key_block = lax.dynamic_slice_in_dim(key_heads, step_index * key_rows, key_rows)
            value_block = lax.dynamic_slice_in_dim(value_heads, step_index * key_rows, key_rows)
            bias = bucket_bias(pos_query, pos_key, table_hb)[1]
            scores = masked_scores(query_heads, key_block, bias, allowed)
            probs_high, probs_rest = split_probs(jnp.exp(scores - log_total[:, :, None]))
            rounded_sum = rounded_sum + jnp.einsum(
                PV, probs_high, value_block, preferred_element_type=jnp.float32
            )
            rest_sum = rest_sum + jnp.einsum(
                PV, probs_rest, value_block, preferred_element_type=jnp.float32
            )
            return (rounded_sum, rest_sum)

        return (
            lax.cond(jnp.any(allowed), output_accumulate, lambda current: current, carried),
            None,
        )

    zero_heads = jnp.zeros(query_heads.shape, jnp.float32)
    (rounded_sum, rest_sum), _ = lax.scan(output_step, (zero_heads, zero_heads), step_list)
    return (log_total, rounded_sum, rounded_sum + rest_sum)


def query_backward(
    query_heads,
    key_heads,
    value_heads,
    grad_heads,
    log_total,
    delta_row,
    seq_all,
    pos_all,
    seq_query,
    pos_query,
    table_hb,
    key_rows,
):
    total_rows = key_heads.shape[0]
    inner_width = key_heads.shape[1] * key_heads.shape[2]
    bucket_count = table_hb.shape[1]
    step_list = jnp.arange(total_rows // key_rows, dtype=jnp.int32)

    def step_body(carried, step_index):
        pos_key, allowed = key_view(seq_all, pos_all, step_index, key_rows, seq_query, pos_query)

        def step_accumulate(current):
            grad_query, grad_bias = current
            key_block = lax.dynamic_slice_in_dim(key_heads, step_index * key_rows, key_rows)
            value_block = lax.dynamic_slice_in_dim(value_heads, step_index * key_rows, key_rows)
            buckets, bias = bucket_bias(pos_query, pos_key, table_hb)
            scores = masked_scores(query_heads, key_block, bias, allowed)
            probs_low, grad_scores = score_grads(
                scores, log_total, delta_row, grad_heads, value_block
            )
            grad_query = grad_query + jnp.einsum(
                PV, grad_scores, key_block, preferred_element_type=jnp.float32
            )
            grad_bias = grad_bias + bucket_grad(buckets, grad_scores, bucket_count)
            grad_key = jnp.einsum(
                PTQ, grad_scores, query_heads, preferred_element_type=jnp.float32
            ).reshape(key_rows, inner_width)
            grad_value = jnp.einsum(
                PTQ, probs_low, grad_heads, preferred_element_type=jnp.float32
            ).reshape(key_rows, inner_width)
            return ((grad_query, grad_bias), jnp.concatenate([grad_key, grad_value], axis=1))

        blank_block = jnp.zeros((key_rows, 2 * inner_width), jnp.float32)
        return lax.cond(
            jnp.any(allowed), step_accumulate, lambda current: (current, blank_block), carried
        )

    start_state = (
        jnp.zeros(query_heads.shape, jnp.float32),
        jnp.zeros(table_hb.shape, jnp.float32),
    )
    final_state, key_blocks = lax.scan(step_body, start_state, step_list)
    return (final_state[0], final_state[1], key_blocks.reshape(total_rows, 2 * inner_width))


def local(
    layer_in,
    encoded,
    cotangent,
    deal_table,
    self_query,
    self_key,
    self_value,
    self_output,
    cross_query,
    cross_key,
    cross_value,
    cross_output,
    feed_gate,
    feed_up,
    feed_down,
    gain_self,
    gain_cross,
    gain_feed,
    relative_bias,
):
    shards = lax.axis_size(AXES)
    device = lax.axis_index(AXES)
    ctx_count = lax.axis_size(CTX)
    core_count = lax.axis_size(WSH)
    local_rows = layer_in.shape[1]
    total_rows = local_rows * shards
    block_len = local_rows // 2
    cont_len = min(CONT_TOK, total_rows // 2)
    prompt_len = total_rows - total_rows // 2 // cont_len * cont_len
    key_rows = min(1024, total_rows)
    head_count = relative_bias.shape[1]
    inner_width = self_query.shape[1]
    head_size = inner_width // head_count
    enc_rows = encoded.shape[1] * shards
    table_hb = relative_bias.astype(jnp.float32).T
    flat_table = deal_table.reshape(-1)
    all_tokens = (
        flat_table[:, None] * block_len + jnp.arange(block_len, dtype=jnp.int32)[None, :]
    ).reshape(-1)
    seq_all, pos_all = token_place(all_tokens, prompt_len, cont_len)
    seq_mine = lax.dynamic_slice_in_dim(seq_all, device * local_rows, local_rows)
    pos_mine = lax.dynamic_slice_in_dim(pos_all, device * local_rows, local_rows)
    forward_weights = (
        lax.all_gather(self_query, AXES, axis=0, tiled=True),
        lax.all_gather(self_key, AXES, axis=0, tiled=True),
        lax.all_gather(self_value, AXES, axis=0, tiled=True),
        lax.all_gather(self_output, AXES, axis=0, tiled=True),
        lax.all_gather(cross_query, AXES, axis=0, tiled=True),
        lax.all_gather(cross_key, AXES, axis=0, tiled=True),
        lax.all_gather(cross_value, AXES, axis=0, tiled=True),
        lax.all_gather(cross_output, AXES, axis=0, tiled=True),
        lax.all_gather(feed_gate, AXES, axis=0, tiled=True),
        lax.all_gather(feed_up, AXES, axis=0, tiled=True),
        lax.all_gather(feed_down, AXES, axis=0, tiled=True),
        lax.all_gather(gain_self, AXES, axis=0, tiled=True),
        lax.all_gather(gain_cross, AXES, axis=0, tiled=True),
        lax.all_gather(gain_feed, AXES, axis=0, tiled=True),
    )
    (
        query_weight,
        key_weight,
        value_weight,
        output_weight,
        cq_weight,
        ck_weight,
        cv_weight,
        co_weight,
        gate_weight,
        up_weight,
        down_weight,
        gain_one,
        gain_two,
        gain_three,
    ) = forward_weights
    inputs32 = layer_in[0].astype(jnp.float32)
    normed_one = rms_norm(inputs32, gain_one.astype(jnp.float32)).astype(jnp.bfloat16)
    queries = jnp.dot(normed_one, query_weight, preferred_element_type=jnp.float32).astype(
        jnp.bfloat16
    )
    keys_local = jnp.dot(normed_one, key_weight, preferred_element_type=jnp.float32).astype(
        jnp.bfloat16
    )
    values_local = jnp.dot(normed_one, value_weight, preferred_element_type=jnp.float32).astype(
        jnp.bfloat16
    )
    keys_all, values_all = (
        lax.all_gather(keys_local, AXES, axis=0, tiled=True),
        lax.all_gather(values_local, AXES, axis=0, tiled=True),
    )
    query_heads = queries.reshape(local_rows, head_count, head_size)
    key_heads = keys_all.reshape(total_rows, head_count, head_size)
    value_heads = values_all.reshape(total_rows, head_count, head_size)
    log_self, attn_sum, attn_exact = self_forward(
        query_heads,
        key_heads,
        value_heads,
        seq_all,
        pos_all,
        seq_mine,
        pos_mine,
        table_hb,
        key_rows,
    )
    attended = attn_sum.reshape(local_rows, inner_width).astype(jnp.bfloat16)
    hidden_one = inputs32 + jnp.dot(attended, output_weight, preferred_element_type=jnp.float32)
    normed_two = rms_norm(hidden_one, gain_two.astype(jnp.float32)).astype(jnp.bfloat16)
    cross_queries = jnp.dot(normed_two, cq_weight, preferred_element_type=jnp.float32).astype(
        jnp.bfloat16
    )
    enc_keys = jnp.dot(encoded[0], ck_weight, preferred_element_type=jnp.float32).astype(
        jnp.bfloat16
    )
    enc_values = jnp.dot(encoded[0], cv_weight, preferred_element_type=jnp.float32).astype(
        jnp.bfloat16
    )
    cross_keys, cross_values = (
        lax.all_gather(enc_keys, AXES, axis=0, tiled=True),
        lax.all_gather(enc_values, AXES, axis=0, tiled=True),
    )
    cq_heads = cross_queries.reshape(local_rows, head_count, head_size)
    ck_heads = cross_keys.reshape(enc_rows, head_count, head_size)
    cv_heads = cross_values.reshape(enc_rows, head_count, head_size)
    cross_scores = jnp.einsum(
        QK, cq_heads, ck_heads, preferred_element_type=jnp.float32
    )
    cross_peak = jnp.max(cross_scores, axis=-1)
    log_cross = cross_peak + jnp.log(
        jnp.sum(jnp.exp(cross_scores - cross_peak[:, :, None]), axis=-1)
    )
    cross_probs = jnp.exp(cross_scores - log_cross[:, :, None])
    cross_high, cross_rest = split_probs(cross_probs)
    cross_sum = jnp.einsum(PV, cross_high, cv_heads, preferred_element_type=jnp.float32)
    cross_exact = cross_sum + jnp.einsum(
        PV, cross_rest, cv_heads, preferred_element_type=jnp.float32
    )
    attended_cross = cross_sum.reshape(local_rows, inner_width).astype(jnp.bfloat16)
    hidden_two = hidden_one + jnp.dot(attended_cross, co_weight, preferred_element_type=jnp.float32)
    normed_three = rms_norm(hidden_two, gain_three.astype(jnp.float32)).astype(jnp.bfloat16)
    gate_pre = jnp.dot(normed_three, gate_weight, preferred_element_type=jnp.float32)
    up_pre = jnp.dot(normed_three, up_weight, preferred_element_type=jnp.float32)
    mixed_hidden = gated(gate_pre, up_pre).astype(jnp.bfloat16)
    output_sum = hidden_two + jnp.dot(mixed_hidden, down_weight, preferred_element_type=jnp.float32)
    layer_out = output_sum.astype(jnp.bfloat16)[None]
    back_weights = (
        lax.all_gather(self_query, AXES, axis=0, tiled=True),
        lax.all_gather(self_key, AXES, axis=0, tiled=True),
        lax.all_gather(self_value, AXES, axis=0, tiled=True),
        lax.all_gather(self_output, AXES, axis=0, tiled=True),
        lax.all_gather(cross_query, AXES, axis=0, tiled=True),
        lax.all_gather(cross_key, AXES, axis=0, tiled=True),
        lax.all_gather(cross_value, AXES, axis=0, tiled=True),
        lax.all_gather(cross_output, AXES, axis=0, tiled=True),
        lax.all_gather(feed_gate, AXES, axis=0, tiled=True),
        lax.all_gather(feed_up, AXES, axis=0, tiled=True),
        lax.all_gather(feed_down, AXES, axis=0, tiled=True),
        lax.all_gather(gain_self, AXES, axis=0, tiled=True),
        lax.all_gather(gain_cross, AXES, axis=0, tiled=True),
        lax.all_gather(gain_feed, AXES, axis=0, tiled=True),
    )
    (
        query_back,
        key_back,
        value_back,
        output_back,
        cq_back,
        ck_back,
        cv_back,
        co_back,
        gate_back,
        up_back,
        down_back,
        gain_one_back,
        gain_two_back,
        gain_three_back,
    ) = back_weights
    grad_out = cotangent[0]
    grad_down_w = jnp.einsum(
        TF_TD, mixed_hidden, grad_out, preferred_element_type=jnp.float32
    )
    grad_mixed = jnp.einsum(TD_FD, grad_out, down_back, preferred_element_type=jnp.float32)
    _, gate_pull = jax.vjp(gated, gate_pre, up_pre)
    grad_gate32, grad_up32 = gate_pull(bounce(grad_mixed))
    grad_gate = grad_gate32.astype(jnp.bfloat16)
    grad_up = grad_up32.astype(jnp.bfloat16)
    grad_gate_w = jnp.einsum(
        TD_TF, normed_three, grad_gate, preferred_element_type=jnp.float32
    )
    grad_up_w = jnp.einsum(TD_TF, normed_three, grad_up, preferred_element_type=jnp.float32)
    grad_normed_three = jnp.einsum(
        TF_DF, grad_gate, gate_back, preferred_element_type=jnp.float32
    ) + jnp.einsum(TF_DF, grad_up, up_back, preferred_element_type=jnp.float32)
    _, norm_pull_three = jax.vjp(rms_norm, hidden_two, gain_three_back.astype(jnp.float32))
    back_two, grad_gain_feed = norm_pull_three(grad_normed_three)
    grad_hidden_two = grad_out.astype(jnp.float32) + back_two
    grad_two_low = grad_hidden_two.astype(jnp.bfloat16)
    grad_co_w = jnp.einsum(
        TC_TD, attended_cross, grad_two_low, preferred_element_type=jnp.float32
    )
    grad_attended_cross = jnp.einsum(
        TD_CD, grad_two_low, co_back, preferred_element_type=jnp.float32
    ).astype(jnp.bfloat16)
    grad_ac_heads = grad_attended_cross.reshape(local_rows, head_count, head_size)
    delta_cross = jnp.sum(grad_ac_heads.astype(jnp.float32) * cross_exact, axis=-1).T
    cross_low, grad_cross_scores = score_grads(
        cross_scores, log_cross, delta_cross, grad_ac_heads, cv_heads
    )
    grad_cq = jnp.einsum(
        PV, grad_cross_scores, ck_heads, preferred_element_type=jnp.float32
    )
    grad_ck_part = jnp.einsum(
        PTQ, grad_cross_scores, cq_heads, preferred_element_type=jnp.float32
    ).reshape(enc_rows, inner_width)
    grad_cv_part = jnp.einsum(
        PTQ, cross_low, grad_ac_heads, preferred_element_type=jnp.float32
    ).reshape(enc_rows, inner_width)
    cross_own = lax.psum_scatter(
        jnp.concatenate([grad_ck_part, grad_cv_part], axis=1),
        AXES,
        scatter_dimension=0,
        tiled=True,
    )
    grad_cross_keys = cross_own[:, :inner_width].astype(jnp.bfloat16)
    grad_cross_values = cross_own[:, inner_width:].astype(jnp.bfloat16)
    grad_ck_w = jnp.einsum(
        TD_TC, encoded[0], grad_cross_keys, preferred_element_type=jnp.float32
    )
    grad_cv_w = jnp.einsum(
        TD_TC, encoded[0], grad_cross_values, preferred_element_type=jnp.float32
    )
    grad_encoded = (
        jnp.einsum(TC_DC, grad_cross_keys, ck_back, preferred_element_type=jnp.float32)
        + jnp.einsum(TC_DC, grad_cross_values, cv_back, preferred_element_type=jnp.float32)
    )[None]
    grad_cq_low = grad_cq.reshape(local_rows, inner_width).astype(jnp.bfloat16)
    grad_cq_w = jnp.einsum(TD_TC, normed_two, grad_cq_low, preferred_element_type=jnp.float32)
    grad_normed_two = jnp.einsum(
        TC_DC, grad_cq_low, cq_back, preferred_element_type=jnp.float32
    )
    _, norm_pull_two = jax.vjp(rms_norm, hidden_one, gain_two_back.astype(jnp.float32))
    back_one, grad_gain_cross = norm_pull_two(grad_normed_two)
    grad_hidden_one = grad_hidden_two + back_one
    grad_one_low = grad_hidden_one.astype(jnp.bfloat16)
    grad_o_w = jnp.einsum(TC_TD, attended, grad_one_low, preferred_element_type=jnp.float32)
    grad_attended = jnp.einsum(
        TD_CD, grad_one_low, output_back, preferred_element_type=jnp.float32
    ).astype(jnp.bfloat16)
    grad_att_heads = grad_attended.reshape(local_rows, head_count, head_size)
    delta_self = jnp.sum(grad_att_heads.astype(jnp.float32) * attn_exact, axis=-1).T
    grad_query32, grad_bias_part, kv_blocks = query_backward(
        query_heads,
        key_heads,
        value_heads,
        grad_att_heads,
        log_self,
        delta_self,
        seq_all,
        pos_all,
        seq_mine,
        pos_mine,
        table_hb,
        key_rows,
    )
    kv_own = lax.psum_scatter(kv_blocks, AXES, scatter_dimension=0, tiled=True)
    grad_keys = kv_own[:, :inner_width].astype(jnp.bfloat16)
    grad_values = kv_own[:, inner_width:].astype(jnp.bfloat16)
    grad_queries = grad_query32.reshape(local_rows, inner_width).astype(jnp.bfloat16)
    grad_q_w = jnp.einsum(TD_TC, normed_one, grad_queries, preferred_element_type=jnp.float32)
    grad_k_w = jnp.einsum(TD_TC, normed_one, grad_keys, preferred_element_type=jnp.float32)
    grad_v_w = jnp.einsum(TD_TC, normed_one, grad_values, preferred_element_type=jnp.float32)
    grad_normed_one = (
        jnp.einsum(TC_DC, grad_queries, query_back, preferred_element_type=jnp.float32)
        + jnp.einsum(TC_DC, grad_keys, key_back, preferred_element_type=jnp.float32)
        + jnp.einsum(TC_DC, grad_values, value_back, preferred_element_type=jnp.float32)
    )
    _, norm_pull_one = jax.vjp(rms_norm, inputs32, gain_one_back.astype(jnp.float32))
    back_input, grad_gain_self = norm_pull_one(grad_normed_one)
    grad_input = (grad_hidden_one + back_input)[None]

    def sectioned(grad_full):
        return grad_full.reshape(
            (ctx_count, core_count, grad_full.shape[0] // (ctx_count * core_count))
            + grad_full.shape[1:]
        )

    core_parts = (
        lax.psum_scatter(
            sectioned(grad_q_w).astype(jnp.bfloat16), WSH, scatter_dimension=1, tiled=True
        ).astype(jnp.float32),
        lax.psum_scatter(
            sectioned(grad_k_w).astype(jnp.bfloat16), WSH, scatter_dimension=1, tiled=True
        ).astype(jnp.float32),
        lax.psum_scatter(
            sectioned(grad_v_w).astype(jnp.bfloat16), WSH, scatter_dimension=1, tiled=True
        ).astype(jnp.float32),
        lax.psum_scatter(
            sectioned(grad_o_w).astype(jnp.bfloat16), WSH, scatter_dimension=1, tiled=True
        ).astype(jnp.float32),
        lax.psum_scatter(
            sectioned(grad_cq_w).astype(jnp.bfloat16), WSH, scatter_dimension=1, tiled=True
        ).astype(jnp.float32),
        lax.psum_scatter(
            sectioned(grad_ck_w).astype(jnp.bfloat16), WSH, scatter_dimension=1, tiled=True
        ).astype(jnp.float32),
        lax.psum_scatter(
            sectioned(grad_cv_w).astype(jnp.bfloat16), WSH, scatter_dimension=1, tiled=True
        ).astype(jnp.float32),
        lax.psum_scatter(
            sectioned(grad_co_w).astype(jnp.bfloat16), WSH, scatter_dimension=1, tiled=True
        ).astype(jnp.float32),
        lax.psum_scatter(
            sectioned(grad_gate_w).astype(jnp.bfloat16), WSH, scatter_dimension=1, tiled=True
        ).astype(jnp.float32),
        lax.psum_scatter(
            sectioned(grad_up_w).astype(jnp.bfloat16), WSH, scatter_dimension=1, tiled=True
        ).astype(jnp.float32),
        lax.psum_scatter(
            sectioned(grad_down_w).astype(jnp.bfloat16), WSH, scatter_dimension=1, tiled=True
        ).astype(jnp.float32),
        lax.psum_scatter(
            sectioned(grad_gain_self).astype(jnp.bfloat16), WSH, scatter_dimension=1, tiled=True
        ).astype(jnp.float32),
        lax.psum_scatter(
            sectioned(grad_gain_cross).astype(jnp.bfloat16), WSH, scatter_dimension=1, tiled=True
        ).astype(jnp.float32),
        lax.psum_scatter(
            sectioned(grad_gain_feed).astype(jnp.bfloat16), WSH, scatter_dimension=1, tiled=True
        ).astype(jnp.float32),
    )
    (
        core_q,
        core_k,
        core_v,
        core_o,
        core_cq,
        core_ck,
        core_cv,
        core_co,
        core_gate,
        core_up,
        core_down,
        core_gs,
        core_gc,
        core_gf,
    ) = core_parts
    owned = (
        lax.psum_scatter(core_q, CTX, scatter_dimension=0, tiled=True),
        lax.psum_scatter(core_k, CTX, scatter_dimension=0, tiled=True),
        lax.psum_scatter(core_v, CTX, scatter_dimension=0, tiled=True),
        lax.psum_scatter(core_o, CTX, scatter_dimension=0, tiled=True),
        lax.psum_scatter(core_cq, CTX, scatter_dimension=0, tiled=True),
        lax.psum_scatter(core_ck, CTX, scatter_dimension=0, tiled=True),
        lax.psum_scatter(core_cv, CTX, scatter_dimension=0, tiled=True),
        lax.psum_scatter(core_co, CTX, scatter_dimension=0, tiled=True),
        lax.psum_scatter(core_gate, CTX, scatter_dimension=0, tiled=True),
        lax.psum_scatter(core_up, CTX, scatter_dimension=0, tiled=True),
        lax.psum_scatter(core_down, CTX, scatter_dimension=0, tiled=True),
        lax.psum_scatter(core_gs, CTX, scatter_dimension=0, tiled=True),
        lax.psum_scatter(core_gc, CTX, scatter_dimension=0, tiled=True),
        lax.psum_scatter(core_gf, CTX, scatter_dimension=0, tiled=True),
    )
    (
        own_q,
        own_k,
        own_v,
        own_o,
        own_cq,
        own_ck,
        own_cv,
        own_co,
        own_gate,
        own_up,
        own_down,
        own_gain_self,
        own_gain_cross,
        own_gain_feed,
    ) = [piece.reshape(piece.shape[2:]) for piece in owned]
    summed = (
        lax.psum(own_q.astype(jnp.bfloat16), GRP).astype(jnp.float32),
        lax.psum(own_k.astype(jnp.bfloat16), GRP).astype(jnp.float32),
        lax.psum(own_v.astype(jnp.bfloat16), GRP).astype(jnp.float32),
        lax.psum(own_o.astype(jnp.bfloat16), GRP).astype(jnp.float32),
        lax.psum(own_cq.astype(jnp.bfloat16), GRP).astype(jnp.float32),
        lax.psum(own_ck.astype(jnp.bfloat16), GRP).astype(jnp.float32),
        lax.psum(own_cv.astype(jnp.bfloat16), GRP).astype(jnp.float32),
        lax.psum(own_co.astype(jnp.bfloat16), GRP).astype(jnp.float32),
        lax.psum(own_gate.astype(jnp.bfloat16), GRP).astype(jnp.float32),
        lax.psum(own_up.astype(jnp.bfloat16), GRP).astype(jnp.float32),
        lax.psum(own_down.astype(jnp.bfloat16), GRP).astype(jnp.float32),
        lax.psum(own_gain_self.astype(jnp.bfloat16), GRP).astype(jnp.float32),
        lax.psum(own_gain_cross.astype(jnp.bfloat16), GRP).astype(jnp.float32),
        lax.psum(own_gain_feed.astype(jnp.bfloat16), GRP).astype(jnp.float32),
    )
    grad_relative_bias = lax.psum(grad_bias_part.T, EVERY)
    return (
        layer_out,
        grad_input,
        grad_encoded,
        summed[0],
        summed[1],
        summed[2],
        summed[3],
        summed[4],
        summed[5],
        summed[6],
        summed[7],
        summed[8],
        summed[9],
        summed[10],
        summed[11],
        summed[12],
        summed[13],
        grad_relative_bias,
    )


BIG = 63 << 20
NT = (((1,), (1,)), ((), ()))
TN = (((0,), (0,)), ((), ()))
NN = (((1,), (0,)), ((), ()))
F32 = jnp.float32
BF16 = jnp.bfloat16
CH = 256
BLK = 64


def mm(left, right, dims):
    return lax.dot_general(left, right, dims, preferred_element_type=F32)


def load_in_order(deal, k_hbm, v_hbm, kvs, sem):
    blocks, inner = k_hbm.shape[0] // BLK, k_hbm.shape[1]

    def one(index, carry):
        here = pl.ds(index * BLK, BLK)
        rows = kvs.at[pl.ds(pl.multiple_of(deal[index // 2, index % 2] * BLK, BLK), BLK)]
        pltpu.make_async_copy(k_hbm.at[here], rows.at[:, pl.ds(0, inner)], sem.at[0]).start()
        pltpu.make_async_copy(v_hbm.at[here], rows.at[:, pl.ds(inner, inner)], sem.at[1]).start()
        return carry

    lax.fori_loop(0, blocks, one, 0)


def loaded(k_hbm, v_hbm, kvs, sem):
    inner = k_hbm.shape[1]
    pltpu.make_async_copy(k_hbm, kvs.at[:, pl.ds(0, inner)], sem.at[0]).wait()
    pltpu.make_async_copy(v_hbm, kvs.at[:, pl.ds(inner, inner)], sem.at[1]).wait()


def stack_pair(block, low_lanes):
    zero = jnp.zeros_like(block)
    return jnp.concatenate([jnp.where(low_lanes, block, zero), jnp.where(low_lanes, zero, block)], axis=0)


def pair_table(table_hb):
    heads = table_hb.shape[0]
    padded = jnp.pad(table_hb, ((0, 0), (0, BLK - BUCKETS)))
    return padded.reshape(heads // 2, 2 * BLK)

MESH = pl.DeviceIdType.MESH


class Place:
    def __init__(self, nz):
        self.nz = nz
        self.g = lax.axis_index(GRP)
        self.c = lax.axis_index(CTX)
        self.w = lax.axis_index(WSH)
        self.z = self.c // 2
        self.y = lax.rem(self.c, 2)
        self.me = self.c * 2 + self.w

    def at(self, g=None, z=None, y=None, w=None):
        z = self.z if z is None else z
        y = self.y if y is None else y
        return (self.g if g is None else g, z * 2 + y, self.w if w is None else w)

    def twin(self):
        return self.at(g=1 - self.g)

    def over(self):
        return self.at(y=1 - self.y)

    def mate(self):
        return self.at(w=1 - self.w)

    def up(self, dz):
        return lax.rem(self.z + dz, self.nz)

    def down(self, dz):
        return lax.rem(self.z + self.nz - dz, self.nz)

    def greet(self):
        partners = [self.twin(), self.over(), self.mate()]
        partners += [self.at(z=self.up(dz)) for dz in range(1, self.nz)]
        for partner in partners:
            pl.semaphore_signal(pltpu.get_barrier_semaphore(), inc=1, device_id=partner, device_id_type=MESH)
        self.greeted = len(partners)

    def met(self):
        pl.semaphore_wait(pltpu.get_barrier_semaphore(), self.greeted)


def push(src, dst, ssem, rsem, to):
    return pltpu.make_async_remote_copy(src, dst, ssem, rsem, device_id=to, device_id_type=MESH)


def half(wide, index):
    return pl.ds(pl.multiple_of(index * (wide // 2), 128), wide // 2)


class Gather:
    COUNT = 9

    def __init__(self, at, part, whole, sems, split, chunk=0, chunks=1):
        self.at, self.nz, self.part, self.whole, self.split = at, at.nz, part, whole, split
        (self.zs, self.zr, self.ys, self.yr, self.xs, self.xr, self.ws, self.wr, self.lc) = sems
        self.wide = whole.shape[-1] // chunks
        self.first = chunk * self.wide
        self.sent = []

    @staticmethod
    def scratch(nz, split):
        dma = pltpu.SemaphoreType.DMA
        x = 2 * nz if split else 1
        w = 4 * nz if split else 2 * nz
        return [dma((nz,))] * 4 + [dma((x,))] * 2 + [dma((w,))] * 2 + [dma((1,))]

    def cols(self, side=None):
        if self.split and side is not None:
            return pl.ds(pl.multiple_of(self.first + side * (self.wide // 2), 128), self.wide // 2)
        return pl.ds(self.first, self.wide)

    def spot(self, z, y, w, side=None):
        return self.whole.at[z, y, w, :, self.cols(side)]

    def post(self, view, ssem, rsem, to, source=None):
        copy = push(view if source is None else source, view, ssem, rsem, to)
        copy.start()
        self.sent.append(copy)

    def to_y(self, z):
        at = self.at
        self.post(self.spot(z, at.y, at.w, at.g), self.ys.at[z], self.yr.at[z], at.over())

    def to_x(self, z, y):
        at = self.at
        if self.split:
            k = z * 2 + y
            self.post(self.spot(z, y, at.w, at.g), self.xs.at[k], self.xr.at[k], at.twin())

    def w_sem(self, z, y, side):
        k = z * 2 + y
        return k * 2 + (0 if side is None else side) if self.split else k

    def to_w(self, z, y, side):
        at = self.at
        k = self.w_sem(z, y, side)
        self.post(self.spot(z, y, at.w, side), self.ws.at[k], self.wr.at[k], at.mate())

    def place(self):
        here = self.spot(self.at.z, self.at.y, self.at.w)
        self.local = pltpu.make_async_copy(self.part.at[:, self.cols()], here, self.lc.at[0])
        self.local.start()

    def send(self):
        at = self.at
        here, source = self.spot(at.z, at.y, at.w, at.g), self.part.at[:, self.cols(at.g)]
        for dz in range(1, self.nz):
            to = at.up(dz)
            self.post(here, self.zs.at[to], self.zr.at[at.z], at.at(z=to), source)
        self.post(here, self.ys.at[at.z], self.yr.at[at.z], at.over(), source)
        k = self.w_sem(at.z, at.y, None)
        self.post(self.spot(at.z, at.y, at.w), self.ws.at[k], self.wr.at[k], at.mate(), self.part.at[:, self.cols()])

    def after_z(self):
        at = self.at
        for dz in range(1, self.nz):
            z = at.down(dz)
            view = self.spot(z, at.y, at.w, at.g)
            push(view, view, self.zs.at[z], self.zr.at[z], at.at(z=z)).wait_recv()
            self.to_y(z)
            self.to_x(z, at.y)
            self.to_w(z, at.y, at.g)

    def after_y(self):
        at = self.at
        for dz in range(self.nz):
            z = at.down(dz)
            view = self.spot(z, 1 - at.y, at.w, at.g)
            push(view, view, self.ys.at[z], self.yr.at[z], at.over()).wait_recv()
            self.to_x(z, 1 - at.y)
            self.to_w(z, 1 - at.y, at.g)

    def others(self):
        for dy in range(2):
            for dz in range(self.nz):
                yield self.at.down(dz), lax.rem(self.at.y + dy, 2), dy == 0 and dz == 0

    def after_x(self):
        at = self.at
        if not self.split:
            return
        for z, y, own in self.others():
            if not own:
                k = z * 2 + y
                view = self.spot(z, y, at.w, 1 - at.g)
                push(view, view, self.xs.at[k], self.xr.at[k], at.twin()).wait_recv()
                self.to_w(z, y, 1 - at.g)

    def end(self):
        at = self.at
        self.local.wait()
        for z, y, own in self.others():
            for side in range(2 if self.split and not own else 1):
                k = self.w_sem(z, y, side)
                view = self.spot(z, y, 1 - at.w, None if own else side)
                push(view, view, self.ws.at[k], self.wr.at[k], at.mate()).wait_recv()

    def close(self):
        for copy in self.sent:
            copy.wait_send()


class Reduce:
    COUNT = 16

    @staticmethod
    def scratch(nz, r, wide, kind, dtype, part=True):
        cols = wide // 2 if kind == "x" else wide
        dma = pltpu.SemaphoreType.DMA
        vmem = pltpu.VMEM
        none = vmem((1, 16, 128), dtype)
        return [
            vmem((nz, 2, 2, r, wide), dtype) if part else none,
            vmem((nz, 2, r, wide), dtype),
            vmem((nz, 2, r, cols), dtype) if kind == "x" else none,
            vmem((nz, r, cols), dtype),
            vmem((nz, r, cols), dtype),
            vmem((2, r, cols), dtype) if kind != "none" else none,
        ] + [dma((1,))] * 6 + [dma((nz,))] * 2 + [dma((1,))] * 2

    def __init__(self, at, out, refs, kind):
        self.at, self.nz, self.out, self.kind = at, at.nz, out, kind
        self.part_cols = None
        (self.part, self.wb, self.xb, self.yb, self.zb, self.fb) = refs[:6]
        (self.ws, self.wr, self.xs, self.xr, self.ys, self.yr, self.zs, self.zr, self.fs, self.fr) = refs[6:]
        self.wide = self.wb.shape[-1]
        self.local_part = None

    def c_w(self):
        at = self.at
        src = self.part.at[:, :, 1 - at.w]
        if self.part_cols is not None:
            src = self.part.at[:, :, 1 - at.w, :, self.part_cols]
        return push(src, self.wb, self.ws.at[0], self.wr.at[0], at.mate())

    def c_x(self):
        at = self.at
        src = self.wb.at[:, :, :, half(self.wide, 1 - at.g)]
        return push(src, self.xb, self.xs.at[0], self.xr.at[0], at.twin())

    def mid(self):
        return self.xb if self.kind == "x" else self.wb

    def c_y(self):
        at = self.at
        return push(self.mid().at[:, 1 - at.y], self.yb, self.ys.at[0], self.yr.at[0], at.over())

    def c_z(self, to):
        at = self.at
        return push(self.yb.at[to], self.zb.at[at.z], self.zs.at[to], self.zr.at[at.z], at.at(z=to))

    def c_zin(self, z):
        return push(self.yb.at[z], self.zb.at[z], self.zs.at[z], self.zr.at[z], self.at.at(z=z))

    def c_f(self):
        return push(self.fb.at[0], self.fb.at[1], self.fs.at[0], self.fr.at[0], self.at.twin())

    def send(self):
        self.c_w().start()

    def after_w(self):
        at = self.at
        self.c_w().wait_recv()

        def one(k, carry):
            z, y = k // 2, lax.rem(k, 2)
            here = self.part[z, y, at.w] if self.local_part is None else self.local_part[z, y, :, self.local_cols]
            self.wb[z, y] = (self.wb[z, y].astype(F32) + here.astype(F32)).astype(self.wb.dtype)
            return carry

        lax.fori_loop(0, 2 * self.nz, one, 0)
        if self.kind == "x":
            self.c_x().start()
        else:
            self.c_y().start()

    def after_x(self):
        if self.kind != "x":
            return
        self.c_x().wait_recv()

        def one(k, carry):
            z, y = k // 2, lax.rem(k, 2)
            total = self.xb[z, y].astype(F32) + self.wb[z, y, :, half(self.wide, self.at.g)].astype(F32)
            self.xb[z, y] = total.astype(self.xb.dtype)
            return carry

        lax.fori_loop(0, 2 * self.nz, one, 0)
        self.c_y().start()

    def after_y(self):
        at, nz = self.at, self.nz
        self.c_y().wait_recv()

        def one(z, carry):
            total = self.yb[z].astype(F32) + self.mid()[z, at.y].astype(F32)
            self.yb[z] = total.astype(self.yb.dtype)
            return carry

        lax.fori_loop(0, nz, one, 0)
        for dz in range(1, nz):
            self.c_z(at.up(dz)).start()

    def after_z(self):
        at, nz = self.at, self.nz
        for dz in range(1, nz):
            self.c_zin(at.up(dz)).wait_recv()
        total = self.yb[at.z].astype(F32)
        for dz in range(1, nz):
            total = total + self.zb[at.up(dz)].astype(F32)
        if self.kind == "x":
            self.out[:, half(self.wide, at.g)] = total
        else:
            self.out[...] = total
        if self.kind != "none":
            self.fb[0] = total.astype(self.fb.dtype)
            self.c_f().start()

    def end(self):
        at = self.at
        if self.kind != "none":
            self.c_f().wait_recv()
            other = self.fb[1].astype(F32)
            if self.kind == "x":
                self.out[:, half(self.wide, 1 - at.g)] = other
            else:
                self.out[...] = self.out[...] + other

    def close(self):
        at, nz = self.at, self.nz
        self.c_w().wait_send()
        if self.kind == "x":
            self.c_x().wait_send()
        self.c_y().wait_send()
        for dz in range(1, nz):
            self.c_z(at.up(dz)).wait_send()
        if self.kind != "none":
            self.c_f().wait_send()


class Total:
    COUNT = 3

    @staticmethod
    def scratch(nz, r, wide):
        dma = pltpu.SemaphoreType.DMA
        return [pltpu.VMEM((4 + nz, r, wide), F32), dma((4 + nz,)), dma((4 + nz,))]

    def __init__(self, at, refs):
        self.at, self.nz = at, at.nz
        self.buf, self.ss, self.rs = refs

    def hop(self, i):
        at = self.at
        to = (at.mate(), at.twin(), at.over())[i]
        return push(self.buf.at[0], self.buf.at[1 + i], self.ss.at[i], self.rs.at[i], to)

    def send(self):
        self.hop(0).start()

    def after(self, i):
        hop = self.hop(i)
        hop.wait_send()
        hop.wait_recv()
        self.buf[0] = self.buf[0] + self.buf[1 + i]
        if i < 2:
            self.hop(i + 1).start()
        else:
            for dz in range(1, self.nz):
                self.along(self.at.z, self.at.up(dz)).start()

    def along(self, source, to):
        base = 4
        return push(self.buf.at[0], self.buf.at[base + source], self.ss.at[base + to], self.rs.at[base + source], self.at.at(z=to))

    def end(self):
        total = None
        for dz in range(1, self.nz):
            z = self.at.up(dz)
            self.along(z, z).wait_recv()
            self.along(self.at.z, z).wait_send()
        self.buf[4 + self.at.z] = self.buf[0]
        total = self.buf[4]
        for z in range(1, self.nz):
            total = total + self.buf[4 + z]
        return total


def normed(hidden, gain):
    return hidden * lax.rsqrt(jnp.mean(hidden * hidden, axis=-1, keepdims=True) + EPSILON) * gain


def norm_back(hidden, gain, grad):
    scale = lax.rsqrt(jnp.mean(hidden * hidden, axis=-1, keepdims=True) + EPSILON)
    inner = jnp.mean(hidden * gain * grad, axis=-1, keepdims=True)
    rows = scale * gain * grad - hidden * (scale * scale * scale) * inner
    return rows, jnp.sum(grad * hidden * scale, axis=0, keepdims=True)


FRONT_PARTS = ("small", "k", "v", "q", "o", "cq", "ck", "cv", "co", "gate", "up", "down", "keys", "values")
FRONT_PLAN = (
    ("small", "keys", "values",),
    dict(gate=2, up=2, down=3, keys=3, values=3),
    (
        ("down", 0), ("up", 0), ("values", 2), ("values", 0), ("keys", 2), ("k", 0), ("values", 1), ("down", 1),
        ("cq", 0), ("down", 2), ("gate", 1), ("keys", 0), ("small", 0), ("cv", 0), ("v", 0), ("co", 0), ("up", 1),
        ("q", 0), ("o", 0), ("gate", 0), ("keys", 1), ("ck", 0),
    ),
    (
        (0, 0), (1, 0), (5, 0), (0, 1), (7, 0), (0, 2), (1, 1), (8, 0), (0, 3), (5, 1), (9, 0), (1, 2), (7, 1),
        (10, 0), (5, 2), (8, 1), (12, 0), (7, 2), (9, 1), (1, 3), (13, 0), (8, 2), (10, 1), (14, 0), (9, 2), (5, 3),
        (12, 1), (15, 0), (10, 2), (13, 1), (16, 0), (7, 3), (12, 2), (14, 1), (17, 0), (12, 4), (5, 4), (8, 3),
        (13, 2), (14, 2), (15, 1), (4, 0), (11, 0), (16, 1), (9, 3), (15, 2), (17, 1), (18, 0), (10, 3), (4, 1),
        (16, 2), (19, 0), (20, 0), (17, 2), (13, 3), (11, 1), (4, 2), (14, 3), (18, 1), (21, 0), (14, 4), (2, 0),
        (19, 1), (3, 0), (6, 0), (11, 2), (18, 2), (15, 3), (20, 1), (21, 1), (19, 2), (16, 3), (17, 3), (2, 1),
        (17, 4), (20, 2), (21, 2), (3, 1), (18, 3), (2, 2), (6, 1), (3, 2), (19, 3), (6, 2), (21, 3), (0, 4), (1, 4),
        (2, 4), (3, 4), (4, 4), (6, 4), (7, 4), (8, 4), (9, 4), (10, 4), (11, 4), (13, 4), (15, 4), (16, 4), (18, 4),
        (19, 4), (20, 4), (21, 4),
    ),
)


def front_kernel(nz, unshared, chunked, order, steps, *refs):
    count = len(FRONT_PARTS)
    x_ref, ins, wholes, refs = refs[0], refs[1 : count - 1], refs[count - 1 : 2 * count - 1], refs[2 * count - 1 :]
    (q_ref, normed_ref, gains_ref), (wbuf, k_own, v_own, wsem), sems = refs[:3], refs[3:7], refs[7:]
    parts = dict(zip(FRONT_PARTS, tuple(ins) + (k_own, v_own)))
    wholes = dict(zip(FRONT_PARTS, wholes))
    at = Place(nz)
    at.greet()
    jobs = []
    for i, (name, chunk) in enumerate(order):
        mine = sems[Gather.COUNT * i : Gather.COUNT * (i + 1)]
        chunks = chunked.get(name, 1)
        job = Gather(at, parts[name], wholes[name], mine, name not in unshared, chunk, chunks)
        jobs.append(job)
        if name not in ("keys", "values"):
            job.place()
    at.met()
    width = x_ref.shape[1]

    def norm():
        every = wholes["small"]
        total = None
        for z in range(nz):
            for y in range(2):
                for w in range(2):
                    here = every[z, y, w].astype(F32)
                    total = here if total is None else total + here
        gains_ref[...] = total
        normed_ref[...] = normed(x_ref[...].astype(F32), total[4:5]).astype(BF16)

    def project(name, index, into):
        load = pltpu.make_async_copy(wholes[name], wbuf.at[index], wsem.at[index])
        load.start()
        load.wait()
        into[...] = mm(normed_ref[...], wbuf[index].reshape(width, -1), NN).astype(BF16)

    def place(name):
        for entry, job in zip(order, jobs):
            if entry[0] == name:
                job.place()

    def follow(name):
        if name == "small":
            norm()
        elif name == "k":
            project(name, 0, k_own)
            place("keys")
        elif name == "v":
            project(name, 1, v_own)
            place("values")
        elif name == "q":
            project(name, 2, q_ref)

    stages = (Gather.send, Gather.after_z, Gather.after_y, Gather.after_x, Gather.end)
    for i, stage in steps:
        stages[stage](jobs[i])
        if stage == len(stages) - 1:
            follow(order[i][0])
    for job in jobs:
        job.close()


def front(x, parts, nz, shards, collective_id=1, plan=FRONT_PLAN):
    hb = pl.BlockSpec(memory_space=pl.ANY)
    vm = pl.BlockSpec(memory_space=pltpu.VMEM)
    unshared, chunked, order, steps = plan
    rows, width = x.shape
    inner = parts[1].shape[1]
    shapes = [(nz, 2, 2) + part.shape for part in parts] + [(nz, 2, 2, rows, inner)] * 2
    scratch = [
        pltpu.VMEM((3,) + shapes[1], BF16), pltpu.VMEM((rows, inner), BF16), pltpu.VMEM((rows, inner), BF16),
        pltpu.SemaphoreType.DMA((3,)),
    ]
    for name, _ in order:
        scratch += Gather.scratch(nz, name not in unshared)
    return pl.pallas_call(
        functools.partial(front_kernel, nz, unshared, chunked, order, steps),
        name="front",
        out_shape=tuple([jax.ShapeDtypeStruct(s, BF16) for s in shapes])
        + (
            jax.ShapeDtypeStruct((rows, inner), BF16),
            jax.ShapeDtypeStruct((rows, width), BF16),
            jax.ShapeDtypeStruct(parts[0].shape, F32),
        ),
        in_specs=[vm] + [hb] * len(parts),
        out_specs=tuple([vm] + [hb] * (len(FRONT_PARTS) - 1) + [vm] * 3),
        scratch_shapes=scratch,
        compiler_params=pltpu.CompilerParams(
            collective_id=collective_id, has_side_effects=True, vmem_limit_bytes=BIG
        ),
    )(x, *parts)


BACK_OUT = ("gate", "up", "down", "co", "cq", "ck", "cv", "q", "o", "k", "v")
BACK_NONE = ("kv", "cross")
BACK_PLAN = (
    ("co", "v",),
    dict(kv=3, gate=2, up=2),
    (
        ("cross", 0), ("o", 0), ("co", 0), ("q", 0), ("kv", 0), ("ck", 0), ("cq", 0), ("down", 0), ("up", 0),
        ("kv", 2), ("v", 0), ("up", 1), ("kv", 1), ("cv", 0), ("k", 0), ("gate", 1), ("gate", 0),
    ),
    (
        (0, 0), (1, 0), (2, 0), (3, 0), (0, 1), (4, 0), (1, 1), (6, 0), (2, 1), (7, 0), (0, 3), (3, 1), (8, 0),
        (4, 1), (1, 2), (9, 0), (6, 1), (11, 0), (0, 4), (0, 5), (2, 3), (3, 2), (7, 1), (5, 0), (8, 1), (12, 0),
        (6, 2), (4, 3), (2, 4), (9, 1), (13, 0), (1, 3), (11, 1), (15, 0), (3, 3), (5, 1), (16, 0), (12, 1), (6, 3),
        (13, 1), (4, 4), (4, 5), (15, 1), (7, 2), (1, 4), (16, 1), (3, 4), (9, 3), (6, 4), (8, 2), (12, 3), (11, 2),
        (9, 4), (9, 5), (5, 2), (7, 3), (8, 3), (12, 4), (12, 5), (11, 3), (13, 2), (10, 0), (14, 0), (5, 3), (7, 4),
        (15, 2), (13, 3), (10, 1), (14, 1), (8, 4), (15, 3), (11, 4), (16, 2), (5, 4), (10, 3), (13, 4), (16, 3),
        (15, 4), (14, 2), (10, 4), (14, 3), (1, 5), (2, 5), (3, 5), (5, 5), (6, 5), (7, 5), (8, 5), (11, 5), (13, 5),
        (15, 5), (10, 5), (16, 4), (14, 4), (16, 5), (14, 5),
    ),
)


def back_kind(name, late):
    return "none" if name in BACK_NONE else "late" if name in late else "x"


def back_kernel(nz, late, chunked, order, steps, *refs):
    (
        kvp, crossp, wq, wk, wv, wck, wcv, x_ref, gains_ref, gh_ref, gpart_ref, enc_ref,
        n3, mixed, att, n2, attc, n1, gg, gu, go, g1, gcq, g2, dq,
    ) = refs[:25]
    refs = refs[25:]
    outs = dict(zip(BACK_OUT, refs[: len(BACK_OUT)]))
    gx_ref, genc_ref, total_ref = refs[len(BACK_OUT) : len(BACK_OUT) + 3]
    refs = refs[len(BACK_OUT) + 3 :]
    kvown, crown, low, wbuf, kvl, kls, wsem = refs[:7]
    refs = refs[7:]
    outs["kv"], outs["cross"] = kvown, crown
    at = Place(nz)
    at.greet()
    jobs = []
    for i, (name, chunk) in enumerate(order):
        mine = list(refs[Reduce.COUNT * i : Reduce.COUNT * (i + 1)])
        chunks = chunked.get(name, 1)
        out = outs[name]
        if chunks > 1:
            wide = out.shape[-1] // chunks
            out = out.at[:, pl.ds(chunk * wide, wide)]
        job = Reduce(at, out, mine, back_kind(name, late))
        if name == "cross":
            job.part = crossp
        if name == "kv":
            job.part = kvp
            job.part_cols = pl.ds(chunk * wide, wide)
            job.local_part, job.local_cols = kvl, job.part_cols
        jobs.append(job)
    everyone = Total(at, refs[Reduce.COUNT * len(order) :])
    load_w = [pltpu.make_async_copy(src, wbuf.at[i], wsem.at[i]) for i, src in enumerate((wq, wk, wv))]
    load_c = [pltpu.make_async_copy(src, wbuf.at[3 + i], wsem.at[3 + i]) for i, src in enumerate((wck, wcv))]
    for copy in load_w + load_c:
        copy.start()
    kv_local = pltpu.make_async_copy(kvp.at[:, :, at.w], kvl, kls)
    kv_local.start()
    width = x_ref.shape[1]
    inner = dq.shape[1]

    def make(name, chunk, part):
        if name in BACK_NONE:
            return
        _, _, _, r, wide = part.shape
        if name in ("ck", "cv"):
            left, right = enc_ref, low.at[:, pl.ds(0 if name == "ck" else inner, inner)]
        elif name in ("k", "v"):
            left, right = n1, kvl.at[0, 0, :, pl.ds(0 if name == "k" else inner, inner)]
        else:
            left, right = {
                "gate": (n3, gg), "up": (n3, gu), "down": (mixed, go), "o": (att, g1), "cq": (n2, gcq), "co": (attc, g2),
                "q": (n1, dq),
            }[name]
        take = 2 if r % 128 else 1
        tile = 512 if wide % 512 == 0 else wide // 2 if wide % 256 == 0 and wide > 256 else wide
        for first in range(0, nz, take):
            piece = left[:, first * 4 * r : (first + take) * 4 * r]
            for c in range(0, wide, tile):
                out = mm(piece, right[:, chunk * wide + c : chunk * wide + c + tile], TN).astype(BF16)
                part[first : first + take, :, :, :, c : c + tile] = out.reshape(take, 2, 2, r, tile)

    def after_cross():
        both = crown[...]
        low[...] = jnp.concatenate([both, jnp.zeros_like(both)], axis=0).astype(BF16)
        for copy in load_c:
            copy.wait()
        genc = mm(low[:, :inner], wbuf[3].reshape(width, inner), NT) + mm(low[:, inner:], wbuf[4].reshape(width, inner), NT)
        genc_ref[...] = genc[:8]

    def after_kv():
        kvl[0, 0] = kvown[...].astype(BF16)
        for copy in load_w:
            copy.wait()
        grad = mm(dq[...], wbuf[0].reshape(width, inner), NT)
        grad = grad + mm(kvl[0, 0, :, :inner], wbuf[1].reshape(width, inner), NT)
        grad = grad + mm(kvl[0, 0, :, inner:], wbuf[2].reshape(width, inner), NT)
        rows, gain = norm_back(x_ref[...].astype(F32), gains_ref[4:5], grad)
        gx_ref[...] = gh_ref[...] + rows
        everyone.buf[0] = gpart_ref[...]
        everyone.buf[0, 0:1, :] = gain
        everyone.send()

    kv_jobs = [i for i, entry in enumerate(order) if entry[0] == "kv"]
    kv_seen = kv_ended = 0
    early = [i for i, stage in steps if stage == 0 and order[i][0] not in BACK_NONE + ("ck", "cv", "k", "v")][:2]
    for i in early:
        make(*order[i], jobs[i].part)
    at.met()
    hops = []
    for count, (i, stage) in enumerate(steps):
        (name, chunk), job = order[i], jobs[i]
        if stage == 0:
            if i not in early:
                make(name, chunk, job.part)
            job.send()
        if stage == 1:
            if i in kv_jobs:
                kv_seen += 1
                if kv_seen == 1:
                    kv_local.wait()
            job.after_w()
        if stage == 2:
            job.after_x()
        if stage == 3:
            job.after_y()
        if stage == 4:
            job.after_z()
        if stage == 5:
            job.end()
            if name == "cross":
                after_cross()
            if i in kv_jobs:
                kv_ended += 1
                if kv_ended == len(kv_jobs):
                    after_kv()
                    hops = [count + 4, count + 8, count + 12]
        if count in hops:
            everyone.after(hops.index(count))
    for i, count in enumerate(hops):
        if count >= len(steps):
            everyone.after(i)
    total_ref[...] = everyone.end()
    for job in jobs:
        job.close()


def back_step(
    kv_part, cross_part, weights, x, gains, grad_hidden, gpart, enc, acts, shapes, nz, collective_id=2,
    plan=BACK_PLAN,
):
    late, chunked, order, steps = plan
    hb = pl.BlockSpec(memory_space=pl.ANY)
    vm = pl.BlockSpec(memory_space=pltpu.VMEM)
    rows, width = x.shape
    inner = acts[-1].shape[1]
    dma = pltpu.SemaphoreType.DMA
    own = [jax.ShapeDtypeStruct(shapes[name], F32) for name in BACK_OUT]
    scratch = [
        pltpu.VMEM((rows, 2 * inner), F32),
        pltpu.VMEM((8, 2 * inner), F32),
        pltpu.VMEM((16, 2 * inner), BF16),
        pltpu.VMEM((5,) + weights[0].shape, BF16),
        pltpu.VMEM((nz, 2, rows, 2 * inner), BF16),
        dma,
        dma((5,)),
    ]
    shapes = dict(shapes, kv=(rows, 2 * inner), cross=(8, 2 * inner))
    for name, _ in order:
        r, wide = shapes[name]
        wide = wide // chunked.get(name, 1)
        held = name not in BACK_NONE
        scratch += Reduce.scratch(nz, r, wide, back_kind(name, late), F32 if name == "cross" else BF16, part=held)
    scratch += Total.scratch(nz, gpart.shape[0], width)
    return pl.pallas_call(
        functools.partial(back_kernel, nz, late, chunked, order, steps),
        name="back",
        out_shape=tuple(own)
        + (
            jax.ShapeDtypeStruct((rows, width), F32),
            jax.ShapeDtypeStruct((8, width), F32),
            jax.ShapeDtypeStruct(gpart.shape, F32),
        ),
        in_specs=[hb, vm] + [hb] * 5 + [vm] * (5 + len(acts)),
        out_specs=tuple([vm] * (len(own) + 3)),
        scratch_shapes=scratch,
        compiler_params=pltpu.CompilerParams(
            collective_id=collective_id, has_side_effects=True, vmem_limit_bytes=BIG
        ),
    )(kv_part, cross_part, *weights, x, gains, grad_hidden, gpart, enc, *acts)


def closing_kernel(count, *refs):
    for source, target in zip(refs[:count], refs[count:]):
        target[...] = source[...]


def closing(arrays):
    vm = pl.BlockSpec(memory_space=pltpu.VMEM)
    count = len(arrays)
    return pl.pallas_call(
        functools.partial(closing_kernel, count),
        name="closing",
        out_shape=tuple(jax.ShapeDtypeStruct(a.shape, a.dtype) for a in arrays),
        in_specs=[vm] * count,
        out_specs=tuple([vm] * count),
    )(*arrays)


class Bag:
    def __init__(self, names, refs):
        for name, ref in zip(names, refs):
            setattr(self, name, ref)


def flat(ref):
    value = ref[...]
    return value.reshape(-1, value.shape[-1])


def unstack(pair_rows, low):
    rows = pair_rows.shape[0] // 2
    return jnp.where(low, pair_rows[:rows], pair_rows[rows:])


def every_encoded(small_ref, take):
    devices, block, width = small_ref.shape
    rows = devices * take
    row = lax.broadcasted_iota(jnp.int32, (rows, devices * block), 0)
    col = lax.broadcasted_iota(jnp.int32, (rows, devices * block), 1)
    pick = (col == (row // take) * block + lax.rem(row, take)).astype(BF16)
    return mm(pick, small_ref[...].reshape(devices * block, width), NN).astype(BF16)


def cross_forward(b, low):
    pairs = b.cq.shape[1] // 128
    for pair in range(pairs):
        lanes = slice(128 * pair, 128 * pair + 128)
        qm = stack_pair(b.cq[:, lanes], low)
        s = mm(qm, b.ckeys[:, lanes], NT)
        peak = jnp.max(s, axis=1, keepdims=True)
        log_total = peak + jnp.log(jnp.sum(jnp.exp(s - peak), axis=1, keepdims=True))
        p = jnp.exp(s - log_total)
        b.cprob[pair] = p
        b.attc[:, lanes] = unstack(mm(p.astype(BF16), b.cvals[:, lanes], NN), low).astype(BF16)


def cross_backward(b, gac, low, keys_each):
    pairs = b.cq.shape[1] // 128
    inner = b.cq.shape[1]
    owners = 4 * b.crossp.shape[0]
    b.crossp[...] = jnp.zeros_like(b.crossp)
    for pair in range(pairs):
        lanes = slice(128 * pair, 128 * pair + 128)
        qm = stack_pair(b.cq[:, lanes], low)
        dom = stack_pair(gac[:, lanes], low)
        p = b.cprob[pair]
        dp = mm(dom, b.cvals[:, lanes], NT)
        ds = (p * (dp - jnp.sum(p * dp, axis=1, keepdims=True))).astype(BF16)
        b.gcq[:, lanes] = unstack(mm(ds, b.ckeys[:, lanes], NN), low).astype(BF16)
        gk = mm(ds, qm, TN)
        gv = mm(p.astype(BF16), dom, TN)
        for owner in range(owners):
            rows = slice(keys_each * owner, keys_each * owner + keys_each)
            b.crossp[owner // 4, owner // 2 % 2, owner % 2, 0:keys_each, lanes] = gk[rows]
            b.crossp[owner // 4, owner // 2 % 2, owner % 2, 0:keys_each, 128 * pair + inner : 128 * pair + inner + 128] = gv[rows]


GELU_A = 0.7978845608028654
GELU_B = 0.044715


def gelu_parts(v):
    t = jnp.tanh(GELU_A * (v + GELU_B * v * v * v))
    value = 0.5 * v * (1.0 + t)
    slope = 0.5 * (1.0 + t) + 0.5 * v * (1.0 - t * t) * (GELU_A * (1.0 + 3.0 * GELU_B * v * v))
    return value, slope


FF_TILE = 512


def after_attention(b, low):
    b.h1[...] = b.x[...].astype(F32) + mm(b.att[...], flat(b.w_o), NN)
    b.n2[...] = normed(b.h1[...], b.gains[5:6]).astype(BF16)
    b.cq[...] = mm(b.n2[...], flat(b.w_cq), NN).astype(BF16)


def after_cross_attention(b):
    b.h2[...] = b.h1[...] + mm(b.attc[...], flat(b.w_co), NN)
    b.n3[...] = normed(b.h2[...], b.gains[6:7]).astype(BF16)


def feed_forward(b):
    ff = b.mixed.shape[1]
    width = b.x.shape[1]
    for c in range(0, ff, FF_TILE):
        cols = slice(c, c + FF_TILE)
        gate = mm(b.n3[...], b.w_gate[:, :, cols].reshape(width, FF_TILE), NN)
        up = mm(b.n3[...], b.w_up[:, :, cols].reshape(width, FF_TILE), NN)
        value, slope = gelu_parts(gate)
        b.mixed[:, cols] = (value * up).astype(BF16)
        b.hg[:, cols] = value
        b.hs[:, cols] = slope * up
    b.layer_out[...] = (b.h2[...] + mm(b.mixed[...], flat(b.w_down), NN)).astype(BF16)


def feed_backward(b):
    ff = b.mixed.shape[1]
    width = b.x.shape[1]
    down = flat(b.w_down)
    total = jnp.zeros(b.h2.shape, F32)
    for c in range(0, ff, FF_TILE):
        cols = slice(c, c + FF_TILE)
        gm = mm(b.go[...], down[cols], NT).astype(BF16).astype(F32)
        gg = (gm * b.hs[:, cols]).astype(BF16)
        gu = (gm * b.hg[:, cols]).astype(BF16)
        b.gg[:, cols] = gg
        b.gu[:, cols] = gu
        total = total + mm(gg, b.w_gate[:, :, cols].reshape(width, FF_TILE), NT)
        total = total + mm(gu, b.w_up[:, :, cols].reshape(width, FF_TILE), NT)
    rows, gain = norm_back(b.h2[...], b.gains[6:7], total)
    b.gpart[2:3, :] = gain
    b.gh[...] = b.go[...].astype(F32) + rows
    b.g2[...] = b.gh[...].astype(BF16)


def before_attention(b):
    rows, gain = norm_back(b.h1[...], b.gains[5:6], mm(b.gcq[...], flat(b.w_cq), NT))
    b.gpart[1:2, :] = gain
    b.gh[...] = b.gh[...] + rows
    b.g1[...] = b.gh[...].astype(BF16)
    b.gatt[...] = mm(b.g1[...], flat(b.w_o), NT).astype(BF16)


def fill_bias(b, qb, rank):
    pairs = b.q.shape[1] // 128
    key_j = lax.broadcasted_iota(jnp.int32, (CH, 128), 0)
    lane_i = lax.broadcasted_iota(jnp.int32, (CH, 128), 1)
    high = lane_i >= BLK
    row_i = jnp.where(high, lane_i - BLK, lane_i)
    shift = jnp.where(high, BLK, 0)
    for kind in range(2):
        dist = (lax.rem(rank, 4) + 4 * kind) * BLK + row_i - key_j
        bucket = bucket_ids(jnp.maximum(dist, 0)) + shift
        for pair in range(pairs):
            tile = jnp.take_along_axis(jnp.broadcast_to(b.tb[pl.ds(pair, 1), :], (CH, 128)), bucket, axis=1)
            if kind == 0:
                tile = jnp.where(dist >= 0, tile, MASKED)
            b.bias[qb, kind, pair] = tile
    for pair in range(pairs):
        b.bias[qb, 2, pair] = jnp.where(
            high,
            b.tb[pl.ds(pair, 1), pl.ds(BLK + BUCKETS - 1, 1)],
            b.tb[pl.ds(pair, 1), pl.ds(BUCKETS - 1, 1)],
        )


def self_forward_block(b, qb, rank, low):
    pairs = b.q.shape[1] // 128
    inner = b.q.shape[1]
    last = rank // 4
    mine = pl.ds(qb * BLK, BLK)
    for pair in range(pairs):
        b.qm[qb, pair] = stack_pair(b.q[mine, 128 * pair : 128 * pair + 128], low)
        b.top[pair] = jnp.full((8, 128), -3e38, F32)
        b.sums[pair] = jnp.zeros((8, 128), F32)
        b.acc[pair] = jnp.zeros((2 * BLK, 128), F32)

    def first(chunk, carry):
        kind = jnp.minimum(last - chunk, 2)
        keys = pl.ds(pl.multiple_of(chunk * CH, CH), CH)
        for pair in range(pairs):
            s = mm(b.kvs[keys, 128 * pair : 128 * pair + 128], b.qm[qb, pair], NT) + b.bias[qb, kind, pair]
            b.sco[pair, keys, :] = s
            b.top[pair] = jnp.maximum(b.top[pair], jnp.max(s.reshape(CH // 8, 8, 128), axis=0))
        return carry

    lax.fori_loop(0, last + 1, first, 0)
    for pair in range(pairs):
        b.top[pair] = jnp.broadcast_to(jnp.max(b.top[pair], axis=0, keepdims=True), (8, 128))

    def second(chunk, carry):
        keys = pl.ds(pl.multiple_of(chunk * CH, CH), CH)
        for pair in range(pairs):
            p = jnp.exp(b.sco[pair, keys, :] - b.top[pair, 0:1, :])
            b.sums[pair] += jnp.sum(p.reshape(CH // 8, 8, 128), axis=0)
            values = b.kvs[keys, inner + 128 * pair : inner + 128 * pair + 128]
            b.acc[pair] += mm(p.astype(BF16), values, TN)
        return carry

    lax.fori_loop(0, last + 1, second, 0)
    for pair in range(pairs):
        total = jnp.sum(b.sums[pair], axis=0, keepdims=True)
        b.rows[qb, pair, 0:1, :] = b.top[pair, 0:1, :] + jnp.log(total)
        scale = jnp.broadcast_to(total, (128, 128)).T
        out = unstack(b.acc[pair] / scale, low)
        b.att32[mine, 128 * pair : 128 * pair + 128] = out
        b.att[mine, 128 * pair : 128 * pair + 128] = out.astype(BF16)


def self_backward_rows(b, qb, low):
    pairs = b.q.shape[1] // 128
    mine = pl.ds(qb * BLK, BLK)
    for pair in range(pairs):
        lanes = slice(128 * pair, 128 * pair + 128)
        grad = b.gatt[mine, lanes]
        b.dom[qb, pair] = stack_pair(grad, low)
        prod = (grad.astype(F32) * b.att32[mine, lanes]).T
        b.rows[qb, pair, 1:2, :] = jnp.concatenate(
            [jnp.sum(prod[:BLK], axis=0, keepdims=True), jnp.sum(prod[BLK:], axis=0, keepdims=True)], axis=1
        )


def self_backward_block(b, qb, rank, low):
    pairs = b.q.shape[1] // 128
    inner = b.q.shape[1]
    last = rank // 4
    b.acc[...] = jnp.zeros_like(b.acc)

    @pl.when(last == 0)
    def _():
        for pair in range(pairs):
            b.near[pair, pl.ds(0, CH), :] = jnp.zeros((CH, 128), F32)

    def step(chunk, carry):
        kind = jnp.minimum(last - chunk, 2)
        keys = pl.ds(pl.multiple_of(chunk * CH, CH), CH)
        keep = jnp.maximum(chunk - last + 1, 0)
        for pair in range(pairs):
            klanes = slice(128 * pair, 128 * pair + 128)
            vlanes = slice(inner + 128 * pair, inner + 128 * pair + 128)
            kp = b.kvs[keys, klanes]
            qp = b.qm[qb, pair]
            gp = b.dom[qb, pair]
            st = mm(kp, qp, NT) + b.bias[qb, kind, pair]
            pt = jnp.exp(st - b.rows[qb, pair, 0:1, :])
            dp = mm(b.kvs[keys, vlanes], gp, NT)
            ds = pt * (dp - b.rows[qb, pair, 1:2, :])
            dsb = ds.astype(BF16)
            b.dkv[keys, vlanes] += mm(pt.astype(BF16), gp, NN)
            b.dkv[keys, klanes] += mm(dsb, qp, NN)
            b.acc[pair] += mm(dsb, kp, TN)
            b.tot[pair] += jnp.sum(ds.reshape(CH // 8, 8, 128), axis=0)
            b.near[pair, pl.ds(pl.multiple_of(keep * CH, CH), CH), :] = ds
        return carry

    lax.fori_loop(0, last + 1, step, 0)
    for pair in range(pairs):
        b.dq[pl.ds(qb * BLK, BLK), 128 * pair : 128 * pair + 128] = unstack(b.acc[pair], low).astype(BF16)
        for gap in range(3):
            offset = pl.multiple_of((rank - gap - 4 * (last - 1)) * BLK, BLK)
            b.nacc[gap, pair] += b.near[pair, pl.ds(offset, BLK), :]


def bias_gradient(b, low):
    pairs = b.q.shape[1] // 128
    key_s = lax.broadcasted_iota(jnp.int32, (BLK, 128), 0)
    lane = lax.broadcasted_iota(jnp.int32, (BLK, 128), 1)
    row_s = jnp.where(low, lane, lane - BLK)
    buckets = [bucket_ids(jnp.maximum(gap * BLK + row_s - key_s, 0)) for gap in range(3)]
    for pair in range(pairs):
        far = jnp.sum(b.tot[pair], axis=0, keepdims=True)
        for gap in range(3):
            far = far - jnp.sum(b.nacc[gap, pair], axis=0, keepdims=True)
        lines = []
        for number in range(BUCKETS):
            part = jnp.where(buckets[0] == number, b.nacc[0, pair], 0.0)
            for gap in range(1, 3):
                part = part + jnp.where(buckets[gap] == number, b.nacc[gap, pair], 0.0)
            line = jnp.sum(part, axis=0, keepdims=True)
            lines.append(line + far if number == BUCKETS - 1 else line)
        grid = jnp.concatenate(lines + [jnp.zeros((128 - BUCKETS, 128), F32)], axis=0).T
        b.gpart[8 + 2 * pair : 9 + 2 * pair, 0:128] = jnp.sum(grid[:BLK], axis=0, keepdims=True)
        b.gpart[9 + 2 * pair : 10 + 2 * pair, 0:128] = jnp.sum(grid[BLK:], axis=0, keepdims=True)


MID_IN = (
    "deal", "k_hbm", "v_hbm", "o", "cq_w", "ck", "cv", "co", "gate", "up", "down", "x", "gains", "small", "q", "go", "tb",
)
MID_OUT = (
    "layer_out", "n3", "mixed", "att", "n2", "attc", "gg", "gu", "g1", "gcq", "g2", "dq", "gh", "gpart", "crossp", "dkv_hbm",
)
MID_SCRATCH = (
    "kvs", "dkv", "w_o", "w_cq", "w_ck", "w_cv", "w_co", "w_gate", "w_up", "w_down", "h1", "h2", "cq", "ckeys", "cvals", "cprob",
    "hg", "hs", "gatt", "bias", "qm", "dom", "top", "sums", "acc", "sco", "rows", "att32", "near", "nacc", "tot", "sem", "osem", "wsem",
)


def mid_kernel(enc_own, *refs):
    b = Bag(MID_IN + MID_OUT + MID_SCRATCH, refs)
    load_in_order(b.deal, b.k_hbm, b.v_hbm, b.kvs, b.sem)
    loads = []
    for i, name in enumerate(("o", "cq", "ck", "cv", "co", "gate", "up", "down")):
        source = b.cq_w if name == "cq" else getattr(b, name)
        loads.append(pltpu.make_async_copy(source, getattr(b, "w_" + name), b.wsem.at[i]))
        loads[-1].start()
    low = lax.broadcasted_iota(jnp.int32, (BLK, 128), 1) < BLK
    low2 = lax.broadcasted_iota(jnp.int32, (2 * BLK, 128), 1) < BLK
    device = lax.axis_index(AXES)
    ranks = [b.deal[device, qb] for qb in range(2)]
    for qb in range(2):
        fill_bias(b, qb, ranks[qb])
    loaded(b.k_hbm, b.v_hbm, b.kvs, b.sem)
    for qb in range(2):
        self_forward_block(b, qb, ranks[qb], low)
    for load in loads[:5]:
        load.wait()
    after_attention(b, low)
    enc = every_encoded(b.small, enc_own)
    b.ckeys[...] = mm(enc, flat(b.w_ck), NN).astype(BF16)
    b.cvals[...] = mm(enc, flat(b.w_cv), NN).astype(BF16)
    cross_forward(b, low2)
    after_cross_attention(b)
    for load in loads[5:]:
        load.wait()
    feed_forward(b)
    b.gpart[...] = jnp.zeros_like(b.gpart)
    feed_backward(b)
    gac = mm(b.g2[...], flat(b.w_co), NT).astype(BF16)
    cross_backward(b, gac, low2, enc_own)
    before_attention(b)
    b.dkv[...] = jnp.zeros_like(b.dkv)
    b.tot[...] = jnp.zeros_like(b.tot)
    b.nacc[...] = jnp.zeros_like(b.nacc)
    for qb in range(2):
        self_backward_rows(b, qb, low)
        self_backward_block(b, qb, ranks[qb], low)
    blocks = b.k_hbm.shape[0] // BLK

    def out_one(index, carry):
        here = pl.ds(pl.multiple_of(b.deal[index // 2, index % 2] * BLK, BLK), BLK)
        b.kvs[here, :] = b.dkv[here, :].astype(BF16)
        pltpu.make_async_copy(b.kvs.at[here], b.dkv_hbm.at[pl.ds(index * BLK, BLK)], b.osem).start()
        return carry

    lax.fori_loop(0, blocks, out_one, 0)
    bias_gradient(b, low)
    pltpu.make_async_copy(b.kvs, b.dkv_hbm, b.osem).wait()


def mid(deal, keys, values, weights, x, gains, small, q, go, tb, enc_own):
    rows, width = x.shape
    inner = q.shape[1]
    total = keys.shape[0]
    ff = weights[5].shape[2]
    h2 = inner // 128
    shards = weights[0].shape[0]
    enc = shards * enc_own
    sm = pl.BlockSpec(memory_space=pltpu.SMEM)
    vm = pl.BlockSpec(memory_space=pltpu.VMEM)
    hb = pl.BlockSpec(memory_space=pl.ANY)
    out = jax.ShapeDtypeStruct
    return pl.pallas_call(
        functools.partial(mid_kernel, enc_own),
        name="mid",
        out_shape=(
            out((rows, width), BF16), out((rows, width), BF16), out((rows, ff), BF16), out((rows, inner), BF16),
            out((rows, width), BF16), out((rows, inner), BF16), out((rows, ff), BF16), out((rows, ff), BF16),
            out((rows, width), BF16), out((rows, inner), BF16), out((rows, width), BF16), out((rows, inner), BF16),
            out((rows, width), F32), out((24, width), F32), out((shards // 4, 2, 2, 8, 2 * inner), F32),
            out((total, 2 * inner), BF16),
        ),
        in_specs=[sm] + [hb] * (2 + len(weights)) + [vm] * 6,
        out_specs=tuple([vm] * 15 + [hb]),
        scratch_shapes=[
            pltpu.VMEM((total, 2 * inner), BF16),
            pltpu.VMEM((total, 2 * inner), F32),
        ]
        + [pltpu.VMEM(weight.shape, BF16) for weight in weights]
        + [
            pltpu.VMEM((rows, width), F32),
            pltpu.VMEM((rows, width), F32),
            pltpu.VMEM((rows, inner), BF16),
            pltpu.VMEM((enc, inner), BF16),
            pltpu.VMEM((enc, inner), BF16),
            pltpu.VMEM((h2, 2 * rows, enc), F32),
            pltpu.VMEM((rows, ff), F32),
            pltpu.VMEM((rows, ff), F32),
            pltpu.VMEM((rows, inner), BF16),
            pltpu.VMEM((2, 3, h2, CH, 128), F32),
            pltpu.VMEM((2, h2, 2 * BLK, 128), BF16),
            pltpu.VMEM((2, h2, 2 * BLK, 128), BF16),
            pltpu.VMEM((h2, 8, 128), F32),
            pltpu.VMEM((h2, 8, 128), F32),
            pltpu.VMEM((h2, 2 * BLK, 128), F32),
            pltpu.VMEM((h2, total, 128), F32),
            pltpu.VMEM((2, h2, 8, 128), F32),
            pltpu.VMEM((rows, inner), F32),
            pltpu.VMEM((h2, 2 * CH, 128), F32),
            pltpu.VMEM((3, h2, BLK, 128), F32),
            pltpu.VMEM((h2, 8, 128), F32),
            pltpu.SemaphoreType.DMA((2,)),
            pltpu.SemaphoreType.DMA,
            pltpu.SemaphoreType.DMA((8,)),
        ],
        compiler_params=pltpu.CompilerParams(vmem_limit_bytes=BIG),
    )(deal, keys, values, *weights, x, gains, small, q, go, tb)


def fits(*operands):
    layer_in, encoded, self_query, relative_bias = operands[0], operands[1], operands[4], operands[18]
    total = layer_in.shape[1] * lax.axis_size(AXES)
    return (
        lax.axis_size(GRP) == 2
        and lax.axis_size(WSH) == 2
        and lax.axis_size(CTX) == 8
        and layer_in.shape[1] == 2 * BLK
        and encoded.shape[1] == 4
        and total // 2 <= CONT_TOK
        and self_query.shape[0] % 16 == 0
        and self_query.shape[1] == relative_bias.shape[1] * BLK
        and self_query.shape[1] % 256 == 0
    )


def fast(
    layer_in, encoded, cotangent, deal_table, self_query, self_key, self_value, self_output, cross_query, cross_key,
    cross_value, cross_output, feed_gate, feed_up, feed_down, gain_self, gain_cross, gain_feed, relative_bias,
):
    nz = lax.axis_size(CTX) // 2
    shards = lax.axis_size(AXES)
    device = lax.axis_index(AXES)
    rows = layer_in.shape[1]
    width = layer_in.shape[2]
    heads = relative_bias.shape[1]
    inner = self_query.shape[1]
    owned = gain_self.shape[0]
    enc_own = encoded.shape[1]
    table_hb = relative_bias.astype(F32).T

    gains_here = lax.dynamic_update_slice(
        jnp.zeros((3, width), BF16), jnp.stack([gain_self, gain_cross, gain_feed]), (0, device * owned)
    )
    small = jnp.concatenate([encoded[0], gains_here, jnp.zeros((9, width), BF16)], axis=0)
    *wholes, queries, normed_one, gains = front(
        layer_in[0],
        (
            small, self_key, self_value, self_query, self_output, cross_query, cross_key, cross_value, cross_output,
            feed_gate, feed_up, feed_down,
        ),
        nz,
        shards,
    )
    whole = {name: value.reshape((shards,) + value.shape[3:]) for name, value in zip(FRONT_PARTS, wholes)}
    in_rows = {name: value.reshape(-1, value.shape[-1]) for name, value in whole.items()}
    (
        layer_out, normed_three, mixed_hidden, attended, normed_two, attended_cross, grad_gate, grad_up, grad_one_low,
        grad_cq_low, grad_two_low, grad_queries, grad_hidden_one, gpart, cross_part, kv_part,
    ) = mid(
        deal_table, in_rows["keys"], in_rows["values"],
        [whole[name] for name in ("o", "cq", "ck", "cv", "co", "gate", "up", "down")],
        layer_in[0], gains, whole["small"], queries, cotangent[0], pair_table(table_hb), enc_own,
    )
    ff = feed_gate.shape[1]
    square = (owned, inner)
    shapes = dict(
        gate=(owned, ff), up=(owned, ff), down=(feed_down.shape[0], width), co=(inner // shards, width), cq=square,
        ck=square, cv=square, q=square, o=(inner // shards, width), k=square, v=square,
    )
    enc_padded = jnp.pad(encoded[0], ((0, 16 - enc_own), (0, 0)))
    result = back_step(
        kv_part.reshape(nz, 2, 2, rows, 2 * inner), cross_part,
        [whole[name] for name in ("q", "k", "v", "ck", "cv")], layer_in[0], gains,
        grad_hidden_one, gpart, enc_padded,
        (
            normed_three, mixed_hidden, attended, normed_two, attended_cross, normed_one, grad_gate, grad_up, cotangent[0],
            grad_one_low, grad_cq_low, grad_two_low, grad_queries,
        ),
        shapes,
        nz,
    )
    grad_enc, total = result[len(BACK_OUT) + 1 :]
    result = closing(result[: len(BACK_OUT) + 1])
    got = dict(zip(BACK_OUT, result))
    grad_input = result[len(BACK_OUT)]
    gain_grads = [lax.dynamic_slice_in_dim(total[i], device * owned, owned) for i in range(3)]
    grad_relative_bias = total[8 : 8 + heads, :BUCKETS].T
    return (
        layer_out[None], grad_input[None], grad_enc[None, :enc_own],
        got["q"], got["k"], got["v"], got["o"], got["cq"], got["ck"], got["cv"], got["co"], got["gate"], got["up"], got["down"],
        gain_grads[0], gain_grads[1], gain_grads[2], grad_relative_bias,
    )


def solution(mesh):
    return jax.shard_map(
        lambda *operands: (fast if fits(*operands) else local)(*operands),
        mesh=mesh,
        in_specs=(
            P(GRP, AXES, None),
            P(GRP, AXES, None),
            P(GRP, AXES, None),
            P(),
            P(AXES, None),
            P(AXES, None),
            P(AXES, None),
            P(AXES, None),
            P(AXES, None),
            P(AXES, None),
            P(AXES, None),
            P(AXES, None),
            P(AXES, None),
            P(AXES, None),
            P(AXES, None),
            P(AXES),
            P(AXES),
            P(AXES),
            P(),
        ),
        out_specs=(
            P(GRP, AXES, None),
            P(GRP, AXES, None),
            P(GRP, AXES, None),
            P(AXES, None),
            P(AXES, None),
            P(AXES, None),
            P(AXES, None),
            P(AXES, None),
            P(AXES, None),
            P(AXES, None),
            P(AXES, None),
            P(AXES, None),
            P(AXES, None),
            P(AXES, None),
            P(AXES),
            P(AXES),
            P(AXES),
            P(),
        ),
        check_vma=False,
    )
```

```python
import functools
import math

import jax
import jax.numpy as jnp
from jax import lax
from jax.experimental import pallas as pl
from jax.experimental.pallas import tpu as pltpu
from jax.sharding import PartitionSpec as P

GRP, CTX, WSH = "grp", "ctx", "wsh"
AXES = (CTX, WSH)
EVERY = (GRP, CTX, WSH)
QK = "qhd,khd->hqk"
PV = "hqk,khd->qhd"
PTQ = "hqk,qhd->khd"
TF_TD = "tf,td->fd"
TD_FD = "td,fd->tf"
TD_TF = "td,tf->df"
TF_DF = "tf,df->td"
TC_TD = "tc,td->cd"
TD_CD = "td,cd->tc"
TD_TC = "td,tc->dc"
TC_DC = "tc,dc->td"

BUCKETS = 32
MAXDIST = 128
CONT_TOK = 2048


MASKED = -1e30
EPSILON = 1e-06


def rms_norm(hidden, gain_vector):
    return (
        hidden
        * lax.rsqrt(jnp.mean(hidden * hidden, axis=-1, keepdims=True) + EPSILON)
        * gain_vector
    )


def gated(gate_pre, up_pre):
    return jax.nn.gelu(gate_pre, approximate=True) * up_pre


def bounce(values):
    return lax.optimization_barrier(values.astype(jnp.bfloat16)).astype(jnp.float32)


def split_probs(probs_full):
    probs_high = probs_full.astype(jnp.bfloat16)
    probs_rest = (probs_full - probs_high.astype(jnp.float32)).astype(jnp.bfloat16)
    return (probs_high, probs_rest)


def bucket_ids(distance):
    exact_half = BUCKETS // 2
    counted = jnp.minimum(distance, exact_half)
    for number in range(1, exact_half):
        boundary = int(math.ceil(exact_half * math.pow(MAXDIST / exact_half, number / exact_half)))
        counted = counted + (distance >= boundary).astype(jnp.int32)
    return counted


def token_place(tokens, prompt_len, cont_len):
    beyond = tokens - prompt_len
    in_prompt = tokens < prompt_len
    sequence = jnp.where(in_prompt, 0, 1 + beyond // cont_len)
    position = jnp.where(in_prompt, tokens, prompt_len + beyond % cont_len)
    return (sequence, position)


def pair_mask(seq_query, pos_query, seq_key, pos_key):
    earlier = pos_key[None, :] <= pos_query[:, None]
    visible = (seq_key[None, :] == seq_query[:, None]) | (seq_key[None, :] == 0)
    return earlier & visible


def bucket_bias(pos_query, pos_key, table_hb):
    buckets = bucket_ids(jnp.maximum(pos_query[:, None] - pos_key[None, :], 0))
    picks = (
        buckets[None, :, :, None]
        == jnp.arange(table_hb.shape[1], dtype=jnp.int32)[None, None, None, :]
    )
    return (buckets, jnp.sum(jnp.where(picks, table_hb[:, None, None, :], 0.0), axis=-1))


def bucket_grad(buckets, grad_scores, bucket_count):
    picks = (
        buckets[None, :, :, None] == jnp.arange(bucket_count, dtype=jnp.int32)[None, None, None, :]
    )
    return jnp.sum(
        jnp.where(picks, grad_scores.astype(jnp.float32)[:, :, :, None], 0.0), axis=(1, 2)
    )


def masked_scores(query_heads, key_heads, bias, allowed):
    direct = jnp.einsum(QK, query_heads, key_heads, preferred_element_type=jnp.float32)
    return jnp.where(allowed[None], direct + bias, MASKED)


def score_grads(scores, log_total, delta_row, grad_heads, value_heads):
    probs_full = jnp.exp(scores - log_total[:, :, None])
    grad_probs = jnp.einsum(
        QK, grad_heads, value_heads, preferred_element_type=jnp.float32
    )
    grad_scores = (probs_full * (grad_probs - delta_row[:, :, None])).astype(jnp.bfloat16)
    return (probs_full.astype(jnp.bfloat16), grad_scores)


def key_view(seq_all, pos_all, step_index, key_rows, seq_query, pos_query):
    seq_key = lax.dynamic_slice_in_dim(seq_all, step_index * key_rows, key_rows)
    pos_key = lax.dynamic_slice_in_dim(pos_all, step_index * key_rows, key_rows)
    return (pos_key, pair_mask(seq_query, pos_query, seq_key, pos_key))


def self_forward(
    query_heads, key_heads, value_heads, seq_all, pos_all, seq_query, pos_query, table_hb, key_rows
):
    total_rows = key_heads.shape[0]
    head_count = query_heads.shape[1]
    rows_here = query_heads.shape[0]
    step_list = jnp.arange(total_rows // key_rows, dtype=jnp.int32)

    def total_step(carried, step_index):
        pos_key, allowed = key_view(seq_all, pos_all, step_index, key_rows, seq_query, pos_query)

        def total_accumulate(current):
            running_max, running_sum = current
            key_block = lax.dynamic_slice_in_dim(key_heads, step_index * key_rows, key_rows)
            bias = bucket_bias(pos_query, pos_key, table_hb)[1]
            scores = masked_scores(query_heads, key_block, bias, allowed)
            new_max = jnp.maximum(running_max, jnp.max(scores, axis=-1))
            weights = jnp.where(allowed[None], jnp.exp(scores - new_max[:, :, None]), 0.0)
            return (
                new_max,
                running_sum * jnp.exp(running_max - new_max) + jnp.sum(weights, axis=-1),
            )

        return (
            lax.cond(jnp.any(allowed), total_accumulate, lambda current: current, carried),
            None,
        )

    start_state = (
        jnp.full((head_count, rows_here), MASKED, jnp.float32),
        jnp.zeros((head_count, rows_here), jnp.float32),
    )
    (running_max, running_sum), _ = lax.scan(total_step, start_state, step_list)
    log_total = running_max + jnp.log(running_sum)

    def output_step(carried, step_index):
        pos_key, allowed = key_view(seq_all, pos_all, step_index, key_rows, seq_query, pos_query)

        def output_accumulate(current):
            rounded_sum, rest_sum = current
            key_block = lax.dynamic_slice_in_dim(key_heads, step_index * key_rows, key_rows)
            value_block = lax.dynamic_slice_in_dim(value_heads, step_index * key_rows, key_rows)
            bias = bucket_bias(pos_query, pos_key, table_hb)[1]
            scores = masked_scores(query_heads, key_block, bias, allowed)
            probs_high, probs_rest = split_probs(jnp.exp(scores - log_total[:, :, None]))
            rounded_sum = rounded_sum + jnp.einsum(
                PV, probs_high, value_block, preferred_element_type=jnp.float32
            )
            rest_sum = rest_sum + jnp.einsum(
                PV, probs_rest, value_block, preferred_element_type=jnp.float32
            )
            return (rounded_sum, rest_sum)

        return (
            lax.cond(jnp.any(allowed), output_accumulate, lambda current: current, carried),
            None,
        )

    zero_heads = jnp.zeros(query_heads.shape, jnp.float32)
    (rounded_sum, rest_sum), _ = lax.scan(output_step, (zero_heads, zero_heads), step_list)
    return (log_total, rounded_sum, rounded_sum + rest_sum)


def query_backward(
    query_heads,
    key_heads,
    value_heads,
    grad_heads,
    log_total,
    delta_row,
    seq_all,
    pos_all,
    seq_query,
    pos_query,
    table_hb,
    key_rows,
):
    total_rows = key_heads.shape[0]
    inner_width = key_heads.shape[1] * key_heads.shape[2]
    bucket_count = table_hb.shape[1]
    step_list = jnp.arange(total_rows // key_rows, dtype=jnp.int32)

    def step_body(carried, step_index):
        pos_key, allowed = key_view(seq_all, pos_all, step_index, key_rows, seq_query, pos_query)

        def step_accumulate(current):
            grad_query, grad_bias = current
            key_block = lax.dynamic_slice_in_dim(key_heads, step_index * key_rows, key_rows)
            value_block = lax.dynamic_slice_in_dim(value_heads, step_index * key_rows, key_rows)
            buckets, bias = bucket_bias(pos_query, pos_key, table_hb)
            scores = masked_scores(query_heads, key_block, bias, allowed)
            probs_low, grad_scores = score_grads(
                scores, log_total, delta_row, grad_heads, value_block
            )
            grad_query = grad_query + jnp.einsum(
                PV, grad_scores, key_block, preferred_element_type=jnp.float32
            )
            grad_bias = grad_bias + bucket_grad(buckets, grad_scores, bucket_count)
            grad_key = jnp.einsum(
                PTQ, grad_scores, query_heads, preferred_element_type=jnp.float32
            ).reshape(key_rows, inner_width)
            grad_value = jnp.einsum(
                PTQ, probs_low, grad_heads, preferred_element_type=jnp.float32
            ).reshape(key_rows, inner_width)
            return ((grad_query, grad_bias), jnp.concatenate([grad_key, grad_value], axis=1))

        blank_block = jnp.zeros((key_rows, 2 * inner_width), jnp.float32)
        return lax.cond(
            jnp.any(allowed), step_accumulate, lambda current: (current, blank_block), carried
        )

    start_state = (
        jnp.zeros(query_heads.shape, jnp.float32),
        jnp.zeros(table_hb.shape, jnp.float32),
    )
    final_state, key_blocks = lax.scan(step_body, start_state, step_list)
    return (final_state[0], final_state[1], key_blocks.reshape(total_rows, 2 * inner_width))


def local(
    layer_in,
    encoded,
    cotangent,
    deal_table,
    self_query,
    self_key,
    self_value,
    self_output,
    cross_query,
    cross_key,
    cross_value,
    cross_output,
    feed_gate,
    feed_up,
    feed_down,
    gain_self,
    gain_cross,
    gain_feed,
    relative_bias,
):
    shards = lax.axis_size(AXES)
    device = lax.axis_index(AXES)
    ctx_count = lax.axis_size(CTX)
    core_count = lax.axis_size(WSH)
    local_rows = layer_in.shape[1]
    total_rows = local_rows * shards
    block_len = local_rows // 2
    cont_len = min(CONT_TOK, total_rows // 2)
    prompt_len = total_rows - total_rows // 2 // cont_len * cont_len
    key_rows = min(1024, total_rows)
    head_count = relative_bias.shape[1]
    inner_width = self_query.shape[1]
    head_size = inner_width // head_count
    enc_rows = encoded.shape[1] * shards
    table_hb = relative_bias.astype(jnp.float32).T
    flat_table = deal_table.reshape(-1)
    all_tokens = (
        flat_table[:, None] * block_len + jnp.arange(block_len, dtype=jnp.int32)[None, :]
    ).reshape(-1)
    seq_all, pos_all = token_place(all_tokens, prompt_len, cont_len)
    seq_mine = lax.dynamic_slice_in_dim(seq_all, device * local_rows, local_rows)
    pos_mine = lax.dynamic_slice_in_dim(pos_all, device * local_rows, local_rows)
    forward_weights = (
        lax.all_gather(self_query, AXES, axis=0, tiled=True),
        lax.all_gather(self_key, AXES, axis=0, tiled=True),
        lax.all_gather(self_value, AXES, axis=0, tiled=True),
        lax.all_gather(self_output, AXES, axis=0, tiled=True),
        lax.all_gather(cross_query, AXES, axis=0, tiled=True),
        lax.all_gather(cross_key, AXES, axis=0, tiled=True),
        lax.all_gather(cross_value, AXES, axis=0, tiled=True),
        lax.all_gather(cross_output, AXES, axis=0, tiled=True),
        lax.all_gather(feed_gate, AXES, axis=0, tiled=True),
        lax.all_gather(feed_up, AXES, axis=0, tiled=True),
        lax.all_gather(feed_down, AXES, axis=0, tiled=True),
        lax.all_gather(gain_self, AXES, axis=0, tiled=True),
        lax.all_gather(gain_cross, AXES, axis=0, tiled=True),
        lax.all_gather(gain_feed, AXES, axis=0, tiled=True),
    )
    (
        query_weight,
        key_weight,
        value_weight,
        output_weight,
        cq_weight,
        ck_weight,
        cv_weight,
        co_weight,
        gate_weight,
        up_weight,
        down_weight,
        gain_one,
        gain_two,
        gain_three,
    ) = forward_weights
    inputs32 = layer_in[0].astype(jnp.float32)
    normed_one = rms_norm(inputs32, gain_one.astype(jnp.float32)).astype(jnp.bfloat16)
    queries = jnp.dot(normed_one, query_weight, preferred_element_type=jnp.float32).astype(
        jnp.bfloat16
    )
    keys_local = jnp.dot(normed_one, key_weight, preferred_element_type=jnp.float32).astype(
        jnp.bfloat16
    )
    values_local = jnp.dot(normed_one, value_weight, preferred_element_type=jnp.float32).astype(
        jnp.bfloat16
    )
    keys_all, values_all = (
        lax.all_gather(keys_local, AXES, axis=0, tiled=True),
        lax.all_gather(values_local, AXES, axis=0, tiled=True),
    )
    query_heads = queries.reshape(local_rows, head_count, head_size)
    key_heads = keys_all.reshape(total_rows, head_count, head_size)
    value_heads = values_all.reshape(total_rows, head_count, head_size)
    log_self, attn_sum, attn_exact = self_forward(
        query_heads,
        key_heads,
        value_heads,
        seq_all,
        pos_all,
        seq_mine,
        pos_mine,
        table_hb,
        key_rows,
    )
    attended = attn_sum.reshape(local_rows, inner_width).astype(jnp.bfloat16)
    hidden_one = inputs32 + jnp.dot(attended, output_weight, preferred_element_type=jnp.float32)
    normed_two = rms_norm(hidden_one, gain_two.astype(jnp.float32)).astype(jnp.bfloat16)
    cross_queries = jnp.dot(normed_two, cq_weight, preferred_element_type=jnp.float32).astype(
        jnp.bfloat16
    )
    enc_keys = jnp.dot(encoded[0], ck_weight, preferred_element_type=jnp.float32).astype(
        jnp.bfloat16
    )
    enc_values = jnp.dot(encoded[0], cv_weight, preferred_element_type=jnp.float32).astype(
        jnp.bfloat16
    )
    cross_keys, cross_values = (
        lax.all_gather(enc_keys, AXES, axis=0, tiled=True),
        lax.all_gather(enc_values, AXES, axis=0, tiled=True),
    )
    cq_heads = cross_queries.reshape(local_rows, head_count, head_size)
    ck_heads = cross_keys.reshape(enc_rows, head_count, head_size)
    cv_heads = cross_values.reshape(enc_rows, head_count, head_size)
    cross_scores = jnp.einsum(
        QK, cq_heads, ck_heads, preferred_element_type=jnp.float32
    )
    cross_peak = jnp.max(cross_scores, axis=-1)
    log_cross = cross_peak + jnp.log(
        jnp.sum(jnp.exp(cross_scores - cross_peak[:, :, None]), axis=-1)
    )
    cross_probs = jnp.exp(cross_scores - log_cross[:, :, None])
    cross_high, cross_rest = split_probs(cross_probs)
    cross_sum = jnp.einsum(PV, cross_high, cv_heads, preferred_element_type=jnp.float32)
    cross_exact = cross_sum + jnp.einsum(
        PV, cross_rest, cv_heads, preferred_element_type=jnp.float32
    )
    attended_cross = cross_sum.reshape(local_rows, inner_width).astype(jnp.bfloat16)
    hidden_two = hidden_one + jnp.dot(attended_cross, co_weight, preferred_element_type=jnp.float32)
    normed_three = rms_norm(hidden_two, gain_three.astype(jnp.float32)).astype(jnp.bfloat16)
    gate_pre = jnp.dot(normed_three, gate_weight, preferred_element_type=jnp.float32)
    up_pre = jnp.dot(normed_three, up_weight, preferred_element_type=jnp.float32)
    mixed_hidden = gated(gate_pre, up_pre).astype(jnp.bfloat16)
    output_sum = hidden_two + jnp.dot(mixed_hidden, down_weight, preferred_element_type=jnp.float32)
    layer_out = output_sum.astype(jnp.bfloat16)[None]
    back_weights = (
        lax.all_gather(self_query, AXES, axis=0, tiled=True),
        lax.all_gather(self_key, AXES, axis=0, tiled=True),
        lax.all_gather(self_value, AXES, axis=0, tiled=True),
        lax.all_gather(self_output, AXES, axis=0, tiled=True),
        lax.all_gather(cross_query, AXES, axis=0, tiled=True),
        lax.all_gather(cross_key, AXES, axis=0, tiled=True),
        lax.all_gather(cross_value, AXES, axis=0, tiled=True),
        lax.all_gather(cross_output, AXES, axis=0, tiled=True),
        lax.all_gather(feed_gate, AXES, axis=0, tiled=True),
        lax.all_gather(feed_up, AXES, axis=0, tiled=True),
        lax.all_gather(feed_down, AXES, axis=0, tiled=True),
        lax.all_gather(gain_self, AXES, axis=0, tiled=True),
        lax.all_gather(gain_cross, AXES, axis=0, tiled=True),
        lax.all_gather(gain_feed, AXES, axis=0, tiled=True),
    )
    (
        query_back,
        key_back,
        value_back,
        output_back,
        cq_back,
        ck_back,
        cv_back,
        co_back,
        gate_back,
        up_back,
        down_back,
        gain_one_back,
        gain_two_back,
        gain_three_back,
    ) = back_weights
    grad_out = cotangent[0]
    grad_down_w = jnp.einsum(
        TF_TD, mixed_hidden, grad_out, preferred_element_type=jnp.float32
    )
    grad_mixed = jnp.einsum(TD_FD, grad_out, down_back, preferred_element_type=jnp.float32)
    _, gate_pull = jax.vjp(gated, gate_pre, up_pre)
    grad_gate32, grad_up32 = gate_pull(bounce(grad_mixed))
    grad_gate = grad_gate32.astype(jnp.bfloat16)
    grad_up = grad_up32.astype(jnp.bfloat16)
    grad_gate_w = jnp.einsum(
        TD_TF, normed_three, grad_gate, preferred_element_type=jnp.float32
    )
    grad_up_w = jnp.einsum(TD_TF, normed_three, grad_up, preferred_element_type=jnp.float32)
    grad_normed_three = jnp.einsum(
        TF_DF, grad_gate, gate_back, preferred_element_type=jnp.float32
    ) + jnp.einsum(TF_DF, grad_up, up_back, preferred_element_type=jnp.float32)
    _, norm_pull_three = jax.vjp(rms_norm, hidden_two, gain_three_back.astype(jnp.float32))
    back_two, grad_gain_feed = norm_pull_three(grad_normed_three)
    grad_hidden_two = grad_out.astype(jnp.float32) + back_two
    grad_two_low = grad_hidden_two.astype(jnp.bfloat16)
    grad_co_w = jnp.einsum(
        TC_TD, attended_cross, grad_two_low, preferred_element_type=jnp.float32
    )
    grad_attended_cross = jnp.einsum(
        TD_CD, grad_two_low, co_back, preferred_element_type=jnp.float32
    ).astype(jnp.bfloat16)
    grad_ac_heads = grad_attended_cross.reshape(local_rows, head_count, head_size)
    delta_cross = jnp.sum(grad_ac_heads.astype(jnp.float32) * cross_exact, axis=-1).T
    cross_low, grad_cross_scores = score_grads(
        cross_scores, log_cross, delta_cross, grad_ac_heads, cv_heads
    )
    grad_cq = jnp.einsum(
        PV, grad_cross_scores, ck_heads, preferred_element_type=jnp.float32
    )
    grad_ck_part = jnp.einsum(
        PTQ, grad_cross_scores, cq_heads, preferred_element_type=jnp.float32
    ).reshape(enc_rows, inner_width)
    grad_cv_part = jnp.einsum(
        PTQ, cross_low, grad_ac_heads, preferred_element_type=jnp.float32
    ).reshape(enc_rows, inner_width)
    cross_own = lax.psum_scatter(
        jnp.concatenate([grad_ck_part, grad_cv_part], axis=1),
        AXES,
        scatter_dimension=0,
        tiled=True,
    )
    grad_cross_keys = cross_own[:, :inner_width].astype(jnp.bfloat16)
    grad_cross_values = cross_own[:, inner_width:].astype(jnp.bfloat16)
    grad_ck_w = jnp.einsum(
        TD_TC, encoded[0], grad_cross_keys, preferred_element_type=jnp.float32
    )
    grad_cv_w = jnp.einsum(
        TD_TC, encoded[0], grad_cross_values, preferred_element_type=jnp.float32
    )
    grad_encoded = (
        jnp.einsum(TC_DC, grad_cross_keys, ck_back, preferred_element_type=jnp.float32)
        + jnp.einsum(TC_DC, grad_cross_values, cv_back, preferred_element_type=jnp.float32)
    )[None]
    grad_cq_low = grad_cq.reshape(local_rows, inner_width).astype(jnp.bfloat16)
    grad_cq_w = jnp.einsum(TD_TC, normed_two, grad_cq_low, preferred_element_type=jnp.float32)
    grad_normed_two = jnp.einsum(
        TC_DC, grad_cq_low, cq_back, preferred_element_type=jnp.float32
    )
    _, norm_pull_two = jax.vjp(rms_norm, hidden_one, gain_two_back.astype(jnp.float32))
    back_one, grad_gain_cross = norm_pull_two(grad_normed_two)
    grad_hidden_one = grad_hidden_two + back_one
    grad_one_low = grad_hidden_one.astype(jnp.bfloat16)
    grad_o_w = jnp.einsum(TC_TD, attended, grad_one_low, preferred_element_type=jnp.float32)
    grad_attended = jnp.einsum(
        TD_CD, grad_one_low, output_back, preferred_element_type=jnp.float32
    ).astype(jnp.bfloat16)
    grad_att_heads = grad_attended.reshape(local_rows, head_count, head_size)
    delta_self = jnp.sum(grad_att_heads.astype(jnp.float32) * attn_exact, axis=-1).T
    grad_query32, grad_bias_part, kv_blocks = query_backward(
        query_heads,
        key_heads,
        value_heads,
        grad_att_heads,
        log_self,
        delta_self,
        seq_all,
        pos_all,
        seq_mine,
        pos_mine,
        table_hb,
        key_rows,
    )
    kv_own = lax.psum_scatter(kv_blocks, AXES, scatter_dimension=0, tiled=True)
    grad_keys = kv_own[:, :inner_width].astype(jnp.bfloat16)
    grad_values = kv_own[:, inner_width:].astype(jnp.bfloat16)
    grad_queries = grad_query32.reshape(local_rows, inner_width).astype(jnp.bfloat16)
    grad_q_w = jnp.einsum(TD_TC, normed_one, grad_queries, preferred_element_type=jnp.float32)
    grad_k_w = jnp.einsum(TD_TC, normed_one, grad_keys, preferred_element_type=jnp.float32)
    grad_v_w = jnp.einsum(TD_TC, normed_one, grad_values, preferred_element_type=jnp.float32)
    grad_normed_one = (
        jnp.einsum(TC_DC, grad_queries, query_back, preferred_element_type=jnp.float32)
        + jnp.einsum(TC_DC, grad_keys, key_back, preferred_element_type=jnp.float32)
        + jnp.einsum(TC_DC, grad_values, value_back, preferred_element_type=jnp.float32)
    )
    _, norm_pull_one = jax.vjp(rms_norm, inputs32, gain_one_back.astype(jnp.float32))
    back_input, grad_gain_self = norm_pull_one(grad_normed_one)
    grad_input = (grad_hidden_one + back_input)[None]

    def sectioned(grad_full):
        return grad_full.reshape(
            (ctx_count, core_count, grad_full.shape[0] // (ctx_count * core_count))
            + grad_full.shape[1:]
        )

    core_parts = (
        lax.psum_scatter(
            sectioned(grad_q_w).astype(jnp.bfloat16), WSH, scatter_dimension=1, tiled=True
        ).astype(jnp.float32),
        lax.psum_scatter(
            sectioned(grad_k_w).astype(jnp.bfloat16), WSH, scatter_dimension=1, tiled=True
        ).astype(jnp.float32),
        lax.psum_scatter(
            sectioned(grad_v_w).astype(jnp.bfloat16), WSH, scatter_dimension=1, tiled=True
        ).astype(jnp.float32),
        lax.psum_scatter(
            sectioned(grad_o_w).astype(jnp.bfloat16), WSH, scatter_dimension=1, tiled=True
        ).astype(jnp.float32),
        lax.psum_scatter(
            sectioned(grad_cq_w).astype(jnp.bfloat16), WSH, scatter_dimension=1, tiled=True
        ).astype(jnp.float32),
        lax.psum_scatter(
            sectioned(grad_ck_w).astype(jnp.bfloat16), WSH, scatter_dimension=1, tiled=True
        ).astype(jnp.float32),
        lax.psum_scatter(
            sectioned(grad_cv_w).astype(jnp.bfloat16), WSH, scatter_dimension=1, tiled=True
        ).astype(jnp.float32),
        lax.psum_scatter(
            sectioned(grad_co_w).astype(jnp.bfloat16), WSH, scatter_dimension=1, tiled=True
        ).astype(jnp.float32),
        lax.psum_scatter(
            sectioned(grad_gate_w).astype(jnp.bfloat16), WSH, scatter_dimension=1, tiled=True
        ).astype(jnp.float32),
        lax.psum_scatter(
            sectioned(grad_up_w).astype(jnp.bfloat16), WSH, scatter_dimension=1, tiled=True
        ).astype(jnp.float32),
        lax.psum_scatter(
            sectioned(grad_down_w).astype(jnp.bfloat16), WSH, scatter_dimension=1, tiled=True
        ).astype(jnp.float32),
        lax.psum_scatter(
            sectioned(grad_gain_self).astype(jnp.bfloat16), WSH, scatter_dimension=1, tiled=True
        ).astype(jnp.float32),
        lax.psum_scatter(
            sectioned(grad_gain_cross).astype(jnp.bfloat16), WSH, scatter_dimension=1, tiled=True
        ).astype(jnp.float32),
        lax.psum_scatter(
            sectioned(grad_gain_feed).astype(jnp.bfloat16), WSH, scatter_dimension=1, tiled=True
        ).astype(jnp.float32),
    )
    (
        core_q,
        core_k,
        core_v,
        core_o,
        core_cq,
        core_ck,
        core_cv,
        core_co,
        core_gate,
        core_up,
        core_down,
        core_gs,
        core_gc,
        core_gf,
    ) = core_parts
    owned = (
        lax.psum_scatter(core_q, CTX, scatter_dimension=0, tiled=True),
        lax.psum_scatter(core_k, CTX, scatter_dimension=0, tiled=True),
        lax.psum_scatter(core_v, CTX, scatter_dimension=0, tiled=True),
        lax.psum_scatter(core_o, CTX, scatter_dimension=0, tiled=True),
        lax.psum_scatter(core_cq, CTX, scatter_dimension=0, tiled=True),
        lax.psum_scatter(core_ck, CTX, scatter_dimension=0, tiled=True),
        lax.psum_scatter(core_cv, CTX, scatter_dimension=0, tiled=True),
        lax.psum_scatter(core_co, CTX, scatter_dimension=0, tiled=True),
        lax.psum_scatter(core_gate, CTX, scatter_dimension=0, tiled=True),
        lax.psum_scatter(core_up, CTX, scatter_dimension=0, tiled=True),
        lax.psum_scatter(core_down, CTX, scatter_dimension=0, tiled=True),
        lax.psum_scatter(core_gs, CTX, scatter_dimension=0, tiled=True),
        lax.psum_scatter(core_gc, CTX, scatter_dimension=0, tiled=True),
        lax.psum_scatter(core_gf, CTX, scatter_dimension=0, tiled=True),
    )
    (
        own_q,
        own_k,
        own_v,
        own_o,
        own_cq,
        own_ck,
        own_cv,
        own_co,
        own_gate,
        own_up,
        own_down,
        own_gain_self,
        own_gain_cross,
        own_gain_feed,
    ) = [piece.reshape(piece.shape[2:]) for piece in owned]
    summed = (
        lax.psum(own_q.astype(jnp.bfloat16), GRP).astype(jnp.float32),
        lax.psum(own_k.astype(jnp.bfloat16), GRP).astype(jnp.float32),
        lax.psum(own_v.astype(jnp.bfloat16), GRP).astype(jnp.float32),
        lax.psum(own_o.astype(jnp.bfloat16), GRP).astype(jnp.float32),
        lax.psum(own_cq.astype(jnp.bfloat16), GRP).astype(jnp.float32),
        lax.psum(own_ck.astype(jnp.bfloat16), GRP).astype(jnp.float32),
        lax.psum(own_cv.astype(jnp.bfloat16), GRP).astype(jnp.float32),
        lax.psum(own_co.astype(jnp.bfloat16), GRP).astype(jnp.float32),
        lax.psum(own_gate.astype(jnp.bfloat16), GRP).astype(jnp.float32),
        lax.psum(own_up.astype(jnp.bfloat16), GRP).astype(jnp.float32),
        lax.psum(own_down.astype(jnp.bfloat16), GRP).astype(jnp.float32),
        lax.psum(own_gain_self.astype(jnp.bfloat16), GRP).astype(jnp.float32),
        lax.psum(own_gain_cross.astype(jnp.bfloat16), GRP).astype(jnp.float32),
        lax.psum(own_gain_feed.astype(jnp.bfloat16), GRP).astype(jnp.float32),
    )
    grad_relative_bias = lax.psum(grad_bias_part.T, EVERY)
    return (
        layer_out,
        grad_input,
        grad_encoded,
        summed[0],
        summed[1],
        summed[2],
        summed[3],
        summed[4],
        summed[5],
        summed[6],
        summed[7],
        summed[8],
        summed[9],
        summed[10],
        summed[11],
        summed[12],
        summed[13],
        grad_relative_bias,
    )


BIG = 63 << 20
NT = (((1,), (1,)), ((), ()))
TN = (((0,), (0,)), ((), ()))
NN = (((1,), (0,)), ((), ()))
F32 = jnp.float32
BF16 = jnp.bfloat16
CH = 256
BLK = 64


def mm(left, right, dims):
    return lax.dot_general(left, right, dims, preferred_element_type=F32)


def load_in_order(deal, k_hbm, v_hbm, kvs, sem):
    blocks, inner = k_hbm.shape[0] // BLK, k_hbm.shape[1]

    def one(index, carry):
        here = pl.ds(index * BLK, BLK)
        rows = kvs.at[pl.ds(pl.multiple_of(deal[index // 2, index % 2] * BLK, BLK), BLK)]
        pltpu.make_async_copy(k_hbm.at[here], rows.at[:, pl.ds(0, inner)], sem.at[0]).start()
        pltpu.make_async_copy(v_hbm.at[here], rows.at[:, pl.ds(inner, inner)], sem.at[1]).start()
        return carry

    lax.fori_loop(0, blocks, one, 0)


def loaded(k_hbm, v_hbm, kvs, sem):
    inner = k_hbm.shape[1]
    pltpu.make_async_copy(k_hbm, kvs.at[:, pl.ds(0, inner)], sem.at[0]).wait()
    pltpu.make_async_copy(v_hbm, kvs.at[:, pl.ds(inner, inner)], sem.at[1]).wait()


def stack_pair(block, low_lanes):
    zero = jnp.zeros_like(block)
    return jnp.concatenate([jnp.where(low_lanes, block, zero), jnp.where(low_lanes, zero, block)], axis=0)


def pair_table(table_hb):
    heads = table_hb.shape[0]
    padded = jnp.pad(table_hb, ((0, 0), (0, BLK - BUCKETS)))
    return padded.reshape(heads // 2, 2 * BLK)

MESH = pl.DeviceIdType.MESH


class Place:
    def __init__(self, nz):
        self.nz = nz
        self.g = lax.axis_index(GRP)
        self.c = lax.axis_index(CTX)
        self.w = lax.axis_index(WSH)
        self.z = self.c // 2
        self.y = lax.rem(self.c, 2)
        self.me = self.c * 2 + self.w

    def at(self, g=None, z=None, y=None, w=None):
        z = self.z if z is None else z
        y = self.y if y is None else y
        return (self.g if g is None else g, z * 2 + y, self.w if w is None else w)

    def twin(self):
        return self.at(g=1 - self.g)

    def over(self):
        return self.at(y=1 - self.y)

    def mate(self):
        return self.at(w=1 - self.w)

    def up(self, dz):
        return lax.rem(self.z + dz, self.nz)

    def down(self, dz):
        return lax.rem(self.z + self.nz - dz, self.nz)

    def greet(self):
        partners = [self.twin(), self.over(), self.mate()]
        partners += [self.at(z=self.up(dz)) for dz in range(1, self.nz)]
        for partner in partners:
            pl.semaphore_signal(pltpu.get_barrier_semaphore(), inc=1, device_id=partner, device_id_type=MESH)
        self.greeted = len(partners)

    def met(self):
        pl.semaphore_wait(pltpu.get_barrier_semaphore(), self.greeted)


def push(src, dst, ssem, rsem, to):
    return pltpu.make_async_remote_copy(src, dst, ssem, rsem, device_id=to, device_id_type=MESH)


def half(wide, index):
    return pl.ds(pl.multiple_of(index * (wide // 2), 128), wide // 2)


class Gather:
    COUNT = 9

    def __init__(self, at, part, whole, sems, split, chunk=0, chunks=1):
        self.at, self.nz, self.part, self.whole, self.split = at, at.nz, part, whole, split
        (self.zs, self.zr, self.ys, self.yr, self.xs, self.xr, self.ws, self.wr, self.lc) = sems
        self.wide = whole.shape[-1] // chunks
        self.first = chunk * self.wide
        self.sent = []

    @staticmethod
    def scratch(nz, split):
        dma = pltpu.SemaphoreType.DMA
        x = 2 * nz if split else 1
        w = 4 * nz if split else 2 * nz
        return [dma((nz,))] * 4 + [dma((x,))] * 2 + [dma((w,))] * 2 + [dma((1,))]

    def cols(self, side=None):
        if self.split and side is not None:
            return pl.ds(pl.multiple_of(self.first + side * (self.wide // 2), 128), self.wide // 2)
        return pl.ds(self.first, self.wide)

    def spot(self, z, y, w, side=None):
        return self.whole.at[z, y, w, :, self.cols(side)]

    def post(self, view, ssem, rsem, to, source=None):
        copy = push(view if source is None else source, view, ssem, rsem, to)
        copy.start()
        self.sent.append(copy)

    def to_y(self, z):
        at = self.at
        self.post(self.spot(z, at.y, at.w, at.g), self.ys.at[z], self.yr.at[z], at.over())

    def to_x(self, z, y):
        at = self.at
        if self.split:
            k = z * 2 + y
            self.post(self.spot(z, y, at.w, at.g), self.xs.at[k], self.xr.at[k], at.twin())

    def w_sem(self, z, y, side):
        k = z * 2 + y
        return k * 2 + (0 if side is None else side) if self.split else k

    def to_w(self, z, y, side):
        at = self.at
        k = self.w_sem(z, y, side)
        self.post(self.spot(z, y, at.w, side), self.ws.at[k], self.wr.at[k], at.mate())

    def place(self):
        here = self.spot(self.at.z, self.at.y, self.at.w)
        self.local = pltpu.make_async_copy(self.part.at[:, self.cols()], here, self.lc.at[0])
        self.local.start()

    def send(self):
        at = self.at
        here, source = self.spot(at.z, at.y, at.w, at.g), self.part.at[:, self.cols(at.g)]
        for dz in range(1, self.nz):
            to = at.up(dz)
            self.post(here, self.zs.at[to], self.zr.at[at.z], at.at(z=to), source)
        self.post(here, self.ys.at[at.z], self.yr.at[at.z], at.over(), source)
        k = self.w_sem(at.z, at.y, None)
        self.post(self.spot(at.z, at.y, at.w), self.ws.at[k], self.wr.at[k], at.mate(), self.part.at[:, self.cols()])

    def after_z(self):
        at = self.at
        for dz in range(1, self.nz):
            z = at.down(dz)
            view = self.spot(z, at.y, at.w, at.g)
            push(view, view, self.zs.at[z], self.zr.at[z], at.at(z=z)).wait_recv()
            self.to_y(z)
            self.to_x(z, at.y)
            self.to_w(z, at.y, at.g)

    def after_y(self):
        at = self.at
        for dz in range(self.nz):
            z = at.down(dz)
            view = self.spot(z, 1 - at.y, at.w, at.g)
            push(view, view, self.ys.at[z], self.yr.at[z], at.over()).wait_recv()
            self.to_x(z, 1 - at.y)
            self.to_w(z, 1 - at.y, at.g)

    def others(self):
        for dy in range(2):
            for dz in range(self.nz):
                yield self.at.down(dz), lax.rem(self.at.y + dy, 2), dy == 0 and dz == 0

    def after_x(self):
        at = self.at
        if not self.split:
            return
        for z, y, own in self.others():
            if not own:
                k = z * 2 + y
                view = self.spot(z, y, at.w, 1 - at.g)
                push(view, view, self.xs.at[k], self.xr.at[k], at.twin()).wait_recv()
                self.to_w(z, y, 1 - at.g)

    def end(self):
        at = self.at
        self.local.wait()
        for z, y, own in self.others():
            for side in range(2 if self.split and not own else 1):
                k = self.w_sem(z, y, side)
                view = self.spot(z, y, 1 - at.w, None if own else side)
                push(view, view, self.ws.at[k], self.wr.at[k], at.mate()).wait_recv()

    def close(self):
        for copy in self.sent:
            copy.wait_send()


class Reduce:
    COUNT = 16

    @staticmethod
    def scratch(nz, r, wide, kind, dtype, part=True):
        cols = wide // 2 if kind == "x" else wide
        dma = pltpu.SemaphoreType.DMA
        vmem = pltpu.VMEM
        none = vmem((1, 16, 128), dtype)
        return [
            vmem((nz, 2, 2, r, wide), dtype) if part else none,
            vmem((nz, 2, r, wide), dtype),
            vmem((nz, 2, r, cols), dtype) if kind == "x" else none,
            vmem((nz, r, cols), dtype),
            vmem((nz, r, cols), dtype),
            vmem((2, r, cols), dtype) if kind != "none" else none,
        ] + [dma((1,))] * 6 + [dma((nz,))] * 2 + [dma((1,))] * 2

    def __init__(self, at, out, refs, kind):
        self.at, self.nz, self.out, self.kind = at, at.nz, out, kind
        self.part_cols = None
        (self.part, self.wb, self.xb, self.yb, self.zb, self.fb) = refs[:6]
        (self.ws, self.wr, self.xs, self.xr, self.ys, self.yr, self.zs, self.zr, self.fs, self.fr) = refs[6:]
        self.wide = self.wb.shape[-1]
        self.local_part = None

    def c_w(self):
        at = self.at
        src = self.part.at[:, :, 1 - at.w]
        if self.part_cols is not None:
            src = self.part.at[:, :, 1 - at.w, :, self.part_cols]
        return push(src, self.wb, self.ws.at[0], self.wr.at[0], at.mate())

    def c_x(self):
        at = self.at
        src = self.wb.at[:, :, :, half(self.wide, 1 - at.g)]
        return push(src, self.xb, self.xs.at[0], self.xr.at[0], at.twin())

    def mid(self):
        return self.xb if self.kind == "x" else self.wb

    def c_y(self):
        at = self.at
        return push(self.mid().at[:, 1 - at.y], self.yb, self.ys.at[0], self.yr.at[0], at.over())

    def c_z(self, to):
        at = self.at
        return push(self.yb.at[to], self.zb.at[at.z], self.zs.at[to], self.zr.at[at.z], at.at(z=to))

    def c_zin(self, z):
        return push(self.yb.at[z], self.zb.at[z], self.zs.at[z], self.zr.at[z], self.at.at(z=z))

    def c_f(self):
        return push(self.fb.at[0], self.fb.at[1], self.fs.at[0], self.fr.at[0], self.at.twin())

    def send(self):
        self.c_w().start()

    def after_w(self):
        at = self.at
        self.c_w().wait_recv()

        def one(k, carry):
            z, y = k // 2, lax.rem(k, 2)
            here = self.part[z, y, at.w] if self.local_part is None else self.local_part[z, y, :, self.local_cols]
            self.wb[z, y] = (self.wb[z, y].astype(F32) + here.astype(F32)).astype(self.wb.dtype)
            return carry

        lax.fori_loop(0, 2 * self.nz, one, 0)
        if self.kind == "x":
            self.c_x().start()
        else:
            self.c_y().start()

    def after_x(self):
        if self.kind != "x":
            return
        self.c_x().wait_recv()

        def one(k, carry):
            z, y = k // 2, lax.rem(k, 2)
            total = self.xb[z, y].astype(F32) + self.wb[z, y, :, half(self.wide, self.at.g)].astype(F32)
            self.xb[z, y] = total.astype(self.xb.dtype)
            return carry

        lax.fori_loop(0, 2 * self.nz, one, 0)
        self.c_y().start()

    def after_y(self):
        at, nz = self.at, self.nz
        self.c_y().wait_recv()

        def one(z, carry):
            total = self.yb[z].astype(F32) + self.mid()[z, at.y].astype(F32)
            self.yb[z] = total.astype(self.yb.dtype)
            return carry

        lax.fori_loop(0, nz, one, 0)
        for dz in range(1, nz):
            self.c_z(at.up(dz)).start()

    def after_z(self):
        at, nz = self.at, self.nz
        for dz in range(1, nz):
            self.c_zin(at.up(dz)).wait_recv()
        total = self.yb[at.z].astype(F32)
        for dz in range(1, nz):
            total = total + self.zb[at.up(dz)].astype(F32)
        if self.kind == "x":
            self.out[:, half(self.wide, at.g)] = total
        else:
            self.out[...] = total
        if self.kind != "none":
            self.fb[0] = total.astype(self.fb.dtype)
            self.c_f().start()

    def end(self):
        at = self.at
        if self.kind != "none":
            self.c_f().wait_recv()
            other = self.fb[1].astype(F32)
            if self.kind == "x":
                self.out[:, half(self.wide, 1 - at.g)] = other
            else:
                self.out[...] = self.out[...] + other

    def close(self):
        at, nz = self.at, self.nz
        self.c_w().wait_send()
        if self.kind == "x":
            self.c_x().wait_send()
        self.c_y().wait_send()
        for dz in range(1, nz):
            self.c_z(at.up(dz)).wait_send()
        if self.kind != "none":
            self.c_f().wait_send()


class Total:
    COUNT = 3

    @staticmethod
    def scratch(nz, r, wide):
        dma = pltpu.SemaphoreType.DMA
        return [pltpu.VMEM((4 + nz, r, wide), F32), dma((4 + nz,)), dma((4 + nz,))]

    def __init__(self, at, refs):
        self.at, self.nz = at, at.nz
        self.buf, self.ss, self.rs = refs

    def hop(self, i):
        at = self.at
        to = (at.mate(), at.twin(), at.over())[i]
        return push(self.buf.at[0], self.buf.at[1 + i], self.ss.at[i], self.rs.at[i], to)

    def send(self):
        self.hop(0).start()

    def after(self, i):
        hop = self.hop(i)
        hop.wait_send()
        hop.wait_recv()
        self.buf[0] = self.buf[0] + self.buf[1 + i]
        if i < 2:
            self.hop(i + 1).start()
        else:
            for dz in range(1, self.nz):
                self.along(self.at.z, self.at.up(dz)).start()

    def along(self, source, to):
        base = 4
        return push(self.buf.at[0], self.buf.at[base + source], self.ss.at[base + to], self.rs.at[base + source], self.at.at(z=to))

    def end(self):
        total = None
        for dz in range(1, self.nz):
            z = self.at.up(dz)
            self.along(z, z).wait_recv()
            self.along(self.at.z, z).wait_send()
        self.buf[4 + self.at.z] = self.buf[0]
        total = self.buf[4]
        for z in range(1, self.nz):
            total = total + self.buf[4 + z]
        return total


def normed(hidden, gain):
    return hidden * lax.rsqrt(jnp.mean(hidden * hidden, axis=-1, keepdims=True) + EPSILON) * gain


def norm_back(hidden, gain, grad):
    scale = lax.rsqrt(jnp.mean(hidden * hidden, axis=-1, keepdims=True) + EPSILON)
    inner = jnp.mean(hidden * gain * grad, axis=-1, keepdims=True)
    rows = scale * gain * grad - hidden * (scale * scale * scale) * inner
    return rows, jnp.sum(grad * hidden * scale, axis=0, keepdims=True)


FRONT_PARTS = ("small", "k", "v", "q", "o", "cq", "ck", "cv", "co", "gate", "up", "down", "keys", "values")
FRONT_REST = 14
FRONT_PLAN = (
    ("small", "keys", "values",),
    dict(gate=2, up=2, down=3, keys=3, values=3),
    (
        ("down", 0), ("up", 0), ("values", 2), ("values", 0), ("keys", 2), ("k", 0), ("values", 1), ("down", 1),
        ("cq", 0), ("down", 2), ("gate", 1), ("keys", 0), ("small", 0), ("cv", 0), ("v", 0), ("co", 0), ("up", 1),
        ("q", 0), ("o", 0), ("gate", 0), ("keys", 1), ("ck", 0),
    ),
    (
        (0, 0), (1, 0), (5, 0), (0, 1), (7, 0), (0, 2), (1, 1), (8, 0), (0, 3), (5, 1), (9, 0), (1, 2), (7, 1),
        (10, 0), (5, 2), (8, 1), (12, 0), (7, 2), (9, 1), (1, 3), (13, 0), (8, 2), (10, 1), (14, 0), (9, 2), (5, 3),
        (12, 1), (15, 0), (10, 2), (13, 1), (16, 0), (7, 3), (12, 2), (14, 1), (17, 0), (12, 4), (5, 4), (8, 3),
        (13, 2), (14, 2), (15, 1), (4, 0), (11, 0), (16, 1), (9, 3), (15, 2), (17, 1), (18, 0), (10, 3), (4, 1),
        (16, 2), (19, 0), (20, 0), (17, 2), (13, 3), (11, 1), (4, 2), (14, 3), (18, 1), (21, 0), (14, 4), (2, 0),
        (19, 1), (3, 0), (6, 0), (11, 2), (18, 2), (15, 3), (20, 1), (21, 1), (19, 2), (16, 3), (17, 3), (2, 1),
        (17, 4), (20, 2), (21, 2), (3, 1), (18, 3), (2, 2), (6, 1), (3, 2), (19, 3), (6, 2), (21, 3), (0, 4), (1, 4),
        (2, 4), (3, 4), (4, 4), (6, 4), (7, 4), (8, 4), (9, 4), (10, 4), (11, 4), (13, 4), (15, 4), (16, 4), (18, 4),
        (19, 4), (20, 4), (21, 4),
    ),
)


def front_kernel(nz, unshared, chunked, order, steps, *refs):
    count = len(FRONT_PARTS)
    x_ref, ins, wholes, refs = refs[0], refs[1 : count - 1], refs[count - 1 : 2 * count - 1], refs[2 * count - 1 :]
    (q_ref, normed_ref, gains_ref), (wbuf, k_own, v_own, wsem), sems = refs[:3], refs[3:7], refs[7:]
    parts = dict(zip(FRONT_PARTS, tuple(ins) + (k_own, v_own)))
    wholes = dict(zip(FRONT_PARTS, wholes))
    at = Place(nz)
    at.greet()
    jobs = []
    for i, (name, chunk) in enumerate(order):
        mine = sems[Gather.COUNT * i : Gather.COUNT * (i + 1)]
        chunks = chunked.get(name, 1)
        job = Gather(at, parts[name], wholes[name], mine, name not in unshared, chunk, chunks)
        jobs.append(job)
        if name not in ("keys", "values"):
            job.place()
    at.met()
    width = x_ref.shape[1]

    def norm():
        every = wholes["small"]
        total = None
        for z in range(nz):
            for y in range(2):
                for w in range(2):
                    here = every[z, y, w].astype(F32)
                    total = here if total is None else total + here
        gains_ref[...] = total
        normed_ref[...] = normed(x_ref[...].astype(F32), total[4:5]).astype(BF16)

    def project(name, index, into):
        load = pltpu.make_async_copy(wholes[name], wbuf.at[index], wsem.at[index])
        load.start()
        load.wait()
        into[...] = mm(normed_ref[...], wbuf[index].reshape(width, -1), NN).astype(BF16)

    def finish(i):
        if order[i][0] not in ("small", "k", "v", "q"):
            jobs[i].end()
        jobs[i].close()

    def place(name):
        for entry, job in zip(order, jobs):
            if entry[0] == name:
                job.place()

    def follow(name):
        if name == "small":
            norm()
        elif name == "k":
            project(name, 0, k_own)
            place("keys")
        elif name == "v":
            project(name, 1, v_own)
            place("values")
        elif name == "q":
            project(name, 2, q_ref)

    stages = (Gather.send, Gather.after_z, Gather.after_y, Gather.after_x, Gather.end)
    rest = {}
    for count, (i, stage) in enumerate(steps):
        name, job = order[i][0], jobs[i]
        if stage == len(stages) - 1:
            if name not in ("small", "k", "v", "q"):
                continue
            job.end()
            follow(name)
        else:
            stages[stage](job)
        if stage == (3 if job.split else 2):
            rest[i] = count + FRONT_REST
        for j in [j for j, due in rest.items() if due <= count]:
            finish(j)
            del rest[j]
    for j in rest:
        finish(j)


def front(x, parts, nz, shards, collective_id=1, plan=FRONT_PLAN):
    hb = pl.BlockSpec(memory_space=pl.ANY)
    vm = pl.BlockSpec(memory_space=pltpu.VMEM)
    unshared, chunked, order, steps = plan
    rows, width = x.shape
    inner = parts[1].shape[1]
    shapes = [(nz, 2, 2) + part.shape for part in parts] + [(nz, 2, 2, rows, inner)] * 2
    scratch = [
        pltpu.VMEM((3,) + shapes[1], BF16), pltpu.VMEM((rows, inner), BF16), pltpu.VMEM((rows, inner), BF16),
        pltpu.SemaphoreType.DMA((3,)),
    ]
    for name, _ in order:
        scratch += Gather.scratch(nz, name not in unshared)
    return pl.pallas_call(
        functools.partial(front_kernel, nz, unshared, chunked, order, steps),
        name="front",
        out_shape=tuple([jax.ShapeDtypeStruct(s, BF16) for s in shapes])
        + (
            jax.ShapeDtypeStruct((rows, inner), BF16),
            jax.ShapeDtypeStruct((rows, width), BF16),
            jax.ShapeDtypeStruct(parts[0].shape, F32),
        ),
        in_specs=[vm] + [hb] * len(parts),
        out_specs=tuple([vm] + [hb] * (len(FRONT_PARTS) - 1) + [vm] * 3),
        scratch_shapes=scratch,
        compiler_params=pltpu.CompilerParams(
            collective_id=collective_id, has_side_effects=True, vmem_limit_bytes=BIG
        ),
    )(x, *parts)


BACK_OUT = ("gate", "up", "down", "co", "cq", "q", "o", "k", "v", "ck", "cv")
BACK_NONE = ("kv", "cross")
BACK_PLAN = (
    ("q",),
    dict(kv=4),
    (
        ("kv", 3), ("k", 0), ("co", 0), ("kv", 1), ("cq", 0), ("gate", 0), ("kv", 0), ("kv", 2), ("cross", 0),
        ("down", 0), ("up", 0), ("o", 0), ("v", 0), ("q", 0),
    ),
    (
        (0, 0), (2, 0), (3, 0), (4, 0), (5, 0), (0, 1), (6, 0), (2, 1), (7, 0), (3, 1), (8, 0), (4, 1), (9, 0),
        (2, 2), (0, 3), (5, 1), (10, 0), (4, 2), (6, 1), (7, 1), (3, 3), (8, 1), (11, 0), (0, 4), (0, 5), (2, 3),
        (13, 0), (4, 3), (9, 1), (3, 4), (3, 5), (10, 1), (6, 3), (2, 4), (5, 2), (11, 1), (13, 1), (4, 4), (7, 3),
        (6, 4), (6, 5), (8, 3), (9, 2), (7, 4), (7, 5), (5, 3), (1, 0), (12, 0), (8, 4), (8, 5), (13, 3), (1, 1),
        (12, 1), (5, 4), (10, 2), (9, 3), (13, 4), (11, 2), (10, 3), (1, 2), (9, 4), (11, 3), (1, 3), (12, 2),
        (10, 4), (11, 4), (12, 3), (2, 5), (4, 5), (5, 5), (9, 5), (13, 5), (10, 5), (11, 5), (1, 4), (12, 4),
        (1, 5), (12, 5),
    ),
)


def back_kind(name, late):
    return "none" if name in BACK_NONE else "late" if name in late else "x"


def back_kernel(nz, late, chunked, order, steps, *refs):
    (
        kvp, crossp, wq, wk, wv, wck, wcv, x_ref, gains_ref, gh_ref, gpart_ref, small_ref,
        n3, mixed, att, n2, attc, n1, gg, gu, go, g1, gcq, g2, dq,
    ) = refs[:25]
    refs = refs[25:]
    outs = dict(zip(BACK_OUT, refs[: len(BACK_OUT)]))
    gx_ref, genc_ref, total_ref = refs[len(BACK_OUT) : len(BACK_OUT) + 3]
    refs = refs[len(BACK_OUT) + 3 :]
    kvown, crown, low, wbuf, kvl, every, pairb, kls, wsem, psem = refs[:10]
    refs = refs[10:]
    outs["kv"], outs["cross"] = kvown, crown
    at = Place(nz)
    at.greet()
    jobs = []
    for i, (name, chunk) in enumerate(order):
        mine = list(refs[Reduce.COUNT * i : Reduce.COUNT * (i + 1)])
        chunks = chunked.get(name, 1)
        out = outs[name]
        if chunks > 1:
            wide = out.shape[-1] // chunks
            out = out.at[:, pl.ds(chunk * wide, wide)]
        job = Reduce(at, out, mine, back_kind(name, late))
        if name == "cross":
            job.part = crossp
        if name == "kv":
            job.part = kvp
            job.part_cols = pl.ds(chunk * wide, wide)
            job.local_part, job.local_cols = kvl, job.part_cols
        jobs.append(job)
    refs = refs[Reduce.COUNT * len(order) :]
    spread = Gather(at, low, every, refs[: Gather.COUNT], False)
    everyone = Total(at, refs[Gather.COUNT :])
    load_w = [pltpu.make_async_copy(src, wbuf.at[i], wsem.at[i]) for i, src in enumerate((wq, wk, wv))]
    load_c = [pltpu.make_async_copy(src, wbuf.at[3 + i], wsem.at[3 + i]) for i, src in enumerate((wck, wcv))]
    for copy in load_w + load_c:
        copy.start()
    kv_local = pltpu.make_async_copy(kvp.at[:, :, at.w], kvl, kls)
    kv_local.start()
    width = x_ref.shape[1]
    inner = dq.shape[1]

    def make(name, chunk, part):
        if name in BACK_NONE:
            return
        _, _, _, r, wide = part.shape
        if name in ("k", "v"):
            left, right = n1, kvl.at[0, 0, :, pl.ds(0 if name == "k" else inner, inner)]
        else:
            left, right = {
                "gate": (n3, gg), "up": (n3, gu), "down": (mixed, go), "o": (att, g1), "cq": (n2, gcq), "co": (attc, g2),
                "q": (n1, dq),
            }[name]
        take = 2 if r % 128 else 1
        tile = 512 if wide % 512 == 0 else wide // 2 if wide % 256 == 0 and wide > 256 else wide
        for first in range(0, nz, take):
            piece = left[:, first * 4 * r : (first + take) * 4 * r]
            for c in range(0, wide, tile):
                out = mm(piece, right[:, chunk * wide + c : chunk * wide + c + tile], TN).astype(BF16)
                part[first : first + take, :, :, :, c : c + tile] = out.reshape(take, 2, 2, r, tile)

    def after_cross():
        both = crown[...]
        low[...] = jnp.concatenate([both, jnp.zeros_like(both)], axis=0).astype(BF16)
        for copy in load_c:
            copy.wait()
        genc = mm(low[:, :inner], wbuf[3].reshape(width, inner), NT) + mm(low[:, inner:], wbuf[4].reshape(width, inner), NT)
        genc_ref[...] = genc[:8]
        spread.place()
        spread.send()

    def pair_copy():
        return push(pairb.at[0], pairb.at[1], psem.at[0], psem.at[1], at.twin())

    def cross_weights():
        spread.end()
        owned = pairb.shape[1]
        rows = small_ref.shape[0] * small_ref.shape[1]
        col = lax.broadcasted_iota(jnp.int32, (width, 128), 0)
        lane = lax.broadcasted_iota(jnp.int32, (width, 128), 1)
        pick = ((col == at.me * owned + lane) & (lane < owned)).astype(BF16)
        mine = mm(small_ref[...].reshape(rows, width), pick, NN).astype(BF16)
        total = mm(mine, every[...].reshape(rows, 2 * inner), TN)[:owned]
        pairb[0] = total.astype(BF16)
        pair_copy().start()
        outs["ck"][...] = total[:, :inner]
        outs["cv"][...] = total[:, inner:]

    def cross_end():
        pair_copy().wait_recv()
        outs["ck"][...] += pairb[1, :, :inner].astype(F32)
        outs["cv"][...] += pairb[1, :, inner:].astype(F32)
        pair_copy().wait_send()
        spread.close()

    def after_kv():
        for copy in load_w:
            copy.wait()
        grad = mm(dq[...], wbuf[0].reshape(width, inner), NT)
        grad = grad + mm(kvl[0, 0, :, :inner], wbuf[1].reshape(width, inner), NT)
        grad = grad + mm(kvl[0, 0, :, inner:], wbuf[2].reshape(width, inner), NT)
        rows, gain = norm_back(x_ref[...].astype(F32), gains_ref[4:5], grad)
        gx_ref[...] = gh_ref[...] + rows
        everyone.buf[0] = gpart_ref[...]
        everyone.buf[0, 0:1, :] = gain
        everyone.send()

    kv_jobs = [i for i, entry in enumerate(order) if entry[0] == "kv"]
    kv_seen = kv_ended = 0
    early = [i for i, stage in steps if stage == 0 and order[i][0] not in BACK_NONE + ("k", "v")][:2]
    for i in early:
        make(*order[i], jobs[i].part)
    at.met()
    kv_sent = 0
    hops, later = [], {}
    for count, (i, stage) in enumerate(steps):
        (name, chunk), job = order[i], jobs[i]
        if stage == 0:
            if i not in early:
                make(name, chunk, job.part)
            job.send()
        if stage == 1:
            if i in kv_jobs:
                kv_seen += 1
                if kv_seen == 1:
                    kv_local.wait()
            job.after_w()
        if stage == 2:
            job.after_x()
        if stage == 3:
            job.after_y()
        if stage == 4:
            job.after_z()
        if stage == 5:
            job.end()
            if name == "cross":
                after_cross()
                later = {count + 5: spread.after_z, count + 10: spread.after_y, count + 15: cross_weights}
            if i in kv_jobs:
                kv_ended += 1
                if kv_ended == len(kv_jobs):
                    kvl[0, 0] = kvown[...].astype(BF16)
        if stage == 0 and name in ("k", "v"):
            kv_sent += 1
            if kv_sent == 2:
                after_kv()
                hops = [count + 4, count + 8, count + 12]
        if count in hops:
            everyone.after(hops.index(count))
        if count in later:
            later.pop(count)()
    for count in sorted(later):
        later[count]()
    for i, count in enumerate(hops):
        if count >= len(steps):
            everyone.after(i)
    cross_end()
    total_ref[...] = everyone.end()
    for job in jobs:
        job.close()


def back_step(
    kv_part, cross_part, weights, x, gains, grad_hidden, gpart, small, acts, shapes, nz, collective_id=2,
    plan=BACK_PLAN,
):
    late, chunked, order, steps = plan
    hb = pl.BlockSpec(memory_space=pl.ANY)
    vm = pl.BlockSpec(memory_space=pltpu.VMEM)
    rows, width = x.shape
    inner = acts[-1].shape[1]
    dma = pltpu.SemaphoreType.DMA
    own = [jax.ShapeDtypeStruct(shapes[name], F32) for name in BACK_OUT]
    scratch = [
        pltpu.VMEM((rows, 2 * inner), F32),
        pltpu.VMEM((8, 2 * inner), F32),
        pltpu.VMEM((16, 2 * inner), BF16),
        pltpu.VMEM((5,) + weights[0].shape, BF16),
        pltpu.VMEM((nz, 2, rows, 2 * inner), BF16),
        pltpu.VMEM((nz, 2, 2, 16, 2 * inner), BF16),
        pltpu.VMEM((2,) + shapes["ck"][:1] + (2 * inner,), BF16),
        dma,
        dma((5,)),
        dma((2,)),
    ]
    shapes = dict(shapes, kv=(rows, 2 * inner), cross=(8, 2 * inner))
    for name, _ in order:
        r, wide = shapes[name]
        wide = wide // chunked.get(name, 1)
        held = name not in BACK_NONE
        scratch += Reduce.scratch(nz, r, wide, back_kind(name, late), F32 if name == "cross" else BF16, part=held)
    scratch += Gather.scratch(nz, False) + Total.scratch(nz, gpart.shape[0], width)
    return pl.pallas_call(
        functools.partial(back_kernel, nz, late, chunked, order, steps),
        name="back",
        out_shape=tuple(own)
        + (
            jax.ShapeDtypeStruct((rows, width), F32),
            jax.ShapeDtypeStruct((8, width), F32),
            jax.ShapeDtypeStruct(gpart.shape, F32),
        ),
        in_specs=[hb, vm] + [hb] * 5 + [vm] * (5 + len(acts)),
        out_specs=tuple([vm] * (len(own) + 3)),
        scratch_shapes=scratch,
        compiler_params=pltpu.CompilerParams(
            collective_id=collective_id, has_side_effects=True, vmem_limit_bytes=BIG
        ),
    )(kv_part, cross_part, *weights, x, gains, grad_hidden, gpart, small, *acts)


def closing_kernel(count, *refs):
    for source, target in zip(refs[:count], refs[count:]):
        target[...] = source[...]


def closing(arrays):
    vm = pl.BlockSpec(memory_space=pltpu.VMEM)
    count = len(arrays)
    return pl.pallas_call(
        functools.partial(closing_kernel, count),
        name="closing",
        out_shape=tuple(jax.ShapeDtypeStruct(a.shape, a.dtype) for a in arrays),
        in_specs=[vm] * count,
        out_specs=tuple([vm] * count),
    )(*arrays)


class Bag:
    def __init__(self, names, refs):
        for name, ref in zip(names, refs):
            setattr(self, name, ref)


def flat(ref):
    value = ref[...]
    return value.reshape(-1, value.shape[-1])


def unstack(pair_rows, low):
    rows = pair_rows.shape[0] // 2
    return jnp.where(low, pair_rows[:rows], pair_rows[rows:])


def every_encoded(small_ref, take):
    devices, block, width = small_ref.shape
    rows = devices * take
    row = lax.broadcasted_iota(jnp.int32, (rows, devices * block), 0)
    col = lax.broadcasted_iota(jnp.int32, (rows, devices * block), 1)
    pick = (col == (row // take) * block + lax.rem(row, take)).astype(BF16)
    return mm(pick, small_ref[...].reshape(devices * block, width), NN).astype(BF16)


def cross_forward(b, low):
    pairs = b.cq.shape[1] // 128
    for pair in range(pairs):
        lanes = slice(128 * pair, 128 * pair + 128)
        qm = stack_pair(b.cq[:, lanes], low)
        s = mm(qm, b.ckeys[:, lanes], NT)
        peak = jnp.max(s, axis=1, keepdims=True)
        log_total = peak + jnp.log(jnp.sum(jnp.exp(s - peak), axis=1, keepdims=True))
        p = jnp.exp(s - log_total)
        b.cprob[pair] = p
        b.attc[:, lanes] = unstack(mm(p.astype(BF16), b.cvals[:, lanes], NN), low).astype(BF16)


def cross_backward(b, gac, low, keys_each):
    pairs = b.cq.shape[1] // 128
    inner = b.cq.shape[1]
    owners = 4 * b.crossp.shape[0]
    b.crossp[...] = jnp.zeros_like(b.crossp)
    for pair in range(pairs):
        lanes = slice(128 * pair, 128 * pair + 128)
        qm = stack_pair(b.cq[:, lanes], low)
        dom = stack_pair(gac[:, lanes], low)
        p = b.cprob[pair]
        dp = mm(dom, b.cvals[:, lanes], NT)
        ds = (p * (dp - jnp.sum(p * dp, axis=1, keepdims=True))).astype(BF16)
        b.gcq[:, lanes] = unstack(mm(ds, b.ckeys[:, lanes], NN), low).astype(BF16)
        gk = mm(ds, qm, TN)
        gv = mm(p.astype(BF16), dom, TN)
        for owner in range(owners):
            rows = slice(keys_each * owner, keys_each * owner + keys_each)
            b.crossp[owner // 4, owner // 2 % 2, owner % 2, 0:keys_each, lanes] = gk[rows]
            b.crossp[owner // 4, owner // 2 % 2, owner % 2, 0:keys_each, 128 * pair + inner : 128 * pair + inner + 128] = gv[rows]


GELU_A = 0.7978845608028654
GELU_B = 0.044715


def gelu_parts(v):
    t = jnp.tanh(GELU_A * (v + GELU_B * v * v * v))
    value = 0.5 * v * (1.0 + t)
    slope = 0.5 * (1.0 + t) + 0.5 * v * (1.0 - t * t) * (GELU_A * (1.0 + 3.0 * GELU_B * v * v))
    return value, slope


FF_TILE = 512


def after_attention(b):
    b.h1[...] = b.x[...].astype(F32) + mm(b.att[...], flat(b.w_o), NN)
    b.n2[...] = normed(b.h1[...], b.gains[5:6]).astype(BF16)
    b.cq[...] = mm(b.n2[...], flat(b.w_cq), NN).astype(BF16)


def after_cross_attention(b):
    b.h2[...] = b.h1[...] + mm(b.attc[...], flat(b.w_co), NN)
    b.n3[...] = normed(b.h2[...], b.gains[6:7]).astype(BF16)


def feed_forward(b):
    ff = b.mixed.shape[1]
    width = b.x.shape[1]
    for c in range(0, ff, FF_TILE):
        cols = slice(c, c + FF_TILE)
        gate = mm(b.n3[...], b.w_gate[:, :, cols].reshape(width, FF_TILE), NN)
        up = mm(b.n3[...], b.w_up[:, :, cols].reshape(width, FF_TILE), NN)
        value, slope = gelu_parts(gate)
        b.mixed[:, cols] = (value * up).astype(BF16)
        b.hg[:, cols] = value
        b.hs[:, cols] = slope * up
    b.layer_out[...] = (b.h2[...] + mm(b.mixed[...], flat(b.w_down), NN)).astype(BF16)


def feed_backward(b):
    ff = b.mixed.shape[1]
    width = b.x.shape[1]
    down = flat(b.w_down)
    total = jnp.zeros(b.h2.shape, F32)
    for c in range(0, ff, FF_TILE):
        cols = slice(c, c + FF_TILE)
        gm = mm(b.go[...], down[cols], NT).astype(BF16).astype(F32)
        gg = (gm * b.hs[:, cols]).astype(BF16)
        gu = (gm * b.hg[:, cols]).astype(BF16)
        b.gg[:, cols] = gg
        b.gu[:, cols] = gu
        total = total + mm(gg, b.w_gate[:, :, cols].reshape(width, FF_TILE), NT)
        total = total + mm(gu, b.w_up[:, :, cols].reshape(width, FF_TILE), NT)
    rows, gain = norm_back(b.h2[...], b.gains[6:7], total)
    b.gpart[2:3, :] = gain
    b.gh[...] = b.go[...].astype(F32) + rows
    b.g2[...] = b.gh[...].astype(BF16)


def before_attention(b):
    rows, gain = norm_back(b.h1[...], b.gains[5:6], mm(b.gcq[...], flat(b.w_cq), NT))
    b.gpart[1:2, :] = gain
    b.gh[...] = b.gh[...] + rows
    b.g1[...] = b.gh[...].astype(BF16)
    b.gatt[...] = mm(b.g1[...], flat(b.w_o), NT).astype(BF16)


GROUP = 4


def stack_group(block):
    head = lax.broadcasted_iota(jnp.int32, block.shape, 1) // BLK
    zero = jnp.zeros_like(block)
    return jnp.concatenate([jnp.where(head == i, block, zero) for i in range(GROUP)], axis=0)


def unstack_group(stacked):
    rows = stacked.shape[0] // GROUP
    head = lax.broadcasted_iota(jnp.int32, (rows, stacked.shape[1]), 1) // BLK
    out = stacked[:rows]
    for i in range(1, GROUP):
        out = jnp.where(head == i, stacked[i * rows : i * rows + rows], out)
    return out


def fill_bias(b, qb, rank):
    pairs = b.q.shape[1] // 128
    key_j = lax.broadcasted_iota(jnp.int32, (CH, 128), 0)
    lane_i = lax.broadcasted_iota(jnp.int32, (CH, 128), 1)
    high = lane_i >= BLK
    row_i = jnp.where(high, lane_i - BLK, lane_i)
    shift = jnp.where(high, BLK, 0)
    for kind in range(2):
        dist = (lax.rem(rank, 4) + 4 * kind) * BLK + row_i - key_j
        bucket = bucket_ids(jnp.maximum(dist, 0)) + shift
        for pair in range(pairs):
            tile = jnp.take_along_axis(jnp.broadcast_to(b.tb[pl.ds(pair, 1), :], (CH, 128)), bucket, axis=1)
            if kind == 0:
                tile = jnp.where(dist >= 0, tile, MASKED)
            b.bias[qb, kind, pair // 2, :, 128 * (pair % 2) : 128 * (pair % 2) + 128] = tile
    for pair in range(pairs):
        b.bias[qb, 2, pair // 2, :, 128 * (pair % 2) : 128 * (pair % 2) + 128] = jnp.where(
            high,
            b.tb[pl.ds(pair, 1), pl.ds(BLK + BUCKETS - 1, 1)],
            b.tb[pl.ds(pair, 1), pl.ds(BUCKETS - 1, 1)],
        )


def self_forward_block(b, qb, rank):
    inner = b.q.shape[1]
    wide = GROUP * BLK
    groups = inner // wide
    last = rank // 4
    mine = pl.ds(qb * BLK, BLK)
    for i in range(groups):
        b.qm[qb, i] = stack_group(b.q[mine, wide * i : wide * i + wide])
        b.top[i] = jnp.full((8, wide), -3e38, F32)
        b.sums[i] = jnp.zeros((8, wide), F32)
        b.acc[i] = jnp.zeros((wide, wide), F32)

    def first(chunk, carry):
        kind = jnp.minimum(last - chunk, 2)
        keys = pl.ds(pl.multiple_of(chunk * CH, CH), CH)
        for i in range(groups):
            s = mm(b.kvs[keys, wide * i : wide * i + wide], b.qm[qb, i], NT) + b.bias[qb, kind, i]
            b.sco[i, keys, :] = s
            b.top[i] = jnp.maximum(b.top[i], jnp.max(s.reshape(CH // 8, 8, wide), axis=0))
        return carry

    lax.fori_loop(0, last + 1, first, 0)
    for i in range(groups):
        b.top[i] = jnp.broadcast_to(jnp.max(b.top[i], axis=0, keepdims=True), (8, wide))

    def second(chunk, carry):
        keys = pl.ds(pl.multiple_of(chunk * CH, CH), CH)
        for i in range(groups):
            p = jnp.exp(b.sco[i, keys, :] - b.top[i, 0:1, :])
            b.sums[i] += jnp.sum(p.reshape(CH // 8, 8, wide), axis=0)
            values = b.kvs[keys, inner + wide * i : inner + wide * i + wide]
            b.acc[i] += mm(p.astype(BF16), values, TN)
        return carry

    lax.fori_loop(0, last + 1, second, 0)
    for i in range(groups):
        total = jnp.sum(b.sums[i], axis=0, keepdims=True)
        b.rows[qb, i, 0:1, :] = b.top[i, 0:1, :] + jnp.log(total)
        parts = []
        for side in range(wide // 128):
            scale = jnp.broadcast_to(total[:, 128 * side : 128 * side + 128], (128, 128)).T
            rows = b.acc[i, 128 * side : 128 * side + 128, :]
            parts.append(rows / jnp.concatenate([scale] * (wide // 128), axis=1))
        out = unstack_group(jnp.concatenate(parts, axis=0))
        b.att32[mine, wide * i : wide * i + wide] = out
        b.att[mine, wide * i : wide * i + wide] = out.astype(BF16)


def self_backward_rows(b, qb):
    inner = b.q.shape[1]
    wide = GROUP * BLK
    mine = pl.ds(qb * BLK, BLK)
    for i in range(inner // wide):
        b.dom[qb, i] = stack_group(b.gatt[mine, wide * i : wide * i + wide])
    for pair in range(inner // 128):
        lanes = slice(128 * pair, 128 * pair + 128)
        prod = (b.gatt[mine, lanes].astype(F32) * b.att32[mine, lanes]).T
        b.rows[qb, pair // 2, 1:2, 128 * (pair % 2) : 128 * (pair % 2) + 128] = jnp.concatenate(
            [jnp.sum(prod[:BLK], axis=0, keepdims=True), jnp.sum(prod[BLK:], axis=0, keepdims=True)], axis=1
        )


def self_backward_block(b, qb, rank, longer):
    inner = b.q.shape[1]
    wide = GROUP * BLK
    groups = inner // wide
    last = rank // 4
    b.acc[...] = jnp.zeros_like(b.acc)

    @pl.when(last == 0)
    def _():
        for i in range(groups):
            b.near[i, pl.ds(0, CH), :] = jnp.zeros((CH, wide), F32)

    def step(chunk, carry):
        kind = jnp.minimum(last - chunk, 2)
        keys = pl.ds(pl.multiple_of(chunk * CH, CH), CH)
        keep = jnp.maximum(chunk - last + 1, 0)
        for i in range(groups):
            klanes = slice(wide * i, wide * i + wide)
            vlanes = slice(inner + wide * i, inner + wide * i + wide)
            kp = b.kvs[keys, klanes]
            qp = b.qm[qb, i]
            gp = b.dom[qb, i]
            st = mm(kp, qp, NT) + b.bias[qb, kind, i]
            pt = jnp.exp(st - b.rows[qb, i, 0:1, :])
            dp = mm(b.kvs[keys, vlanes], gp, NT)
            ds = pt * (dp - b.rows[qb, i, 1:2, :])
            dsb = ds.astype(BF16)
            gv = mm(pt.astype(BF16), gp, NN)
            gk = mm(dsb, qp, NN)
            b.dkv[keys, vlanes] = gv if longer else b.dkv[keys, vlanes] + gv
            b.dkv[keys, klanes] = gk if longer else b.dkv[keys, klanes] + gk
            b.acc[i] += mm(dsb, kp, TN)
            b.tot[i] += jnp.sum(ds.reshape(CH // 8, 8, wide), axis=0)
            b.near[i, pl.ds(pl.multiple_of(keep * CH, CH), CH), :] = ds
        return carry

    lax.fori_loop(0, last + 1, step, 0)
    if longer:

        def unseen(chunk, carry):
            keys = pl.ds(pl.multiple_of(chunk * CH, CH), CH)
            b.dkv[keys, :] = jnp.zeros((CH, 2 * inner), F32)
            return carry

        lax.fori_loop(last + 1, b.dkv.shape[0] // CH, unseen, 0)
    mine = pl.ds(pl.multiple_of(qb * BLK, BLK), BLK)
    for i in range(groups):
        b.dq[mine, wide * i : wide * i + wide] = unstack_group(b.acc[i]).astype(BF16)
        for gap in range(3):
            offset = pl.multiple_of((rank - gap - 4 * (last - 1)) * BLK, BLK)
            b.nacc[gap, i] += b.near[i, pl.ds(offset, BLK), :]


def bias_gradient(b):
    pairs = b.q.shape[1] // 128
    key_s = lax.broadcasted_iota(jnp.int32, (BLK, 128), 0)
    lane = lax.broadcasted_iota(jnp.int32, (BLK, 128), 1)
    row_s = jnp.where(lane < BLK, lane, lane - BLK)
    buckets = [bucket_ids(jnp.maximum(gap * BLK + row_s - key_s, 0)) for gap in range(3)]
    for pair in range(pairs):
        lanes = slice(128 * (pair % 2), 128 * (pair % 2) + 128)
        tiles = [b.nacc[gap, pair // 2, :, lanes] for gap in range(3)]
        far = jnp.sum(b.tot[pair // 2, :, lanes], axis=0, keepdims=True)
        for tile in tiles:
            far = far - jnp.sum(tile, axis=0, keepdims=True)
        lines = []
        for number in range(BUCKETS):
            part = jnp.where(buckets[0] == number, tiles[0], 0.0)
            for gap in range(1, 3):
                part = part + jnp.where(buckets[gap] == number, tiles[gap], 0.0)
            line = jnp.sum(part, axis=0, keepdims=True)
            lines.append(line + far if number == BUCKETS - 1 else line)
        grid = jnp.concatenate(lines + [jnp.zeros((128 - BUCKETS, 128), F32)], axis=0).T
        b.gpart[8 + 2 * pair : 9 + 2 * pair, 0:128] = jnp.sum(grid[:BLK], axis=0, keepdims=True)
        b.gpart[9 + 2 * pair : 10 + 2 * pair, 0:128] = jnp.sum(grid[BLK:], axis=0, keepdims=True)


MID_IN = (
    "deal", "k_hbm", "v_hbm", "o", "cq_w", "ck", "cv", "co", "gate", "up", "down", "x", "gains", "small", "q", "go", "tb",
)
MID_OUT = (
    "layer_out", "n3", "mixed", "att", "n2", "attc", "gg", "gu", "g1", "gcq", "g2", "dq", "gh", "gpart", "crossp", "dkv_hbm",
)
MID_SCRATCH = (
    "kvs", "dkv", "w_o", "w_cq", "w_ck", "w_cv", "w_co", "w_gate", "w_up", "w_down", "h1", "h2", "cq", "ckeys", "cvals", "cprob",
    "hg", "hs", "gatt", "bias", "qm", "dom", "top", "sums", "acc", "sco", "rows", "att32", "near", "nacc", "tot", "sem", "osem", "wsem",
)


def mid_kernel(enc_own, *refs):
    b = Bag(MID_IN + MID_OUT + MID_SCRATCH, refs)
    load_in_order(b.deal, b.k_hbm, b.v_hbm, b.kvs, b.sem)
    loads = []
    for i, name in enumerate(("o", "cq", "ck", "cv", "co", "gate", "up", "down")):
        source = b.cq_w if name == "cq" else getattr(b, name)
        loads.append(pltpu.make_async_copy(source, getattr(b, "w_" + name), b.wsem.at[i]))
        loads[-1].start()
    low = lax.broadcasted_iota(jnp.int32, (2 * BLK, 128), 1) < BLK
    device = lax.axis_index(AXES)
    ranks = [b.deal[device, qb] for qb in range(2)]
    for qb in range(2):
        fill_bias(b, qb, ranks[qb])
    loaded(b.k_hbm, b.v_hbm, b.kvs, b.sem)
    for qb in range(2):
        self_forward_block(b, qb, ranks[qb])
    for load in loads[:5]:
        load.wait()
    after_attention(b)
    enc = every_encoded(b.small, enc_own)
    b.ckeys[...] = mm(enc, flat(b.w_ck), NN).astype(BF16)
    b.cvals[...] = mm(enc, flat(b.w_cv), NN).astype(BF16)
    cross_forward(b, low)
    after_cross_attention(b)
    for load in loads[5:]:
        load.wait()
    feed_forward(b)
    b.gpart[...] = jnp.zeros_like(b.gpart)
    feed_backward(b)
    gac = mm(b.g2[...], flat(b.w_co), NT).astype(BF16)
    cross_backward(b, gac, low, enc_own)
    before_attention(b)
    b.tot[...] = jnp.zeros_like(b.tot)
    b.nacc[...] = jnp.zeros_like(b.nacc)
    for qb in range(2):
        self_backward_rows(b, qb)
    longer = jnp.where(ranks[0] > ranks[1], 0, 1)
    self_backward_block(b, longer, jnp.maximum(ranks[0], ranks[1]), True)
    self_backward_block(b, 1 - longer, jnp.minimum(ranks[0], ranks[1]), False)
    blocks = b.k_hbm.shape[0] // BLK

    def out_one(index, carry):
        here = pl.ds(pl.multiple_of(b.deal[index // 2, index % 2] * BLK, BLK), BLK)
        b.kvs[here, :] = b.dkv[here, :].astype(BF16)
        pltpu.make_async_copy(b.kvs.at[here], b.dkv_hbm.at[pl.ds(index * BLK, BLK)], b.osem).start()
        return carry

    lax.fori_loop(0, blocks, out_one, 0)
    bias_gradient(b)
    pltpu.make_async_copy(b.kvs, b.dkv_hbm, b.osem).wait()


def mid(deal, keys, values, weights, x, gains, small, q, go, tb, enc_own):
    rows, width = x.shape
    inner = q.shape[1]
    total = keys.shape[0]
    ff = weights[5].shape[2]
    wide = GROUP * BLK
    h2, h4 = inner // 128, inner // wide
    shards = weights[0].shape[0]
    enc = shards * enc_own
    sm = pl.BlockSpec(memory_space=pltpu.SMEM)
    vm = pl.BlockSpec(memory_space=pltpu.VMEM)
    hb = pl.BlockSpec(memory_space=pl.ANY)
    out = jax.ShapeDtypeStruct
    return pl.pallas_call(
        functools.partial(mid_kernel, enc_own),
        name="mid",
        out_shape=(
            out((rows, width), BF16), out((rows, width), BF16), out((rows, ff), BF16), out((rows, inner), BF16),
            out((rows, width), BF16), out((rows, inner), BF16), out((rows, ff), BF16), out((rows, ff), BF16),
            out((rows, width), BF16), out((rows, inner), BF16), out((rows, width), BF16), out((rows, inner), BF16),
            out((rows, width), F32), out((24, width), F32), out((shards // 4, 2, 2, 8, 2 * inner), F32),
            out((total, 2 * inner), BF16),
        ),
        in_specs=[sm] + [hb] * (2 + len(weights)) + [vm] * 6,
        out_specs=tuple([vm] * 15 + [hb]),
        scratch_shapes=[
            pltpu.VMEM((total, 2 * inner), BF16),
            pltpu.VMEM((total, 2 * inner), F32),
        ]
        + [pltpu.VMEM(weight.shape, BF16) for weight in weights]
        + [
            pltpu.VMEM((rows, width), F32),
            pltpu.VMEM((rows, width), F32),
            pltpu.VMEM((rows, inner), BF16),
            pltpu.VMEM((enc, inner), BF16),
            pltpu.VMEM((enc, inner), BF16),
            pltpu.VMEM((h2, 2 * rows, enc), F32),
            pltpu.VMEM((rows, ff), F32),
            pltpu.VMEM((rows, ff), F32),
            pltpu.VMEM((rows, inner), BF16),
            pltpu.VMEM((2, 3, h4, CH, wide), F32),
            pltpu.VMEM((2, h4, wide, wide), BF16),
            pltpu.VMEM((2, h4, wide, wide), BF16),
            pltpu.VMEM((h4, 8, wide), F32),
            pltpu.VMEM((h4, 8, wide), F32),
            pltpu.VMEM((h4, wide, wide), F32),
            pltpu.VMEM((h4, total, wide), F32),
            pltpu.VMEM((2, h4, 8, wide), F32),
            pltpu.VMEM((rows, inner), F32),
            pltpu.VMEM((h4, 2 * CH, wide), F32),
            pltpu.VMEM((3, h4, BLK, wide), F32),
            pltpu.VMEM((h4, 8, wide), F32),
            pltpu.SemaphoreType.DMA((2,)),
            pltpu.SemaphoreType.DMA,
            pltpu.SemaphoreType.DMA((8,)),
        ],
        compiler_params=pltpu.CompilerParams(vmem_limit_bytes=BIG),
    )(deal, keys, values, *weights, x, gains, small, q, go, tb)


def fits(*operands):
    layer_in, encoded, self_query, relative_bias = operands[0], operands[1], operands[4], operands[18]
    total = layer_in.shape[1] * lax.axis_size(AXES)
    return (
        lax.axis_size(GRP) == 2
        and lax.axis_size(WSH) == 2
        and lax.axis_size(CTX) == 8
        and layer_in.shape[1] == 2 * BLK
        and encoded.shape[1] == 4
        and total // 2 <= CONT_TOK
        and self_query.shape[0] % 16 == 0
        and self_query.shape[1] == relative_bias.shape[1] * BLK
        and self_query.shape[1] % 256 == 0
    )


def fast(
    layer_in, encoded, cotangent, deal_table, self_query, self_key, self_value, self_output, cross_query, cross_key,
    cross_value, cross_output, feed_gate, feed_up, feed_down, gain_self, gain_cross, gain_feed, relative_bias,
):
    nz = lax.axis_size(CTX) // 2
    shards = lax.axis_size(AXES)
    device = lax.axis_index(AXES)
    rows = layer_in.shape[1]
    width = layer_in.shape[2]
    heads = relative_bias.shape[1]
    inner = self_query.shape[1]
    owned = gain_self.shape[0]
    enc_own = encoded.shape[1]
    table_hb = relative_bias.astype(F32).T

    gains_here = lax.dynamic_update_slice(
        jnp.zeros((3, width), BF16), jnp.stack([gain_self, gain_cross, gain_feed]), (0, device * owned)
    )
    small = jnp.concatenate([encoded[0], gains_here, jnp.zeros((9, width), BF16)], axis=0)
    *wholes, queries, normed_one, gains = front(
        layer_in[0],
        (
            small, self_key, self_value, self_query, self_output, cross_query, cross_key, cross_value, cross_output,
            feed_gate, feed_up, feed_down,
        ),
        nz,
        shards,
    )
    whole = {name: value.reshape((shards,) + value.shape[3:]) for name, value in zip(FRONT_PARTS, wholes)}
    in_rows = {name: value.reshape(-1, value.shape[-1]) for name, value in whole.items()}
    (
        layer_out, normed_three, mixed_hidden, attended, normed_two, attended_cross, grad_gate, grad_up, grad_one_low,
        grad_cq_low, grad_two_low, grad_queries, grad_hidden_one, gpart, cross_part, kv_part,
    ) = mid(
        deal_table, in_rows["keys"], in_rows["values"],
        [whole[name] for name in ("o", "cq", "ck", "cv", "co", "gate", "up", "down")],
        layer_in[0], gains, whole["small"], queries, cotangent[0], pair_table(table_hb), enc_own,
    )
    ff = feed_gate.shape[1]
    square = (owned, inner)
    shapes = dict(
        gate=(owned, ff), up=(owned, ff), down=(feed_down.shape[0], width), co=(inner // shards, width), cq=square,
        ck=square, cv=square, q=square, o=(inner // shards, width), k=square, v=square,
    )
    result = back_step(
        kv_part.reshape(nz, 2, 2, rows, 2 * inner), cross_part,
        [whole[name] for name in ("q", "k", "v", "ck", "cv")], layer_in[0], gains,
        grad_hidden_one, gpart, whole["small"],
        (
            normed_three, mixed_hidden, attended, normed_two, attended_cross, normed_one, grad_gate, grad_up, cotangent[0],
            grad_one_low, grad_cq_low, grad_two_low, grad_queries,
        ),
        shapes,
        nz,
    )
    grad_enc, total = result[len(BACK_OUT) + 1 :]
    result = closing(result[: len(BACK_OUT) + 1])
    got = dict(zip(BACK_OUT, result))
    grad_input = result[len(BACK_OUT)]
    gain_grads = [lax.dynamic_slice_in_dim(total[i], device * owned, owned) for i in range(3)]
    grad_relative_bias = total[8 : 8 + heads, :BUCKETS].T
    return (
        layer_out[None], grad_input[None], grad_enc[None, :enc_own],
        got["q"], got["k"], got["v"], got["o"], got["cq"], got["ck"], got["cv"], got["co"], got["gate"], got["up"], got["down"],
        gain_grads[0], gain_grads[1], gain_grads[2], grad_relative_bias,
    )


def solution(mesh):
    return jax.shard_map(
        lambda *operands: (fast if fits(*operands) else local)(*operands),
        mesh=mesh,
        in_specs=(
            P(GRP, AXES, None),
            P(GRP, AXES, None),
            P(GRP, AXES, None),
            P(),
            P(AXES, None),
            P(AXES, None),
            P(AXES, None),
            P(AXES, None),
            P(AXES, None),
            P(AXES, None),
            P(AXES, None),
            P(AXES, None),
            P(AXES, None),
            P(AXES, None),
            P(AXES, None),
            P(AXES),
            P(AXES),
            P(AXES),
            P(),
        ),
        out_specs=(
            P(GRP, AXES, None),
            P(GRP, AXES, None),
            P(GRP, AXES, None),
            P(AXES, None),
            P(AXES, None),
            P(AXES, None),
            P(AXES, None),
            P(AXES, None),
            P(AXES, None),
            P(AXES, None),
            P(AXES, None),
            P(AXES, None),
            P(AXES, None),
            P(AXES, None),
            P(AXES),
            P(AXES),
            P(AXES),
            P(),
        ),
        check_vma=False,
    )
```

```python
import functools
import math

import jax
import jax.numpy as jnp
from jax import lax
from jax.experimental import pallas as pl
from jax.experimental.pallas import tpu as pltpu
from jax.sharding import PartitionSpec as P

GRP, CTX, WSH = "grp", "ctx", "wsh"
AXES = (CTX, WSH)
EVERY = (GRP, CTX, WSH)
QK = "qhd,khd->hqk"
PV = "hqk,khd->qhd"
PTQ = "hqk,qhd->khd"
TF_TD = "tf,td->fd"
TD_FD = "td,fd->tf"
TD_TF = "td,tf->df"
TF_DF = "tf,df->td"
TC_TD = "tc,td->cd"
TD_CD = "td,cd->tc"
TD_TC = "td,tc->dc"
TC_DC = "tc,dc->td"

BUCKETS = 32
MAXDIST = 128
CONT_TOK = 2048


MASKED = -1e30
EPSILON = 1e-06


def rms_norm(hidden, gain_vector):
    return (
        hidden
        * lax.rsqrt(jnp.mean(hidden * hidden, axis=-1, keepdims=True) + EPSILON)
        * gain_vector
    )


def gated(gate_pre, up_pre):
    return jax.nn.gelu(gate_pre, approximate=True) * up_pre


def bounce(values):
    return lax.optimization_barrier(values.astype(jnp.bfloat16)).astype(jnp.float32)


def split_probs(probs_full):
    probs_high = probs_full.astype(jnp.bfloat16)
    probs_rest = (probs_full - probs_high.astype(jnp.float32)).astype(jnp.bfloat16)
    return (probs_high, probs_rest)


def bucket_ids(distance):
    exact_half = BUCKETS // 2
    counted = jnp.minimum(distance, exact_half)
    for number in range(1, exact_half):
        boundary = int(math.ceil(exact_half * math.pow(MAXDIST / exact_half, number / exact_half)))
        counted = counted + (distance >= boundary).astype(jnp.int32)
    return counted


def token_place(tokens, prompt_len, cont_len):
    beyond = tokens - prompt_len
    in_prompt = tokens < prompt_len
    sequence = jnp.where(in_prompt, 0, 1 + beyond // cont_len)
    position = jnp.where(in_prompt, tokens, prompt_len + beyond % cont_len)
    return (sequence, position)


def pair_mask(seq_query, pos_query, seq_key, pos_key):
    earlier = pos_key[None, :] <= pos_query[:, None]
    visible = (seq_key[None, :] == seq_query[:, None]) | (seq_key[None, :] == 0)
    return earlier & visible


def bucket_bias(pos_query, pos_key, table_hb):
    buckets = bucket_ids(jnp.maximum(pos_query[:, None] - pos_key[None, :], 0))
    picks = (
        buckets[None, :, :, None]
        == jnp.arange(table_hb.shape[1], dtype=jnp.int32)[None, None, None, :]
    )
    return (buckets, jnp.sum(jnp.where(picks, table_hb[:, None, None, :], 0.0), axis=-1))


def bucket_grad(buckets, grad_scores, bucket_count):
    picks = (
        buckets[None, :, :, None] == jnp.arange(bucket_count, dtype=jnp.int32)[None, None, None, :]
    )
    return jnp.sum(
        jnp.where(picks, grad_scores.astype(jnp.float32)[:, :, :, None], 0.0), axis=(1, 2)
    )


def masked_scores(query_heads, key_heads, bias, allowed):
    direct = jnp.einsum(QK, query_heads, key_heads, preferred_element_type=jnp.float32)
    return jnp.where(allowed[None], direct + bias, MASKED)


def score_grads(scores, log_total, delta_row, grad_heads, value_heads):
    probs_full = jnp.exp(scores - log_total[:, :, None])
    grad_probs = jnp.einsum(
        QK, grad_heads, value_heads, preferred_element_type=jnp.float32
    )
    grad_scores = (probs_full * (grad_probs - delta_row[:, :, None])).astype(jnp.bfloat16)
    return (probs_full.astype(jnp.bfloat16), grad_scores)


def key_view(seq_all, pos_all, step_index, key_rows, seq_query, pos_query):
    seq_key = lax.dynamic_slice_in_dim(seq_all, step_index * key_rows, key_rows)
    pos_key = lax.dynamic_slice_in_dim(pos_all, step_index * key_rows, key_rows)
    return (pos_key, pair_mask(seq_query, pos_query, seq_key, pos_key))


def self_forward(
    query_heads, key_heads, value_heads, seq_all, pos_all, seq_query, pos_query, table_hb, key_rows
):
    total_rows = key_heads.shape[0]
    head_count = query_heads.shape[1]
    rows_here = query_heads.shape[0]
    step_list = jnp.arange(total_rows // key_rows, dtype=jnp.int32)

    def total_step(carried, step_index):
        pos_key, allowed = key_view(seq_all, pos_all, step_index, key_rows, seq_query, pos_query)

        def total_accumulate(current):
            running_max, running_sum = current
            key_block = lax.dynamic_slice_in_dim(key_heads, step_index * key_rows, key_rows)
            bias = bucket_bias(pos_query, pos_key, table_hb)[1]
            scores = masked_scores(query_heads, key_block, bias, allowed)
            new_max = jnp.maximum(running_max, jnp.max(scores, axis=-1))
            weights = jnp.where(allowed[None], jnp.exp(scores - new_max[:, :, None]), 0.0)
            return (
                new_max,
                running_sum * jnp.exp(running_max - new_max) + jnp.sum(weights, axis=-1),
            )

        return (
            lax.cond(jnp.any(allowed), total_accumulate, lambda current: current, carried),
            None,
        )

    start_state = (
        jnp.full((head_count, rows_here), MASKED, jnp.float32),
        jnp.zeros((head_count, rows_here), jnp.float32),
    )
    (running_max, running_sum), _ = lax.scan(total_step, start_state, step_list)
    log_total = running_max + jnp.log(running_sum)

    def output_step(carried, step_index):
        pos_key, allowed = key_view(seq_all, pos_all, step_index, key_rows, seq_query, pos_query)

        def output_accumulate(current):
            rounded_sum, rest_sum = current
            key_block = lax.dynamic_slice_in_dim(key_heads, step_index * key_rows, key_rows)
            value_block = lax.dynamic_slice_in_dim(value_heads, step_index * key_rows, key_rows)
            bias = bucket_bias(pos_query, pos_key, table_hb)[1]
            scores = masked_scores(query_heads, key_block, bias, allowed)
            probs_high, probs_rest = split_probs(jnp.exp(scores - log_total[:, :, None]))
            rounded_sum = rounded_sum + jnp.einsum(
                PV, probs_high, value_block, preferred_element_type=jnp.float32
            )
            rest_sum = rest_sum + jnp.einsum(
                PV, probs_rest, value_block, preferred_element_type=jnp.float32
            )
            return (rounded_sum, rest_sum)

        return (
            lax.cond(jnp.any(allowed), output_accumulate, lambda current: current, carried),
            None,
        )

    zero_heads = jnp.zeros(query_heads.shape, jnp.float32)
    (rounded_sum, rest_sum), _ = lax.scan(output_step, (zero_heads, zero_heads), step_list)
    return (log_total, rounded_sum, rounded_sum + rest_sum)


def query_backward(
    query_heads,
    key_heads,
    value_heads,
    grad_heads,
    log_total,
    delta_row,
    seq_all,
    pos_all,
    seq_query,
    pos_query,
    table_hb,
    key_rows,
):
    total_rows = key_heads.shape[0]
    inner_width = key_heads.shape[1] * key_heads.shape[2]
    bucket_count = table_hb.shape[1]
    step_list = jnp.arange(total_rows // key_rows, dtype=jnp.int32)

    def step_body(carried, step_index):
        pos_key, allowed = key_view(seq_all, pos_all, step_index, key_rows, seq_query, pos_query)

        def step_accumulate(current):
            grad_query, grad_bias = current
            key_block = lax.dynamic_slice_in_dim(key_heads, step_index * key_rows, key_rows)
            value_block = lax.dynamic_slice_in_dim(value_heads, step_index * key_rows, key_rows)
            buckets, bias = bucket_bias(pos_query, pos_key, table_hb)
            scores = masked_scores(query_heads, key_block, bias, allowed)
            probs_low, grad_scores = score_grads(
                scores, log_total, delta_row, grad_heads, value_block
            )
            grad_query = grad_query + jnp.einsum(
                PV, grad_scores, key_block, preferred_element_type=jnp.float32
            )
            grad_bias = grad_bias + bucket_grad(buckets, grad_scores, bucket_count)
            grad_key = jnp.einsum(
                PTQ, grad_scores, query_heads, preferred_element_type=jnp.float32
            ).reshape(key_rows, inner_width)
            grad_value = jnp.einsum(
                PTQ, probs_low, grad_heads, preferred_element_type=jnp.float32
            ).reshape(key_rows, inner_width)
            return ((grad_query, grad_bias), jnp.concatenate([grad_key, grad_value], axis=1))

        blank_block = jnp.zeros((key_rows, 2 * inner_width), jnp.float32)
        return lax.cond(
            jnp.any(allowed), step_accumulate, lambda current: (current, blank_block), carried
        )

    start_state = (
        jnp.zeros(query_heads.shape, jnp.float32),
        jnp.zeros(table_hb.shape, jnp.float32),
    )
    final_state, key_blocks = lax.scan(step_body, start_state, step_list)
    return (final_state[0], final_state[1], key_blocks.reshape(total_rows, 2 * inner_width))


def local(
    layer_in,
    encoded,
    cotangent,
    deal_table,
    self_query,
    self_key,
    self_value,
    self_output,
    cross_query,
    cross_key,
    cross_value,
    cross_output,
    feed_gate,
    feed_up,
    feed_down,
    gain_self,
    gain_cross,
    gain_feed,
    relative_bias,
):
    shards = lax.axis_size(AXES)
    device = lax.axis_index(AXES)
    ctx_count = lax.axis_size(CTX)
    core_count = lax.axis_size(WSH)
    local_rows = layer_in.shape[1]
    total_rows = local_rows * shards
    block_len = local_rows // 2
    cont_len = min(CONT_TOK, total_rows // 2)
    prompt_len = total_rows - total_rows // 2 // cont_len * cont_len
    key_rows = min(1024, total_rows)
    head_count = relative_bias.shape[1]
    inner_width = self_query.shape[1]
    head_size = inner_width // head_count
    enc_rows = encoded.shape[1] * shards
    table_hb = relative_bias.astype(jnp.float32).T
    flat_table = deal_table.reshape(-1)
    all_tokens = (
        flat_table[:, None] * block_len + jnp.arange(block_len, dtype=jnp.int32)[None, :]
    ).reshape(-1)
    seq_all, pos_all = token_place(all_tokens, prompt_len, cont_len)
    seq_mine = lax.dynamic_slice_in_dim(seq_all, device * local_rows, local_rows)
    pos_mine = lax.dynamic_slice_in_dim(pos_all, device * local_rows, local_rows)
    forward_weights = (
        lax.all_gather(self_query, AXES, axis=0, tiled=True),
        lax.all_gather(self_key, AXES, axis=0, tiled=True),
        lax.all_gather(self_value, AXES, axis=0, tiled=True),
        lax.all_gather(self_output, AXES, axis=0, tiled=True),
        lax.all_gather(cross_query, AXES, axis=0, tiled=True),
        lax.all_gather(cross_key, AXES, axis=0, tiled=True),
        lax.all_gather(cross_value, AXES, axis=0, tiled=True),
        lax.all_gather(cross_output, AXES, axis=0, tiled=True),
        lax.all_gather(feed_gate, AXES, axis=0, tiled=True),
        lax.all_gather(feed_up, AXES, axis=0, tiled=True),
        lax.all_gather(feed_down, AXES, axis=0, tiled=True),
        lax.all_gather(gain_self, AXES, axis=0, tiled=True),
        lax.all_gather(gain_cross, AXES, axis=0, tiled=True),
        lax.all_gather(gain_feed, AXES, axis=0, tiled=True),
    )
    (
        query_weight,
        key_weight,
        value_weight,
        output_weight,
        cq_weight,
        ck_weight,
        cv_weight,
        co_weight,
        gate_weight,
        up_weight,
        down_weight,
        gain_one,
        gain_two,
        gain_three,
    ) = forward_weights
    inputs32 = layer_in[0].astype(jnp.float32)
    normed_one = rms_norm(inputs32, gain_one.astype(jnp.float32)).astype(jnp.bfloat16)
    queries = jnp.dot(normed_one, query_weight, preferred_element_type=jnp.float32).astype(
        jnp.bfloat16
    )
    keys_local = jnp.dot(normed_one, key_weight, preferred_element_type=jnp.float32).astype(
        jnp.bfloat16
    )
    values_local = jnp.dot(normed_one, value_weight, preferred_element_type=jnp.float32).astype(
        jnp.bfloat16
    )
    keys_all, values_all = (
        lax.all_gather(keys_local, AXES, axis=0, tiled=True),
        lax.all_gather(values_local, AXES, axis=0, tiled=True),
    )
    query_heads = queries.reshape(local_rows, head_count, head_size)
    key_heads = keys_all.reshape(total_rows, head_count, head_size)
    value_heads = values_all.reshape(total_rows, head_count, head_size)
    log_self, attn_sum, attn_exact = self_forward(
        query_heads,
        key_heads,
        value_heads,
        seq_all,
        pos_all,
        seq_mine,
        pos_mine,
        table_hb,
        key_rows,
    )
    attended = attn_sum.reshape(local_rows, inner_width).astype(jnp.bfloat16)
    hidden_one = inputs32 + jnp.dot(attended, output_weight, preferred_element_type=jnp.float32)
    normed_two = rms_norm(hidden_one, gain_two.astype(jnp.float32)).astype(jnp.bfloat16)
    cross_queries = jnp.dot(normed_two, cq_weight, preferred_element_type=jnp.float32).astype(
        jnp.bfloat16
    )
    enc_keys = jnp.dot(encoded[0], ck_weight, preferred_element_type=jnp.float32).astype(
        jnp.bfloat16
    )
    enc_values = jnp.dot(encoded[0], cv_weight, preferred_element_type=jnp.float32).astype(
        jnp.bfloat16
    )
    cross_keys, cross_values = (
        lax.all_gather(enc_keys, AXES, axis=0, tiled=True),
        lax.all_gather(enc_values, AXES, axis=0, tiled=True),
    )
    cq_heads = cross_queries.reshape(local_rows, head_count, head_size)
    ck_heads = cross_keys.reshape(enc_rows, head_count, head_size)
    cv_heads = cross_values.reshape(enc_rows, head_count, head_size)
    cross_scores = jnp.einsum(
        QK, cq_heads, ck_heads, preferred_element_type=jnp.float32
    )
    cross_peak = jnp.max(cross_scores, axis=-1)
    log_cross = cross_peak + jnp.log(
        jnp.sum(jnp.exp(cross_scores - cross_peak[:, :, None]), axis=-1)
    )
    cross_probs = jnp.exp(cross_scores - log_cross[:, :, None])
    cross_high, cross_rest = split_probs(cross_probs)
    cross_sum = jnp.einsum(PV, cross_high, cv_heads, preferred_element_type=jnp.float32)
    cross_exact = cross_sum + jnp.einsum(
        PV, cross_rest, cv_heads, preferred_element_type=jnp.float32
    )
    attended_cross = cross_sum.reshape(local_rows, inner_width).astype(jnp.bfloat16)
    hidden_two = hidden_one + jnp.dot(attended_cross, co_weight, preferred_element_type=jnp.float32)
    normed_three = rms_norm(hidden_two, gain_three.astype(jnp.float32)).astype(jnp.bfloat16)
    gate_pre = jnp.dot(normed_three, gate_weight, preferred_element_type=jnp.float32)
    up_pre = jnp.dot(normed_three, up_weight, preferred_element_type=jnp.float32)
    mixed_hidden = gated(gate_pre, up_pre).astype(jnp.bfloat16)
    output_sum = hidden_two + jnp.dot(mixed_hidden, down_weight, preferred_element_type=jnp.float32)
    layer_out = output_sum.astype(jnp.bfloat16)[None]
    back_weights = (
        lax.all_gather(self_query, AXES, axis=0, tiled=True),
        lax.all_gather(self_key, AXES, axis=0, tiled=True),
        lax.all_gather(self_value, AXES, axis=0, tiled=True),
        lax.all_gather(self_output, AXES, axis=0, tiled=True),
        lax.all_gather(cross_query, AXES, axis=0, tiled=True),
        lax.all_gather(cross_key, AXES, axis=0, tiled=True),
        lax.all_gather(cross_value, AXES, axis=0, tiled=True),
        lax.all_gather(cross_output, AXES, axis=0, tiled=True),
        lax.all_gather(feed_gate, AXES, axis=0, tiled=True),
        lax.all_gather(feed_up, AXES, axis=0, tiled=True),
        lax.all_gather(feed_down, AXES, axis=0, tiled=True),
        lax.all_gather(gain_self, AXES, axis=0, tiled=True),
        lax.all_gather(gain_cross, AXES, axis=0, tiled=True),
        lax.all_gather(gain_feed, AXES, axis=0, tiled=True),
    )
    (
        query_back,
        key_back,
        value_back,
        output_back,
        cq_back,
        ck_back,
        cv_back,
        co_back,
        gate_back,
        up_back,
        down_back,
        gain_one_back,
        gain_two_back,
        gain_three_back,
    ) = back_weights
    grad_out = cotangent[0]
    grad_down_w = jnp.einsum(
        TF_TD, mixed_hidden, grad_out, preferred_element_type=jnp.float32
    )
    grad_mixed = jnp.einsum(TD_FD, grad_out, down_back, preferred_element_type=jnp.float32)
    _, gate_pull = jax.vjp(gated, gate_pre, up_pre)
    grad_gate32, grad_up32 = gate_pull(bounce(grad_mixed))
    grad_gate = grad_gate32.astype(jnp.bfloat16)
    grad_up = grad_up32.astype(jnp.bfloat16)
    grad_gate_w = jnp.einsum(
        TD_TF, normed_three, grad_gate, preferred_element_type=jnp.float32
    )
    grad_up_w = jnp.einsum(TD_TF, normed_three, grad_up, preferred_element_type=jnp.float32)
    grad_normed_three = jnp.einsum(
        TF_DF, grad_gate, gate_back, preferred_element_type=jnp.float32
    ) + jnp.einsum(TF_DF, grad_up, up_back, preferred_element_type=jnp.float32)
    _, norm_pull_three = jax.vjp(rms_norm, hidden_two, gain_three_back.astype(jnp.float32))
    back_two, grad_gain_feed = norm_pull_three(grad_normed_three)
    grad_hidden_two = grad_out.astype(jnp.float32) + back_two
    grad_two_low = grad_hidden_two.astype(jnp.bfloat16)
    grad_co_w = jnp.einsum(
        TC_TD, attended_cross, grad_two_low, preferred_element_type=jnp.float32
    )
    grad_attended_cross = jnp.einsum(
        TD_CD, grad_two_low, co_back, preferred_element_type=jnp.float32
    ).astype(jnp.bfloat16)
    grad_ac_heads = grad_attended_cross.reshape(local_rows, head_count, head_size)
    delta_cross = jnp.sum(grad_ac_heads.astype(jnp.float32) * cross_exact, axis=-1).T
    cross_low, grad_cross_scores = score_grads(
        cross_scores, log_cross, delta_cross, grad_ac_heads, cv_heads
    )
    grad_cq = jnp.einsum(
        PV, grad_cross_scores, ck_heads, preferred_element_type=jnp.float32
    )
    grad_ck_part = jnp.einsum(
        PTQ, grad_cross_scores, cq_heads, preferred_element_type=jnp.float32
    ).reshape(enc_rows, inner_width)
    grad_cv_part = jnp.einsum(
        PTQ, cross_low, grad_ac_heads, preferred_element_type=jnp.float32
    ).reshape(enc_rows, inner_width)
    cross_own = lax.psum_scatter(
        jnp.concatenate([grad_ck_part, grad_cv_part], axis=1),
        AXES,
        scatter_dimension=0,
        tiled=True,
    )
    grad_cross_keys = cross_own[:, :inner_width].astype(jnp.bfloat16)
    grad_cross_values = cross_own[:, inner_width:].astype(jnp.bfloat16)
    grad_ck_w = jnp.einsum(
        TD_TC, encoded[0], grad_cross_keys, preferred_element_type=jnp.float32
    )
    grad_cv_w = jnp.einsum(
        TD_TC, encoded[0], grad_cross_values, preferred_element_type=jnp.float32
    )
    grad_encoded = (
        jnp.einsum(TC_DC, grad_cross_keys, ck_back, preferred_element_type=jnp.float32)
        + jnp.einsum(TC_DC, grad_cross_values, cv_back, preferred_element_type=jnp.float32)
    )[None]
    grad_cq_low = grad_cq.reshape(local_rows, inner_width).astype(jnp.bfloat16)
    grad_cq_w = jnp.einsum(TD_TC, normed_two, grad_cq_low, preferred_element_type=jnp.float32)
    grad_normed_two = jnp.einsum(
        TC_DC, grad_cq_low, cq_back, preferred_element_type=jnp.float32
    )
    _, norm_pull_two = jax.vjp(rms_norm, hidden_one, gain_two_back.astype(jnp.float32))
    back_one, grad_gain_cross = norm_pull_two(grad_normed_two)
    grad_hidden_one = grad_hidden_two + back_one
    grad_one_low = grad_hidden_one.astype(jnp.bfloat16)
    grad_o_w = jnp.einsum(TC_TD, attended, grad_one_low, preferred_element_type=jnp.float32)
    grad_attended = jnp.einsum(
        TD_CD, grad_one_low, output_back, preferred_element_type=jnp.float32
    ).astype(jnp.bfloat16)
    grad_att_heads = grad_attended.reshape(local_rows, head_count, head_size)
    delta_self = jnp.sum(grad_att_heads.astype(jnp.float32) * attn_exact, axis=-1).T
    grad_query32, grad_bias_part, kv_blocks = query_backward(
        query_heads,
        key_heads,
        value_heads,
        grad_att_heads,
        log_self,
        delta_self,
        seq_all,
        pos_all,
        seq_mine,
        pos_mine,
        table_hb,
        key_rows,
    )
    kv_own = lax.psum_scatter(kv_blocks, AXES, scatter_dimension=0, tiled=True)
    grad_keys = kv_own[:, :inner_width].astype(jnp.bfloat16)
    grad_values = kv_own[:, inner_width:].astype(jnp.bfloat16)
    grad_queries = grad_query32.reshape(local_rows, inner_width).astype(jnp.bfloat16)
    grad_q_w = jnp.einsum(TD_TC, normed_one, grad_queries, preferred_element_type=jnp.float32)
    grad_k_w = jnp.einsum(TD_TC, normed_one, grad_keys, preferred_element_type=jnp.float32)
    grad_v_w = jnp.einsum(TD_TC, normed_one, grad_values, preferred_element_type=jnp.float32)
    grad_normed_one = (
        jnp.einsum(TC_DC, grad_queries, query_back, preferred_element_type=jnp.float32)
        + jnp.einsum(TC_DC, grad_keys, key_back, preferred_element_type=jnp.float32)
        + jnp.einsum(TC_DC, grad_values, value_back, preferred_element_type=jnp.float32)
    )
    _, norm_pull_one = jax.vjp(rms_norm, inputs32, gain_one_back.astype(jnp.float32))
    back_input, grad_gain_self = norm_pull_one(grad_normed_one)
    grad_input = (grad_hidden_one + back_input)[None]

    def sectioned(grad_full):
        return grad_full.reshape(
            (ctx_count, core_count, grad_full.shape[0] // (ctx_count * core_count))
            + grad_full.shape[1:]
        )

    core_parts = (
        lax.psum_scatter(
            sectioned(grad_q_w).astype(jnp.bfloat16), WSH, scatter_dimension=1, tiled=True
        ).astype(jnp.float32),
        lax.psum_scatter(
            sectioned(grad_k_w).astype(jnp.bfloat16), WSH, scatter_dimension=1, tiled=True
        ).astype(jnp.float32),
        lax.psum_scatter(
            sectioned(grad_v_w).astype(jnp.bfloat16), WSH, scatter_dimension=1, tiled=True
        ).astype(jnp.float32),
        lax.psum_scatter(
            sectioned(grad_o_w).astype(jnp.bfloat16), WSH, scatter_dimension=1, tiled=True
        ).astype(jnp.float32),
        lax.psum_scatter(
            sectioned(grad_cq_w).astype(jnp.bfloat16), WSH, scatter_dimension=1, tiled=True
        ).astype(jnp.float32),
        lax.psum_scatter(
            sectioned(grad_ck_w).astype(jnp.bfloat16), WSH, scatter_dimension=1, tiled=True
        ).astype(jnp.float32),
        lax.psum_scatter(
            sectioned(grad_cv_w).astype(jnp.bfloat16), WSH, scatter_dimension=1, tiled=True
        ).astype(jnp.float32),
        lax.psum_scatter(
            sectioned(grad_co_w).astype(jnp.bfloat16), WSH, scatter_dimension=1, tiled=True
        ).astype(jnp.float32),
        lax.psum_scatter(
            sectioned(grad_gate_w).astype(jnp.bfloat16), WSH, scatter_dimension=1, tiled=True
        ).astype(jnp.float32),
        lax.psum_scatter(
            sectioned(grad_up_w).astype(jnp.bfloat16), WSH, scatter_dimension=1, tiled=True
        ).astype(jnp.float32),
        lax.psum_scatter(
            sectioned(grad_down_w).astype(jnp.bfloat16), WSH, scatter_dimension=1, tiled=True
        ).astype(jnp.float32),
        lax.psum_scatter(
            sectioned(grad_gain_self).astype(jnp.bfloat16), WSH, scatter_dimension=1, tiled=True
        ).astype(jnp.float32),
        lax.psum_scatter(
            sectioned(grad_gain_cross).astype(jnp.bfloat16), WSH, scatter_dimension=1, tiled=True
        ).astype(jnp.float32),
        lax.psum_scatter(
            sectioned(grad_gain_feed).astype(jnp.bfloat16), WSH, scatter_dimension=1, tiled=True
        ).astype(jnp.float32),
    )
    (
        core_q,
        core_k,
        core_v,
        core_o,
        core_cq,
        core_ck,
        core_cv,
        core_co,
        core_gate,
        core_up,
        core_down,
        core_gs,
        core_gc,
        core_gf,
    ) = core_parts
    owned = (
        lax.psum_scatter(core_q, CTX, scatter_dimension=0, tiled=True),
        lax.psum_scatter(core_k, CTX, scatter_dimension=0, tiled=True),
        lax.psum_scatter(core_v, CTX, scatter_dimension=0, tiled=True),
        lax.psum_scatter(core_o, CTX, scatter_dimension=0, tiled=True),
        lax.psum_scatter(core_cq, CTX, scatter_dimension=0, tiled=True),
        lax.psum_scatter(core_ck, CTX, scatter_dimension=0, tiled=True),
        lax.psum_scatter(core_cv, CTX, scatter_dimension=0, tiled=True),
        lax.psum_scatter(core_co, CTX, scatter_dimension=0, tiled=True),
        lax.psum_scatter(core_gate, CTX, scatter_dimension=0, tiled=True),
        lax.psum_scatter(core_up, CTX, scatter_dimension=0, tiled=True),
        lax.psum_scatter(core_down, CTX, scatter_dimension=0, tiled=True),
        lax.psum_scatter(core_gs, CTX, scatter_dimension=0, tiled=True),
        lax.psum_scatter(core_gc, CTX, scatter_dimension=0, tiled=True),
        lax.psum_scatter(core_gf, CTX, scatter_dimension=0, tiled=True),
    )
    (
        own_q,
        own_k,
        own_v,
        own_o,
        own_cq,
        own_ck,
        own_cv,
        own_co,
        own_gate,
        own_up,
        own_down,
        own_gain_self,
        own_gain_cross,
        own_gain_feed,
    ) = [piece.reshape(piece.shape[2:]) for piece in owned]
    summed = (
        lax.psum(own_q.astype(jnp.bfloat16), GRP).astype(jnp.float32),
        lax.psum(own_k.astype(jnp.bfloat16), GRP).astype(jnp.float32),
        lax.psum(own_v.astype(jnp.bfloat16), GRP).astype(jnp.float32),
        lax.psum(own_o.astype(jnp.bfloat16), GRP).astype(jnp.float32),
        lax.psum(own_cq.astype(jnp.bfloat16), GRP).astype(jnp.float32),
        lax.psum(own_ck.astype(jnp.bfloat16), GRP).astype(jnp.float32),
        lax.psum(own_cv.astype(jnp.bfloat16), GRP).astype(jnp.float32),
        lax.psum(own_co.astype(jnp.bfloat16), GRP).astype(jnp.float32),
        lax.psum(own_gate.astype(jnp.bfloat16), GRP).astype(jnp.float32),
        lax.psum(own_up.astype(jnp.bfloat16), GRP).astype(jnp.float32),
        lax.psum(own_down.astype(jnp.bfloat16), GRP).astype(jnp.float32),
        lax.psum(own_gain_self.astype(jnp.bfloat16), GRP).astype(jnp.float32),
        lax.psum(own_gain_cross.astype(jnp.bfloat16), GRP).astype(jnp.float32),
        lax.psum(own_gain_feed.astype(jnp.bfloat16), GRP).astype(jnp.float32),
    )
    grad_relative_bias = lax.psum(grad_bias_part.T, EVERY)
    return (
        layer_out,
        grad_input,
        grad_encoded,
        summed[0],
        summed[1],
        summed[2],
        summed[3],
        summed[4],
        summed[5],
        summed[6],
        summed[7],
        summed[8],
        summed[9],
        summed[10],
        summed[11],
        summed[12],
        summed[13],
        grad_relative_bias,
    )


BIG = 63 << 20
NT = (((1,), (1,)), ((), ()))
TN = (((0,), (0,)), ((), ()))
NN = (((1,), (0,)), ((), ()))
F32 = jnp.float32
BF16 = jnp.bfloat16
CH = 256
BLK = 64


def mm(left, right, dims):
    return lax.dot_general(left, right, dims, preferred_element_type=F32)


def load_in_order(deal, k_hbm, v_hbm, kvs, sem):
    blocks, inner = k_hbm.shape[0] // BLK, k_hbm.shape[1]

    def one(index, carry):
        here = pl.ds(index * BLK, BLK)
        rows = kvs.at[pl.ds(pl.multiple_of(deal[index // 2, index % 2] * BLK, BLK), BLK)]
        pltpu.make_async_copy(k_hbm.at[here], rows.at[:, pl.ds(0, inner)], sem.at[0]).start()
        pltpu.make_async_copy(v_hbm.at[here], rows.at[:, pl.ds(inner, inner)], sem.at[1]).start()
        return carry

    lax.fori_loop(0, blocks, one, 0)


def loaded(k_hbm, v_hbm, kvs, sem):
    inner = k_hbm.shape[1]
    pltpu.make_async_copy(k_hbm, kvs.at[:, pl.ds(0, inner)], sem.at[0]).wait()
    pltpu.make_async_copy(v_hbm, kvs.at[:, pl.ds(inner, inner)], sem.at[1]).wait()


def stack_pair(block, low_lanes):
    zero = jnp.zeros_like(block)
    return jnp.concatenate([jnp.where(low_lanes, block, zero), jnp.where(low_lanes, zero, block)], axis=0)


def pair_table(table_hb):
    heads = table_hb.shape[0]
    padded = jnp.pad(table_hb, ((0, 0), (0, BLK - BUCKETS)))
    return padded.reshape(heads // 2, 2 * BLK)

MESH = pl.DeviceIdType.MESH


class Place:
    def __init__(self, nz):
        self.nz = nz
        self.g = lax.axis_index(GRP)
        self.c = lax.axis_index(CTX)
        self.w = lax.axis_index(WSH)
        self.z = self.c // 2
        self.y = lax.rem(self.c, 2)
        self.me = self.c * 2 + self.w

    def at(self, g=None, z=None, y=None, w=None):
        z = self.z if z is None else z
        y = self.y if y is None else y
        return (self.g if g is None else g, z * 2 + y, self.w if w is None else w)

    def twin(self):
        return self.at(g=1 - self.g)

    def over(self):
        return self.at(y=1 - self.y)

    def mate(self):
        return self.at(w=1 - self.w)

    def up(self, dz):
        return lax.rem(self.z + dz, self.nz)

    def down(self, dz):
        return lax.rem(self.z + self.nz - dz, self.nz)

    def greet(self):
        partners = [self.twin(), self.over(), self.mate()]
        partners += [self.at(z=self.up(dz)) for dz in range(1, self.nz)]
        for partner in partners:
            pl.semaphore_signal(pltpu.get_barrier_semaphore(), inc=1, device_id=partner, device_id_type=MESH)
        self.greeted = len(partners)

    def met(self):
        pl.semaphore_wait(pltpu.get_barrier_semaphore(), self.greeted)


def push(src, dst, ssem, rsem, to):
    return pltpu.make_async_remote_copy(src, dst, ssem, rsem, device_id=to, device_id_type=MESH)


def half(wide, index):
    return pl.ds(pl.multiple_of(index * (wide // 2), 128), wide // 2)


class Gather:
    COUNT = 9

    def __init__(self, at, part, whole, sems, split, chunk=0, chunks=1):
        self.at, self.nz, self.part, self.whole, self.split = at, at.nz, part, whole, split
        (self.zs, self.zr, self.ys, self.yr, self.xs, self.xr, self.ws, self.wr, self.lc) = sems
        self.wide = whole.shape[-1] // chunks
        self.first = chunk * self.wide
        self.sent = []

    @staticmethod
    def scratch(nz, split):
        dma = pltpu.SemaphoreType.DMA
        x = 2 * nz if split else 1
        w = 4 * nz if split else 2 * nz
        return [dma((nz,))] * 4 + [dma((x,))] * 2 + [dma((w,))] * 2 + [dma((1,))]

    def cols(self, side=None):
        if self.split and side is not None:
            return pl.ds(pl.multiple_of(self.first + side * (self.wide // 2), 128), self.wide // 2)
        return pl.ds(self.first, self.wide)

    def spot(self, z, y, w, side=None):
        return self.whole.at[z, y, w, :, self.cols(side)]

    def post(self, view, ssem, rsem, to, source=None):
        copy = push(view if source is None else source, view, ssem, rsem, to)
        copy.start()
        self.sent.append(copy)

    def to_y(self, z):
        at = self.at
        self.post(self.spot(z, at.y, at.w, at.g), self.ys.at[z], self.yr.at[z], at.over())

    def to_x(self, z, y):
        at = self.at
        if self.split:
            k = z * 2 + y
            self.post(self.spot(z, y, at.w, at.g), self.xs.at[k], self.xr.at[k], at.twin())

    def w_sem(self, z, y, side):
        k = z * 2 + y
        return k * 2 + (0 if side is None else side) if self.split else k

    def to_w(self, z, y, side):
        at = self.at
        k = self.w_sem(z, y, side)
        self.post(self.spot(z, y, at.w, side), self.ws.at[k], self.wr.at[k], at.mate())

    def place(self):
        here = self.spot(self.at.z, self.at.y, self.at.w)
        self.local = pltpu.make_async_copy(self.part.at[:, self.cols()], here, self.lc.at[0])
        self.local.start()

    def send(self):
        at = self.at
        here, source = self.spot(at.z, at.y, at.w, at.g), self.part.at[:, self.cols(at.g)]
        for dz in range(1, self.nz):
            to = at.up(dz)
            self.post(here, self.zs.at[to], self.zr.at[at.z], at.at(z=to), source)
        self.post(here, self.ys.at[at.z], self.yr.at[at.z], at.over(), source)
        k = self.w_sem(at.z, at.y, None)
        self.post(self.spot(at.z, at.y, at.w), self.ws.at[k], self.wr.at[k], at.mate(), self.part.at[:, self.cols()])

    def after_z(self):
        at = self.at
        for dz in range(1, self.nz):
            z = at.down(dz)
            view = self.spot(z, at.y, at.w, at.g)
            push(view, view, self.zs.at[z], self.zr.at[z], at.at(z=z)).wait_recv()
            self.to_y(z)
            self.to_x(z, at.y)
            self.to_w(z, at.y, at.g)

    def after_y(self):
        at = self.at
        for dz in range(self.nz):
            z = at.down(dz)
            view = self.spot(z, 1 - at.y, at.w, at.g)
            push(view, view, self.ys.at[z], self.yr.at[z], at.over()).wait_recv()
            self.to_x(z, 1 - at.y)
            self.to_w(z, 1 - at.y, at.g)

    def others(self):
        for dy in range(2):
            for dz in range(self.nz):
                yield self.at.down(dz), lax.rem(self.at.y + dy, 2), dy == 0 and dz == 0

    def after_x(self):
        at = self.at
        if not self.split:
            return
        for z, y, own in self.others():
            if not own:
                k = z * 2 + y
                view = self.spot(z, y, at.w, 1 - at.g)
                push(view, view, self.xs.at[k], self.xr.at[k], at.twin()).wait_recv()
                self.to_w(z, y, 1 - at.g)

    def end(self):
        at = self.at
        self.local.wait()
        for z, y, own in self.others():
            for side in range(2 if self.split and not own else 1):
                k = self.w_sem(z, y, side)
                view = self.spot(z, y, 1 - at.w, None if own else side)
                push(view, view, self.ws.at[k], self.wr.at[k], at.mate()).wait_recv()

    def close(self):
        for copy in self.sent:
            copy.wait_send()


class Reduce:
    COUNT = 16

    @staticmethod
    def scratch(nz, r, wide, kind, dtype, part=True):
        cols = wide // 2 if kind == "x" else wide
        dma = pltpu.SemaphoreType.DMA
        vmem = pltpu.VMEM
        none = vmem((1, 16, 128), dtype)
        return [
            vmem((nz, 2, 2, r, wide), dtype) if part else none,
            vmem((nz, 2, r, wide), dtype),
            vmem((nz, 2, r, cols), dtype) if kind == "x" else none,
            vmem((nz, r, cols), dtype),
            vmem((nz, r, cols), dtype),
            vmem((2, r, cols), dtype) if kind != "none" else none,
        ] + [dma((1,))] * 6 + [dma((nz,))] * 2 + [dma((1,))] * 2

    def __init__(self, at, out, refs, kind):
        self.at, self.nz, self.out, self.kind = at, at.nz, out, kind
        self.part_cols = None
        (self.part, self.wb, self.xb, self.yb, self.zb, self.fb) = refs[:6]
        (self.ws, self.wr, self.xs, self.xr, self.ys, self.yr, self.zs, self.zr, self.fs, self.fr) = refs[6:]
        self.wide = self.wb.shape[-1]
        self.local_part = None

    def c_w(self):
        at = self.at
        src = self.part.at[:, :, 1 - at.w]
        if self.part_cols is not None:
            src = self.part.at[:, :, 1 - at.w, :, self.part_cols]
        return push(src, self.wb, self.ws.at[0], self.wr.at[0], at.mate())

    def c_x(self):
        at = self.at
        src = self.wb.at[:, :, :, half(self.wide, 1 - at.g)]
        return push(src, self.xb, self.xs.at[0], self.xr.at[0], at.twin())

    def mid(self):
        return self.xb if self.kind == "x" else self.wb

    def c_y(self):
        at = self.at
        return push(self.mid().at[:, 1 - at.y], self.yb, self.ys.at[0], self.yr.at[0], at.over())

    def c_z(self, to):
        at = self.at
        return push(self.yb.at[to], self.zb.at[at.z], self.zs.at[to], self.zr.at[at.z], at.at(z=to))

    def c_zin(self, z):
        return push(self.yb.at[z], self.zb.at[z], self.zs.at[z], self.zr.at[z], self.at.at(z=z))

    def c_f(self):
        return push(self.fb.at[0], self.fb.at[1], self.fs.at[0], self.fr.at[0], self.at.twin())

    def send(self):
        self.c_w().start()

    def after_w(self):
        at = self.at
        self.c_w().wait_recv()

        def one(k, carry):
            z, y = k // 2, lax.rem(k, 2)
            here = self.part[z, y, at.w] if self.local_part is None else self.local_part[z, y, :, self.local_cols]
            self.wb[z, y] = (self.wb[z, y].astype(F32) + here.astype(F32)).astype(self.wb.dtype)
            return carry

        lax.fori_loop(0, 2 * self.nz, one, 0)
        if self.kind == "x":
            self.c_x().start()
        else:
            self.c_y().start()

    def after_x(self):
        if self.kind != "x":
            return
        self.c_x().wait_recv()

        def one(k, carry):
            z, y = k // 2, lax.rem(k, 2)
            total = self.xb[z, y].astype(F32) + self.wb[z, y, :, half(self.wide, self.at.g)].astype(F32)
            self.xb[z, y] = total.astype(self.xb.dtype)
            return carry

        lax.fori_loop(0, 2 * self.nz, one, 0)
        self.c_y().start()

    def after_y(self):
        at, nz = self.at, self.nz
        self.c_y().wait_recv()

        def one(z, carry):
            total = self.yb[z].astype(F32) + self.mid()[z, at.y].astype(F32)
            self.yb[z] = total.astype(self.yb.dtype)
            return carry

        lax.fori_loop(0, nz, one, 0)
        for dz in range(1, nz):
            self.c_z(at.up(dz)).start()

    def after_z(self):
        at, nz = self.at, self.nz
        for dz in range(1, nz):
            self.c_zin(at.up(dz)).wait_recv()
        total = self.yb[at.z].astype(F32)
        for dz in range(1, nz):
            total = total + self.zb[at.up(dz)].astype(F32)
        if self.kind == "x":
            self.out[:, half(self.wide, at.g)] = total
        else:
            self.out[...] = total
        if self.kind != "none":
            self.fb[0] = total.astype(self.fb.dtype)
            self.c_f().start()

    def end(self):
        at = self.at
        if self.kind != "none":
            self.c_f().wait_recv()
            other = self.fb[1].astype(F32)
            if self.kind == "x":
                self.out[:, half(self.wide, 1 - at.g)] = other
            else:
                self.out[...] = self.out[...] + other

    def close(self):
        at, nz = self.at, self.nz
        self.c_w().wait_send()
        if self.kind == "x":
            self.c_x().wait_send()
        self.c_y().wait_send()
        for dz in range(1, nz):
            self.c_z(at.up(dz)).wait_send()
        if self.kind != "none":
            self.c_f().wait_send()


class Total:
    COUNT = 3

    @staticmethod
    def scratch(nz, r, wide):
        dma = pltpu.SemaphoreType.DMA
        return [pltpu.VMEM((4 + nz, r, wide), F32), dma((4 + nz,)), dma((4 + nz,))]

    def __init__(self, at, refs):
        self.at, self.nz = at, at.nz
        self.buf, self.ss, self.rs = refs

    def hop(self, i):
        at = self.at
        to = (at.mate(), at.twin(), at.over())[i]
        return push(self.buf.at[0], self.buf.at[1 + i], self.ss.at[i], self.rs.at[i], to)

    def send(self):
        self.hop(0).start()

    def after(self, i):
        hop = self.hop(i)
        hop.wait_send()
        hop.wait_recv()
        self.buf[0] = self.buf[0] + self.buf[1 + i]
        if i < 2:
            self.hop(i + 1).start()
        else:
            for dz in range(1, self.nz):
                self.along(self.at.z, self.at.up(dz)).start()

    def along(self, source, to):
        base = 4
        return push(self.buf.at[0], self.buf.at[base + source], self.ss.at[base + to], self.rs.at[base + source], self.at.at(z=to))

    def end(self):
        total = None
        for dz in range(1, self.nz):
            z = self.at.up(dz)
            self.along(z, z).wait_recv()
            self.along(self.at.z, z).wait_send()
        self.buf[4 + self.at.z] = self.buf[0]
        total = self.buf[4]
        for z in range(1, self.nz):
            total = total + self.buf[4 + z]
        return total


def normed(hidden, gain):
    return hidden * lax.rsqrt(jnp.mean(hidden * hidden, axis=-1, keepdims=True) + EPSILON) * gain


def norm_back(hidden, gain, grad):
    scale = lax.rsqrt(jnp.mean(hidden * hidden, axis=-1, keepdims=True) + EPSILON)
    inner = jnp.mean(hidden * gain * grad, axis=-1, keepdims=True)
    rows = scale * gain * grad - hidden * (scale * scale * scale) * inner
    return rows, jnp.sum(grad * hidden * scale, axis=0, keepdims=True)


FRONT_PARTS = ("small", "k", "v", "q", "o", "cq", "ck", "cv", "co", "gate", "up", "down", "keys", "values")
FRONT_REST = 14
FRONT_PLAN = (
    ("small", "keys", "values",),
    dict(gate=2, up=2, down=3, keys=3, values=3),
    (
        ("down", 0), ("up", 0), ("values", 2), ("values", 0), ("keys", 2), ("k", 0), ("values", 1), ("down", 1),
        ("cq", 0), ("down", 2), ("gate", 1), ("keys", 0), ("small", 0), ("cv", 0), ("v", 0), ("co", 0), ("up", 1),
        ("q", 0), ("o", 0), ("gate", 0), ("keys", 1), ("ck", 0),
    ),
    (
        (0, 0), (1, 0), (5, 0), (0, 1), (7, 0), (0, 2), (1, 1), (8, 0), (0, 3), (5, 1), (9, 0), (1, 2), (7, 1),
        (10, 0), (5, 2), (8, 1), (12, 0), (7, 2), (9, 1), (1, 3), (13, 0), (8, 2), (10, 1), (14, 0), (9, 2), (5, 3),
        (12, 1), (15, 0), (10, 2), (13, 1), (16, 0), (7, 3), (12, 2), (14, 1), (17, 0), (12, 4), (5, 4), (8, 3),
        (13, 2), (14, 2), (15, 1), (4, 0), (11, 0), (16, 1), (9, 3), (15, 2), (17, 1), (18, 0), (10, 3), (4, 1),
        (16, 2), (19, 0), (20, 0), (17, 2), (13, 3), (11, 1), (4, 2), (14, 3), (18, 1), (21, 0), (14, 4), (2, 0),
        (19, 1), (3, 0), (6, 0), (11, 2), (18, 2), (15, 3), (20, 1), (21, 1), (19, 2), (16, 3), (17, 3), (2, 1),
        (17, 4), (20, 2), (21, 2), (3, 1), (18, 3), (2, 2), (6, 1), (3, 2), (19, 3), (6, 2), (21, 3), (0, 4), (1, 4),
        (2, 4), (3, 4), (4, 4), (6, 4), (7, 4), (8, 4), (9, 4), (10, 4), (11, 4), (13, 4), (15, 4), (16, 4), (18, 4),
        (19, 4), (20, 4), (21, 4),
    ),
)


def front_kernel(nz, unshared, chunked, order, steps, *refs):
    count = len(FRONT_PARTS)
    x_ref, ins, wholes, refs = refs[0], refs[1 : count - 1], refs[count - 1 : 2 * count - 1], refs[2 * count - 1 :]
    (q_ref, normed_ref, gains_ref), (wbuf, k_own, v_own, wsem), sems = refs[:3], refs[3:7], refs[7:]
    parts = dict(zip(FRONT_PARTS, tuple(ins) + (k_own, v_own)))
    wholes = dict(zip(FRONT_PARTS, wholes))
    at = Place(nz)
    at.greet()
    jobs = []
    for i, (name, chunk) in enumerate(order):
        mine = sems[Gather.COUNT * i : Gather.COUNT * (i + 1)]
        chunks = chunked.get(name, 1)
        job = Gather(at, parts[name], wholes[name], mine, name not in unshared, chunk, chunks)
        jobs.append(job)
        if name not in ("keys", "values"):
            job.place()
    at.met()
    width = x_ref.shape[1]

    def norm():
        every = wholes["small"]
        total = None
        for z in range(nz):
            for y in range(2):
                for w in range(2):
                    here = every[z, y, w].astype(F32)
                    total = here if total is None else total + here
        gains_ref[...] = total
        normed_ref[...] = normed(x_ref[...].astype(F32), total[4:5]).astype(BF16)

    def project(name, index, into):
        load = pltpu.make_async_copy(wholes[name], wbuf.at[index], wsem.at[index])
        load.start()
        load.wait()
        into[...] = mm(normed_ref[...], wbuf[index].reshape(width, -1), NN).astype(BF16)

    def finish(i):
        if order[i][0] not in ("small", "k", "v", "q"):
            jobs[i].end()
        jobs[i].close()

    def place(name):
        for entry, job in zip(order, jobs):
            if entry[0] == name:
                job.place()

    def follow(name):
        if name == "small":
            norm()
        elif name == "k":
            project(name, 0, k_own)
            place("keys")
        elif name == "v":
            project(name, 1, v_own)
            place("values")
        elif name == "q":
            project(name, 2, q_ref)

    stages = (Gather.send, Gather.after_z, Gather.after_y, Gather.after_x, Gather.end)
    rest = {}
    for count, (i, stage) in enumerate(steps):
        name, job = order[i][0], jobs[i]
        if stage == len(stages) - 1:
            if name not in ("small", "k", "v", "q"):
                continue
            job.end()
            follow(name)
        else:
            stages[stage](job)
        if stage == (3 if job.split else 2):
            rest[i] = count + FRONT_REST
        for j in [j for j, due in rest.items() if due <= count]:
            finish(j)
            del rest[j]
    for j in rest:
        finish(j)


def front(x, parts, nz, shards, collective_id=1, plan=FRONT_PLAN):
    hb = pl.BlockSpec(memory_space=pl.ANY)
    vm = pl.BlockSpec(memory_space=pltpu.VMEM)
    unshared, chunked, order, steps = plan
    rows, width = x.shape
    inner = parts[1].shape[1]
    shapes = [(nz, 2, 2) + part.shape for part in parts] + [(nz, 2, 2, rows, inner)] * 2
    scratch = [
        pltpu.VMEM((3,) + shapes[1], BF16), pltpu.VMEM((rows, inner), BF16), pltpu.VMEM((rows, inner), BF16),
        pltpu.SemaphoreType.DMA((3,)),
    ]
    for name, _ in order:
        scratch += Gather.scratch(nz, name not in unshared)
    return pl.pallas_call(
        functools.partial(front_kernel, nz, unshared, chunked, order, steps),
        name="front",
        out_shape=tuple([jax.ShapeDtypeStruct(s, BF16) for s in shapes])
        + (
            jax.ShapeDtypeStruct((rows, inner), BF16),
            jax.ShapeDtypeStruct((rows, width), BF16),
            jax.ShapeDtypeStruct(parts[0].shape, F32),
        ),
        in_specs=[vm] + [hb] * len(parts),
        out_specs=tuple([vm] + [hb] * (len(FRONT_PARTS) - 1) + [vm] * 3),
        scratch_shapes=scratch,
        compiler_params=pltpu.CompilerParams(
            collective_id=collective_id, has_side_effects=True, vmem_limit_bytes=BIG
        ),
    )(x, *parts)


BACK_OUT = ("gate", "up", "down", "co", "cq", "q", "o", "k", "v", "ck", "cv")
BACK_NONE = ("kv", "cross")
BACK_PLAN = (
    ("q",),
    dict(kv=4),
    (
        ("kv", 3), ("k", 0), ("co", 0), ("kv", 1), ("cq", 0), ("gate", 0), ("kv", 0), ("kv", 2), ("cross", 0),
        ("down", 0), ("up", 0), ("o", 0), ("v", 0), ("q", 0),
    ),
    (
        (0, 0), (2, 0), (3, 0), (4, 0), (5, 0), (0, 1), (6, 0), (2, 1), (7, 0), (3, 1), (8, 0), (4, 1), (9, 0),
        (2, 2), (0, 3), (5, 1), (10, 0), (4, 2), (6, 1), (7, 1), (3, 3), (8, 1), (11, 0), (0, 4), (0, 5), (2, 3),
        (13, 0), (4, 3), (9, 1), (3, 4), (3, 5), (10, 1), (6, 3), (2, 4), (5, 2), (11, 1), (13, 1), (4, 4), (7, 3),
        (6, 4), (6, 5), (8, 3), (9, 2), (7, 4), (7, 5), (5, 3), (1, 0), (12, 0), (8, 4), (8, 5), (13, 3), (1, 1),
        (12, 1), (5, 4), (10, 2), (9, 3), (13, 4), (11, 2), (10, 3), (1, 2), (9, 4), (11, 3), (1, 3), (12, 2),
        (10, 4), (11, 4), (12, 3), (2, 5), (4, 5), (5, 5), (9, 5), (13, 5), (10, 5), (11, 5), (1, 4), (12, 4),
        (1, 5), (12, 5),
    ),
)


def back_kind(name, late):
    return "none" if name in BACK_NONE else "late" if name in late else "x"


def back_kernel(nz, late, chunked, order, steps, *refs):
    (
        kvp, crossp, wq, wk, wv, wck, wcv, x_ref, gains_ref, gh_ref, gpart_ref, small_ref,
        n3, mixed, att, n2, attc, n1, gg, gu, go, g1, gcq, g2, dq,
    ) = refs[:25]
    refs = refs[25:]
    outs = dict(zip(BACK_OUT, refs[: len(BACK_OUT)]))
    gx_ref, genc_ref, total_ref = refs[len(BACK_OUT) : len(BACK_OUT) + 3]
    refs = refs[len(BACK_OUT) + 3 :]
    kvown, crown, low, wbuf, kvl, every, pairb, kls, wsem, psem = refs[:10]
    refs = refs[10:]
    outs["kv"], outs["cross"] = kvown, crown
    at = Place(nz)
    at.greet()
    jobs = []
    for i, (name, chunk) in enumerate(order):
        mine = list(refs[Reduce.COUNT * i : Reduce.COUNT * (i + 1)])
        chunks = chunked.get(name, 1)
        out = outs[name]
        if chunks > 1:
            wide = out.shape[-1] // chunks
            out = out.at[:, pl.ds(chunk * wide, wide)]
        job = Reduce(at, out, mine, back_kind(name, late))
        if name == "cross":
            job.part = crossp
        if name == "kv":
            job.part = kvp
            job.part_cols = pl.ds(chunk * wide, wide)
            job.local_part, job.local_cols = kvl, job.part_cols
        jobs.append(job)
    refs = refs[Reduce.COUNT * len(order) :]
    spread = Gather(at, low, every, refs[: Gather.COUNT], False)
    everyone = Total(at, refs[Gather.COUNT :])
    load_w = [pltpu.make_async_copy(src, wbuf.at[i], wsem.at[i]) for i, src in enumerate((wq, wk, wv))]
    load_c = [pltpu.make_async_copy(src, wbuf.at[3 + i], wsem.at[3 + i]) for i, src in enumerate((wck, wcv))]
    for copy in load_w + load_c:
        copy.start()
    kv_local = pltpu.make_async_copy(kvp.at[:, :, at.w], kvl, kls)
    kv_local.start()
    width = x_ref.shape[1]
    inner = dq.shape[1]

    def make(name, chunk, part):
        if name in BACK_NONE:
            return
        _, _, _, r, wide = part.shape
        if name in ("k", "v"):
            left, right = n1, kvl.at[0, 0, :, pl.ds(0 if name == "k" else inner, inner)]
        else:
            left, right = {
                "gate": (n3, gg), "up": (n3, gu), "down": (mixed, go), "o": (att, g1), "cq": (n2, gcq), "co": (attc, g2),
                "q": (n1, dq),
            }[name]
        take = 2 if r % 128 else 1
        tile = 512 if wide % 512 == 0 else wide // 2 if wide % 256 == 0 and wide > 256 else wide
        for first in range(0, nz, take):
            piece = left[:, first * 4 * r : (first + take) * 4 * r]
            for c in range(0, wide, tile):
                out = mm(piece, right[:, chunk * wide + c : chunk * wide + c + tile], TN).astype(BF16)
                part[first : first + take, :, :, :, c : c + tile] = out.reshape(take, 2, 2, r, tile)

    def after_cross():
        both = crown[...]
        low[...] = jnp.concatenate([both, jnp.zeros_like(both)], axis=0).astype(BF16)
        for copy in load_c:
            copy.wait()
        genc = mm(low[:, :inner], wbuf[3].reshape(width, inner), NT) + mm(low[:, inner:], wbuf[4].reshape(width, inner), NT)
        genc_ref[...] = genc[:8]
        spread.place()
        spread.send()

    def pair_copy():
        return push(pairb.at[0], pairb.at[1], psem.at[0], psem.at[1], at.twin())

    def cross_weights():
        spread.end()
        owned = pairb.shape[1]
        rows = small_ref.shape[0] * small_ref.shape[1]
        col = lax.broadcasted_iota(jnp.int32, (width, 128), 0)
        lane = lax.broadcasted_iota(jnp.int32, (width, 128), 1)
        pick = ((col == at.me * owned + lane) & (lane < owned)).astype(BF16)
        mine = mm(small_ref[...].reshape(rows, width), pick, NN).astype(BF16)
        total = mm(mine, every[...].reshape(rows, 2 * inner), TN)[:owned]
        pairb[0] = total.astype(BF16)
        pair_copy().start()
        outs["ck"][...] = total[:, :inner]
        outs["cv"][...] = total[:, inner:]

    def cross_end():
        pair_copy().wait_recv()
        outs["ck"][...] += pairb[1, :, :inner].astype(F32)
        outs["cv"][...] += pairb[1, :, inner:].astype(F32)
        pair_copy().wait_send()
        spread.close()

    def after_kv():
        for copy in load_w:
            copy.wait()
        grad = mm(dq[...], wbuf[0].reshape(width, inner), NT)
        grad = grad + mm(kvl[0, 0, :, :inner], wbuf[1].reshape(width, inner), NT)
        grad = grad + mm(kvl[0, 0, :, inner:], wbuf[2].reshape(width, inner), NT)
        rows, gain = norm_back(x_ref[...].astype(F32), gains_ref[4:5], grad)
        gx_ref[...] = gh_ref[...] + rows
        everyone.buf[0] = gpart_ref[...]
        everyone.buf[0, 0:1, :] = gain
        everyone.send()

    kv_jobs = [i for i, entry in enumerate(order) if entry[0] == "kv"]
    kv_seen = kv_ended = 0
    early = [i for i, stage in steps if stage == 0 and order[i][0] not in BACK_NONE + ("k", "v")][:2]
    for i in early:
        make(*order[i], jobs[i].part)
    at.met()
    kv_sent = 0
    hops, later = [], {}
    for count, (i, stage) in enumerate(steps):
        (name, chunk), job = order[i], jobs[i]
        if stage == 0:
            if i not in early:
                make(name, chunk, job.part)
            job.send()
        if stage == 1:
            if i in kv_jobs:
                kv_seen += 1
                if kv_seen == 1:
                    kv_local.wait()
            job.after_w()
        if stage == 2:
            job.after_x()
        if stage == 3:
            job.after_y()
        if stage == 4:
            job.after_z()
        if stage == 5:
            job.end()
            if name == "cross":
                after_cross()
                later = {count + 5: spread.after_z, count + 10: spread.after_y, count + 15: cross_weights}
            if i in kv_jobs:
                kv_ended += 1
                if kv_ended == len(kv_jobs):
                    kvl[0, 0] = kvown[...].astype(BF16)
        if stage == 0 and name in ("k", "v"):
            kv_sent += 1
            if kv_sent == 2:
                after_kv()
                hops = [count + 4, count + 8, count + 12]
        if count in hops:
            everyone.after(hops.index(count))
        if count in later:
            later.pop(count)()
    for count in sorted(later):
        later[count]()
    for i, count in enumerate(hops):
        if count >= len(steps):
            everyone.after(i)
    cross_end()
    total_ref[...] = everyone.end()
    for job in jobs:
        job.close()


def back_step(
    kv_part, cross_part, weights, x, gains, grad_hidden, gpart, small, acts, shapes, nz, collective_id=2,
    plan=BACK_PLAN,
):
    late, chunked, order, steps = plan
    hb = pl.BlockSpec(memory_space=pl.ANY)
    vm = pl.BlockSpec(memory_space=pltpu.VMEM)
    rows, width = x.shape
    inner = acts[-1].shape[1]
    dma = pltpu.SemaphoreType.DMA
    own = [jax.ShapeDtypeStruct(shapes[name], F32) for name in BACK_OUT]
    scratch = [
        pltpu.VMEM((rows, 2 * inner), F32),
        pltpu.VMEM((8, 2 * inner), F32),
        pltpu.VMEM((16, 2 * inner), BF16),
        pltpu.VMEM((5,) + weights[0].shape, BF16),
        pltpu.VMEM((nz, 2, rows, 2 * inner), BF16),
        pltpu.VMEM((nz, 2, 2, 16, 2 * inner), BF16),
        pltpu.VMEM((2,) + shapes["ck"][:1] + (2 * inner,), BF16),
        dma,
        dma((5,)),
        dma((2,)),
    ]
    shapes = dict(shapes, kv=(rows, 2 * inner), cross=(8, 2 * inner))
    for name, _ in order:
        r, wide = shapes[name]
        wide = wide // chunked.get(name, 1)
        held = name not in BACK_NONE
        scratch += Reduce.scratch(nz, r, wide, back_kind(name, late), F32 if name == "cross" else BF16, part=held)
    scratch += Gather.scratch(nz, False) + Total.scratch(nz, gpart.shape[0], width)
    return pl.pallas_call(
        functools.partial(back_kernel, nz, late, chunked, order, steps),
        name="back",
        out_shape=tuple(own)
        + (
            jax.ShapeDtypeStruct((rows, width), F32),
            jax.ShapeDtypeStruct((8, width), F32),
            jax.ShapeDtypeStruct(gpart.shape, F32),
        ),
        in_specs=[hb, vm] + [hb] * 5 + [vm] * (5 + len(acts)),
        out_specs=tuple([vm] * (len(own) + 3)),
        scratch_shapes=scratch,
        compiler_params=pltpu.CompilerParams(
            collective_id=collective_id, has_side_effects=True, vmem_limit_bytes=BIG
        ),
    )(kv_part, cross_part, *weights, x, gains, grad_hidden, gpart, small, *acts)


def closing_kernel(count, *refs):
    for source, target in zip(refs[:count], refs[count:]):
        target[...] = source[...]


def closing(arrays):
    vm = pl.BlockSpec(memory_space=pltpu.VMEM)
    count = len(arrays)
    return pl.pallas_call(
        functools.partial(closing_kernel, count),
        name="closing",
        out_shape=tuple(jax.ShapeDtypeStruct(a.shape, a.dtype) for a in arrays),
        in_specs=[vm] * count,
        out_specs=tuple([vm] * count),
    )(*arrays)


class Bag:
    def __init__(self, names, refs):
        for name, ref in zip(names, refs):
            setattr(self, name, ref)


def flat(ref):
    value = ref[...]
    return value.reshape(-1, value.shape[-1])


def unstack(pair_rows, low):
    rows = pair_rows.shape[0] // 2
    return jnp.where(low, pair_rows[:rows], pair_rows[rows:])


def every_encoded(small_ref, take):
    devices, block, width = small_ref.shape
    rows = devices * take
    row = lax.broadcasted_iota(jnp.int32, (rows, devices * block), 0)
    col = lax.broadcasted_iota(jnp.int32, (rows, devices * block), 1)
    pick = (col == (row // take) * block + lax.rem(row, take)).astype(BF16)
    return mm(pick, small_ref[...].reshape(devices * block, width), NN).astype(BF16)


def cross_forward(b, low):
    pairs = b.cq.shape[1] // 128
    for pair in range(pairs):
        lanes = slice(128 * pair, 128 * pair + 128)
        qm = stack_pair(b.cq[:, lanes], low)
        s = mm(qm, b.ckeys[:, lanes], NT)
        peak = jnp.max(s, axis=1, keepdims=True)
        log_total = peak + jnp.log(jnp.sum(jnp.exp(s - peak), axis=1, keepdims=True))
        p = jnp.exp(s - log_total)
        b.cprob[pair] = p
        b.attc[:, lanes] = unstack(mm(p.astype(BF16), b.cvals[:, lanes], NN), low).astype(BF16)


def cross_backward(b, gac, low, keys_each):
    pairs = b.cq.shape[1] // 128
    inner = b.cq.shape[1]
    owners = 4 * b.crossp.shape[0]
    b.crossp[...] = jnp.zeros_like(b.crossp)
    for pair in range(pairs):
        lanes = slice(128 * pair, 128 * pair + 128)
        qm = stack_pair(b.cq[:, lanes], low)
        dom = stack_pair(gac[:, lanes], low)
        p = b.cprob[pair]
        dp = mm(dom, b.cvals[:, lanes], NT)
        ds = (p * (dp - jnp.sum(p * dp, axis=1, keepdims=True))).astype(BF16)
        b.gcq[:, lanes] = unstack(mm(ds, b.ckeys[:, lanes], NN), low).astype(BF16)
        gk = mm(ds, qm, TN)
        gv = mm(p.astype(BF16), dom, TN)
        for owner in range(owners):
            rows = slice(keys_each * owner, keys_each * owner + keys_each)
            b.crossp[owner // 4, owner // 2 % 2, owner % 2, 0:keys_each, lanes] = gk[rows]
            b.crossp[owner // 4, owner // 2 % 2, owner % 2, 0:keys_each, 128 * pair + inner : 128 * pair + inner + 128] = gv[rows]


GELU_A = 0.7978845608028654
GELU_B = 0.044715


def gelu_parts(v):
    t = jnp.tanh(GELU_A * (v + GELU_B * v * v * v))
    value = 0.5 * v * (1.0 + t)
    slope = 0.5 * (1.0 + t) + 0.5 * v * (1.0 - t * t) * (GELU_A * (1.0 + 3.0 * GELU_B * v * v))
    return value, slope


FF_TILE = 1024


def after_attention(b):
    b.h1[...] = b.x[...].astype(F32) + mm(b.att[...], flat(b.w_o), NN)
    b.n2[...] = normed(b.h1[...], b.gains[5:6]).astype(BF16)
    b.cq[...] = mm(b.n2[...], flat(b.w_cq), NN).astype(BF16)


def after_cross_attention(b):
    b.h2[...] = b.h1[...] + mm(b.attc[...], flat(b.w_co), NN)
    b.n3[...] = normed(b.h2[...], b.gains[6:7]).astype(BF16)


def feed_forward(b):
    ff = b.mixed.shape[1]
    width = b.x.shape[1]
    for c in range(0, ff, FF_TILE):
        cols = slice(c, c + FF_TILE)
        gate = mm(b.n3[...], b.w_gate[:, :, cols].reshape(width, FF_TILE), NN)
        up = mm(b.n3[...], b.w_up[:, :, cols].reshape(width, FF_TILE), NN)
        value, slope = gelu_parts(gate)
        b.mixed[:, cols] = (value * up).astype(BF16)
        b.hg[:, cols] = value
        b.hs[:, cols] = slope * up
    b.layer_out[...] = (b.h2[...] + mm(b.mixed[...], flat(b.w_down), NN)).astype(BF16)


def feed_backward(b):
    ff = b.mixed.shape[1]
    width = b.x.shape[1]
    down = flat(b.w_down)
    total = jnp.zeros(b.h2.shape, F32)
    for c in range(0, ff, FF_TILE):
        cols = slice(c, c + FF_TILE)
        gm = mm(b.go[...], down[cols], NT).astype(BF16).astype(F32)
        gg = (gm * b.hs[:, cols]).astype(BF16)
        gu = (gm * b.hg[:, cols]).astype(BF16)
        b.gg[:, cols] = gg
        b.gu[:, cols] = gu
        total = total + mm(gg, b.w_gate[:, :, cols].reshape(width, FF_TILE), NT)
        total = total + mm(gu, b.w_up[:, :, cols].reshape(width, FF_TILE), NT)
    rows, gain = norm_back(b.h2[...], b.gains[6:7], total)
    b.gpart[2:3, :] = gain
    b.gh[...] = b.go[...].astype(F32) + rows
    b.g2[...] = b.gh[...].astype(BF16)


def before_attention(b):
    rows, gain = norm_back(b.h1[...], b.gains[5:6], mm(b.gcq[...], flat(b.w_cq), NT))
    b.gpart[1:2, :] = gain
    b.gh[...] = b.gh[...] + rows
    b.g1[...] = b.gh[...].astype(BF16)
    b.gatt[...] = mm(b.g1[...], flat(b.w_o), NT).astype(BF16)


GROUP = 4


def stack_group(block):
    head = lax.broadcasted_iota(jnp.int32, block.shape, 1) // BLK
    zero = jnp.zeros_like(block)
    return jnp.concatenate([jnp.where(head == i, block, zero) for i in range(GROUP)], axis=0)


def unstack_group(stacked):
    rows = stacked.shape[0] // GROUP
    head = lax.broadcasted_iota(jnp.int32, (rows, stacked.shape[1]), 1) // BLK
    out = stacked[:rows]
    for i in range(1, GROUP):
        out = jnp.where(head == i, stacked[i * rows : i * rows + rows], out)
    return out


def fill_bias(b, qb, rank):
    pairs = b.q.shape[1] // 128
    key_j = lax.broadcasted_iota(jnp.int32, (CH, 128), 0)
    lane_i = lax.broadcasted_iota(jnp.int32, (CH, 128), 1)
    high = lane_i >= BLK
    row_i = jnp.where(high, lane_i - BLK, lane_i)
    shift = jnp.where(high, BLK, 0)
    for kind in range(2):
        dist = (lax.rem(rank, 4) + 4 * kind) * BLK + row_i - key_j
        bucket = bucket_ids(jnp.maximum(dist, 0)) + shift
        for pair in range(pairs):
            tile = jnp.take_along_axis(jnp.broadcast_to(b.tb[pl.ds(pair, 1), :], (CH, 128)), bucket, axis=1)
            if kind == 0:
                tile = jnp.where(dist >= 0, tile, MASKED)
            b.bias[qb, kind, pair // 2, :, 128 * (pair % 2) : 128 * (pair % 2) + 128] = tile
    for pair in range(pairs):
        b.bias[qb, 2, pair // 2, :, 128 * (pair % 2) : 128 * (pair % 2) + 128] = jnp.where(
            high,
            b.tb[pl.ds(pair, 1), pl.ds(BLK + BUCKETS - 1, 1)],
            b.tb[pl.ds(pair, 1), pl.ds(BUCKETS - 1, 1)],
        )


def self_forward_block(b, qb, rank):
    inner = b.q.shape[1]
    wide = GROUP * BLK
    groups = inner // wide
    last = rank // 4
    mine = pl.ds(qb * BLK, BLK)
    for i in range(groups):
        b.qm[qb, i] = stack_group(b.q[mine, wide * i : wide * i + wide])
        b.top[i] = jnp.full((8, wide), -3e38, F32)
        b.sums[i] = jnp.zeros((8, wide), F32)
        b.acc[i] = jnp.zeros((wide, wide), F32)

    def first(chunk, carry):
        kind = jnp.minimum(last - chunk, 2)
        keys = pl.ds(pl.multiple_of(chunk * CH, CH), CH)
        for i in range(groups):
            s = mm(b.kvs[keys, wide * i : wide * i + wide], b.qm[qb, i], NT) + b.bias[qb, kind, i]
            b.sco[i, keys, :] = s
            b.top[i] = jnp.maximum(b.top[i], jnp.max(s.reshape(CH // 8, 8, wide), axis=0))
        return carry

    lax.fori_loop(0, last + 1, first, 0)
    for i in range(groups):
        b.top[i] = jnp.broadcast_to(jnp.max(b.top[i], axis=0, keepdims=True), (8, wide))

    def second(chunk, carry):
        keys = pl.ds(pl.multiple_of(chunk * CH, CH), CH)
        for i in range(groups):
            p = jnp.exp(b.sco[i, keys, :] - b.top[i, 0:1, :])
            b.sums[i] += jnp.sum(p.reshape(CH // 8, 8, wide), axis=0)
            values = b.kvs[keys, inner + wide * i : inner + wide * i + wide]
            b.acc[i] += mm(p.astype(BF16), values, TN)
        return carry

    lax.fori_loop(0, last + 1, second, 0)
    for i in range(groups):
        total = jnp.sum(b.sums[i], axis=0, keepdims=True)
        b.rows[qb, i, 0:1, :] = b.top[i, 0:1, :] + jnp.log(total)
        parts = []
        for side in range(wide // 128):
            scale = jnp.broadcast_to(total[:, 128 * side : 128 * side + 128], (128, 128)).T
            rows = b.acc[i, 128 * side : 128 * side + 128, :]
            parts.append(rows / jnp.concatenate([scale] * (wide // 128), axis=1))
        out = unstack_group(jnp.concatenate(parts, axis=0))
        b.att32[mine, wide * i : wide * i + wide] = out
        b.att[mine, wide * i : wide * i + wide] = out.astype(BF16)


def self_backward_rows(b, qb):
    inner = b.q.shape[1]
    wide = GROUP * BLK
    mine = pl.ds(qb * BLK, BLK)
    for i in range(inner // wide):
        b.dom[qb, i] = stack_group(b.gatt[mine, wide * i : wide * i + wide])
    for pair in range(inner // 128):
        lanes = slice(128 * pair, 128 * pair + 128)
        prod = (b.gatt[mine, lanes].astype(F32) * b.att32[mine, lanes]).T
        b.rows[qb, pair // 2, 1:2, 128 * (pair % 2) : 128 * (pair % 2) + 128] = jnp.concatenate(
            [jnp.sum(prod[:BLK], axis=0, keepdims=True), jnp.sum(prod[BLK:], axis=0, keepdims=True)], axis=1
        )


def self_backward_block(b, qb, rank, longer):
    inner = b.q.shape[1]
    wide = GROUP * BLK
    groups = inner // wide
    last = rank // 4
    b.acc[...] = jnp.zeros_like(b.acc)

    @pl.when(last == 0)
    def _():
        for i in range(groups):
            b.near[i, pl.ds(0, CH), :] = jnp.zeros((CH, wide), F32)

    def step(chunk, carry):
        kind = jnp.minimum(last - chunk, 2)
        keys = pl.ds(pl.multiple_of(chunk * CH, CH), CH)
        keep = jnp.maximum(chunk - last + 1, 0)
        for i in range(groups):
            klanes = slice(wide * i, wide * i + wide)
            vlanes = slice(inner + wide * i, inner + wide * i + wide)
            kp = b.kvs[keys, klanes]
            qp = b.qm[qb, i]
            gp = b.dom[qb, i]
            st = mm(kp, qp, NT) + b.bias[qb, kind, i]
            pt = jnp.exp(st - b.rows[qb, i, 0:1, :])
            dp = mm(b.kvs[keys, vlanes], gp, NT)
            ds = pt * (dp - b.rows[qb, i, 1:2, :])
            dsb = ds.astype(BF16)
            gv = mm(pt.astype(BF16), gp, NN)
            gk = mm(dsb, qp, NN)
            b.dkv[keys, vlanes] = gv if longer else b.dkv[keys, vlanes] + gv
            b.dkv[keys, klanes] = gk if longer else b.dkv[keys, klanes] + gk
            b.acc[i] += mm(dsb, kp, TN)
            b.tot[i] += jnp.sum(ds.reshape(CH // 8, 8, wide), axis=0)
            b.near[i, pl.ds(pl.multiple_of(keep * CH, CH), CH), :] = ds
        return carry

    lax.fori_loop(0, last + 1, step, 0)
    if longer:

        def unseen(chunk, carry):
            keys = pl.ds(pl.multiple_of(chunk * CH, CH), CH)
            b.dkv[keys, :] = jnp.zeros((CH, 2 * inner), F32)
            return carry

        lax.fori_loop(last + 1, b.dkv.shape[0] // CH, unseen, 0)
    mine = pl.ds(pl.multiple_of(qb * BLK, BLK), BLK)
    for i in range(groups):
        b.dq[mine, wide * i : wide * i + wide] = unstack_group(b.acc[i]).astype(BF16)
        for gap in range(3):
            offset = pl.multiple_of((rank - gap - 4 * (last - 1)) * BLK, BLK)
            b.nacc[gap, i] += b.near[i, pl.ds(offset, BLK), :]


def bucket_of(distance):
    half_count = BUCKETS // 2
    edges = [math.ceil(half_count * math.pow(MAXDIST / half_count, k / half_count)) for k in range(1, half_count)]
    return min(distance, half_count) + sum(distance >= edge for edge in edges)


def bias_gradient(b):
    pairs = b.q.shape[1] // 128
    key_s = lax.broadcasted_iota(jnp.int32, (BLK, 128), 0)
    lane = lax.broadcasted_iota(jnp.int32, (BLK, 128), 1)
    row_s = jnp.where(lane < BLK, lane, lane - BLK)
    buckets = [bucket_ids(jnp.maximum(gap * BLK + row_s - key_s, 0)) for gap in range(3)]
    spans = [(bucket_of(max(BLK * (gap - 1) + 1, 0)), bucket_of(BLK * (gap + 1) - 1)) for gap in range(3)]
    for pair in range(pairs):
        lanes = slice(128 * (pair % 2), 128 * (pair % 2) + 128)
        tiles = [b.nacc[gap, pair // 2, :, lanes] for gap in range(3)]
        far = jnp.sum(b.tot[pair // 2, :, lanes], axis=0, keepdims=True)
        for tile in tiles:
            far = far - jnp.sum(tile, axis=0, keepdims=True)
        lines = []
        for number in range(BUCKETS):
            met = [gap for gap in range(3) if spans[gap][0] <= number <= spans[gap][1]]
            part = jnp.where(buckets[met[0]] == number, tiles[met[0]], 0.0)
            for gap in met[1:]:
                part = part + jnp.where(buckets[gap] == number, tiles[gap], 0.0)
            line = jnp.sum(part, axis=0, keepdims=True)
            lines.append(line + far if number == BUCKETS - 1 else line)
        grid = jnp.concatenate(lines + [jnp.zeros((128 - BUCKETS, 128), F32)], axis=0).T
        b.gpart[8 + 2 * pair : 9 + 2 * pair, 0:128] = jnp.sum(grid[:BLK], axis=0, keepdims=True)
        b.gpart[9 + 2 * pair : 10 + 2 * pair, 0:128] = jnp.sum(grid[BLK:], axis=0, keepdims=True)


MID_IN = (
    "deal", "k_hbm", "v_hbm", "o", "cq_w", "ck", "cv", "co", "gate", "up", "down", "x", "gains", "small", "q", "go", "tb",
)
MID_OUT = (
    "layer_out", "n3", "mixed", "att", "n2", "attc", "gg", "gu", "g1", "gcq", "g2", "dq", "gh", "gpart", "crossp", "dkv_hbm",
)
MID_SCRATCH = (
    "kvs", "dkv", "w_o", "w_cq", "w_ck", "w_cv", "w_co", "w_gate", "w_up", "w_down", "h1", "h2", "cq", "ckeys", "cvals", "cprob",
    "hg", "hs", "gatt", "bias", "qm", "dom", "top", "sums", "acc", "sco", "rows", "att32", "near", "nacc", "tot", "sem", "osem", "wsem",
)


def mid_kernel(enc_own, *refs):
    b = Bag(MID_IN + MID_OUT + MID_SCRATCH, refs)
    load_in_order(b.deal, b.k_hbm, b.v_hbm, b.kvs, b.sem)
    loads = []
    for i, name in enumerate(("o", "cq", "ck", "cv", "co", "gate", "up", "down")):
        source = b.cq_w if name == "cq" else getattr(b, name)
        loads.append(pltpu.make_async_copy(source, getattr(b, "w_" + name), b.wsem.at[i]))
        loads[-1].start()
    low = lax.broadcasted_iota(jnp.int32, (2 * BLK, 128), 1) < BLK
    device = lax.axis_index(AXES)
    ranks = [b.deal[device, qb] for qb in range(2)]
    for qb in range(2):
        fill_bias(b, qb, ranks[qb])
    loaded(b.k_hbm, b.v_hbm, b.kvs, b.sem)
    for qb in range(2):
        self_forward_block(b, qb, ranks[qb])
    for load in loads[:5]:
        load.wait()
    after_attention(b)
    enc = every_encoded(b.small, enc_own)
    b.ckeys[...] = mm(enc, flat(b.w_ck), NN).astype(BF16)
    b.cvals[...] = mm(enc, flat(b.w_cv), NN).astype(BF16)
    cross_forward(b, low)
    after_cross_attention(b)
    for load in loads[5:]:
        load.wait()
    feed_forward(b)
    b.gpart[...] = jnp.zeros_like(b.gpart)
    feed_backward(b)
    gac = mm(b.g2[...], flat(b.w_co), NT).astype(BF16)
    cross_backward(b, gac, low, enc_own)
    before_attention(b)
    b.tot[...] = jnp.zeros_like(b.tot)
    b.nacc[...] = jnp.zeros_like(b.nacc)
    for qb in range(2):
        self_backward_rows(b, qb)
    longer = jnp.where(ranks[0] > ranks[1], 0, 1)
    self_backward_block(b, longer, jnp.maximum(ranks[0], ranks[1]), True)
    self_backward_block(b, 1 - longer, jnp.minimum(ranks[0], ranks[1]), False)
    blocks = b.k_hbm.shape[0] // BLK

    def out_one(index, carry):
        here = pl.ds(pl.multiple_of(b.deal[index // 2, index % 2] * BLK, BLK), BLK)
        b.kvs[here, :] = b.dkv[here, :].astype(BF16)
        pltpu.make_async_copy(b.kvs.at[here], b.dkv_hbm.at[pl.ds(index * BLK, BLK)], b.osem).start()
        return carry

    lax.fori_loop(0, blocks, out_one, 0)
    bias_gradient(b)
    pltpu.make_async_copy(b.kvs, b.dkv_hbm, b.osem).wait()


def mid(deal, keys, values, weights, x, gains, small, q, go, tb, enc_own):
    rows, width = x.shape
    inner = q.shape[1]
    total = keys.shape[0]
    ff = weights[5].shape[2]
    wide = GROUP * BLK
    h2, h4 = inner // 128, inner // wide
    shards = weights[0].shape[0]
    enc = shards * enc_own
    sm = pl.BlockSpec(memory_space=pltpu.SMEM)
    vm = pl.BlockSpec(memory_space=pltpu.VMEM)
    hb = pl.BlockSpec(memory_space=pl.ANY)
    out = jax.ShapeDtypeStruct
    return pl.pallas_call(
        functools.partial(mid_kernel, enc_own),
        name="mid",
        out_shape=(
            out((rows, width), BF16), out((rows, width), BF16), out((rows, ff), BF16), out((rows, inner), BF16),
            out((rows, width), BF16), out((rows, inner), BF16), out((rows, ff), BF16), out((rows, ff), BF16),
            out((rows, width), BF16), out((rows, inner), BF16), out((rows, width), BF16), out((rows, inner), BF16),
            out((rows, width), F32), out((24, width), F32), out((shards // 4, 2, 2, 8, 2 * inner), F32),
            out((total, 2 * inner), BF16),
        ),
        in_specs=[sm] + [hb] * (2 + len(weights)) + [vm] * 6,
        out_specs=tuple([vm] * 15 + [hb]),
        scratch_shapes=[
            pltpu.VMEM((total, 2 * inner), BF16),
            pltpu.VMEM((total, 2 * inner), F32),
        ]
        + [pltpu.VMEM(weight.shape, BF16) for weight in weights]
        + [
            pltpu.VMEM((rows, width), F32),
            pltpu.VMEM((rows, width), F32),
            pltpu.VMEM((rows, inner), BF16),
            pltpu.VMEM((enc, inner), BF16),
            pltpu.VMEM((enc, inner), BF16),
            pltpu.VMEM((h2, 2 * rows, enc), F32),
            pltpu.VMEM((rows, ff), F32),
            pltpu.VMEM((rows, ff), F32),
            pltpu.VMEM((rows, inner), BF16),
            pltpu.VMEM((2, 3, h4, CH, wide), F32),
            pltpu.VMEM((2, h4, wide, wide), BF16),
            pltpu.VMEM((2, h4, wide, wide), BF16),
            pltpu.VMEM((h4, 8, wide), F32),
            pltpu.VMEM((h4, 8, wide), F32),
            pltpu.VMEM((h4, wide, wide), F32),
            pltpu.VMEM((h4, total, wide), F32),
            pltpu.VMEM((2, h4, 8, wide), F32),
            pltpu.VMEM((rows, inner), F32),
            pltpu.VMEM((h4, 2 * CH, wide), F32),
            pltpu.VMEM((3, h4, BLK, wide), F32),
            pltpu.VMEM((h4, 8, wide), F32),
            pltpu.SemaphoreType.DMA((2,)),
            pltpu.SemaphoreType.DMA,
            pltpu.SemaphoreType.DMA((8,)),
        ],
        compiler_params=pltpu.CompilerParams(vmem_limit_bytes=BIG),
    )(deal, keys, values, *weights, x, gains, small, q, go, tb)


def fits(*operands):
    layer_in, encoded, self_query, relative_bias = operands[0], operands[1], operands[4], operands[18]
    total = layer_in.shape[1] * lax.axis_size(AXES)
    return (
        lax.axis_size(GRP) == 2
        and lax.axis_size(WSH) == 2
        and lax.axis_size(CTX) == 8
        and layer_in.shape[1] == 2 * BLK
        and encoded.shape[1] == 4
        and total // 2 <= CONT_TOK
        and self_query.shape[0] % 16 == 0
        and self_query.shape[1] == relative_bias.shape[1] * BLK
        and self_query.shape[1] % 256 == 0
    )


def fast(
    layer_in, encoded, cotangent, deal_table, self_query, self_key, self_value, self_output, cross_query, cross_key,
    cross_value, cross_output, feed_gate, feed_up, feed_down, gain_self, gain_cross, gain_feed, relative_bias,
):
    nz = lax.axis_size(CTX) // 2
    shards = lax.axis_size(AXES)
    device = lax.axis_index(AXES)
    rows = layer_in.shape[1]
    width = layer_in.shape[2]
    heads = relative_bias.shape[1]
    inner = self_query.shape[1]
    owned = gain_self.shape[0]
    enc_own = encoded.shape[1]
    table_hb = relative_bias.astype(F32).T

    gains_here = lax.dynamic_update_slice(
        jnp.zeros((3, width), BF16), jnp.stack([gain_self, gain_cross, gain_feed]), (0, device * owned)
    )
    small = jnp.concatenate([encoded[0], gains_here, jnp.zeros((9, width), BF16)], axis=0)
    *wholes, queries, normed_one, gains = front(
        layer_in[0],
        (
            small, self_key, self_value, self_query, self_output, cross_query, cross_key, cross_value, cross_output,
            feed_gate, feed_up, feed_down,
        ),
        nz,
        shards,
    )
    whole = {name: value.reshape((shards,) + value.shape[3:]) for name, value in zip(FRONT_PARTS, wholes)}
    in_rows = {name: value.reshape(-1, value.shape[-1]) for name, value in whole.items()}
    (
        layer_out, normed_three, mixed_hidden, attended, normed_two, attended_cross, grad_gate, grad_up, grad_one_low,
        grad_cq_low, grad_two_low, grad_queries, grad_hidden_one, gpart, cross_part, kv_part,
    ) = mid(
        deal_table, in_rows["keys"], in_rows["values"],
        [whole[name] for name in ("o", "cq", "ck", "cv", "co", "gate", "up", "down")],
        layer_in[0], gains, whole["small"], queries, cotangent[0], pair_table(table_hb), enc_own,
    )
    ff = feed_gate.shape[1]
    square = (owned, inner)
    shapes = dict(
        gate=(owned, ff), up=(owned, ff), down=(feed_down.shape[0], width), co=(inner // shards, width), cq=square,
        ck=square, cv=square, q=square, o=(inner // shards, width), k=square, v=square,
    )
    result = back_step(
        kv_part.reshape(nz, 2, 2, rows, 2 * inner), cross_part,
        [whole[name] for name in ("q", "k", "v", "ck", "cv")], layer_in[0], gains,
        grad_hidden_one, gpart, whole["small"],
        (
            normed_three, mixed_hidden, attended, normed_two, attended_cross, normed_one, grad_gate, grad_up, cotangent[0],
            grad_one_low, grad_cq_low, grad_two_low, grad_queries,
        ),
        shapes,
        nz,
    )
    grad_enc, total = result[len(BACK_OUT) + 1 :]
    result = closing(result[: len(BACK_OUT) + 1])
    got = dict(zip(BACK_OUT, result))
    grad_input = result[len(BACK_OUT)]
    gain_grads = [lax.dynamic_slice_in_dim(total[i], device * owned, owned) for i in range(3)]
    grad_relative_bias = total[8 : 8 + heads, :BUCKETS].T
    return (
        layer_out[None], grad_input[None], grad_enc[None, :enc_own],
        got["q"], got["k"], got["v"], got["o"], got["cq"], got["ck"], got["cv"], got["co"], got["gate"], got["up"], got["down"],
        gain_grads[0], gain_grads[1], gain_grads[2], grad_relative_bias,
    )


def solution(mesh):
    return jax.shard_map(
        lambda *operands: (fast if fits(*operands) else local)(*operands),
        mesh=mesh,
        in_specs=(
            P(GRP, AXES, None),
            P(GRP, AXES, None),
            P(GRP, AXES, None),
            P(),
            P(AXES, None),
            P(AXES, None),
            P(AXES, None),
            P(AXES, None),
            P(AXES, None),
            P(AXES, None),
            P(AXES, None),
            P(AXES, None),
            P(AXES, None),
            P(AXES, None),
            P(AXES, None),
            P(AXES),
            P(AXES),
            P(AXES),
            P(),
        ),
        out_specs=(
            P(GRP, AXES, None),
            P(GRP, AXES, None),
            P(GRP, AXES, None),
            P(AXES, None),
            P(AXES, None),
            P(AXES, None),
            P(AXES, None),
            P(AXES, None),
            P(AXES, None),
            P(AXES, None),
            P(AXES, None),
            P(AXES, None),
            P(AXES, None),
            P(AXES, None),
            P(AXES),
            P(AXES),
            P(AXES),
            P(),
        ),
        check_vma=False,
    )
```

```python
import functools
import math

import jax
import jax.numpy as jnp
from jax import lax
from jax.experimental import pallas as pl
from jax.experimental.pallas import tpu as pltpu
from jax.sharding import PartitionSpec as P

GRP, CTX, WSH = "grp", "ctx", "wsh"
AXES = (CTX, WSH)
EVERY = (GRP, CTX, WSH)
QK = "qhd,khd->hqk"
PV = "hqk,khd->qhd"
PTQ = "hqk,qhd->khd"
TF_TD = "tf,td->fd"
TD_FD = "td,fd->tf"
TD_TF = "td,tf->df"
TF_DF = "tf,df->td"
TC_TD = "tc,td->cd"
TD_CD = "td,cd->tc"
TD_TC = "td,tc->dc"
TC_DC = "tc,dc->td"

BUCKETS = 32
MAXDIST = 128
CONT_TOK = 2048


MASKED = -1e30
EPSILON = 1e-06


def rms_norm(hidden, gain_vector):
    return (
        hidden
        * lax.rsqrt(jnp.mean(hidden * hidden, axis=-1, keepdims=True) + EPSILON)
        * gain_vector
    )


def gated(gate_pre, up_pre):
    return jax.nn.gelu(gate_pre, approximate=True) * up_pre


def bounce(values):
    return lax.optimization_barrier(values.astype(jnp.bfloat16)).astype(jnp.float32)


def split_probs(probs_full):
    probs_high = probs_full.astype(jnp.bfloat16)
    probs_rest = (probs_full - probs_high.astype(jnp.float32)).astype(jnp.bfloat16)
    return (probs_high, probs_rest)


def bucket_ids(distance):
    exact_half = BUCKETS // 2
    counted = jnp.minimum(distance, exact_half)
    for number in range(1, exact_half):
        boundary = int(math.ceil(exact_half * math.pow(MAXDIST / exact_half, number / exact_half)))
        counted = counted + (distance >= boundary).astype(jnp.int32)
    return counted


def token_place(tokens, prompt_len, cont_len):
    beyond = tokens - prompt_len
    in_prompt = tokens < prompt_len
    sequence = jnp.where(in_prompt, 0, 1 + beyond // cont_len)
    position = jnp.where(in_prompt, tokens, prompt_len + beyond % cont_len)
    return (sequence, position)


def pair_mask(seq_query, pos_query, seq_key, pos_key):
    earlier = pos_key[None, :] <= pos_query[:, None]
    visible = (seq_key[None, :] == seq_query[:, None]) | (seq_key[None, :] == 0)
    return earlier & visible


def bucket_bias(pos_query, pos_key, table_hb):
    buckets = bucket_ids(jnp.maximum(pos_query[:, None] - pos_key[None, :], 0))
    picks = (
        buckets[None, :, :, None]
        == jnp.arange(table_hb.shape[1], dtype=jnp.int32)[None, None, None, :]
    )
    return (buckets, jnp.sum(jnp.where(picks, table_hb[:, None, None, :], 0.0), axis=-1))


def bucket_grad(buckets, grad_scores, bucket_count):
    picks = (
        buckets[None, :, :, None] == jnp.arange(bucket_count, dtype=jnp.int32)[None, None, None, :]
    )
    return jnp.sum(
        jnp.where(picks, grad_scores.astype(jnp.float32)[:, :, :, None], 0.0), axis=(1, 2)
    )


def masked_scores(query_heads, key_heads, bias, allowed):
    direct = jnp.einsum(QK, query_heads, key_heads, preferred_element_type=jnp.float32)
    return jnp.where(allowed[None], direct + bias, MASKED)


def score_grads(scores, log_total, delta_row, grad_heads, value_heads):
    probs_full = jnp.exp(scores - log_total[:, :, None])
    grad_probs = jnp.einsum(
        QK, grad_heads, value_heads, preferred_element_type=jnp.float32
    )
    grad_scores = (probs_full * (grad_probs - delta_row[:, :, None])).astype(jnp.bfloat16)
    return (probs_full.astype(jnp.bfloat16), grad_scores)


def key_view(seq_all, pos_all, step_index, key_rows, seq_query, pos_query):
    seq_key = lax.dynamic_slice_in_dim(seq_all, step_index * key_rows, key_rows)
    pos_key = lax.dynamic_slice_in_dim(pos_all, step_index * key_rows, key_rows)
    return (pos_key, pair_mask(seq_query, pos_query, seq_key, pos_key))


def self_forward(
    query_heads, key_heads, value_heads, seq_all, pos_all, seq_query, pos_query, table_hb, key_rows
):
    total_rows = key_heads.shape[0]
    head_count = query_heads.shape[1]
    rows_here = query_heads.shape[0]
    step_list = jnp.arange(total_rows // key_rows, dtype=jnp.int32)

    def total_step(carried, step_index):
        pos_key, allowed = key_view(seq_all, pos_all, step_index, key_rows, seq_query, pos_query)

        def total_accumulate(current):
            running_max, running_sum = current
            key_block = lax.dynamic_slice_in_dim(key_heads, step_index * key_rows, key_rows)
            bias = bucket_bias(pos_query, pos_key, table_hb)[1]
            scores = masked_scores(query_heads, key_block, bias, allowed)
            new_max = jnp.maximum(running_max, jnp.max(scores, axis=-1))
            weights = jnp.where(allowed[None], jnp.exp(scores - new_max[:, :, None]), 0.0)
            return (
                new_max,
                running_sum * jnp.exp(running_max - new_max) + jnp.sum(weights, axis=-1),
            )

        return (
            lax.cond(jnp.any(allowed), total_accumulate, lambda current: current, carried),
            None,
        )

    start_state = (
        jnp.full((head_count, rows_here), MASKED, jnp.float32),
        jnp.zeros((head_count, rows_here), jnp.float32),
    )
    (running_max, running_sum), _ = lax.scan(total_step, start_state, step_list)
    log_total = running_max + jnp.log(running_sum)

    def output_step(carried, step_index):
        pos_key, allowed = key_view(seq_all, pos_all, step_index, key_rows, seq_query, pos_query)

        def output_accumulate(current):
            rounded_sum, rest_sum = current
            key_block = lax.dynamic_slice_in_dim(key_heads, step_index * key_rows, key_rows)
            value_block = lax.dynamic_slice_in_dim(value_heads, step_index * key_rows, key_rows)
            bias = bucket_bias(pos_query, pos_key, table_hb)[1]
            scores = masked_scores(query_heads, key_block, bias, allowed)
            probs_high, probs_rest = split_probs(jnp.exp(scores - log_total[:, :, None]))
            rounded_sum = rounded_sum + jnp.einsum(
                PV, probs_high, value_block, preferred_element_type=jnp.float32
            )
            rest_sum = rest_sum + jnp.einsum(
                PV, probs_rest, value_block, preferred_element_type=jnp.float32
            )
            return (rounded_sum, rest_sum)

        return (
            lax.cond(jnp.any(allowed), output_accumulate, lambda current: current, carried),
            None,
        )

    zero_heads = jnp.zeros(query_heads.shape, jnp.float32)
    (rounded_sum, rest_sum), _ = lax.scan(output_step, (zero_heads, zero_heads), step_list)
    return (log_total, rounded_sum, rounded_sum + rest_sum)


def query_backward(
    query_heads,
    key_heads,
    value_heads,
    grad_heads,
    log_total,
    delta_row,
    seq_all,
    pos_all,
    seq_query,
    pos_query,
    table_hb,
    key_rows,
):
    total_rows = key_heads.shape[0]
    inner_width = key_heads.shape[1] * key_heads.shape[2]
    bucket_count = table_hb.shape[1]
    step_list = jnp.arange(total_rows // key_rows, dtype=jnp.int32)

    def step_body(carried, step_index):
        pos_key, allowed = key_view(seq_all, pos_all, step_index, key_rows, seq_query, pos_query)

        def step_accumulate(current):
            grad_query, grad_bias = current
            key_block = lax.dynamic_slice_in_dim(key_heads, step_index * key_rows, key_rows)
            value_block = lax.dynamic_slice_in_dim(value_heads, step_index * key_rows, key_rows)
            buckets, bias = bucket_bias(pos_query, pos_key, table_hb)
            scores = masked_scores(query_heads, key_block, bias, allowed)
            probs_low, grad_scores = score_grads(
                scores, log_total, delta_row, grad_heads, value_block
            )
            grad_query = grad_query + jnp.einsum(
                PV, grad_scores, key_block, preferred_element_type=jnp.float32
            )
            grad_bias = grad_bias + bucket_grad(buckets, grad_scores, bucket_count)
            grad_key = jnp.einsum(
                PTQ, grad_scores, query_heads, preferred_element_type=jnp.float32
            ).reshape(key_rows, inner_width)
            grad_value = jnp.einsum(
                PTQ, probs_low, grad_heads, preferred_element_type=jnp.float32
            ).reshape(key_rows, inner_width)
            return ((grad_query, grad_bias), jnp.concatenate([grad_key, grad_value], axis=1))

        blank_block = jnp.zeros((key_rows, 2 * inner_width), jnp.float32)
        return lax.cond(
            jnp.any(allowed), step_accumulate, lambda current: (current, blank_block), carried
        )

    start_state = (
        jnp.zeros(query_heads.shape, jnp.float32),
        jnp.zeros(table_hb.shape, jnp.float32),
    )
    final_state, key_blocks = lax.scan(step_body, start_state, step_list)
    return (final_state[0], final_state[1], key_blocks.reshape(total_rows, 2 * inner_width))


def local(
    layer_in,
    encoded,
    cotangent,
    deal_table,
    self_query,
    self_key,
    self_value,
    self_output,
    cross_query,
    cross_key,
    cross_value,
    cross_output,
    feed_gate,
    feed_up,
    feed_down,
    gain_self,
    gain_cross,
    gain_feed,
    relative_bias,
):
    shards = lax.axis_size(AXES)
    device = lax.axis_index(AXES)
    ctx_count = lax.axis_size(CTX)
    core_count = lax.axis_size(WSH)
    local_rows = layer_in.shape[1]
    total_rows = local_rows * shards
    block_len = local_rows // 2
    cont_len = min(CONT_TOK, total_rows // 2)
    prompt_len = total_rows - total_rows // 2 // cont_len * cont_len
    key_rows = min(1024, total_rows)
    head_count = relative_bias.shape[1]
    inner_width = self_query.shape[1]
    head_size = inner_width // head_count
    enc_rows = encoded.shape[1] * shards
    table_hb = relative_bias.astype(jnp.float32).T
    flat_table = deal_table.reshape(-1)
    all_tokens = (
        flat_table[:, None] * block_len + jnp.arange(block_len, dtype=jnp.int32)[None, :]
    ).reshape(-1)
    seq_all, pos_all = token_place(all_tokens, prompt_len, cont_len)
    seq_mine = lax.dynamic_slice_in_dim(seq_all, device * local_rows, local_rows)
    pos_mine = lax.dynamic_slice_in_dim(pos_all, device * local_rows, local_rows)
    forward_weights = (
        lax.all_gather(self_query, AXES, axis=0, tiled=True),
        lax.all_gather(self_key, AXES, axis=0, tiled=True),
        lax.all_gather(self_value, AXES, axis=0, tiled=True),
        lax.all_gather(self_output, AXES, axis=0, tiled=True),
        lax.all_gather(cross_query, AXES, axis=0, tiled=True),
        lax.all_gather(cross_key, AXES, axis=0, tiled=True),
        lax.all_gather(cross_value, AXES, axis=0, tiled=True),
        lax.all_gather(cross_output, AXES, axis=0, tiled=True),
        lax.all_gather(feed_gate, AXES, axis=0, tiled=True),
        lax.all_gather(feed_up, AXES, axis=0, tiled=True),
        lax.all_gather(feed_down, AXES, axis=0, tiled=True),
        lax.all_gather(gain_self, AXES, axis=0, tiled=True),
        lax.all_gather(gain_cross, AXES, axis=0, tiled=True),
        lax.all_gather(gain_feed, AXES, axis=0, tiled=True),
    )
    (
        query_weight,
        key_weight,
        value_weight,
        output_weight,
        cq_weight,
        ck_weight,
        cv_weight,
        co_weight,
        gate_weight,
        up_weight,
        down_weight,
        gain_one,
        gain_two,
        gain_three,
    ) = forward_weights
    inputs32 = layer_in[0].astype(jnp.float32)
    normed_one = rms_norm(inputs32, gain_one.astype(jnp.float32)).astype(jnp.bfloat16)
    queries = jnp.dot(normed_one, query_weight, preferred_element_type=jnp.float32).astype(
        jnp.bfloat16
    )
    keys_local = jnp.dot(normed_one, key_weight, preferred_element_type=jnp.float32).astype(
        jnp.bfloat16
    )
    values_local = jnp.dot(normed_one, value_weight, preferred_element_type=jnp.float32).astype(
        jnp.bfloat16
    )
    keys_all, values_all = (
        lax.all_gather(keys_local, AXES, axis=0, tiled=True),
        lax.all_gather(values_local, AXES, axis=0, tiled=True),
    )
    query_heads = queries.reshape(local_rows, head_count, head_size)
    key_heads = keys_all.reshape(total_rows, head_count, head_size)
    value_heads = values_all.reshape(total_rows, head_count, head_size)
    log_self, attn_sum, attn_exact = self_forward(
        query_heads,
        key_heads,
        value_heads,
        seq_all,
        pos_all,
        seq_mine,
        pos_mine,
        table_hb,
        key_rows,
    )
    attended = attn_sum.reshape(local_rows, inner_width).astype(jnp.bfloat16)
    hidden_one = inputs32 + jnp.dot(attended, output_weight, preferred_element_type=jnp.float32)
    normed_two = rms_norm(hidden_one, gain_two.astype(jnp.float32)).astype(jnp.bfloat16)
    cross_queries = jnp.dot(normed_two, cq_weight, preferred_element_type=jnp.float32).astype(
        jnp.bfloat16
    )
    enc_keys = jnp.dot(encoded[0], ck_weight, preferred_element_type=jnp.float32).astype(
        jnp.bfloat16
    )
    enc_values = jnp.dot(encoded[0], cv_weight, preferred_element_type=jnp.float32).astype(
        jnp.bfloat16
    )
    cross_keys, cross_values = (
        lax.all_gather(enc_keys, AXES, axis=0, tiled=True),
        lax.all_gather(enc_values, AXES, axis=0, tiled=True),
    )
    cq_heads = cross_queries.reshape(local_rows, head_count, head_size)
    ck_heads = cross_keys.reshape(enc_rows, head_count, head_size)
    cv_heads = cross_values.reshape(enc_rows, head_count, head_size)
    cross_scores = jnp.einsum(
        QK, cq_heads, ck_heads, preferred_element_type=jnp.float32
    )
    cross_peak = jnp.max(cross_scores, axis=-1)
    log_cross = cross_peak + jnp.log(
        jnp.sum(jnp.exp(cross_scores - cross_peak[:, :, None]), axis=-1)
    )
    cross_probs = jnp.exp(cross_scores - log_cross[:, :, None])
    cross_high, cross_rest = split_probs(cross_probs)
    cross_sum = jnp.einsum(PV, cross_high, cv_heads, preferred_element_type=jnp.float32)
    cross_exact = cross_sum + jnp.einsum(
        PV, cross_rest, cv_heads, preferred_element_type=jnp.float32
    )
    attended_cross = cross_sum.reshape(local_rows, inner_width).astype(jnp.bfloat16)
    hidden_two = hidden_one + jnp.dot(attended_cross, co_weight, preferred_element_type=jnp.float32)
    normed_three = rms_norm(hidden_two, gain_three.astype(jnp.float32)).astype(jnp.bfloat16)
    gate_pre = jnp.dot(normed_three, gate_weight, preferred_element_type=jnp.float32)
    up_pre = jnp.dot(normed_three, up_weight, preferred_element_type=jnp.float32)
    mixed_hidden = gated(gate_pre, up_pre).astype(jnp.bfloat16)
    output_sum = hidden_two + jnp.dot(mixed_hidden, down_weight, preferred_element_type=jnp.float32)
    layer_out = output_sum.astype(jnp.bfloat16)[None]
    back_weights = (
        lax.all_gather(self_query, AXES, axis=0, tiled=True),
        lax.all_gather(self_key, AXES, axis=0, tiled=True),
        lax.all_gather(self_value, AXES, axis=0, tiled=True),
        lax.all_gather(self_output, AXES, axis=0, tiled=True),
        lax.all_gather(cross_query, AXES, axis=0, tiled=True),
        lax.all_gather(cross_key, AXES, axis=0, tiled=True),
        lax.all_gather(cross_value, AXES, axis=0, tiled=True),
        lax.all_gather(cross_output, AXES, axis=0, tiled=True),
        lax.all_gather(feed_gate, AXES, axis=0, tiled=True),
        lax.all_gather(feed_up, AXES, axis=0, tiled=True),
        lax.all_gather(feed_down, AXES, axis=0, tiled=True),
        lax.all_gather(gain_self, AXES, axis=0, tiled=True),
        lax.all_gather(gain_cross, AXES, axis=0, tiled=True),
        lax.all_gather(gain_feed, AXES, axis=0, tiled=True),
    )
    (
        query_back,
        key_back,
        value_back,
        output_back,
        cq_back,
        ck_back,
        cv_back,
        co_back,
        gate_back,
        up_back,
        down_back,
        gain_one_back,
        gain_two_back,
        gain_three_back,
    ) = back_weights
    grad_out = cotangent[0]
    grad_down_w = jnp.einsum(
        TF_TD, mixed_hidden, grad_out, preferred_element_type=jnp.float32
    )
    grad_mixed = jnp.einsum(TD_FD, grad_out, down_back, preferred_element_type=jnp.float32)
    _, gate_pull = jax.vjp(gated, gate_pre, up_pre)
    grad_gate32, grad_up32 = gate_pull(bounce(grad_mixed))
    grad_gate = grad_gate32.astype(jnp.bfloat16)
    grad_up = grad_up32.astype(jnp.bfloat16)
    grad_gate_w = jnp.einsum(
        TD_TF, normed_three, grad_gate, preferred_element_type=jnp.float32
    )
    grad_up_w = jnp.einsum(TD_TF, normed_three, grad_up, preferred_element_type=jnp.float32)
    grad_normed_three = jnp.einsum(
        TF_DF, grad_gate, gate_back, preferred_element_type=jnp.float32
    ) + jnp.einsum(TF_DF, grad_up, up_back, preferred_element_type=jnp.float32)
    _, norm_pull_three = jax.vjp(rms_norm, hidden_two, gain_three_back.astype(jnp.float32))
    back_two, grad_gain_feed = norm_pull_three(grad_normed_three)
    grad_hidden_two = grad_out.astype(jnp.float32) + back_two
    grad_two_low = grad_hidden_two.astype(jnp.bfloat16)
    grad_co_w = jnp.einsum(
        TC_TD, attended_cross, grad_two_low, preferred_element_type=jnp.float32
    )
    grad_attended_cross = jnp.einsum(
        TD_CD, grad_two_low, co_back, preferred_element_type=jnp.float32
    ).astype(jnp.bfloat16)
    grad_ac_heads = grad_attended_cross.reshape(local_rows, head_count, head_size)
    delta_cross = jnp.sum(grad_ac_heads.astype(jnp.float32) * cross_exact, axis=-1).T
    cross_low, grad_cross_scores = score_grads(
        cross_scores, log_cross, delta_cross, grad_ac_heads, cv_heads
    )
    grad_cq = jnp.einsum(
        PV, grad_cross_scores, ck_heads, preferred_element_type=jnp.float32
    )
    grad_ck_part = jnp.einsum(
        PTQ, grad_cross_scores, cq_heads, preferred_element_type=jnp.float32
    ).reshape(enc_rows, inner_width)
    grad_cv_part = jnp.einsum(
        PTQ, cross_low, grad_ac_heads, preferred_element_type=jnp.float32
    ).reshape(enc_rows, inner_width)
    cross_own = lax.psum_scatter(
        jnp.concatenate([grad_ck_part, grad_cv_part], axis=1),
        AXES,
        scatter_dimension=0,
        tiled=True,
    )
    grad_cross_keys = cross_own[:, :inner_width].astype(jnp.bfloat16)
    grad_cross_values = cross_own[:, inner_width:].astype(jnp.bfloat16)
    grad_ck_w = jnp.einsum(
        TD_TC, encoded[0], grad_cross_keys, preferred_element_type=jnp.float32
    )
    grad_cv_w = jnp.einsum(
        TD_TC, encoded[0], grad_cross_values, preferred_element_type=jnp.float32
    )
    grad_encoded = (
        jnp.einsum(TC_DC, grad_cross_keys, ck_back, preferred_element_type=jnp.float32)
        + jnp.einsum(TC_DC, grad_cross_values, cv_back, preferred_element_type=jnp.float32)
    )[None]
    grad_cq_low = grad_cq.reshape(local_rows, inner_width).astype(jnp.bfloat16)
    grad_cq_w = jnp.einsum(TD_TC, normed_two, grad_cq_low, preferred_element_type=jnp.float32)
    grad_normed_two = jnp.einsum(
        TC_DC, grad_cq_low, cq_back, preferred_element_type=jnp.float32
    )
    _, norm_pull_two = jax.vjp(rms_norm, hidden_one, gain_two_back.astype(jnp.float32))
    back_one, grad_gain_cross = norm_pull_two(grad_normed_two)
    grad_hidden_one = grad_hidden_two + back_one
    grad_one_low = grad_hidden_one.astype(jnp.bfloat16)
    grad_o_w = jnp.einsum(TC_TD, attended, grad_one_low, preferred_element_type=jnp.float32)
    grad_attended = jnp.einsum(
        TD_CD, grad_one_low, output_back, preferred_element_type=jnp.float32
    ).astype(jnp.bfloat16)
    grad_att_heads = grad_attended.reshape(local_rows, head_count, head_size)
    delta_self = jnp.sum(grad_att_heads.astype(jnp.float32) * attn_exact, axis=-1).T
    grad_query32, grad_bias_part, kv_blocks = query_backward(
        query_heads,
        key_heads,
        value_heads,
        grad_att_heads,
        log_self,
        delta_self,
        seq_all,
        pos_all,
        seq_mine,
        pos_mine,
        table_hb,
        key_rows,
    )
    kv_own = lax.psum_scatter(kv_blocks, AXES, scatter_dimension=0, tiled=True)
    grad_keys = kv_own[:, :inner_width].astype(jnp.bfloat16)
    grad_values = kv_own[:, inner_width:].astype(jnp.bfloat16)
    grad_queries = grad_query32.reshape(local_rows, inner_width).astype(jnp.bfloat16)
    grad_q_w = jnp.einsum(TD_TC, normed_one, grad_queries, preferred_element_type=jnp.float32)
    grad_k_w = jnp.einsum(TD_TC, normed_one, grad_keys, preferred_element_type=jnp.float32)
    grad_v_w = jnp.einsum(TD_TC, normed_one, grad_values, preferred_element_type=jnp.float32)
    grad_normed_one = (
        jnp.einsum(TC_DC, grad_queries, query_back, preferred_element_type=jnp.float32)
        + jnp.einsum(TC_DC, grad_keys, key_back, preferred_element_type=jnp.float32)
        + jnp.einsum(TC_DC, grad_values, value_back, preferred_element_type=jnp.float32)
    )
    _, norm_pull_one = jax.vjp(rms_norm, inputs32, gain_one_back.astype(jnp.float32))
    back_input, grad_gain_self = norm_pull_one(grad_normed_one)
    grad_input = (grad_hidden_one + back_input)[None]

    def sectioned(grad_full):
        return grad_full.reshape(
            (ctx_count, core_count, grad_full.shape[0] // (ctx_count * core_count))
            + grad_full.shape[1:]
        )

    core_parts = (
        lax.psum_scatter(
            sectioned(grad_q_w).astype(jnp.bfloat16), WSH, scatter_dimension=1, tiled=True
        ).astype(jnp.float32),
        lax.psum_scatter(
            sectioned(grad_k_w).astype(jnp.bfloat16), WSH, scatter_dimension=1, tiled=True
        ).astype(jnp.float32),
        lax.psum_scatter(
            sectioned(grad_v_w).astype(jnp.bfloat16), WSH, scatter_dimension=1, tiled=True
        ).astype(jnp.float32),
        lax.psum_scatter(
            sectioned(grad_o_w).astype(jnp.bfloat16), WSH, scatter_dimension=1, tiled=True
        ).astype(jnp.float32),
        lax.psum_scatter(
            sectioned(grad_cq_w).astype(jnp.bfloat16), WSH, scatter_dimension=1, tiled=True
        ).astype(jnp.float32),
        lax.psum_scatter(
            sectioned(grad_ck_w).astype(jnp.bfloat16), WSH, scatter_dimension=1, tiled=True
        ).astype(jnp.float32),
        lax.psum_scatter(
            sectioned(grad_cv_w).astype(jnp.bfloat16), WSH, scatter_dimension=1, tiled=True
        ).astype(jnp.float32),
        lax.psum_scatter(
            sectioned(grad_co_w).astype(jnp.bfloat16), WSH, scatter_dimension=1, tiled=True
        ).astype(jnp.float32),
        lax.psum_scatter(
            sectioned(grad_gate_w).astype(jnp.bfloat16), WSH, scatter_dimension=1, tiled=True
        ).astype(jnp.float32),
        lax.psum_scatter(
            sectioned(grad_up_w).astype(jnp.bfloat16), WSH, scatter_dimension=1, tiled=True
        ).astype(jnp.float32),
        lax.psum_scatter(
            sectioned(grad_down_w).astype(jnp.bfloat16), WSH, scatter_dimension=1, tiled=True
        ).astype(jnp.float32),
        lax.psum_scatter(
            sectioned(grad_gain_self).astype(jnp.bfloat16), WSH, scatter_dimension=1, tiled=True
        ).astype(jnp.float32),
        lax.psum_scatter(
            sectioned(grad_gain_cross).astype(jnp.bfloat16), WSH, scatter_dimension=1, tiled=True
        ).astype(jnp.float32),
        lax.psum_scatter(
            sectioned(grad_gain_feed).astype(jnp.bfloat16), WSH, scatter_dimension=1, tiled=True
        ).astype(jnp.float32),
    )
    (
        core_q,
        core_k,
        core_v,
        core_o,
        core_cq,
        core_ck,
        core_cv,
        core_co,
        core_gate,
        core_up,
        core_down,
        core_gs,
        core_gc,
        core_gf,
    ) = core_parts
    owned = (
        lax.psum_scatter(core_q, CTX, scatter_dimension=0, tiled=True),
        lax.psum_scatter(core_k, CTX, scatter_dimension=0, tiled=True),
        lax.psum_scatter(core_v, CTX, scatter_dimension=0, tiled=True),
        lax.psum_scatter(core_o, CTX, scatter_dimension=0, tiled=True),
        lax.psum_scatter(core_cq, CTX, scatter_dimension=0, tiled=True),
        lax.psum_scatter(core_ck, CTX, scatter_dimension=0, tiled=True),
        lax.psum_scatter(core_cv, CTX, scatter_dimension=0, tiled=True),
        lax.psum_scatter(core_co, CTX, scatter_dimension=0, tiled=True),
        lax.psum_scatter(core_gate, CTX, scatter_dimension=0, tiled=True),
        lax.psum_scatter(core_up, CTX, scatter_dimension=0, tiled=True),
        lax.psum_scatter(core_down, CTX, scatter_dimension=0, tiled=True),
        lax.psum_scatter(core_gs, CTX, scatter_dimension=0, tiled=True),
        lax.psum_scatter(core_gc, CTX, scatter_dimension=0, tiled=True),
        lax.psum_scatter(core_gf, CTX, scatter_dimension=0, tiled=True),
    )
    (
        own_q,
        own_k,
        own_v,
        own_o,
        own_cq,
        own_ck,
        own_cv,
        own_co,
        own_gate,
        own_up,
        own_down,
        own_gain_self,
        own_gain_cross,
        own_gain_feed,
    ) = [piece.reshape(piece.shape[2:]) for piece in owned]
    summed = (
        lax.psum(own_q.astype(jnp.bfloat16), GRP).astype(jnp.float32),
        lax.psum(own_k.astype(jnp.bfloat16), GRP).astype(jnp.float32),
        lax.psum(own_v.astype(jnp.bfloat16), GRP).astype(jnp.float32),
        lax.psum(own_o.astype(jnp.bfloat16), GRP).astype(jnp.float32),
        lax.psum(own_cq.astype(jnp.bfloat16), GRP).astype(jnp.float32),
        lax.psum(own_ck.astype(jnp.bfloat16), GRP).astype(jnp.float32),
        lax.psum(own_cv.astype(jnp.bfloat16), GRP).astype(jnp.float32),
        lax.psum(own_co.astype(jnp.bfloat16), GRP).astype(jnp.float32),
        lax.psum(own_gate.astype(jnp.bfloat16), GRP).astype(jnp.float32),
        lax.psum(own_up.astype(jnp.bfloat16), GRP).astype(jnp.float32),
        lax.psum(own_down.astype(jnp.bfloat16), GRP).astype(jnp.float32),
        lax.psum(own_gain_self.astype(jnp.bfloat16), GRP).astype(jnp.float32),
        lax.psum(own_gain_cross.astype(jnp.bfloat16), GRP).astype(jnp.float32),
        lax.psum(own_gain_feed.astype(jnp.bfloat16), GRP).astype(jnp.float32),
    )
    grad_relative_bias = lax.psum(grad_bias_part.T, EVERY)
    return (
        layer_out,
        grad_input,
        grad_encoded,
        summed[0],
        summed[1],
        summed[2],
        summed[3],
        summed[4],
        summed[5],
        summed[6],
        summed[7],
        summed[8],
        summed[9],
        summed[10],
        summed[11],
        summed[12],
        summed[13],
        grad_relative_bias,
    )


BIG = 63 << 20
NT = (((1,), (1,)), ((), ()))
TN = (((0,), (0,)), ((), ()))
NN = (((1,), (0,)), ((), ()))
F32 = jnp.float32
BF16 = jnp.bfloat16
CH = 256
BLK = 64


def mm(left, right, dims):
    return lax.dot_general(left, right, dims, preferred_element_type=F32)


def load_in_order(deal, k_hbm, v_hbm, kvs, sem):
    blocks, inner = k_hbm.shape[0] // BLK, k_hbm.shape[1]

    def one(index, carry):
        here = pl.ds(index * BLK, BLK)
        rows = kvs.at[pl.ds(pl.multiple_of(deal[index // 2, index % 2] * BLK, BLK), BLK)]
        pltpu.make_async_copy(k_hbm.at[here], rows.at[:, pl.ds(0, inner)], sem.at[0]).start()
        pltpu.make_async_copy(v_hbm.at[here], rows.at[:, pl.ds(inner, inner)], sem.at[1]).start()
        return carry

    lax.fori_loop(0, blocks, one, 0)


def loaded(k_hbm, v_hbm, kvs, sem):
    inner = k_hbm.shape[1]
    pltpu.make_async_copy(k_hbm, kvs.at[:, pl.ds(0, inner)], sem.at[0]).wait()
    pltpu.make_async_copy(v_hbm, kvs.at[:, pl.ds(inner, inner)], sem.at[1]).wait()


def stack_pair(block, low_lanes):
    zero = jnp.zeros_like(block)
    return jnp.concatenate([jnp.where(low_lanes, block, zero), jnp.where(low_lanes, zero, block)], axis=0)


def pair_table(table_hb):
    heads = table_hb.shape[0]
    padded = jnp.pad(table_hb, ((0, 0), (0, BLK - BUCKETS)))
    return padded.reshape(heads // 2, 2 * BLK)

MESH = pl.DeviceIdType.MESH


class Place:
    def __init__(self, nz):
        self.nz = nz
        self.g = lax.axis_index(GRP)
        self.c = lax.axis_index(CTX)
        self.w = lax.axis_index(WSH)
        self.z = self.c // 2
        self.y = lax.rem(self.c, 2)
        self.me = self.c * 2 + self.w

    def at(self, g=None, z=None, y=None, w=None):
        z = self.z if z is None else z
        y = self.y if y is None else y
        return (self.g if g is None else g, z * 2 + y, self.w if w is None else w)

    def twin(self):
        return self.at(g=1 - self.g)

    def over(self):
        return self.at(y=1 - self.y)

    def mate(self):
        return self.at(w=1 - self.w)

    def up(self, dz):
        return lax.rem(self.z + dz, self.nz)

    def down(self, dz):
        return lax.rem(self.z + self.nz - dz, self.nz)

    def greet(self):
        partners = [self.twin(), self.over(), self.mate()]
        partners += [self.at(z=self.up(dz)) for dz in range(1, self.nz)]
        for partner in partners:
            pl.semaphore_signal(pltpu.get_barrier_semaphore(), inc=1, device_id=partner, device_id_type=MESH)
        self.greeted = len(partners)

    def met(self):
        pl.semaphore_wait(pltpu.get_barrier_semaphore(), self.greeted)


def push(src, dst, ssem, rsem, to):
    return pltpu.make_async_remote_copy(src, dst, ssem, rsem, device_id=to, device_id_type=MESH)


def half(wide, index):
    return pl.ds(pl.multiple_of(index * (wide // 2), 128), wide // 2)


class Gather:
    COUNT = 9

    def __init__(self, at, part, whole, sems, split, chunk=0, chunks=1):
        self.at, self.nz, self.part, self.whole, self.split = at, at.nz, part, whole, split
        (self.zs, self.zr, self.ys, self.yr, self.xs, self.xr, self.ws, self.wr, self.lc) = sems
        self.wide = whole.shape[-1] // chunks
        self.first = chunk * self.wide
        self.sent = []

    @staticmethod
    def scratch(nz, split):
        dma = pltpu.SemaphoreType.DMA
        x = 2 * nz if split else 1
        w = 4 * nz if split else 2 * nz
        return [dma((nz,))] * 4 + [dma((x,))] * 2 + [dma((w,))] * 2 + [dma((1,))]

    def cols(self, side=None):
        if self.split and side is not None:
            return pl.ds(pl.multiple_of(self.first + side * (self.wide // 2), 128), self.wide // 2)
        return pl.ds(self.first, self.wide)

    def spot(self, z, y, w, side=None):
        return self.whole.at[z, y, w, :, self.cols(side)]

    def post(self, view, ssem, rsem, to, source=None):
        copy = push(view if source is None else source, view, ssem, rsem, to)
        copy.start()
        self.sent.append(copy)

    def to_y(self, z):
        at = self.at
        self.post(self.spot(z, at.y, at.w, at.g), self.ys.at[z], self.yr.at[z], at.over())

    def to_x(self, z, y):
        at = self.at
        if self.split:
            k = z * 2 + y
            self.post(self.spot(z, y, at.w, at.g), self.xs.at[k], self.xr.at[k], at.twin())

    def w_sem(self, z, y, side):
        k = z * 2 + y
        return k * 2 + (0 if side is None else side) if self.split else k

    def to_w(self, z, y, side):
        at = self.at
        k = self.w_sem(z, y, side)
        self.post(self.spot(z, y, at.w, side), self.ws.at[k], self.wr.at[k], at.mate())

    def place(self):
        here = self.spot(self.at.z, self.at.y, self.at.w)
        self.local = pltpu.make_async_copy(self.part.at[:, self.cols()], here, self.lc.at[0])
        self.local.start()

    def send(self):
        at = self.at
        here, source = self.spot(at.z, at.y, at.w, at.g), self.part.at[:, self.cols(at.g)]
        for dz in range(1, self.nz):
            to = at.up(dz)
            self.post(here, self.zs.at[to], self.zr.at[at.z], at.at(z=to), source)
        self.post(here, self.ys.at[at.z], self.yr.at[at.z], at.over(), source)
        k = self.w_sem(at.z, at.y, None)
        self.post(self.spot(at.z, at.y, at.w), self.ws.at[k], self.wr.at[k], at.mate(), self.part.at[:, self.cols()])

    def after_z(self):
        at = self.at
        for dz in range(1, self.nz):
            z = at.down(dz)
            view = self.spot(z, at.y, at.w, at.g)
            push(view, view, self.zs.at[z], self.zr.at[z], at.at(z=z)).wait_recv()
            self.to_y(z)
            self.to_x(z, at.y)
            self.to_w(z, at.y, at.g)

    def after_y(self):
        at = self.at
        for dz in range(self.nz):
            z = at.down(dz)
            view = self.spot(z, 1 - at.y, at.w, at.g)
            push(view, view, self.ys.at[z], self.yr.at[z], at.over()).wait_recv()
            self.to_x(z, 1 - at.y)
            self.to_w(z, 1 - at.y, at.g)

    def others(self):
        for dy in range(2):
            for dz in range(self.nz):
                yield self.at.down(dz), lax.rem(self.at.y + dy, 2), dy == 0 and dz == 0

    def after_x(self):
        at = self.at
        if not self.split:
            return
        for z, y, own in self.others():
            if not own:
                k = z * 2 + y
                view = self.spot(z, y, at.w, 1 - at.g)
                push(view, view, self.xs.at[k], self.xr.at[k], at.twin()).wait_recv()
                self.to_w(z, y, 1 - at.g)

    def end(self):
        at = self.at
        self.local.wait()
        for z, y, own in self.others():
            for side in range(2 if self.split and not own else 1):
                k = self.w_sem(z, y, side)
                view = self.spot(z, y, 1 - at.w, None if own else side)
                push(view, view, self.ws.at[k], self.wr.at[k], at.mate()).wait_recv()

    def close(self):
        for copy in self.sent:
            copy.wait_send()


class Reduce:
    COUNT = 16

    @staticmethod
    def scratch(nz, r, wide, kind, dtype, part=True):
        cols = wide // 2 if kind == "x" else wide
        dma = pltpu.SemaphoreType.DMA
        vmem = pltpu.VMEM
        none = vmem((1, 16, 128), dtype)
        return [
            vmem((nz, 2, 2, r, wide), dtype) if part else none,
            vmem((nz, 2, r, wide), dtype),
            vmem((nz, 2, r, cols), dtype) if kind == "x" else none,
            vmem((nz, r, cols), dtype),
            vmem((nz, r, cols), dtype),
            vmem((2, r, cols), dtype) if kind != "none" else none,
        ] + [dma((1,))] * 6 + [dma((nz,))] * 2 + [dma((1,))] * 2

    def __init__(self, at, out, refs, kind):
        self.at, self.nz, self.out, self.kind = at, at.nz, out, kind
        self.part_cols = None
        (self.part, self.wb, self.xb, self.yb, self.zb, self.fb) = refs[:6]
        (self.ws, self.wr, self.xs, self.xr, self.ys, self.yr, self.zs, self.zr, self.fs, self.fr) = refs[6:]
        self.wide = self.wb.shape[-1]
        self.local_part = None

    def c_w(self):
        at = self.at
        src = self.part.at[:, :, 1 - at.w]
        if self.part_cols is not None:
            src = self.part.at[:, :, 1 - at.w, :, self.part_cols]
        return push(src, self.wb, self.ws.at[0], self.wr.at[0], at.mate())

    def c_x(self):
        at = self.at
        src = self.wb.at[:, :, :, half(self.wide, 1 - at.g)]
        return push(src, self.xb, self.xs.at[0], self.xr.at[0], at.twin())

    def mid(self):
        return self.xb if self.kind == "x" else self.wb

    def c_y(self):
        at = self.at
        return push(self.mid().at[:, 1 - at.y], self.yb, self.ys.at[0], self.yr.at[0], at.over())

    def c_z(self, to):
        at = self.at
        return push(self.yb.at[to], self.zb.at[at.z], self.zs.at[to], self.zr.at[at.z], at.at(z=to))

    def c_zin(self, z):
        return push(self.yb.at[z], self.zb.at[z], self.zs.at[z], self.zr.at[z], self.at.at(z=z))

    def c_f(self):
        return push(self.fb.at[0], self.fb.at[1], self.fs.at[0], self.fr.at[0], self.at.twin())

    def send(self):
        self.c_w().start()

    def after_w(self):
        at = self.at
        self.c_w().wait_recv()

        def one(k, carry):
            z, y = k // 2, lax.rem(k, 2)
            here = self.part[z, y, at.w] if self.local_part is None else self.local_part[z, y, :, self.local_cols]
            self.wb[z, y] = (self.wb[z, y].astype(F32) + here.astype(F32)).astype(self.wb.dtype)
            return carry

        lax.fori_loop(0, 2 * self.nz, one, 0)
        if self.kind == "x":
            self.c_x().start()
        else:
            self.c_y().start()

    def after_x(self):
        if self.kind != "x":
            return
        self.c_x().wait_recv()

        def one(k, carry):
            z, y = k // 2, lax.rem(k, 2)
            total = self.xb[z, y].astype(F32) + self.wb[z, y, :, half(self.wide, self.at.g)].astype(F32)
            self.xb[z, y] = total.astype(self.xb.dtype)
            return carry

        lax.fori_loop(0, 2 * self.nz, one, 0)
        self.c_y().start()

    def after_y(self):
        at, nz = self.at, self.nz
        self.c_y().wait_recv()

        def one(z, carry):
            total = self.yb[z].astype(F32) + self.mid()[z, at.y].astype(F32)
            self.yb[z] = total.astype(self.yb.dtype)
            return carry

        lax.fori_loop(0, nz, one, 0)
        for dz in range(1, nz):
            self.c_z(at.up(dz)).start()

    def after_z(self):
        at, nz = self.at, self.nz
        for dz in range(1, nz):
            self.c_zin(at.up(dz)).wait_recv()
        total = self.yb[at.z].astype(F32)
        for dz in range(1, nz):
            total = total + self.zb[at.up(dz)].astype(F32)
        if self.kind == "x":
            self.out[:, half(self.wide, at.g)] = total
        else:
            self.out[...] = total
        if self.kind != "none":
            self.fb[0] = total.astype(self.fb.dtype)
            self.c_f().start()

    def end(self):
        at = self.at
        if self.kind != "none":
            self.c_f().wait_recv()
            other = self.fb[1].astype(F32)
            if self.kind == "x":
                self.out[:, half(self.wide, 1 - at.g)] = other
            else:
                self.out[...] = self.out[...] + other

    def close(self):
        at, nz = self.at, self.nz
        self.c_w().wait_send()
        if self.kind == "x":
            self.c_x().wait_send()
        self.c_y().wait_send()
        for dz in range(1, nz):
            self.c_z(at.up(dz)).wait_send()
        if self.kind != "none":
            self.c_f().wait_send()


class Total:
    COUNT = 3

    @staticmethod
    def scratch(nz, r, wide):
        dma = pltpu.SemaphoreType.DMA
        return [pltpu.VMEM((4 + nz, r, wide), F32), dma((4 + nz,)), dma((4 + nz,))]

    def __init__(self, at, refs):
        self.at, self.nz = at, at.nz
        self.buf, self.ss, self.rs = refs

    def hop(self, i):
        at = self.at
        to = (at.mate(), at.twin(), at.over())[i]
        return push(self.buf.at[0], self.buf.at[1 + i], self.ss.at[i], self.rs.at[i], to)

    def send(self):
        self.hop(0).start()

    def after(self, i):
        hop = self.hop(i)
        hop.wait_send()
        hop.wait_recv()
        self.buf[0] = self.buf[0] + self.buf[1 + i]
        if i < 2:
            self.hop(i + 1).start()
        else:
            for dz in range(1, self.nz):
                self.along(self.at.z, self.at.up(dz)).start()

    def along(self, source, to):
        base = 4
        return push(self.buf.at[0], self.buf.at[base + source], self.ss.at[base + to], self.rs.at[base + source], self.at.at(z=to))

    def end(self):
        total = None
        for dz in range(1, self.nz):
            z = self.at.up(dz)
            self.along(z, z).wait_recv()
            self.along(self.at.z, z).wait_send()
        self.buf[4 + self.at.z] = self.buf[0]
        total = self.buf[4]
        for z in range(1, self.nz):
            total = total + self.buf[4 + z]
        return total


def normed(hidden, gain):
    return hidden * lax.rsqrt(jnp.mean(hidden * hidden, axis=-1, keepdims=True) + EPSILON) * gain


def norm_back(hidden, gain, grad):
    scale = lax.rsqrt(jnp.mean(hidden * hidden, axis=-1, keepdims=True) + EPSILON)
    inner = jnp.mean(hidden * gain * grad, axis=-1, keepdims=True)
    rows = scale * gain * grad - hidden * (scale * scale * scale) * inner
    return rows, jnp.sum(grad * hidden * scale, axis=0, keepdims=True)


FRONT_PARTS = ("small", "k", "v", "q", "o", "cq", "ck", "cv", "co", "gate", "up", "down", "keys", "values")
FRONT_REST = 14
FRONT_PLAN = (
    ("small", "keys", "values",),
    dict(gate=2, up=2, down=3, keys=3, values=3),
    (
        ("down", 0), ("up", 0), ("values", 2), ("values", 0), ("keys", 2), ("k", 0), ("values", 1), ("down", 1),
        ("cq", 0), ("down", 2), ("gate", 1), ("keys", 0), ("small", 0), ("cv", 0), ("v", 0), ("co", 0), ("up", 1),
        ("q", 0), ("o", 0), ("gate", 0), ("keys", 1), ("ck", 0),
    ),
    (
        (0, 0), (1, 0), (5, 0), (0, 1), (7, 0), (0, 2), (1, 1), (8, 0), (0, 3), (5, 1), (9, 0), (1, 2), (7, 1),
        (10, 0), (5, 2), (8, 1), (12, 0), (7, 2), (9, 1), (1, 3), (13, 0), (8, 2), (10, 1), (14, 0), (9, 2), (5, 3),
        (12, 1), (15, 0), (10, 2), (13, 1), (16, 0), (7, 3), (12, 2), (14, 1), (17, 0), (12, 4), (5, 4), (8, 3),
        (13, 2), (14, 2), (15, 1), (4, 0), (11, 0), (16, 1), (9, 3), (15, 2), (17, 1), (18, 0), (10, 3), (4, 1),
        (16, 2), (19, 0), (20, 0), (17, 2), (13, 3), (11, 1), (4, 2), (14, 3), (18, 1), (21, 0), (14, 4), (2, 0),
        (19, 1), (3, 0), (6, 0), (11, 2), (18, 2), (15, 3), (20, 1), (21, 1), (19, 2), (16, 3), (17, 3), (2, 1),
        (17, 4), (20, 2), (21, 2), (3, 1), (18, 3), (2, 2), (6, 1), (3, 2), (19, 3), (6, 2), (21, 3), (0, 4), (1, 4),
        (2, 4), (3, 4), (4, 4), (6, 4), (7, 4), (8, 4), (9, 4), (10, 4), (11, 4), (13, 4), (15, 4), (16, 4), (18, 4),
        (19, 4), (20, 4), (21, 4),
    ),
)


def front_kernel(nz, unshared, chunked, order, steps, *refs):
    count = len(FRONT_PARTS)
    x_ref, ins, wholes, refs = refs[0], refs[1 : count - 1], refs[count - 1 : 2 * count - 1], refs[2 * count - 1 :]
    (q_ref, normed_ref, gains_ref), (wbuf, k_own, v_own, wsem), sems = refs[:3], refs[3:7], refs[7:]
    parts = dict(zip(FRONT_PARTS, tuple(ins) + (k_own, v_own)))
    wholes = dict(zip(FRONT_PARTS, wholes))
    at = Place(nz)
    at.greet()
    jobs = []
    for i, (name, chunk) in enumerate(order):
        mine = sems[Gather.COUNT * i : Gather.COUNT * (i + 1)]
        chunks = chunked.get(name, 1)
        job = Gather(at, parts[name], wholes[name], mine, name not in unshared, chunk, chunks)
        jobs.append(job)
        if name not in ("keys", "values"):
            job.place()
    at.met()
    width = x_ref.shape[1]

    def norm():
        every = wholes["small"]
        total = None
        for z in range(nz):
            for y in range(2):
                for w in range(2):
                    here = every[z, y, w].astype(F32)
                    total = here if total is None else total + here
        gains_ref[...] = total
        normed_ref[...] = normed(x_ref[...].astype(F32), total[4:5]).astype(BF16)

    def project(name, index, into):
        load = pltpu.make_async_copy(wholes[name], wbuf.at[index], wsem.at[index])
        load.start()
        load.wait()
        into[...] = mm(normed_ref[...], wbuf[index].reshape(width, -1), NN).astype(BF16)

    def finish(i):
        if order[i][0] not in ("small", "k", "v", "q"):
            jobs[i].end()
        jobs[i].close()

    def place(name):
        for entry, job in zip(order, jobs):
            if entry[0] == name:
                job.place()

    def follow(name):
        if name == "small":
            norm()
        elif name == "k":
            project(name, 0, k_own)
            place("keys")
        elif name == "v":
            project(name, 1, v_own)
            place("values")
        elif name == "q":
            project(name, 2, q_ref)

    stages = (Gather.send, Gather.after_z, Gather.after_y, Gather.after_x, Gather.end)
    rest = {}
    for count, (i, stage) in enumerate(steps):
        name, job = order[i][0], jobs[i]
        if stage == len(stages) - 1:
            if name not in ("small", "k", "v", "q"):
                continue
            job.end()
            follow(name)
        else:
            stages[stage](job)
        if stage == (3 if job.split else 2):
            rest[i] = count + FRONT_REST
        for j in [j for j, due in rest.items() if due <= count]:
            finish(j)
            del rest[j]
    for j in rest:
        finish(j)


def front(x, parts, nz, shards, collective_id=1, plan=FRONT_PLAN):
    hb = pl.BlockSpec(memory_space=pl.ANY)
    vm = pl.BlockSpec(memory_space=pltpu.VMEM)
    unshared, chunked, order, steps = plan
    rows, width = x.shape
    inner = parts[1].shape[1]
    shapes = [(nz, 2, 2) + part.shape for part in parts] + [(nz, 2, 2, rows, inner)] * 2
    scratch = [
        pltpu.VMEM((3,) + shapes[1], BF16), pltpu.VMEM((rows, inner), BF16), pltpu.VMEM((rows, inner), BF16),
        pltpu.SemaphoreType.DMA((3,)),
    ]
    for name, _ in order:
        scratch += Gather.scratch(nz, name not in unshared)
    return pl.pallas_call(
        functools.partial(front_kernel, nz, unshared, chunked, order, steps),
        name="front",
        out_shape=tuple([jax.ShapeDtypeStruct(s, BF16) for s in shapes])
        + (
            jax.ShapeDtypeStruct((rows, inner), BF16),
            jax.ShapeDtypeStruct((rows, width), BF16),
            jax.ShapeDtypeStruct(parts[0].shape, F32),
        ),
        in_specs=[vm] + [hb] * len(parts),
        out_specs=tuple([vm] + [hb] * (len(FRONT_PARTS) - 1) + [vm] * 3),
        scratch_shapes=scratch,
        compiler_params=pltpu.CompilerParams(
            collective_id=collective_id, has_side_effects=True, vmem_limit_bytes=BIG
        ),
    )(x, *parts)


BACK_OUT = ("gate", "up", "down", "co", "cq", "q", "o", "k", "v", "ck", "cv")
BACK_NONE = ("kv", "cross")
BACK_PLAN = (
    ("q",),
    dict(kv=4),
    (
        ("kv", 3), ("k", 0), ("co", 0), ("kv", 1), ("cq", 0), ("gate", 0), ("kv", 0), ("kv", 2), ("cross", 0),
        ("down", 0), ("up", 0), ("o", 0), ("v", 0), ("q", 0),
    ),
    (
        (0, 0), (2, 0), (3, 0), (4, 0), (5, 0), (0, 1), (6, 0), (2, 1), (7, 0), (3, 1), (8, 0), (4, 1), (9, 0),
        (2, 2), (0, 3), (5, 1), (10, 0), (4, 2), (6, 1), (7, 1), (3, 3), (8, 1), (11, 0), (0, 4), (0, 5), (2, 3),
        (13, 0), (4, 3), (9, 1), (3, 4), (3, 5), (10, 1), (6, 3), (2, 4), (5, 2), (11, 1), (13, 1), (4, 4), (7, 3),
        (6, 4), (6, 5), (8, 3), (9, 2), (7, 4), (7, 5), (5, 3), (1, 0), (12, 0), (8, 4), (8, 5), (13, 3), (1, 1),
        (12, 1), (5, 4), (10, 2), (9, 3), (13, 4), (11, 2), (10, 3), (1, 2), (9, 4), (11, 3), (1, 3), (12, 2),
        (10, 4), (11, 4), (12, 3), (2, 5), (4, 5), (5, 5), (9, 5), (13, 5), (10, 5), (11, 5), (1, 4), (12, 4),
        (1, 5), (12, 5),
    ),
)


def back_kind(name, late):
    return "none" if name in BACK_NONE else "late" if name in late else "x"


def back_kernel(nz, late, chunked, order, steps, *refs):
    (
        kvp, crossp, wq, wk, wv, wck, wcv, x_ref, gains_ref, gh_ref, gpart_ref, small_ref,
        n3, mixed, att, n2, attc, n1, gg, gu, go, g1, gcq, g2, dq,
    ) = refs[:25]
    refs = refs[25:]
    outs = dict(zip(BACK_OUT, refs[: len(BACK_OUT)]))
    gx_ref, genc_ref, total_ref = refs[len(BACK_OUT) : len(BACK_OUT) + 3]
    refs = refs[len(BACK_OUT) + 3 :]
    kvown, crown, low, wbuf, kvl, every, pairb, kls, wsem, psem = refs[:10]
    refs = refs[10:]
    outs["kv"], outs["cross"] = kvown, crown
    at = Place(nz)
    at.greet()
    jobs = []
    for i, (name, chunk) in enumerate(order):
        mine = list(refs[Reduce.COUNT * i : Reduce.COUNT * (i + 1)])
        chunks = chunked.get(name, 1)
        out = outs[name]
        if chunks > 1:
            wide = out.shape[-1] // chunks
            out = out.at[:, pl.ds(chunk * wide, wide)]
        job = Reduce(at, out, mine, back_kind(name, late))
        if name == "cross":
            job.part = crossp
        if name == "kv":
            job.part = kvp
            job.part_cols = pl.ds(chunk * wide, wide)
            job.local_part, job.local_cols = kvl, job.part_cols
        jobs.append(job)
    refs = refs[Reduce.COUNT * len(order) :]
    spread = Gather(at, low, every, refs[: Gather.COUNT], False)
    everyone = Total(at, refs[Gather.COUNT :])
    load_w = [pltpu.make_async_copy(src, wbuf.at[i], wsem.at[i]) for i, src in enumerate((wq, wk, wv))]
    load_c = [pltpu.make_async_copy(src, wbuf.at[3 + i], wsem.at[3 + i]) for i, src in enumerate((wck, wcv))]
    for copy in load_w + load_c:
        copy.start()
    kv_local = pltpu.make_async_copy(kvp.at[:, :, at.w], kvl, kls)
    kv_local.start()
    width = x_ref.shape[1]
    inner = dq.shape[1]

    def make(name, chunk, part):
        if name in BACK_NONE:
            return
        _, _, _, r, wide = part.shape
        if name in ("k", "v"):
            left, right = n1, kvl.at[0, 0, :, pl.ds(0 if name == "k" else inner, inner)]
        else:
            left, right = {
                "gate": (n3, gg), "up": (n3, gu), "down": (mixed, go), "o": (att, g1), "cq": (n2, gcq), "co": (attc, g2),
                "q": (n1, dq),
            }[name]
        take = 2 if r % 128 else 1
        tile = 512 if wide % 512 == 0 else wide // 2 if wide % 256 == 0 and wide > 256 else wide
        for first in range(0, nz, take):
            piece = left[:, first * 4 * r : (first + take) * 4 * r]
            for c in range(0, wide, tile):
                out = mm(piece, right[:, chunk * wide + c : chunk * wide + c + tile], TN).astype(BF16)
                part[first : first + take, :, :, :, c : c + tile] = out.reshape(take, 2, 2, r, tile)

    def after_cross():
        both = crown[...]
        low[...] = jnp.concatenate([both, jnp.zeros_like(both)], axis=0).astype(BF16)
        for copy in load_c:
            copy.wait()
        genc = mm(low[:, :inner], wbuf[3].reshape(width, inner), NT) + mm(low[:, inner:], wbuf[4].reshape(width, inner), NT)
        genc_ref[...] = genc[:8]
        spread.place()
        spread.send()

    def pair_copy():
        return push(pairb.at[0], pairb.at[1], psem.at[0], psem.at[1], at.twin())

    def cross_weights():
        spread.end()
        owned = pairb.shape[1]
        rows = small_ref.shape[0] * small_ref.shape[1]
        col = lax.broadcasted_iota(jnp.int32, (width, 128), 0)
        lane = lax.broadcasted_iota(jnp.int32, (width, 128), 1)
        pick = ((col == at.me * owned + lane) & (lane < owned)).astype(BF16)
        mine = mm(small_ref[...].reshape(rows, width), pick, NN).astype(BF16)
        total = mm(mine, every[...].reshape(rows, 2 * inner), TN)[:owned]
        pairb[0] = total.astype(BF16)
        pair_copy().start()
        outs["ck"][...] = total[:, :inner]
        outs["cv"][...] = total[:, inner:]

    def cross_end():
        pair_copy().wait_recv()
        outs["ck"][...] += pairb[1, :, :inner].astype(F32)
        outs["cv"][...] += pairb[1, :, inner:].astype(F32)
        pair_copy().wait_send()
        spread.close()

    def after_kv():
        for copy in load_w:
            copy.wait()
        grad = mm(dq[...], wbuf[0].reshape(width, inner), NT)
        grad = grad + mm(kvl[0, 0, :, :inner], wbuf[1].reshape(width, inner), NT)
        grad = grad + mm(kvl[0, 0, :, inner:], wbuf[2].reshape(width, inner), NT)
        rows, gain = norm_back(x_ref[...].astype(F32), gains_ref[4:5], grad)
        gx_ref[...] = gh_ref[...] + rows
        everyone.buf[0] = gpart_ref[...]
        everyone.buf[0, 0:1, :] = gain
        everyone.send()

    kv_jobs = [i for i, entry in enumerate(order) if entry[0] == "kv"]
    kv_seen = kv_ended = 0
    early = [i for i, stage in steps if stage == 0 and order[i][0] not in BACK_NONE + ("k", "v")][:2]
    for i in early:
        make(*order[i], jobs[i].part)
    at.met()
    kv_sent = 0
    hops, later = [], {}
    for count, (i, stage) in enumerate(steps):
        (name, chunk), job = order[i], jobs[i]
        if stage == 0:
            if i not in early:
                make(name, chunk, job.part)
            job.send()
        if stage == 1:
            if i in kv_jobs:
                kv_seen += 1
                if kv_seen == 1:
                    kv_local.wait()
            job.after_w()
        if stage == 2:
            job.after_x()
        if stage == 3:
            job.after_y()
        if stage == 4:
            job.after_z()
        if stage == 5:
            job.end()
            if name == "cross":
                after_cross()
                later = {count + 5: spread.after_z, count + 10: spread.after_y, count + 15: cross_weights}
            if i in kv_jobs:
                kv_ended += 1
                if kv_ended == len(kv_jobs):
                    kvl[0, 0] = kvown[...].astype(BF16)
        if stage == 0 and name in ("k", "v"):
            kv_sent += 1
            if kv_sent == 2:
                after_kv()
                hops = [count + 4, count + 8, count + 12]
        if count in hops:
            everyone.after(hops.index(count))
        if count in later:
            later.pop(count)()
    for count in sorted(later):
        later[count]()
    for i, count in enumerate(hops):
        if count >= len(steps):
            everyone.after(i)
    cross_end()
    total_ref[...] = everyone.end()
    for job in jobs:
        job.close()


def back_step(
    kv_part, cross_part, weights, x, gains, grad_hidden, gpart, small, acts, shapes, nz, collective_id=2,
    plan=BACK_PLAN,
):
    late, chunked, order, steps = plan
    hb = pl.BlockSpec(memory_space=pl.ANY)
    vm = pl.BlockSpec(memory_space=pltpu.VMEM)
    rows, width = x.shape
    inner = acts[-1].shape[1]
    dma = pltpu.SemaphoreType.DMA
    own = [jax.ShapeDtypeStruct(shapes[name], F32) for name in BACK_OUT]
    scratch = [
        pltpu.VMEM((rows, 2 * inner), F32),
        pltpu.VMEM((8, 2 * inner), F32),
        pltpu.VMEM((16, 2 * inner), BF16),
        pltpu.VMEM((5,) + weights[0].shape, BF16),
        pltpu.VMEM((nz, 2, rows, 2 * inner), BF16),
        pltpu.VMEM((nz, 2, 2, 16, 2 * inner), BF16),
        pltpu.VMEM((2,) + shapes["ck"][:1] + (2 * inner,), BF16),
        dma,
        dma((5,)),
        dma((2,)),
    ]
    shapes = dict(shapes, kv=(rows, 2 * inner), cross=(8, 2 * inner))
    for name, _ in order:
        r, wide = shapes[name]
        wide = wide // chunked.get(name, 1)
        held = name not in BACK_NONE
        scratch += Reduce.scratch(nz, r, wide, back_kind(name, late), F32 if name == "cross" else BF16, part=held)
    scratch += Gather.scratch(nz, False) + Total.scratch(nz, gpart.shape[0], width)
    return pl.pallas_call(
        functools.partial(back_kernel, nz, late, chunked, order, steps),
        name="back",
        out_shape=tuple(own)
        + (
            jax.ShapeDtypeStruct((rows, width), F32),
            jax.ShapeDtypeStruct((8, width), F32),
            jax.ShapeDtypeStruct(gpart.shape, F32),
        ),
        in_specs=[hb, vm] + [hb] * 5 + [vm] * (5 + len(acts)),
        out_specs=tuple([vm] * (len(own) + 3)),
        scratch_shapes=scratch,
        compiler_params=pltpu.CompilerParams(
            collective_id=collective_id, has_side_effects=True, vmem_limit_bytes=BIG
        ),
    )(kv_part, cross_part, *weights, x, gains, grad_hidden, gpart, small, *acts)


def closing_kernel(count, heads, *refs):
    total, bias = refs[count], refs[-1]
    for source, target in zip(refs[:count], refs[count + 1 :]):
        target[...] = source[...]
    bias[...] = total[8:24, 0:128].T[:BUCKETS, :heads]


def closing(arrays, total, heads):
    vm = pl.BlockSpec(memory_space=pltpu.VMEM)
    count = len(arrays)
    return pl.pallas_call(
        functools.partial(closing_kernel, count, heads),
        name="closing",
        out_shape=tuple(jax.ShapeDtypeStruct(a.shape, a.dtype) for a in arrays)
        + (jax.ShapeDtypeStruct((BUCKETS, heads), F32),),
        in_specs=[vm] * (count + 1),
        out_specs=tuple([vm] * (count + 1)),
    )(*arrays, total)


class Bag:
    def __init__(self, names, refs):
        for name, ref in zip(names, refs):
            setattr(self, name, ref)


def flat(ref):
    value = ref[...]
    return value.reshape(-1, value.shape[-1])


def unstack(pair_rows, low):
    rows = pair_rows.shape[0] // 2
    return jnp.where(low, pair_rows[:rows], pair_rows[rows:])


def every_encoded(small_ref, take):
    devices, block, width = small_ref.shape
    rows = devices * take
    row = lax.broadcasted_iota(jnp.int32, (rows, devices * block), 0)
    col = lax.broadcasted_iota(jnp.int32, (rows, devices * block), 1)
    pick = (col == (row // take) * block + lax.rem(row, take)).astype(BF16)
    return mm(pick, small_ref[...].reshape(devices * block, width), NN).astype(BF16)


def cross_forward(b, low):
    pairs = b.cq.shape[1] // 128
    for pair in range(pairs):
        lanes = slice(128 * pair, 128 * pair + 128)
        qm = stack_pair(b.cq[:, lanes], low)
        s = mm(qm, b.ckeys[:, lanes], NT)
        peak = jnp.max(s, axis=1, keepdims=True)
        log_total = peak + jnp.log(jnp.sum(jnp.exp(s - peak), axis=1, keepdims=True))
        p = jnp.exp(s - log_total)
        b.cprob[pair] = p
        b.attc[:, lanes] = unstack(mm(p.astype(BF16), b.cvals[:, lanes], NN), low).astype(BF16)


def cross_backward(b, gac, low, keys_each):
    pairs = b.cq.shape[1] // 128
    inner = b.cq.shape[1]
    owners = 4 * b.crossp.shape[0]
    b.crossp[...] = jnp.zeros_like(b.crossp)
    for pair in range(pairs):
        lanes = slice(128 * pair, 128 * pair + 128)
        qm = stack_pair(b.cq[:, lanes], low)
        dom = stack_pair(gac[:, lanes], low)
        p = b.cprob[pair]
        dp = mm(dom, b.cvals[:, lanes], NT)
        ds = (p * (dp - jnp.sum(p * dp, axis=1, keepdims=True))).astype(BF16)
        b.gcq[:, lanes] = unstack(mm(ds, b.ckeys[:, lanes], NN), low).astype(BF16)
        gk = mm(ds, qm, TN)
        gv = mm(p.astype(BF16), dom, TN)
        for owner in range(owners):
            rows = slice(keys_each * owner, keys_each * owner + keys_each)
            b.crossp[owner // 4, owner // 2 % 2, owner % 2, 0:keys_each, lanes] = gk[rows]
            b.crossp[owner // 4, owner // 2 % 2, owner % 2, 0:keys_each, 128 * pair + inner : 128 * pair + inner + 128] = gv[rows]


GELU_A = 0.7978845608028654
GELU_B = 0.044715


def gelu_parts(v):
    t = jnp.tanh(GELU_A * (v + GELU_B * v * v * v))
    value = 0.5 * v * (1.0 + t)
    slope = 0.5 * (1.0 + t) + 0.5 * v * (1.0 - t * t) * (GELU_A * (1.0 + 3.0 * GELU_B * v * v))
    return value, slope


FF_TILE = 1024


def after_attention(b):
    b.h1[...] = b.x[...].astype(F32) + mm(b.att[...], flat(b.w_o), NN)
    b.n2[...] = normed(b.h1[...], b.gains[5:6]).astype(BF16)
    b.cq[...] = mm(b.n2[...], flat(b.w_cq), NN).astype(BF16)


def after_cross_attention(b):
    b.h2[...] = b.h1[...] + mm(b.attc[...], flat(b.w_co), NN)
    b.n3[...] = normed(b.h2[...], b.gains[6:7]).astype(BF16)


def feed_forward(b):
    ff = b.mixed.shape[1]
    width = b.x.shape[1]
    for c in range(0, ff, FF_TILE):
        cols = slice(c, c + FF_TILE)
        gate = mm(b.n3[...], b.w_gate[:, :, cols].reshape(width, FF_TILE), NN)
        up = mm(b.n3[...], b.w_up[:, :, cols].reshape(width, FF_TILE), NN)
        value, slope = gelu_parts(gate)
        b.mixed[:, cols] = (value * up).astype(BF16)
        b.hg[:, cols] = value
        b.hs[:, cols] = slope * up
    b.layer_out[...] = (b.h2[...] + mm(b.mixed[...], flat(b.w_down), NN)).astype(BF16)


def feed_backward(b):
    ff = b.mixed.shape[1]
    width = b.x.shape[1]
    down = flat(b.w_down)
    total = jnp.zeros(b.h2.shape, F32)
    for c in range(0, ff, FF_TILE):
        cols = slice(c, c + FF_TILE)
        gm = mm(b.go[...], down[cols], NT).astype(BF16).astype(F32)
        gg = (gm * b.hs[:, cols]).astype(BF16)
        gu = (gm * b.hg[:, cols]).astype(BF16)
        b.gg[:, cols] = gg
        b.gu[:, cols] = gu
        total = total + mm(gg, b.w_gate[:, :, cols].reshape(width, FF_TILE), NT)
        total = total + mm(gu, b.w_up[:, :, cols].reshape(width, FF_TILE), NT)
    rows, gain = norm_back(b.h2[...], b.gains[6:7], total)
    b.gpart[2:3, :] = gain
    b.gh[...] = b.go[...].astype(F32) + rows
    b.g2[...] = b.gh[...].astype(BF16)


def before_attention(b):
    rows, gain = norm_back(b.h1[...], b.gains[5:6], mm(b.gcq[...], flat(b.w_cq), NT))
    b.gpart[1:2, :] = gain
    b.gh[...] = b.gh[...] + rows
    b.g1[...] = b.gh[...].astype(BF16)
    b.gatt[...] = mm(b.g1[...], flat(b.w_o), NT).astype(BF16)


GROUP = 4


def stack_group(block):
    head = lax.broadcasted_iota(jnp.int32, block.shape, 1) // BLK
    zero = jnp.zeros_like(block)
    return jnp.concatenate([jnp.where(head == i, block, zero) for i in range(GROUP)], axis=0)


def unstack_group(stacked):
    rows = stacked.shape[0] // GROUP
    head = lax.broadcasted_iota(jnp.int32, (rows, stacked.shape[1]), 1) // BLK
    out = stacked[:rows]
    for i in range(1, GROUP):
        out = jnp.where(head == i, stacked[i * rows : i * rows + rows], out)
    return out


def fill_bias(b, qb, rank):
    pairs = b.q.shape[1] // 128
    key_j = lax.broadcasted_iota(jnp.int32, (CH, 128), 0)
    lane_i = lax.broadcasted_iota(jnp.int32, (CH, 128), 1)
    high = lane_i >= BLK
    row_i = jnp.where(high, lane_i - BLK, lane_i)
    shift = jnp.where(high, BLK, 0)
    for kind in range(2):
        dist = (lax.rem(rank, 4) + 4 * kind) * BLK + row_i - key_j
        bucket = bucket_ids(jnp.maximum(dist, 0)) + shift
        for pair in range(pairs):
            tile = jnp.take_along_axis(jnp.broadcast_to(b.tb[pl.ds(pair, 1), :], (CH, 128)), bucket, axis=1)
            if kind == 0:
                tile = jnp.where(dist >= 0, tile, MASKED)
            b.bias[qb, kind, pair // 2, :, 128 * (pair % 2) : 128 * (pair % 2) + 128] = tile
    for pair in range(pairs):
        b.bias[qb, 2, pair // 2, :, 128 * (pair % 2) : 128 * (pair % 2) + 128] = jnp.where(
            high,
            b.tb[pl.ds(pair, 1), pl.ds(BLK + BUCKETS - 1, 1)],
            b.tb[pl.ds(pair, 1), pl.ds(BUCKETS - 1, 1)],
        )


def self_forward_block(b, qb, rank):
    inner = b.q.shape[1]
    wide = GROUP * BLK
    groups = inner // wide
    last = rank // 4
    mine = pl.ds(qb * BLK, BLK)
    for i in range(groups):
        b.qm[qb, i] = stack_group(b.q[mine, wide * i : wide * i + wide])
        b.top[i] = jnp.full((8, wide), -3e38, F32)
        b.sums[i] = jnp.zeros((8, wide), F32)
        b.acc[i] = jnp.zeros((wide, wide), F32)

    def first(chunk, carry):
        kind = jnp.minimum(last - chunk, 2)
        keys = pl.ds(pl.multiple_of(chunk * CH, CH), CH)
        for i in range(groups):
            s = mm(b.kvs[keys, wide * i : wide * i + wide], b.qm[qb, i], NT) + b.bias[qb, kind, i]
            b.sco[i, keys, :] = s
            b.top[i] = jnp.maximum(b.top[i], jnp.max(s.reshape(CH // 8, 8, wide), axis=0))
        return carry

    lax.fori_loop(0, last + 1, first, 0)
    for i in range(groups):
        b.top[i] = jnp.broadcast_to(jnp.max(b.top[i], axis=0, keepdims=True), (8, wide))

    def second(chunk, carry):
        keys = pl.ds(pl.multiple_of(chunk * CH, CH), CH)
        for i in range(groups):
            p = jnp.exp(b.sco[i, keys, :] - b.top[i, 0:1, :])
            b.sums[i] += jnp.sum(p.reshape(CH // 8, 8, wide), axis=0)
            values = b.kvs[keys, inner + wide * i : inner + wide * i + wide]
            b.acc[i] += mm(p.astype(BF16), values, TN)
        return carry

    lax.fori_loop(0, last + 1, second, 0)
    for i in range(groups):
        total = jnp.sum(b.sums[i], axis=0, keepdims=True)
        b.rows[qb, i, 0:1, :] = b.top[i, 0:1, :] + jnp.log(total)
        parts = []
        for side in range(wide // 128):
            scale = jnp.broadcast_to(total[:, 128 * side : 128 * side + 128], (128, 128)).T
            rows = b.acc[i, 128 * side : 128 * side + 128, :]
            parts.append(rows / jnp.concatenate([scale] * (wide // 128), axis=1))
        out = unstack_group(jnp.concatenate(parts, axis=0))
        b.att32[mine, wide * i : wide * i + wide] = out
        b.att[mine, wide * i : wide * i + wide] = out.astype(BF16)


def self_backward_rows(b, qb):
    inner = b.q.shape[1]
    wide = GROUP * BLK
    mine = pl.ds(qb * BLK, BLK)
    for i in range(inner // wide):
        b.dom[qb, i] = stack_group(b.gatt[mine, wide * i : wide * i + wide])
    for pair in range(inner // 128):
        lanes = slice(128 * pair, 128 * pair + 128)
        prod = (b.gatt[mine, lanes].astype(F32) * b.att32[mine, lanes]).T
        b.rows[qb, pair // 2, 1:2, 128 * (pair % 2) : 128 * (pair % 2) + 128] = jnp.concatenate(
            [jnp.sum(prod[:BLK], axis=0, keepdims=True), jnp.sum(prod[BLK:], axis=0, keepdims=True)], axis=1
        )


def self_backward_block(b, qb, rank, longer):
    inner = b.q.shape[1]
    wide = GROUP * BLK
    groups = inner // wide
    last = rank // 4
    b.acc[...] = jnp.zeros_like(b.acc)

    @pl.when(last == 0)
    def _():
        for i in range(groups):
            b.near[i, pl.ds(0, CH), :] = jnp.zeros((CH, wide), F32)

    def step(chunk, carry):
        kind = jnp.minimum(last - chunk, 2)
        keys = pl.ds(pl.multiple_of(chunk * CH, CH), CH)
        keep = jnp.maximum(chunk - last + 1, 0)
        for i in range(groups):
            klanes = slice(wide * i, wide * i + wide)
            vlanes = slice(inner + wide * i, inner + wide * i + wide)
            kp = b.kvs[keys, klanes]
            qp = b.qm[qb, i]
            gp = b.dom[qb, i]
            st = mm(kp, qp, NT) + b.bias[qb, kind, i]
            pt = jnp.exp(st - b.rows[qb, i, 0:1, :])
            dp = mm(b.kvs[keys, vlanes], gp, NT)
            ds = pt * (dp - b.rows[qb, i, 1:2, :])
            dsb = ds.astype(BF16)
            gv = mm(pt.astype(BF16), gp, NN)
            gk = mm(dsb, qp, NN)
            b.dkv[keys, vlanes] = gv if longer else b.dkv[keys, vlanes] + gv
            b.dkv[keys, klanes] = gk if longer else b.dkv[keys, klanes] + gk
            b.acc[i] += mm(dsb, kp, TN)
            b.tot[i] += jnp.sum(ds.reshape(CH // 8, 8, wide), axis=0)
            b.near[i, pl.ds(pl.multiple_of(keep * CH, CH), CH), :] = ds
        return carry

    lax.fori_loop(0, last + 1, step, 0)
    if longer:

        def unseen(chunk, carry):
            keys = pl.ds(pl.multiple_of(chunk * CH, CH), CH)
            b.dkv[keys, :] = jnp.zeros((CH, 2 * inner), F32)
            return carry

        lax.fori_loop(last + 1, b.dkv.shape[0] // CH, unseen, 0)
    mine = pl.ds(pl.multiple_of(qb * BLK, BLK), BLK)
    for i in range(groups):
        b.dq[mine, wide * i : wide * i + wide] = unstack_group(b.acc[i]).astype(BF16)
        for gap in range(3):
            offset = pl.multiple_of((rank - gap - 4 * (last - 1)) * BLK, BLK)
            b.nacc[gap, i] += b.near[i, pl.ds(offset, BLK), :]


def bucket_of(distance):
    half_count = BUCKETS // 2
    edges = [math.ceil(half_count * math.pow(MAXDIST / half_count, k / half_count)) for k in range(1, half_count)]
    return min(distance, half_count) + sum(distance >= edge for edge in edges)


def bias_gradient(b):
    pairs = b.q.shape[1] // 128
    key_s = lax.broadcasted_iota(jnp.int32, (BLK, 128), 0)
    lane = lax.broadcasted_iota(jnp.int32, (BLK, 128), 1)
    row_s = jnp.where(lane < BLK, lane, lane - BLK)
    buckets = [bucket_ids(jnp.maximum(gap * BLK + row_s - key_s, 0)) for gap in range(3)]
    spans = [(bucket_of(max(BLK * (gap - 1) + 1, 0)), bucket_of(BLK * (gap + 1) - 1)) for gap in range(3)]
    for pair in range(pairs):
        lanes = slice(128 * (pair % 2), 128 * (pair % 2) + 128)
        tiles = [b.nacc[gap, pair // 2, :, lanes] for gap in range(3)]
        far = jnp.sum(b.tot[pair // 2, :, lanes], axis=0, keepdims=True)
        for tile in tiles:
            far = far - jnp.sum(tile, axis=0, keepdims=True)
        lines = []
        for number in range(BUCKETS):
            met = [gap for gap in range(3) if spans[gap][0] <= number <= spans[gap][1]]
            part = jnp.where(buckets[met[0]] == number, tiles[met[0]], 0.0)
            for gap in met[1:]:
                part = part + jnp.where(buckets[gap] == number, tiles[gap], 0.0)
            line = jnp.sum(part, axis=0, keepdims=True)
            lines.append(line + far if number == BUCKETS - 1 else line)
        grid = jnp.concatenate(lines + [jnp.zeros((128 - BUCKETS, 128), F32)], axis=0).T
        b.gpart[8 + 2 * pair : 9 + 2 * pair, 0:128] = jnp.sum(grid[:BLK], axis=0, keepdims=True)
        b.gpart[9 + 2 * pair : 10 + 2 * pair, 0:128] = jnp.sum(grid[BLK:], axis=0, keepdims=True)


MID_IN = (
    "deal", "k_hbm", "v_hbm", "o", "cq_w", "ck", "cv", "co", "gate", "up", "down", "x", "gains", "small", "q", "go", "tb",
)
MID_OUT = (
    "layer_out", "n3", "mixed", "att", "n2", "attc", "gg", "gu", "g1", "gcq", "g2", "dq", "gh", "gpart", "crossp", "dkv_hbm",
)
MID_SCRATCH = (
    "kvs", "dkv", "w_o", "w_cq", "w_ck", "w_cv", "w_co", "w_gate", "w_up", "w_down", "h1", "h2", "cq", "ckeys", "cvals", "cprob",
    "hg", "hs", "gatt", "bias", "qm", "dom", "top", "sums", "acc", "sco", "rows", "att32", "near", "nacc", "tot", "sem", "osem", "wsem",
)


def mid_kernel(enc_own, *refs):
    b = Bag(MID_IN + MID_OUT + MID_SCRATCH, refs)
    load_in_order(b.deal, b.k_hbm, b.v_hbm, b.kvs, b.sem)
    loads = []
    for i, name in enumerate(("o", "cq", "ck", "cv", "co", "gate", "up", "down")):
        source = b.cq_w if name == "cq" else getattr(b, name)
        loads.append(pltpu.make_async_copy(source, getattr(b, "w_" + name), b.wsem.at[i]))
        loads[-1].start()
    low = lax.broadcasted_iota(jnp.int32, (2 * BLK, 128), 1) < BLK
    device = lax.axis_index(AXES)
    ranks = [b.deal[device, qb] for qb in range(2)]
    for qb in range(2):
        fill_bias(b, qb, ranks[qb])
    loaded(b.k_hbm, b.v_hbm, b.kvs, b.sem)
    for qb in range(2):
        self_forward_block(b, qb, ranks[qb])
    for load in loads[:5]:
        load.wait()
    after_attention(b)
    enc = every_encoded(b.small, enc_own)
    b.ckeys[...] = mm(enc, flat(b.w_ck), NN).astype(BF16)
    b.cvals[...] = mm(enc, flat(b.w_cv), NN).astype(BF16)
    cross_forward(b, low)
    after_cross_attention(b)
    for load in loads[5:]:
        load.wait()
    feed_forward(b)
    b.gpart[...] = jnp.zeros_like(b.gpart)
    feed_backward(b)
    gac = mm(b.g2[...], flat(b.w_co), NT).astype(BF16)
    cross_backward(b, gac, low, enc_own)
    before_attention(b)
    b.tot[...] = jnp.zeros_like(b.tot)
    b.nacc[...] = jnp.zeros_like(b.nacc)
    for qb in range(2):
        self_backward_rows(b, qb)
    longer = jnp.where(ranks[0] > ranks[1], 0, 1)
    self_backward_block(b, longer, jnp.maximum(ranks[0], ranks[1]), True)
    self_backward_block(b, 1 - longer, jnp.minimum(ranks[0], ranks[1]), False)
    blocks = b.k_hbm.shape[0] // BLK

    def out_one(index, carry):
        here = pl.ds(pl.multiple_of(b.deal[index // 2, index % 2] * BLK, BLK), BLK)
        b.kvs[here, :] = b.dkv[here, :].astype(BF16)
        pltpu.make_async_copy(b.kvs.at[here], b.dkv_hbm.at[pl.ds(index * BLK, BLK)], b.osem).start()
        return carry

    lax.fori_loop(0, blocks, out_one, 0)
    bias_gradient(b)
    pltpu.make_async_copy(b.kvs, b.dkv_hbm, b.osem).wait()


def mid(deal, keys, values, weights, x, gains, small, q, go, tb, enc_own):
    rows, width = x.shape
    inner = q.shape[1]
    total = keys.shape[0]
    ff = weights[5].shape[2]
    wide = GROUP * BLK
    h2, h4 = inner // 128, inner // wide
    shards = weights[0].shape[0]
    enc = shards * enc_own
    sm = pl.BlockSpec(memory_space=pltpu.SMEM)
    vm = pl.BlockSpec(memory_space=pltpu.VMEM)
    hb = pl.BlockSpec(memory_space=pl.ANY)
    out = jax.ShapeDtypeStruct
    return pl.pallas_call(
        functools.partial(mid_kernel, enc_own),
        name="mid",
        out_shape=(
            out((rows, width), BF16), out((rows, width), BF16), out((rows, ff), BF16), out((rows, inner), BF16),
            out((rows, width), BF16), out((rows, inner), BF16), out((rows, ff), BF16), out((rows, ff), BF16),
            out((rows, width), BF16), out((rows, inner), BF16), out((rows, width), BF16), out((rows, inner), BF16),
            out((rows, width), F32), out((24, width), F32), out((shards // 4, 2, 2, 8, 2 * inner), F32),
            out((total, 2 * inner), BF16),
        ),
        in_specs=[sm] + [hb] * (2 + len(weights)) + [vm] * 6,
        out_specs=tuple([vm] * 15 + [hb]),
        scratch_shapes=[
            pltpu.VMEM((total, 2 * inner), BF16),
            pltpu.VMEM((total, 2 * inner), F32),
        ]
        + [pltpu.VMEM(weight.shape, BF16) for weight in weights]
        + [
            pltpu.VMEM((rows, width), F32),
            pltpu.VMEM((rows, width), F32),
            pltpu.VMEM((rows, inner), BF16),
            pltpu.VMEM((enc, inner), BF16),
            pltpu.VMEM((enc, inner), BF16),
            pltpu.VMEM((h2, 2 * rows, enc), F32),
            pltpu.VMEM((rows, ff), F32),
            pltpu.VMEM((rows, ff), F32),
            pltpu.VMEM((rows, inner), BF16),
            pltpu.VMEM((2, 3, h4, CH, wide), F32),
            pltpu.VMEM((2, h4, wide, wide), BF16),
            pltpu.VMEM((2, h4, wide, wide), BF16),
            pltpu.VMEM((h4, 8, wide), F32),
            pltpu.VMEM((h4, 8, wide), F32),
            pltpu.VMEM((h4, wide, wide), F32),
            pltpu.VMEM((h4, total, wide), F32),
            pltpu.VMEM((2, h4, 8, wide), F32),
            pltpu.VMEM((rows, inner), F32),
            pltpu.VMEM((h4, 2 * CH, wide), F32),
            pltpu.VMEM((3, h4, BLK, wide), F32),
            pltpu.VMEM((h4, 8, wide), F32),
            pltpu.SemaphoreType.DMA((2,)),
            pltpu.SemaphoreType.DMA,
            pltpu.SemaphoreType.DMA((8,)),
        ],
        compiler_params=pltpu.CompilerParams(vmem_limit_bytes=BIG),
    )(deal, keys, values, *weights, x, gains, small, q, go, tb)


def fits(*operands):
    layer_in, encoded, self_query, relative_bias = operands[0], operands[1], operands[4], operands[18]
    total = layer_in.shape[1] * lax.axis_size(AXES)
    return (
        lax.axis_size(GRP) == 2
        and lax.axis_size(WSH) == 2
        and lax.axis_size(CTX) == 8
        and layer_in.shape[1] == 2 * BLK
        and encoded.shape[1] == 4
        and total // 2 <= CONT_TOK
        and self_query.shape[0] % 16 == 0
        and self_query.shape[1] == relative_bias.shape[1] * BLK
        and self_query.shape[1] % 256 == 0
    )


def fast(
    layer_in, encoded, cotangent, deal_table, self_query, self_key, self_value, self_output, cross_query, cross_key,
    cross_value, cross_output, feed_gate, feed_up, feed_down, gain_self, gain_cross, gain_feed, relative_bias,
):
    nz = lax.axis_size(CTX) // 2
    shards = lax.axis_size(AXES)
    device = lax.axis_index(AXES)
    rows = layer_in.shape[1]
    width = layer_in.shape[2]
    heads = relative_bias.shape[1]
    inner = self_query.shape[1]
    owned = gain_self.shape[0]
    enc_own = encoded.shape[1]
    table_hb = relative_bias.astype(F32).T

    gains_here = lax.dynamic_update_slice(
        jnp.zeros((3, width), BF16), jnp.stack([gain_self, gain_cross, gain_feed]), (0, device * owned)
    )
    small = jnp.concatenate([encoded[0], gains_here, jnp.zeros((9, width), BF16)], axis=0)
    *wholes, queries, normed_one, gains = front(
        layer_in[0],
        (
            small, self_key, self_value, self_query, self_output, cross_query, cross_key, cross_value, cross_output,
            feed_gate, feed_up, feed_down,
        ),
        nz,
        shards,
    )
    whole = {name: value.reshape((shards,) + value.shape[3:]) for name, value in zip(FRONT_PARTS, wholes)}
    in_rows = {name: value.reshape(-1, value.shape[-1]) for name, value in whole.items()}
    (
        layer_out, normed_three, mixed_hidden, attended, normed_two, attended_cross, grad_gate, grad_up, grad_one_low,
        grad_cq_low, grad_two_low, grad_queries, grad_hidden_one, gpart, cross_part, kv_part,
    ) = mid(
        deal_table, in_rows["keys"], in_rows["values"],
        [whole[name] for name in ("o", "cq", "ck", "cv", "co", "gate", "up", "down")],
        layer_in[0], gains, whole["small"], queries, cotangent[0], pair_table(table_hb), enc_own,
    )
    ff = feed_gate.shape[1]
    square = (owned, inner)
    shapes = dict(
        gate=(owned, ff), up=(owned, ff), down=(feed_down.shape[0], width), co=(inner // shards, width), cq=square,
        ck=square, cv=square, q=square, o=(inner // shards, width), k=square, v=square,
    )
    result = back_step(
        kv_part.reshape(nz, 2, 2, rows, 2 * inner), cross_part,
        [whole[name] for name in ("q", "k", "v", "ck", "cv")], layer_in[0], gains,
        grad_hidden_one, gpart, whole["small"],
        (
            normed_three, mixed_hidden, attended, normed_two, attended_cross, normed_one, grad_gate, grad_up, cotangent[0],
            grad_one_low, grad_cq_low, grad_two_low, grad_queries,
        ),
        shapes,
        nz,
    )
    grad_enc, total = result[len(BACK_OUT) + 1 :]
    *result, grad_relative_bias = closing(result[: len(BACK_OUT) + 1], total, heads)
    got = dict(zip(BACK_OUT, result))
    grad_input = result[len(BACK_OUT)]
    gain_grads = [lax.dynamic_slice_in_dim(total[i], device * owned, owned) for i in range(3)]
    return (
        layer_out[None], grad_input[None], grad_enc[None, :enc_own],
        got["q"], got["k"], got["v"], got["o"], got["cq"], got["ck"], got["cv"], got["co"], got["gate"], got["up"], got["down"],
        gain_grads[0], gain_grads[1], gain_grads[2], grad_relative_bias,
    )


def solution(mesh):
    return jax.shard_map(
        lambda *operands: (fast if fits(*operands) else local)(*operands),
        mesh=mesh,
        in_specs=(
            P(GRP, AXES, None),
            P(GRP, AXES, None),
            P(GRP, AXES, None),
            P(),
            P(AXES, None),
            P(AXES, None),
            P(AXES, None),
            P(AXES, None),
            P(AXES, None),
            P(AXES, None),
            P(AXES, None),
            P(AXES, None),
            P(AXES, None),
            P(AXES, None),
            P(AXES, None),
            P(AXES),
            P(AXES),
            P(AXES),
            P(),
        ),
        out_specs=(
            P(GRP, AXES, None),
            P(GRP, AXES, None),
            P(GRP, AXES, None),
            P(AXES, None),
            P(AXES, None),
            P(AXES, None),
            P(AXES, None),
            P(AXES, None),
            P(AXES, None),
            P(AXES, None),
            P(AXES, None),
            P(AXES, None),
            P(AXES, None),
            P(AXES, None),
            P(AXES),
            P(AXES),
            P(AXES),
            P(),
        ),
        check_vma=False,
    )
```
